32 devices in a mesh: seq: 4 (over y, core), ctx: 8 (over z, x).
Axes of the slice: x: 2, y: 2, z: 4, core: 2. Of those that a mesh axis runs over, the one named last changes fastest.
Arguments:
- tokens: bfloat16 [4, 2048, 1152], P('seq', 'ctx'), may hold values from -6 to 6
- prefix: int32 [4], P('seq'), may hold values from 204 to 1024
- gain_one: bfloat16 [1152], P('seq'), may hold values from 0.5 to 1.5
- w_query: bfloat16 [1152, 1152], P('seq', 'ctx'), may hold values from -0.1875 to 0.1875
- w_key: bfloat16 [1152, 384], P('seq', 'ctx'), may hold values from -0.1875 to 0.1875
- value_weight: bfloat16 [1152, 384], P('seq', 'ctx'), may hold values from -0.1875 to 0.1875
- w_out: bfloat16 [1152, 1152], P('seq', 'ctx'), may hold values from -6 to 6
- gain_two: bfloat16 [1152], P('seq'), may hold values from 0.5 to 1.5
- w_gate: bfloat16 [1152, 3072], P('seq', 'ctx'), may hold values from -0.1875 to 0.1875
- w_up: bfloat16 [1152, 3072], P('seq', 'ctx'), may hold values from -0.1875 to 0.1875
- w_down: bfloat16 [3072, 1152], P('seq', 'ctx'), may hold values from -0.109375 to 0.109375
- cotangent: bfloat16 [4, 2048, 1152], P('seq', 'ctx'), may hold values from -6 to 6
Outputs:
- output: bfloat16 [4, 2048, 1152], P('seq', 'ctx')
- input_grad: float32 [4, 2048, 1152], P('seq', 'ctx')
- first_gain_gradient: float32 [1152], P('seq')
- grad_query: float32 [1152, 1152], P('seq', 'ctx')
- grad_key: float32 [1152, 384], P('seq', 'ctx')
- grad_value: float32 [1152, 384], P('seq', 'ctx')
- grad_out: float32 [1152, 1152], P('seq', 'ctx')
- second_gain_gradient: float32 [1152], P('seq')
- grad_gate: float32 [1152, 3072], P('seq', 'ctx')
- grad_up: float32 [1152, 3072], P('seq', 'ctx')
- grad_down: float32 [3072, 1152], P('seq', 'ctx')
The draws below stay inside these ranges and needn't reach their ends.
All inputs are finite; a program needn't handle non-finite values.
Results may differ from the reference program's by a relative error of at most 0.022.
Values may be sent and summed in bfloat16 or wider, within the bound.
A program may use at most 192 MiB of HBM per device.

```python
import math
import jax
import jax.numpy as jnp
from jax import lax

D = 1152
QUERY_HEADS = 18
KEY_VALUE_HEADS = 6
HEAD_SIZE = 64
FF = 3072
SEQ_LEN = 2048
SEQS = 4
QW = 1152
KVW = 384


def touch_ends(drawn, own_key, low, largest):
    longest = drawn.shape.index(max(drawn.shape))
    spots = []
    for shift in (0, 1):
        where = [jax.random.randint(jax.random.fold_in(own_key, axis), (), 0, length) for axis, length in enumerate(drawn.shape)]
        where[longest] = (where[longest] + shift) % drawn.shape[longest]
        spots.append(tuple(where))
    return drawn.at[spots[0]].set(low).at[spots[1]].set(largest)


def strengthened(values, stream_key, source, target, parts, factor):
    def block_of(dim):
        return (jnp.arange(values.shape[dim]) // (values.shape[dim] // parts)).reshape((-1,) + (1,) * (values.ndim - 1 - dim))

    one_side = jax.random.permutation(stream_key, parts)[block_of(target)]
    far = (block_of(target) + parts // 2) % parts
    return jnp.where((block_of(source) == one_side) | (block_of(source) == far), factor * values, values)


def level_of(own_key, shape, cuts, low, high):
    gain = 1.0
    for axis_at, blocks in cuts:
        draws = jax.random.uniform(jax.random.fold_in(jax.random.fold_in(own_key, 6), axis_at), (blocks,), jnp.float32, low / len(cuts), high / len(cuts))
        gain = gain * jnp.repeat(jnp.exp(draws), shape[axis_at] // blocks).reshape((-1,) + (1,) * (len(shape) - 1 - axis_at))
    return gain


def normal_values(own_key, extent, spread, bound, cuts=(), held_as=jnp.bfloat16):
    level = level_of(own_key, extent, cuts, -0.22, 0.18) if cuts else 1.0
    entries = jax.random.normal(own_key, extent, jnp.float32) * spread * level
    return jnp.minimum(jnp.maximum(entries, -bound), bound).astype(held_as)


def bell_draw_with(rng, shape, deviation, reach, pieces, heavy, kind=jnp.bfloat16):
    entries = deviation * jax.random.normal(rng, shape, jnp.float32)
    if pieces:
        entries = entries * level_of(rng, shape, pieces, -0.22, 0.18)
    return jnp.clip(strengthened(entries, jax.random.fold_in(rng, 3), *heavy), -reach, reach).astype(kind)


def setup_inputs(seed: int = 0) -> dict:
    keys = jax.random.split(jax.random.key(seed), 13)
    return {
        "tokens": normal_values(keys[0], (SEQS, SEQ_LEN, D), 1.0, 6.0, ((0, 4), (1, 8))),
        "prefix": touch_ends(jax.random.randint(keys[1], (SEQS,), SEQ_LEN // 10, SEQ_LEN // 2 + 1), jax.random.fold_in(keys[1], 1), SEQ_LEN // 10, (SEQ_LEN // 2 + 1) - 1).astype(jnp.int32),
        "gain_one": jnp.clip(1.0 + 0.1 * jax.random.normal(keys[2], (D,), jnp.float32), 0.5, 1.5).astype(jnp.bfloat16),
        "w_query": normal_values(keys[3], (D, QW), D ** -0.5, 0.1875, ((0, 4), (1, 8))),
        "w_key": normal_values(keys[4], (D, KVW), D ** -0.5, 0.1875, ((0, 4), (1, 8))),
        "value_weight": normal_values(keys[5], (D, KVW), D ** -0.5, 0.1875, ((0, 4), (1, 8))),
        "w_out": normal_values(keys[6], (QW, D), (max(1, QW // 1024)) ** -0.5, 6.0, ((0, 4), (1, 8))),
        "gain_two": jnp.clip(1.0 + 0.1 * jax.random.normal(keys[7], (D,), jnp.float32), 0.5, 1.5).astype(jnp.bfloat16),
        "w_gate": normal_values(keys[8], (D, FF), D ** -0.5, 0.1875, ((0, 4), (1, 8))),
        "w_up": normal_values(keys[9], (D, FF), D ** -0.5, 0.1875, ((0, 4), (1, 8))),
        "w_down": normal_values(keys[10], (FF, D), FF ** -0.5, 0.109375, ((0, 4), (1, 8))),
        "cotangent": bell_draw_with(keys[11], (SEQS, SEQ_LEN, D), 1.0, 6.0, ((0, 4), (1, 8)), (1, 2, 8, 2.0)),
    }


EPSILON = 1e-05
ROTARY_BASE = 10000.0
PRECISE = lax.Precision.HIGHEST

@jax.custom_vjp
def reduced_precision(v):
    return lax.optimization_barrier(v.astype(jnp.bfloat16)).astype(jnp.float32)

@jax.custom_vjp
def reduced_precision_backward(v):
    return v

def low_keep(v):
    return (reduced_precision(v), None)

def low_pass(kept, grad):
    return (grad,)

def back_keep(v):
    return (v, None)

def back_low(kept, grad):
    return (reduced_precision(grad),)
reduced_precision.defvjp(low_keep, low_pass)
reduced_precision_backward.defvjp(back_keep, back_low)

def product_result(left, right):
    return jnp.dot(left, right, precision=PRECISE, preferred_element_type=jnp.float32)

def rms_norm(values_in, gain_vec):
    factor = lax.rsqrt(lax.optimization_barrier(jnp.mean(values_in * values_in, axis=-1, keepdims=True)) + EPSILON)
    return values_in * factor * gain_vec

def rotary_tables(positions, head_width):
    half_width = head_width // 2
    frequency = ROTARY_BASE ** (-jnp.arange(half_width, dtype=jnp.float32) * 2.0 / head_width)
    angles = positions.astype(jnp.float32)[:, None] * frequency[None, :]
    return (jnp.cos(angles)[:, None, :], jnp.sin(angles)[:, None, :])

def apply_rotation(values_in, cosine_table, sine_values):
    half_width = values_in.shape[-1] // 2
    first = values_in[..., :half_width]
    second = values_in[..., half_width:]
    return jnp.concatenate([first * cosine_table - second * sine_values, second * cosine_table + first * sine_values], axis=-1)

def layer(seq_tokens, prefix_len, gain_one, w_query, w_key, value_weight, w_out, gain_two, w_gate, w_up, w_down):
    length_total = seq_tokens.shape[0]
    queries_per_key_head = QUERY_HEADS // KEY_VALUE_HEADS
    normalized_rows = reduced_precision(rms_norm(seq_tokens, gain_one))
    query_pre = reduced_precision_backward(product_result(normalized_rows, w_query))
    key_prerotation = reduced_precision_backward(product_result(normalized_rows, w_key))
    value_rows = reduced_precision(reduced_precision_backward(product_result(normalized_rows, value_weight))).reshape(length_total, KEY_VALUE_HEADS, HEAD_SIZE)
    cosine_table, sine_values = rotary_tables(jnp.arange(length_total, dtype=jnp.int32), HEAD_SIZE)
    query_rows = reduced_precision(apply_rotation(query_pre.reshape(length_total, QUERY_HEADS, HEAD_SIZE), cosine_table, sine_values))
    key_rotated = reduced_precision(apply_rotation(key_prerotation.reshape(length_total, KEY_VALUE_HEADS, HEAD_SIZE), cosine_table, sine_values))
    rows_per_block = math.gcd(length_total, 512)
    number_of_blocks = length_total // rows_per_block
    key_place = jnp.arange(length_total, dtype=jnp.int32)
    score_scale = HEAD_SIZE ** (-0.5)

    def attend_block(block_item):
        query_block, first_row = block_item
        query_place = first_row + jnp.arange(rows_per_block, dtype=jnp.int32)
        scores = reduced_precision_backward(jnp.einsum('qhgd,khd->hgqk', query_block, key_rotated, precision=PRECISE) * score_scale)
        visible = (key_place[None, :] <= query_place[:, None]) | (key_place[None, :] < prefix_len)
        scores = jnp.where(visible[None, None], scores, -1e+30)
        probs = jax.nn.softmax(scores, axis=-1)
        return jnp.einsum('hgqk,khd->qhgd', reduced_precision(probs), value_rows, precision=PRECISE)
    block_list = query_rows.reshape(number_of_blocks, rows_per_block, KEY_VALUE_HEADS, queries_per_key_head, HEAD_SIZE)
    firsts = jnp.arange(number_of_blocks, dtype=jnp.int32) * rows_per_block
    attention_result = lax.map(jax.checkpoint(attend_block), (block_list, firsts))
    attention_result = reduced_precision(reduced_precision_backward(attention_result.reshape(length_total, QUERY_HEADS * HEAD_SIZE)))
    mixed_output = seq_tokens + reduced_precision_backward(product_result(attention_result, w_out))
    normalized_second = reduced_precision(rms_norm(mixed_output, gain_two))
    gate = reduced_precision_backward(product_result(normalized_second, w_gate))
    up_part = reduced_precision_backward(product_result(normalized_second, w_up))
    hidden = reduced_precision(jax.nn.silu(gate) * up_part)
    return mixed_output + reduced_precision_backward(product_result(hidden, w_down))

def reference(tokens, prefix, gain_one, w_query, w_key, value_weight, w_out, gain_two, w_gate, w_up, w_down, cotangent):
    weights = (gain_one.astype(jnp.float32), w_query.astype(jnp.float32), w_key.astype(jnp.float32), value_weight.astype(jnp.float32), w_out.astype(jnp.float32), gain_two.astype(jnp.float32), w_gate.astype(jnp.float32), w_up.astype(jnp.float32), w_down.astype(jnp.float32))
    zeros_init = tuple((jnp.zeros(weight.shape, jnp.float32) for weight in weights))

    def per_seq(totals, seq_item):
        seq_tokens, prefix_len, seq_cot = seq_item

        def forward(input_rows, weight_set):
            return layer(input_rows, prefix_len, *weight_set)
        result, pullback = jax.vjp(forward, seq_tokens.astype(jnp.float32), weights)
        input_part, weight_grads = pullback(seq_cot.astype(jnp.float32))
        totals = tuple((total + grad_part for total, grad_part in zip(totals, weight_grads)))
        return (totals, (result.astype(jnp.bfloat16), input_part))
    totals, outputs = lax.scan(per_seq, zeros_init, (tokens, prefix, cotangent))
    return (outputs[0], outputs[1], totals[0], totals[1], totals[2], totals[3], totals[4], totals[5], totals[6], totals[7], totals[8])
```

```python
import functools

import jax
import jax.numpy as jnp
from jax import lax
from jax.experimental import pallas as pl
from jax.experimental.pallas import tpu as pltpu
from jax.sharding import PartitionSpec as P

QUERY_HEADS = 18
KEY_VALUE_HEADS = 6
HEAD_SIZE = 64


EPSILON = 1e-05
ROTARY_BASE = 10000.0

LANES = 128
Z_SIZE = 4
FLIPS = ((0, 0, 0), (0, 0, 1), (0, 1, 0), (0, 1, 1), (1, 0, 0), (1, 0, 1), (1, 1, 0), (1, 1, 1))
VMEM_LIMIT = 66_000_000
F32 = jnp.float32
BF16 = jnp.bfloat16
NT = (((1,), (1,)), ((), ()))


def rotary_tables(positions, head_width):
    half_width = head_width // 2
    frequency = ROTARY_BASE ** (-jnp.arange(half_width, dtype=jnp.float32) * 2.0 / head_width)
    angles = positions.astype(jnp.float32)[:, None] * frequency[None, :]
    return (jnp.cos(angles)[:, None, :], jnp.sin(angles)[:, None, :])


def apply_rotation(values_in, cosine_table, sine_values):
    half_width = values_in.shape[-1] // 2
    first = values_in[..., :half_width]
    second = values_in[..., half_width:]
    return jnp.concatenate(
        [first * cosine_table - second * sine_values, second * cosine_table + first * sine_values],
        axis=-1,
    )


def inverse_rotation(grads_in, cosine_table, sine_values):
    half_width = grads_in.shape[-1] // 2
    first = grads_in[..., :half_width]
    second = grads_in[..., half_width:]
    return jnp.concatenate(
        [first * cosine_table + second * sine_values, second * cosine_table - first * sine_values],
        axis=-1,
    )


def gather_weights(w_query, w_key, value_weight, w_out, w_gate, w_up, w_down, gain_one, gain_two):
    columns = (
        lax.all_gather(w_query, "ctx", axis=1, tiled=True),
        lax.all_gather(w_key, "ctx", axis=1, tiled=True),
        lax.all_gather(value_weight, "ctx", axis=1, tiled=True),
        lax.all_gather(w_out, "ctx", axis=1, tiled=True),
        lax.all_gather(w_gate, "ctx", axis=1, tiled=True),
        lax.all_gather(w_up, "ctx", axis=1, tiled=True),
        lax.all_gather(w_down, "ctx", axis=1, tiled=True),
    )
    return (
        lax.all_gather(columns[0], "seq", axis=0, tiled=True),
        lax.all_gather(columns[1], "seq", axis=0, tiled=True),
        lax.all_gather(columns[2], "seq", axis=0, tiled=True),
        lax.all_gather(columns[3], "seq", axis=0, tiled=True),
        lax.all_gather(columns[4], "seq", axis=0, tiled=True),
        lax.all_gather(columns[5], "seq", axis=0, tiled=True),
        lax.all_gather(columns[6], "seq", axis=0, tiled=True),
        lax.all_gather(gain_one, "seq", axis=0, tiled=True),
        lax.all_gather(gain_two, "seq", axis=0, tiled=True),
    )


def gather_pairs(key_rotated, value_reduced):
    return (
        lax.all_gather(key_rotated, "ctx", axis=1, tiled=True),
        lax.all_gather(value_reduced, "ctx", axis=1, tiled=True),
    )


def head_major(whole_result, sequence_count):
    sequence_length = whole_result.shape[1]
    return (
        whole_result.reshape(sequence_count, sequence_length, KEY_VALUE_HEADS, HEAD_SIZE)
        .transpose(0, 2, 1, 3)
        .reshape(sequence_count * KEY_VALUE_HEADS, sequence_length, HEAD_SIZE)
    )


def per_device(
    tokens,
    prefix,
    gain_one,
    w_query,
    w_key,
    value_weight,
    w_out,
    gain_two,
    w_gate,
    w_up,
    w_down,
    cotangent,
):
    sequence_count, token_local, model_width = tokens.shape
    sequence_length = token_local * lax.axis_size("ctx")
    number_of_rows = sequence_count * token_local
    queries_per_key_head = QUERY_HEADS // KEY_VALUE_HEADS
    score_scale = HEAD_SIZE ** (-0.5)
    gathered = gather_weights(
        w_query, w_key, value_weight, w_out, w_gate, w_up, w_down, gain_one, gain_two
    )
    full_query, full_key, full_value, full_out, full_gate, full_up, full_down = gathered[:7]
    first_norm = gathered[7].astype(jnp.float32)
    second_norm = gathered[8].astype(jnp.float32)
    input_rows = tokens.reshape(number_of_rows, model_width).astype(jnp.float32)
    first_factor = lax.rsqrt(jnp.mean(input_rows * input_rows, axis=-1, keepdims=True) + EPSILON)
    first_normalized_input = input_rows * first_factor
    normalized_rows = (first_normalized_input * first_norm).astype(jnp.bfloat16)
    query_pre = jnp.dot(normalized_rows, full_query, preferred_element_type=jnp.float32)
    key_prerotation = jnp.dot(normalized_rows, full_key, preferred_element_type=jnp.float32)
    value_reduced = jnp.dot(normalized_rows, full_value, preferred_element_type=jnp.float32).astype(
        jnp.bfloat16
    )
    positions = lax.axis_index("ctx") * token_local + jnp.arange(token_local, dtype=jnp.int32)
    cosine_table, sine_values = rotary_tables(positions, HEAD_SIZE)
    query_rows = apply_rotation(
        query_pre.reshape(sequence_count, token_local, QUERY_HEADS, HEAD_SIZE),
        cosine_table,
        sine_values,
    ).astype(jnp.bfloat16)
    key_rotated = apply_rotation(
        key_prerotation.reshape(sequence_count, token_local, KEY_VALUE_HEADS, HEAD_SIZE),
        cosine_table,
        sine_values,
    ).astype(jnp.bfloat16)
    key_rotated = key_rotated.reshape(sequence_count, token_local, KEY_VALUE_HEADS * HEAD_SIZE)
    value_reduced = value_reduced.reshape(sequence_count, token_local, KEY_VALUE_HEADS * HEAD_SIZE)
    keys_all, values_all = gather_pairs(key_rotated, value_reduced)
    query_block_list = query_rows.reshape(
        sequence_count, token_local, KEY_VALUE_HEADS, queries_per_key_head, HEAD_SIZE
    ).transpose(0, 2, 3, 1, 4)
    query_block_list = query_block_list.reshape(
        sequence_count * KEY_VALUE_HEADS, queries_per_key_head, token_local, HEAD_SIZE
    )
    key_blocks = head_major(keys_all, sequence_count)
    value_blocks = head_major(values_all, sequence_count)
    prefix_repeated = jnp.repeat(prefix, KEY_VALUE_HEADS)
    key_place = jnp.arange(sequence_length, dtype=jnp.int32)

    def visible_for(prefix_len):
        return (key_place[None, :] <= positions[:, None]) | (key_place[None, :] < prefix_len)

    def attend(block_item):
        query_block, key_block, value_block, prefix_len = block_item
        scores = (
            jnp.einsum("gqd,kd->gqk", query_block, key_block, preferred_element_type=jnp.float32)
            * score_scale
        )
        scores = jnp.where(visible_for(prefix_len)[None], scores, -1e30)
        row_max = jnp.max(scores, axis=-1, keepdims=True)
        expo = jnp.exp(scores - row_max)
        total = jnp.sum(expo, axis=-1, keepdims=True)
        probs_low = (expo / total).astype(jnp.bfloat16)
        result = jnp.einsum(
            "gqk,kd->gqd", probs_low, value_block, preferred_element_type=jnp.float32
        )
        return (result.astype(jnp.bfloat16), (row_max + jnp.log(total))[..., 0])

    attention_result_blocks, log_totals = lax.map(
        attend, (query_block_list, key_blocks, value_blocks, prefix_repeated)
    )
    attention_result = attention_result_blocks.reshape(
        sequence_count, KEY_VALUE_HEADS, queries_per_key_head, token_local, HEAD_SIZE
    ).transpose(0, 3, 1, 2, 4)
    attention_result = attention_result.reshape(number_of_rows, QUERY_HEADS * HEAD_SIZE)
    mixed_output = input_rows + jnp.dot(
        attention_result, full_out, preferred_element_type=jnp.float32
    )
    second_factor = lax.rsqrt(
        jnp.mean(mixed_output * mixed_output, axis=-1, keepdims=True) + EPSILON
    )
    second_normalized_input = mixed_output * second_factor
    normalized_second = (second_normalized_input * second_norm).astype(jnp.bfloat16)
    gate = jnp.dot(normalized_second, full_gate, preferred_element_type=jnp.float32)
    up_part = jnp.dot(normalized_second, full_up, preferred_element_type=jnp.float32)
    sigmoid_gate = jax.nn.sigmoid(gate)
    activated = gate * sigmoid_gate
    hidden = (activated * up_part).astype(jnp.bfloat16)
    result_rows = mixed_output + jnp.dot(hidden, full_down, preferred_element_type=jnp.float32)
    output = result_rows.astype(jnp.bfloat16).reshape(sequence_count, token_local, model_width)
    gathered = gather_weights(
        w_query, w_key, value_weight, w_out, w_gate, w_up, w_down, gain_one, gain_two
    )
    full_query, full_key, full_value, full_out, full_gate, full_up, full_down = gathered[:7]
    grad_rows_in = cotangent.reshape(number_of_rows, model_width)
    grad_down = jnp.dot(hidden.T, grad_rows_in, preferred_element_type=jnp.float32)
    dhidden = jnp.dot(grad_rows_in, full_down.T, preferred_element_type=jnp.float32)
    dgate = (dhidden * up_part * sigmoid_gate * (1.0 + gate * (1.0 - sigmoid_gate))).astype(
        jnp.bfloat16
    )
    dup_part = (dhidden * activated).astype(jnp.bfloat16)
    grad_gate = jnp.dot(normalized_second.T, dgate, preferred_element_type=jnp.float32)
    grad_up = jnp.dot(normalized_second.T, dup_part, preferred_element_type=jnp.float32)
    normalized_second_grad = jnp.dot(dgate, full_gate.T, preferred_element_type=jnp.float32)
    normalized_second_grad = normalized_second_grad + jnp.dot(
        dup_part, full_up.T, preferred_element_type=jnp.float32
    )
    second_gain_gradient = jnp.sum(normalized_second_grad * second_normalized_input, axis=0)
    second_scaled = normalized_second_grad * second_norm
    dmixed = grad_rows_in.astype(jnp.float32) + second_factor * (
        second_scaled
        - second_normalized_input
        * jnp.mean(second_scaled * second_normalized_input, axis=-1, keepdims=True)
    )
    dproj = dmixed.astype(jnp.bfloat16)
    grad_out = jnp.dot(attention_result.T, dproj, preferred_element_type=jnp.float32)
    attention_result_grad = jnp.dot(dproj, full_out.T, preferred_element_type=jnp.float32).astype(
        jnp.bfloat16
    )
    attention_result_block_grads = attention_result_grad.reshape(
        sequence_count, token_local, KEY_VALUE_HEADS, queries_per_key_head, HEAD_SIZE
    ).transpose(0, 2, 3, 1, 4)
    attention_result_block_grads = attention_result_block_grads.reshape(
        sequence_count * KEY_VALUE_HEADS, queries_per_key_head, token_local, HEAD_SIZE
    )
    keys_all, values_all = gather_pairs(key_rotated, value_reduced)
    key_blocks = head_major(keys_all, sequence_count)
    value_blocks = head_major(values_all, sequence_count)

    def attend_back(block_item):
        query_block, key_block, value_block, prefix_len, log_total, dout_block = block_item
        scores = (
            jnp.einsum("gqd,kd->gqk", query_block, key_block, preferred_element_type=jnp.float32)
            * score_scale
        )
        visible = visible_for(prefix_len)[None]
        probs = jnp.where(
            visible, jnp.exp(jnp.where(visible, scores, -1e30) - log_total[..., None]), 0.0
        )
        dvalues = jnp.einsum(
            "gqk,gqd->kd",
            probs.astype(jnp.bfloat16),
            dout_block,
            preferred_element_type=jnp.float32,
        )
        dprobs = jnp.einsum(
            "gqd,kd->gqk", dout_block, value_block, preferred_element_type=jnp.float32
        )
        dscores = (probs * (dprobs - jnp.sum(probs * dprobs, axis=-1, keepdims=True))).astype(
            jnp.bfloat16
        )
        dquery = (
            jnp.einsum("gqk,kd->gqd", dscores, key_block, preferred_element_type=jnp.float32)
            * score_scale
        )
        dkeys = (
            jnp.einsum("gqk,gqd->kd", dscores, query_block, preferred_element_type=jnp.float32)
            * score_scale
        )
        return (dquery, dkeys, dvalues)

    query_block_grads, key_block_grads, value_block_grads = lax.map(
        attend_back,
        (
            query_block_list,
            key_blocks,
            value_blocks,
            prefix_repeated,
            log_totals,
            attention_result_block_grads,
        ),
    )
    key_grads_combined = key_block_grads.reshape(
        sequence_count, KEY_VALUE_HEADS, sequence_length, HEAD_SIZE
    ).transpose(0, 2, 1, 3)
    key_grads_combined = key_grads_combined.reshape(
        sequence_count, sequence_length, KEY_VALUE_HEADS * HEAD_SIZE
    )
    value_grads_combined = value_block_grads.reshape(
        sequence_count, KEY_VALUE_HEADS, sequence_length, HEAD_SIZE
    ).transpose(0, 2, 1, 3)
    value_grads_combined = value_grads_combined.reshape(
        sequence_count, sequence_length, KEY_VALUE_HEADS * HEAD_SIZE
    )
    key_grads_local, value_grads_local = (
        lax.psum_scatter(
            key_grads_combined.astype(jnp.bfloat16), "ctx", scatter_dimension=1, tiled=True
        ).astype(jnp.float32),
        lax.psum_scatter(
            value_grads_combined.astype(jnp.bfloat16), "ctx", scatter_dimension=1, tiled=True
        ).astype(jnp.float32),
    )
    key_prerotation_grad = inverse_rotation(
        key_grads_local.reshape(sequence_count, token_local, KEY_VALUE_HEADS, HEAD_SIZE),
        cosine_table,
        sine_values,
    )
    key_prerotation_grad = key_prerotation_grad.astype(jnp.bfloat16).reshape(
        number_of_rows, KEY_VALUE_HEADS * HEAD_SIZE
    )
    value_reduced_grad = value_grads_local.astype(jnp.bfloat16).reshape(
        number_of_rows, KEY_VALUE_HEADS * HEAD_SIZE
    )
    query_row_grads = query_block_grads.reshape(
        sequence_count, KEY_VALUE_HEADS, queries_per_key_head, token_local, HEAD_SIZE
    ).transpose(0, 3, 1, 2, 4)
    query_row_grads = query_row_grads.reshape(sequence_count, token_local, QUERY_HEADS, HEAD_SIZE)
    dquery_pre = (
        inverse_rotation(query_row_grads, cosine_table, sine_values)
        .astype(jnp.bfloat16)
        .reshape(number_of_rows, QUERY_HEADS * HEAD_SIZE)
    )
    grad_query = jnp.dot(normalized_rows.T, dquery_pre, preferred_element_type=jnp.float32)
    grad_key = jnp.dot(normalized_rows.T, key_prerotation_grad, preferred_element_type=jnp.float32)
    grad_value = jnp.dot(normalized_rows.T, value_reduced_grad, preferred_element_type=jnp.float32)
    normalized_grad = jnp.dot(dquery_pre, full_query.T, preferred_element_type=jnp.float32)
    normalized_grad = normalized_grad + jnp.dot(
        key_prerotation_grad, full_key.T, preferred_element_type=jnp.float32
    )
    normalized_grad = normalized_grad + jnp.dot(
        value_reduced_grad, full_value.T, preferred_element_type=jnp.float32
    )
    first_gain_gradient = jnp.sum(normalized_grad * first_normalized_input, axis=0)
    first_scaled = normalized_grad * first_norm
    input_grad = dmixed + first_factor * (
        first_scaled
        - first_normalized_input
        * jnp.mean(first_scaled * first_normalized_input, axis=-1, keepdims=True)
    )
    input_grad = input_grad.reshape(sequence_count, token_local, model_width)
    partial_value = (
        lax.psum_scatter(
            grad_query.astype(jnp.bfloat16), "seq", scatter_dimension=0, tiled=True
        ).astype(jnp.float32),
        lax.psum_scatter(
            grad_key.astype(jnp.bfloat16), "seq", scatter_dimension=0, tiled=True
        ).astype(jnp.float32),
        lax.psum_scatter(
            grad_value.astype(jnp.bfloat16), "seq", scatter_dimension=0, tiled=True
        ).astype(jnp.float32),
        lax.psum_scatter(
            grad_out.astype(jnp.bfloat16), "seq", scatter_dimension=0, tiled=True
        ).astype(jnp.float32),
        lax.psum_scatter(
            grad_gate.astype(jnp.bfloat16), "seq", scatter_dimension=0, tiled=True
        ).astype(jnp.float32),
        lax.psum_scatter(
            grad_up.astype(jnp.bfloat16), "seq", scatter_dimension=0, tiled=True
        ).astype(jnp.float32),
        lax.psum_scatter(
            grad_down.astype(jnp.bfloat16), "seq", scatter_dimension=0, tiled=True
        ).astype(jnp.float32),
        lax.psum_scatter(
            first_gain_gradient.astype(jnp.bfloat16), "seq", scatter_dimension=0, tiled=True
        ).astype(jnp.float32),
        lax.psum_scatter(
            second_gain_gradient.astype(jnp.bfloat16), "seq", scatter_dimension=0, tiled=True
        ).astype(jnp.float32),
    )
    owned = (
        lax.psum_scatter(
            partial_value[0].astype(jnp.bfloat16), "ctx", scatter_dimension=1, tiled=True
        ).astype(jnp.float32),
        lax.psum_scatter(
            partial_value[1].astype(jnp.bfloat16), "ctx", scatter_dimension=1, tiled=True
        ).astype(jnp.float32),
        lax.psum_scatter(
            partial_value[2].astype(jnp.bfloat16), "ctx", scatter_dimension=1, tiled=True
        ).astype(jnp.float32),
        lax.psum_scatter(
            partial_value[3].astype(jnp.bfloat16), "ctx", scatter_dimension=1, tiled=True
        ).astype(jnp.float32),
        lax.psum_scatter(
            partial_value[4].astype(jnp.bfloat16), "ctx", scatter_dimension=1, tiled=True
        ).astype(jnp.float32),
        lax.psum_scatter(
            partial_value[5].astype(jnp.bfloat16), "ctx", scatter_dimension=1, tiled=True
        ).astype(jnp.float32),
        lax.psum_scatter(
            partial_value[6].astype(jnp.bfloat16), "ctx", scatter_dimension=1, tiled=True
        ).astype(jnp.float32),
    )
    gains_owned = lax.psum((partial_value[7], partial_value[8]), "ctx")
    final_grads = owned + gains_owned
    return (
        output,
        input_grad,
        final_grads[7],
        final_grads[0],
        final_grads[1],
        final_grads[2],
        final_grads[3],
        final_grads[8],
        final_grads[4],
        final_grads[5],
        final_grads[6],
    )


def permute_pairs(axis, step):
    pairs = []
    for seq_at in range(4):
        for ctx_at in range(8):
            target_seq, target_ctx = seq_at, ctx_at
            if axis == "core":
                target_seq = seq_at ^ 1
            elif axis == "y":
                target_seq = seq_at ^ 2
            elif axis == "x":
                target_ctx = ctx_at ^ 1
            elif axis == "z":
                target_ctx = (ctx_at + 2 * step) % 8
            elif axis == "z_flip":
                target_ctx = ctx_at ^ (2 * step)
            pairs.append((seq_at * 8 + ctx_at, target_seq * 8 + target_ctx))
    return pairs


def hop(array, axis, step=1):
    return lax.ppermute(array, ("seq", "ctx"), permute_pairs(axis, step))


def gather_shards(shard, order):
    held = {(0, 0, 0): shard}
    for axis in order:
        if axis == "z":
            for place, array in list(held.items()):
                ring = [array]
                for _ in range(Z_SIZE - 1):
                    ring.append(hop(ring[-1], "z", 1))
                held[place] = jnp.stack(ring)
        else:
            at = ("x", "y", "core").index(axis)
            for place, array in list(held.items()):
                held[place[:at] + (1,) + place[at + 1 :]] = hop(array, axis)
    return [held[flip] for flip in FLIPS]


def add_pair(left, right):
    return (left.astype(F32) + right.astype(F32)).astype(BF16)


def scatter_ring(array):
    total = array[Z_SIZE - 1]
    for t in range(Z_SIZE - 2, -1, -1):
        arrived = hop(total, "z", -1)
        if t:
            total = add_pair(array[t], arrived)
        else:
            total = array[0].astype(F32) + arrived.astype(F32)
    return total


def scatter_rest(near, far, first):
    second = "x" if first == "y" else "y"
    arrived = hop(far, first)
    far_two = add_pair(near[:, 1], arrived[:, 1])
    near_two = add_pair(near[:, 0], arrived[:, 0])
    return scatter_ring(add_pair(near_two, hop(far_two, second)))


def sum_everywhere(vector):
    for axis, step in (("core", 1), ("y", 1), ("x", 1), ("z_flip", 1), ("z_flip", 2)):
        vector = vector + hop(vector, axis, step)
    return vector


def my_place():
    seq_at, ctx_at = lax.axis_index("seq"), lax.axis_index("ctx")
    return ctx_at // 2, lax.rem(ctx_at, 2), seq_at // 2, lax.rem(seq_at, 2)


def flipped(at, flip):
    return 1 - at if flip else at


def block_copies(arrays, buffer, sems, column_major):
    z, x, y, core = my_place()
    copies = {}
    for number, (dx, dy, dcore) in enumerate(FLIPS):
        row, column = flipped(y, dy) * 2 + flipped(core, dcore), flipped(x, dx)
        for t in range(Z_SIZE):
            ctx_block = lax.rem(z - t + Z_SIZE, Z_SIZE) * 2 + column
            target = buffer.at[ctx_block, row] if column_major else buffer.at[row, ctx_block]
            copies[t, dx, dy, dcore] = pltpu.make_async_copy(
                arrays[number].at[t], target, sems.at[number * Z_SIZE + t]
            )
    return copies


def lane_ids(rows):
    return lax.broadcasted_iota(jnp.int32, (rows, LANES), 1)


def rotate_halves(tile, cosine, sine):
    lower = lax.rem(lane_ids(tile.shape[0]), HEAD_SIZE) < HEAD_SIZE // 2
    swapped = jnp.where(
        lower, pltpu.roll(tile, LANES - HEAD_SIZE // 2, 1), pltpu.roll(tile, HEAD_SIZE // 2, 1)
    )
    return tile * cosine + swapped * sine


def pair_tiles(natural):
    lower = lane_ids(natural[0].shape[0]) < HEAD_SIZE
    tiles = []
    for pair in range(3):
        for member in range(3):
            one, two = 6 * pair + member, 6 * pair + 3 + member
            left, right = natural[one // 2], natural[two // 2]
            if one % 2:
                left, right = pltpu.roll(left, HEAD_SIZE, 1), pltpu.roll(right, HEAD_SIZE, 1)
            tiles.append(jnp.where(lower, left, right))
    return tiles


def natural_tiles(paired):
    lower = lane_ids(paired[0].shape[0]) < HEAD_SIZE
    tiles = []
    for at in range(9):
        sides = []
        for side in range(2):
            head = 2 * at + side
            tile = paired[head // 6 * 3 + head % 3]
            if (head % 6) // 3 != side:
                tile = pltpu.roll(tile, HEAD_SIZE, 1)
            sides.append(tile)
        tiles.append(jnp.where(lower, sides[0], sides[1]))
    return tiles


def normalized(rows):
    factor = lax.rsqrt(jnp.mean(rows * rows, axis=-1, keepdims=True) + EPSILON)
    return factor, rows * factor


def project_kernel(tokens, gain, cosine, sine, *refs):
    weights, (query_out, pair_out, buffer, pieces, wide, sems) = refs[:8], refs[8:]
    z, x, _, _ = my_place()
    copies = block_copies(weights, buffer, sems, True)
    for copy in copies.values():
        copy.start()
    _, hat = normalized(tokens[...].astype(F32))
    rows = (hat * gain[...]).astype(BF16)
    for t in range(Z_SIZE):
        for dx in range(2):
            for dy in range(2):
                for dcore in range(2):
                    copies[t, dx, dy, dcore].wait()
            ctx_block = lax.rem(z - t + Z_SIZE, Z_SIZE) * 2 + flipped(x, dx)
            matrix = buffer[ctx_block].reshape(tokens.shape[1], buffer.shape[3])
            pieces[ctx_block] = jnp.dot(rows, matrix, preferred_element_type=F32)
    q_part, kv_part = 144, 48
    for at in range(8):
        wide[:, at * q_part : (at + 1) * q_part] = pieces[at, :, :q_part]
        wide[:, 1152 + at * kv_part : 1152 + (at + 1) * kv_part] = pieces[at, :, q_part : q_part + kv_part]
        wide[:, 1536 + at * kv_part : 1536 + (at + 1) * kv_part] = pieces[at, :, q_part + kv_part :]
    cos_tile, sin_tile = cosine[...], sine[...]
    natural = [
        rotate_halves(wide[:, at * LANES : (at + 1) * LANES], cos_tile, sin_tile) * HEAD_SIZE**-0.5
        for at in range(9)
    ]
    for at, tile in enumerate(pair_tiles(natural)):
        query_out[at] = tile.astype(BF16)
    for pair in range(3):
        key_tile = wide[:, 1152 + pair * LANES : 1152 + (pair + 1) * LANES]
        pair_out[:, 2 * pair * LANES : (2 * pair + 1) * LANES] = rotate_halves(
            key_tile, cos_tile, sin_tile
        ).astype(BF16)
        pair_out[:, (2 * pair + 1) * LANES : (2 * pair + 2) * LANES] = wide[
            :, 1536 + pair * LANES : 1536 + (pair + 1) * LANES
        ].astype(BF16)


def vmem_specs(count):
    return [pl.BlockSpec(memory_space=pltpu.VMEM)] * count


def any_specs(count):
    return [pl.BlockSpec(memory_space=pl.ANY)] * count


def cost(flops, moved, transcendentals=0):
    return pl.CostEstimate(flops=int(flops), bytes_accessed=int(moved), transcendentals=int(transcendentals))


def params():
    return pltpu.CompilerParams(vmem_limit_bytes=VMEM_LIMIT)


def project(tokens, gain, cosine, sine, weights):
    rows, width = tokens.shape
    _, shard_rows, shard_width = weights[0].shape
    return pl.pallas_call(
        project_kernel,
        out_shape=(
            jax.ShapeDtypeStruct((9, rows, LANES), BF16),
            jax.ShapeDtypeStruct((rows, 768), BF16),
        ),
        in_specs=vmem_specs(4) + any_specs(8),
        out_specs=tuple(vmem_specs(2)),
        scratch_shapes=[
            pltpu.VMEM((8, 4, shard_rows, shard_width), BF16),
            pltpu.VMEM((8, rows, shard_width), F32),
            pltpu.VMEM((rows, 1920), F32),
            pltpu.SemaphoreType.DMA((32,)),
        ],
        compiler_params=params(),
        cost_estimate=cost(2 * rows * width * 1920, 6e6),
        name="project",
    )(tokens, gain, cosine, sine, *weights)


def slot_start(number):
    z, x, _, _ = my_place()
    return (lax.rem(z - number // 2 + Z_SIZE, Z_SIZE) * 2 + flipped(x, number % 2)) * 256


def masked_pair(block, half, other):
    inside = (lane_ids(block.shape[0]) < HEAD_SIZE) == (half == 0)
    return jnp.where(inside, block.astype(F32), other)


def attend_kernel(query, limit, *refs):
    slots, (out, log_total, keys, values, scores) = refs[:8], refs[8:]

    @pl.when(pl.program_id(1) == 0)
    def _():
        for at in range(8):
            for half in range(2):
                keys[half, at] = masked_pair(slots[at][:, :LANES], half, 0.0).astype(BF16)
                values[half, at] = masked_pair(slots[at][:, LANES:], half, 1.0).T.astype(BF16)

    rows = query.shape[1]
    tile = query[0]
    key_ids = lax.broadcasted_iota(jnp.int32, (256, rows), 0)
    parts = []
    for half in range(2):
        top = None
        for at in range(8):
            part = lax.dot_general(keys[half, at], tile, NT, preferred_element_type=F32)
            part = jnp.where(key_ids < limit[...] - slot_start(at), part, -1e30)
            scores[at] = part
            block_top = jnp.max(part, axis=0, keepdims=True)
            top = block_top if top is None else jnp.maximum(top, block_top)
        total = jnp.zeros((LANES, rows), F32)
        for at in range(8):
            weight = jnp.exp(scores[at] - top).astype(BF16)
            total = total + jnp.dot(values[half, at], weight, preferred_element_type=F32)
        norm = total[HEAD_SIZE : HEAD_SIZE + 1] if half == 0 else total[:1]
        log_total[0, half : half + 1, :] = top + jnp.log(norm)
        own = total[:HEAD_SIZE] if half == 0 else total[HEAD_SIZE:]
        parts.append(own / norm)
    out[0] = jnp.concatenate(parts, axis=0).T.astype(BF16)


def attend(query, limit, slots):
    rows = query.shape[1]
    return pl.pallas_call(
        attend_kernel,
        grid=(3, 3),
        out_shape=(
            jax.ShapeDtypeStruct((9, rows, LANES), BF16),
            jax.ShapeDtypeStruct((9, 2, rows), F32),
        ),
        in_specs=[
            pl.BlockSpec((1, rows, LANES), lambda p, g: (3 * p + g, 0, 0)),
            pl.BlockSpec((1, rows), lambda p, g: (0, 0)),
        ]
        + [pl.BlockSpec((256, 2 * LANES), lambda p, g: (0, p))] * 8,
        out_specs=(
            pl.BlockSpec((1, rows, LANES), lambda p, g: (3 * p + g, 0, 0)),
            pl.BlockSpec((1, 2, rows), lambda p, g: (3 * p + g, 0, 0)),
        ),
        scratch_shapes=[
            pltpu.VMEM((2, 8, 256, LANES), BF16),
            pltpu.VMEM((2, 8, LANES, 256), BF16),
            pltpu.VMEM((8, 256, rows), F32),
        ],
        compiler_params=params(),
        cost_estimate=cost(4 * 18 * rows * 2048 * 128 * 4, 6e6, 18 * rows * 2048),
        name="attend",
    )(query, limit, *slots)


def attend_back_kernel(query, attended, grad, log_total, limit, cosine, sine, *refs):
    slots, near, far = refs[:8], refs[8], refs[9:13]
    query_grad, keys, keys_turned, values, key_sum, value_sum = refs[13:]

    @pl.when(pl.program_id(1) == 0)
    def _():
        key_sum[...] = jnp.zeros_like(key_sum)
        value_sum[...] = jnp.zeros_like(value_sum)
        for at in range(8):
            for half in range(2):
                masked = masked_pair(slots[at][:, :LANES], half, 0.0)
                keys[half, at] = masked.astype(BF16)
                keys_turned[half, at] = masked.T.astype(BF16)
                values[half, at] = masked_pair(slots[at][:, LANES:], half, 0.0).astype(BF16)

    rows = query.shape[1]
    tile, grad_tile = query[0], grad[0]
    product = (attended[0].astype(F32) * grad_tile.astype(F32)).T
    key_ids = lax.broadcasted_iota(jnp.int32, (256, rows), 0)
    turned = jnp.zeros((LANES, rows), F32)
    for half in range(2):
        own = slice(half * HEAD_SIZE, (half + 1) * HEAD_SIZE)
        shift = jnp.sum(product[own], axis=0, keepdims=True)
        log_row = log_total[0, half : half + 1, :]
        query_half = masked_pair(tile, half, 0.0).astype(BF16)
        grad_half = masked_pair(grad_tile, half, 0.0).astype(BF16)
        for at in range(8):
            part = lax.dot_general(keys[half, at], tile, NT, preferred_element_type=F32)
            part = jnp.where(key_ids < limit[...] - slot_start(at), part, -1e30)
            probs = jnp.exp(part - log_row)
            back = lax.dot_general(values[half, at], grad_tile, NT, preferred_element_type=F32)
            scored = (probs * (back - shift)).astype(BF16)
            value_sum[at] += jnp.dot(probs.astype(BF16), grad_half, preferred_element_type=F32)
            key_sum[at] += jnp.dot(scored, query_half, preferred_element_type=F32)
            turned = turned + jnp.dot(keys_turned[half, at], scored, preferred_element_type=F32)
    query_grad[0] = rotate_halves(turned.T * HEAD_SIZE**-0.5, cosine[...], -sine[...]).astype(BF16)

    @pl.when(pl.program_id(1) == 2)
    def _():
        for at in range(8):
            ref = far[at // 2] if at % 2 else near.at[at // 2]
            ref[:, :LANES] = key_sum[at].astype(BF16)
            ref[:, LANES:] = value_sum[at].astype(BF16)


def attend_back(query, attended, grad, log_total, limit, cosine, sine, slots):
    rows = query.shape[1]
    tile_spec = pl.BlockSpec((1, rows, LANES), lambda p, g: (3 * p + g, 0, 0))
    pair_spec = pl.BlockSpec((256, 2 * LANES), lambda p, g: (0, p))
    table_spec = pl.BlockSpec((rows, LANES), lambda p, g: (0, 0))
    return pl.pallas_call(
        attend_back_kernel,
        grid=(3, 3),
        out_shape=(jax.ShapeDtypeStruct((4, 256, 768), BF16),)
        + (jax.ShapeDtypeStruct((256, 768), BF16),) * 4
        + (jax.ShapeDtypeStruct((9, rows, LANES), BF16),),
        in_specs=[
            tile_spec,
            tile_spec,
            tile_spec,
            pl.BlockSpec((1, 2, rows), lambda p, g: (3 * p + g, 0, 0)),
            pl.BlockSpec((1, rows), lambda p, g: (0, 0)),
            table_spec,
            table_spec,
        ]
        + [pair_spec] * 8,
        out_specs=(pl.BlockSpec((4, 256, 2 * LANES), lambda p, g: (0, 0, p)),) + (pair_spec,) * 4 + (tile_spec,),
        scratch_shapes=[
            pltpu.VMEM((2, 8, 256, LANES), BF16),
            pltpu.VMEM((2, 8, LANES, 256), BF16),
            pltpu.VMEM((2, 8, 256, LANES), BF16),
            pltpu.VMEM((8, 256, LANES), F32),
            pltpu.VMEM((8, 256, LANES), F32),
        ],
        compiler_params=params(),
        cost_estimate=cost(4 * 18 * rows * 2048 * 128 * 10, 12e6, 18 * rows * 2048),
        name="attend_back",
    )(query, attended, grad, log_total, limit, cosine, sine, *slots)


def middle_kernel(tokens, attended, cotangent, gain, *refs):
    down_in, gate_in, up_in = refs[:8], refs[8:16], refs[16:24]
    (output, hidden, gate_grad, up_grad, rows_two, mixed_grad, proj_grad, attended_out, attended_grad, gain_grad) = refs[24:34]
    down, gate_w, up_w, gates, ups, wide, down_sems, gate_sems, up_sems = refs[34:]
    z, x, _, _ = my_place()
    down_copies = block_copies(down_in, down, down_sems, False)
    gate_copies = block_copies(gate_in, gate_w, gate_sems, True)
    up_copies = block_copies(up_in, up_w, up_sems, True)
    for copies in (down_copies, gate_copies, up_copies):
        for copy in copies.values():
            copy.start()
    width = tokens.shape[1]
    for at, tile in enumerate(natural_tiles([attended[at].astype(F32) for at in range(9)])):
        wide[:, at * LANES : (at + 1) * LANES] = tile
    for copy in down_copies.values():
        copy.wait()

    def out_block(row):
        return down[row, :, :, 768:].reshape(width, 288)

    def down_block(row):
        return down[row, :, :, :768].reshape(width, 768)

    mixed_grad[...] = tokens[...].astype(F32)
    for row in range(4):
        part = wide[:, row * 288 : (row + 1) * 288].astype(BF16)
        attended_out[row] = part
        mixed_grad[...] += lax.dot_general(part, out_block(row), NT, preferred_element_type=F32)
    factor, hat = normalized(mixed_grad[...])
    gains = gain[...]
    wide[...] = hat
    rows_two[...] = (hat * gains).astype(BF16)
    for t in range(Z_SIZE):
        for dx in range(2):
            for dy in range(2):
                for dcore in range(2):
                    gate_copies[t, dx, dy, dcore].wait()
                    up_copies[t, dx, dy, dcore].wait()
            block = lax.rem(z - t + Z_SIZE, Z_SIZE) * 2 + flipped(x, dx)
            gates[block] = jnp.dot(rows_two[...], gate_w[block].reshape(width, 384), preferred_element_type=F32)
            ups[block] = jnp.dot(rows_two[...], up_w[block].reshape(width, 384), preferred_element_type=F32)
    for row in range(4):
        for side in range(2):
            gate, up = gates[2 * row + side], ups[2 * row + side]
            sigmoid = 1.0 / (1.0 + jnp.exp(-gate))
            hidden[row, :, side * 384 : (side + 1) * 384] = (gate * sigmoid * up).astype(BF16)
        mixed_grad[...] += lax.dot_general(hidden[row], down_block(row), NT, preferred_element_type=F32)
        back = jnp.dot(cotangent[...], down_block(row), preferred_element_type=F32)
        for side in range(2):
            gate, up = gates[2 * row + side], ups[2 * row + side]
            sigmoid = 1.0 / (1.0 + jnp.exp(-gate))
            part = back[:, side * 384 : (side + 1) * 384]
            gate_grad[2 * row + side] = (part * up * sigmoid * (1.0 + gate * (1.0 - sigmoid))).astype(BF16)
            up_grad[2 * row + side] = (part * (gate * sigmoid)).astype(BF16)
    output[...] = mixed_grad[...].astype(BF16)
    for block in range(8):
        grad_two = lax.dot_general(
            gate_grad[block], gate_w[block].reshape(width, 384), NT, preferred_element_type=F32
        )
        grad_two = grad_two + lax.dot_general(
            up_grad[block], up_w[block].reshape(width, 384), NT, preferred_element_type=F32
        )
        mixed_grad[...] = grad_two if block == 0 else mixed_grad[...] + grad_two
    grad_two, hat = mixed_grad[...], wide[...]
    gain_grad[...] = jnp.sum(grad_two * hat, axis=0, keepdims=True)
    scaled = grad_two * gains
    total = cotangent[...].astype(F32) + factor * (
        scaled - hat * jnp.mean(scaled * hat, axis=-1, keepdims=True)
    )
    mixed_grad[...] = total
    proj_grad[...] = total.astype(BF16)
    for row in range(4):
        wide[:, row * 288 : (row + 1) * 288] = jnp.dot(
            proj_grad[...], out_block(row), preferred_element_type=F32
        )
    tiles = pair_tiles([wide[:, at * LANES : (at + 1) * LANES] for at in range(9)])
    for at, tile in enumerate(tiles):
        attended_grad[at] = tile.astype(BF16)


def middle(tokens, attended, cotangent, gain, down, gate, up):
    rows, width = tokens.shape
    return pl.pallas_call(
        middle_kernel,
        out_shape=(
            jax.ShapeDtypeStruct((rows, width), BF16),
            jax.ShapeDtypeStruct((4, rows, 768), BF16),
            jax.ShapeDtypeStruct((8, rows, 384), BF16),
            jax.ShapeDtypeStruct((8, rows, 384), BF16),
            jax.ShapeDtypeStruct((rows, width), BF16),
            jax.ShapeDtypeStruct((rows, width), F32),
            jax.ShapeDtypeStruct((rows, width), BF16),
            jax.ShapeDtypeStruct((4, rows, 288), BF16),
            jax.ShapeDtypeStruct((9, rows, LANES), BF16),
            jax.ShapeDtypeStruct((1, width), F32),
        ),
        in_specs=vmem_specs(4) + any_specs(24),
        out_specs=tuple(vmem_specs(10)),
        scratch_shapes=[
            pltpu.VMEM((4, 8) + down[0].shape[1:], BF16),
            pltpu.VMEM((8, 4) + gate[0].shape[1:], BF16),
            pltpu.VMEM((8, 4) + up[0].shape[1:], BF16),
            pltpu.VMEM((8, rows, 384), F32),
            pltpu.VMEM((8, rows, 384), F32),
            pltpu.VMEM((rows, width), F32),
            pltpu.SemaphoreType.DMA((32,)),
            pltpu.SemaphoreType.DMA((32,)),
            pltpu.SemaphoreType.DMA((32,)),
        ],
        compiler_params=params(),
        cost_estimate=cost(2 * rows * width * (6 * 3072 + 2 * 1152), 4e7),
        name="middle",
    )(tokens, attended, cotangent, gain, *down, *gate, *up)


def turned_rows(matrix, parts):
    flat = matrix.astype(F32).T.astype(BF16)
    return flat.reshape(parts, flat.shape[0] // parts, flat.shape[1])


def weight_grad_kernel(keep, first, rows_two, gate_grad, up_grad, hidden, cotangent, proj_grad, attended, *refs):
    if keep:
        arrived, refs = refs[:3], refs[3:]
        near, far, turned = refs[:3], refs[3:6], refs[6:]
    else:
        outs, turned = refs[:3], refs[3:]
    rows_turned, cot_turned, proj_turned = turned
    z, x, y, core = my_place()
    t = pl.program_id(0)

    @pl.when(t == 0)
    def _():
        rows_turned[...] = turned_rows(rows_two[...], 4)
        cot_turned[...] = turned_rows(cotangent[...], 8)
        proj_turned[...] = turned_rows(proj_grad[...], 8)

    target_core = core if keep else 1 - core
    z_at = lax.rem(z - t + Z_SIZE, Z_SIZE)

    def put(group, dx, dy, value):
        if not keep:
            outs[group][0, dx, dy] = value.astype(BF16)
            return
        value = (value + arrived[group][0, dx, dy].astype(F32)).astype(BF16)
        flip, other = (dy, dx) if first[group] == "y" else (dx, dy)
        (far if flip else near)[group][0, other] = value

    for dx in range(2):
        ctx_block = z_at * 2 + flipped(x, dx)
        for dy in range(2):
            row = flipped(y, dy) * 2 + target_core
            left = rows_turned[row]
            put(1, dx, dy, jnp.dot(left, gate_grad[ctx_block], preferred_element_type=F32))
            put(2, dx, dy, jnp.dot(left, up_grad[ctx_block], preferred_element_type=F32))
            value = jnp.concatenate(
                [
                    jnp.dot(cot_turned[ctx_block], hidden[row], preferred_element_type=F32),
                    jnp.dot(proj_turned[ctx_block], attended[row], preferred_element_type=F32),
                ],
                axis=1,
            )
            put(0, dx, dy, value)


def weight_grads(keep, first, rows_two, gate_grad, up_grad, hidden, cotangent, proj_grad, attended, arrived=()):
    rows, width = rows_two.shape
    shapes = ((144, 1056), (288, 384), (288, 384))
    both = [(Z_SIZE, 2, 2) + shape for shape in shapes]
    half = [(Z_SIZE, 2) + shape for shape in shapes]

    def spec(shape):
        return pl.BlockSpec((1,) + shape[1:], lambda t: (t,) + (0,) * (len(shape) - 1))

    whole = [rows_two, gate_grad, up_grad, hidden, cotangent, proj_grad, attended]
    out = half + half if keep else both
    return pl.pallas_call(
        functools.partial(weight_grad_kernel, keep, first),
        grid=(Z_SIZE,),
        out_shape=tuple(jax.ShapeDtypeStruct(shape, BF16) for shape in out),
        in_specs=[
            pl.BlockSpec(array.shape, lambda t, rank=array.ndim: (0,) * rank) for array in whole
        ]
        + [spec(shape) for shape in (both if keep else [])],
        out_specs=tuple(spec(shape) for shape in out),
        scratch_shapes=[
            pltpu.VMEM((4, 288, rows), BF16),
            pltpu.VMEM((8, 144, rows), BF16),
            pltpu.VMEM((8, 144, rows), BF16),
        ],
        compiler_params=params(),
        cost_estimate=cost(rows * width * (3 * 3072 + 1152), 3e7),
        name="weight_grads_keep" if keep else "weight_grads_send",
    )(*whole, *arrived)


def project_back_kernel(tokens, gain, query_grad, pair_grad, mixed_grad, cosine, sine, *refs):
    weights = refs[:8]
    input_grad, gain_grad, send, kept, buffer, pieces, wide, rows_turned, sems = refs[8:]
    z, x, y, core = my_place()
    copies = block_copies(weights, buffer, sems, True)
    for copy in copies.values():
        copy.start()
    width = tokens.shape[1]
    factor, hat = normalized(tokens[...].astype(F32))
    gains = gain[...]
    rows_turned[...] = turned_rows((hat * gains).astype(BF16), 4)
    for at, tile in enumerate(natural_tiles([query_grad[at].astype(F32) for at in range(9)])):
        wide[:, at * LANES : (at + 1) * LANES] = tile
    cos_tile, sin_tile = cosine[...], -sine[...]
    for pair in range(3):
        key_tile = pair_grad[:, 2 * pair * LANES : (2 * pair + 1) * LANES].astype(F32)
        wide[:, 1152 + pair * LANES : 1152 + (pair + 1) * LANES] = rotate_halves(key_tile, cos_tile, sin_tile)
        wide[:, 1536 + pair * LANES : 1536 + (pair + 1) * LANES] = pair_grad[
            :, (2 * pair + 1) * LANES : (2 * pair + 2) * LANES
        ].astype(F32)
    q_part, kv_part = 144, 48
    for at in range(8):
        pieces[at] = jnp.concatenate(
            [
                wide[:, at * q_part : (at + 1) * q_part],
                wide[:, 1152 + at * kv_part : 1152 + (at + 1) * kv_part],
                wide[:, 1536 + at * kv_part : 1536 + (at + 1) * kv_part],
            ],
            axis=1,
        ).astype(BF16)
    for t in range(Z_SIZE):
        for dx in range(2):
            block = lax.rem(z - t + Z_SIZE, Z_SIZE) * 2 + flipped(x, dx)
            for dy in range(2):
                for keep in range(2):
                    row = flipped(y, dy) * 2 + (core if keep else 1 - core)
                    value = jnp.dot(rows_turned[row], pieces[block], preferred_element_type=F32)
                    (kept if keep else send)[t, dx, dy] = value.astype(BF16)
    for copy in copies.values():
        copy.wait()
    grad_one = jnp.zeros_like(hat)
    for block in range(8):
        grad_one = grad_one + lax.dot_general(
            pieces[block], buffer[block].reshape(width, 240), NT, preferred_element_type=F32
        )
    gain_grad[...] = jnp.sum(grad_one * hat, axis=0, keepdims=True)
    scaled = grad_one * gains
    input_grad[...] = mixed_grad[...] + factor * (
        scaled - hat * jnp.mean(scaled * hat, axis=-1, keepdims=True)
    )


def project_back(tokens, gain, query_grad, pair_grad, mixed_grad, cosine, sine, weights):
    rows, width = tokens.shape
    piece = weights[0].shape[1:]
    return pl.pallas_call(
        project_back_kernel,
        out_shape=(
            jax.ShapeDtypeStruct((rows, width), F32),
            jax.ShapeDtypeStruct((1, width), F32),
            jax.ShapeDtypeStruct((Z_SIZE, 2, 2) + piece, BF16),
            jax.ShapeDtypeStruct((Z_SIZE, 2, 2) + piece, BF16),
        ),
        in_specs=vmem_specs(7) + any_specs(8),
        out_specs=tuple(vmem_specs(4)),
        scratch_shapes=[
            pltpu.VMEM((8, 4) + piece, BF16),
            pltpu.VMEM((8, rows, 240), BF16),
            pltpu.VMEM((rows, 1920), F32),
            pltpu.VMEM((4, 288, rows), BF16),
            pltpu.SemaphoreType.DMA((32,)),
        ],
        compiler_params=params(),
        cost_estimate=cost(4 * rows * width * 1920, 1.4e7),
        name="project_back",
    )(tokens, gain, query_grad, pair_grad, mixed_grad, cosine, sine, *weights)


def lane_tables(first, rows):
    half = HEAD_SIZE // 2
    frequency = ROTARY_BASE ** (-jnp.arange(half, dtype=F32) * 2.0 / HEAD_SIZE)
    angles = (first + jnp.arange(rows, dtype=jnp.int32)).astype(F32)[:, None] * frequency[None, :]
    cosine, sine = jnp.cos(angles), jnp.sin(angles)
    return jnp.tile(cosine, (1, 4)), jnp.tile(jnp.concatenate([-sine, sine], axis=1), (1, 2))


def gather_gains(gain_one, gain_two):
    held = jnp.stack([gain_one, gain_two])
    near = jnp.stack([held, hop(held, "core")])
    every = jnp.concatenate([near, hop(near, "y")])
    order = jnp.arange(4) ^ lax.axis_index("seq")
    every = jnp.take(every, order, axis=0).astype(F32)
    return every[:, 0].reshape(1, -1), every[:, 1].reshape(1, -1)


def permuted_device(
    tokens, prefix, gain_one, w_query, w_key, value_weight, w_out, gain_two, w_gate, w_up, w_down, cotangent
):
    _, rows, width = tokens.shape
    tokens, cotangent = tokens[0], cotangent[0]
    ctx_at, seq_at = lax.axis_index("ctx"), lax.axis_index("seq")
    first_norm, second_norm = gather_gains(gain_one, gain_two)
    qkv = gather_shards(jnp.concatenate([w_query, w_key, value_weight], axis=1), ("z", "x", "y", "core"))
    down = gather_shards(jnp.concatenate([w_down.T, w_out.T], axis=1), ("z", "y", "x", "core"))
    gate = gather_shards(w_gate, ("x", "z", "y", "core"))
    up = gather_shards(w_up, ("z", "x", "y", "core"))
    cosine, sine = lane_tables(ctx_at * rows, rows)
    limit = jnp.maximum(ctx_at * rows + jnp.arange(rows, dtype=jnp.int32) + 1, prefix[0])[None, :]

    query, pair = project(tokens, first_norm, cosine, sine, qkv)
    slots, held = [], pair
    for t in range(Z_SIZE):
        slots += [held, hop(held, "x")]
        if t < Z_SIZE - 1:
            held = hop(held, "z", 1)
    attended, log_total = attend(query, limit, slots)
    (
        output,
        hidden,
        gate_grad,
        up_grad,
        rows_two,
        mixed_grad,
        proj_grad,
        attended_rows,
        attended_grad,
        second_gain_part,
    ) = middle(tokens, attended, cotangent, second_norm, down, gate, up)

    first = ("x", "y", "x")
    factors = (rows_two, gate_grad, up_grad, hidden, cotangent, proj_grad, attended_rows)
    sent = weight_grads(False, first, *factors)
    arrived = [hop(array, "core") for array in sent]
    parts = weight_grads(True, first, *factors, arrived)
    grad_down_out, grad_gate, grad_up = [
        scatter_rest(parts[at], parts[3 + at], first[at]) for at in range(3)
    ]
    second_gain_gradient = sum_everywhere(second_gain_part)

    near, *far, query_grad = attend_back(
        query, attended, attended_grad, log_total, limit, cosine, sine, slots
    )
    total = add_pair(near[3], hop(far[3], "x"))
    for t in (2, 1, 0):
        local = near[t].astype(F32) + hop(far[t], "x").astype(F32)
        total = (local + hop(total, "z", -1).astype(F32)).astype(BF16)
    input_grad, first_gain_part, qkv_send, qkv_keep = project_back(
        tokens, first_norm, query_grad, total, mixed_grad, cosine, sine, qkv
    )
    qkv_sum = add_pair(qkv_keep, hop(qkv_send, "core"))
    grad_qkv = scatter_rest(qkv_sum[:, :, 0], qkv_sum[:, :, 1], "y")
    first_gain_gradient = sum_everywhere(first_gain_part)

    def own_gain(vector):
        return lax.dynamic_slice(vector[0], (seq_at * 288,), (288,))

    return (
        output[None],
        input_grad[None],
        own_gain(first_gain_gradient),
        grad_qkv[:, :144],
        grad_qkv[:, 144:192],
        grad_qkv[:, 192:],
        grad_down_out[:, 768:].T,
        own_gain(second_gain_gradient),
        grad_gate,
        grad_up,
        grad_down_out[:, :768].T,
    )


def permute_plan_fits(mesh, tokens):
    return dict(mesh.shape) == {"seq": 4, "ctx": 8} and tokens.shape == (4, 2048, 1152)


def solution(mesh):
    placed = (
        P("seq", "ctx", None),
        P("seq"),
        P("seq"),
        P("seq", "ctx"),
        P("seq", "ctx"),
        P("seq", "ctx"),
        P("seq", "ctx"),
        P("seq"),
        P("seq", "ctx"),
        P("seq", "ctx"),
        P("seq", "ctx"),
        P("seq", "ctx", None),
    )

    def mapped(device_function):
        return jax.shard_map(
            device_function,
            mesh=mesh,
            in_specs=placed,
            out_specs=(
                P("seq", "ctx", None),
                P("seq", "ctx", None),
                P("seq"),
                P("seq", "ctx"),
                P("seq", "ctx"),
                P("seq", "ctx"),
                P("seq", "ctx"),
                P("seq"),
                P("seq", "ctx"),
                P("seq", "ctx"),
                P("seq", "ctx"),
            ),
            check_vma=False,
        )

    def layer(tokens, *rest):
        return mapped(permuted_device if permute_plan_fits(mesh, tokens) else per_device)(tokens, *rest)

    return layer
```

```python
import functools

import jax
import jax.numpy as jnp
from jax import lax
from jax.experimental import pallas as pl
from jax.experimental.pallas import tpu as pltpu
from jax.sharding import PartitionSpec as P

QUERY_HEADS = 18
KEY_VALUE_HEADS = 6
HEAD_SIZE = 64


EPSILON = 1e-05
ROTARY_BASE = 10000.0

LANES = 128
Z_SIZE = 4
VMEM_LIMIT = 66_000_000
F32 = jnp.float32
BF16 = jnp.bfloat16
NT = (((1,), (1,)), ((), ()))


def rotary_tables(positions, head_width):
    half_width = head_width // 2
    frequency = ROTARY_BASE ** (-jnp.arange(half_width, dtype=jnp.float32) * 2.0 / head_width)
    angles = positions.astype(jnp.float32)[:, None] * frequency[None, :]
    return (jnp.cos(angles)[:, None, :], jnp.sin(angles)[:, None, :])


def apply_rotation(values_in, cosine_table, sine_values):
    half_width = values_in.shape[-1] // 2
    first = values_in[..., :half_width]
    second = values_in[..., half_width:]
    return jnp.concatenate(
        [first * cosine_table - second * sine_values, second * cosine_table + first * sine_values],
        axis=-1,
    )


def inverse_rotation(grads_in, cosine_table, sine_values):
    half_width = grads_in.shape[-1] // 2
    first = grads_in[..., :half_width]
    second = grads_in[..., half_width:]
    return jnp.concatenate(
        [first * cosine_table + second * sine_values, second * cosine_table - first * sine_values],
        axis=-1,
    )


def gather_weights(w_query, w_key, value_weight, w_out, w_gate, w_up, w_down, gain_one, gain_two):
    columns = (
        lax.all_gather(w_query, "ctx", axis=1, tiled=True),
        lax.all_gather(w_key, "ctx", axis=1, tiled=True),
        lax.all_gather(value_weight, "ctx", axis=1, tiled=True),
        lax.all_gather(w_out, "ctx", axis=1, tiled=True),
        lax.all_gather(w_gate, "ctx", axis=1, tiled=True),
        lax.all_gather(w_up, "ctx", axis=1, tiled=True),
        lax.all_gather(w_down, "ctx", axis=1, tiled=True),
    )
    return (
        lax.all_gather(columns[0], "seq", axis=0, tiled=True),
        lax.all_gather(columns[1], "seq", axis=0, tiled=True),
        lax.all_gather(columns[2], "seq", axis=0, tiled=True),
        lax.all_gather(columns[3], "seq", axis=0, tiled=True),
        lax.all_gather(columns[4], "seq", axis=0, tiled=True),
        lax.all_gather(columns[5], "seq", axis=0, tiled=True),
        lax.all_gather(columns[6], "seq", axis=0, tiled=True),
        lax.all_gather(gain_one, "seq", axis=0, tiled=True),
        lax.all_gather(gain_two, "seq", axis=0, tiled=True),
    )


def gather_pairs(key_rotated, value_reduced):
    return (
        lax.all_gather(key_rotated, "ctx", axis=1, tiled=True),
        lax.all_gather(value_reduced, "ctx", axis=1, tiled=True),
    )


def head_major(whole_result, sequence_count):
    sequence_length = whole_result.shape[1]
    return (
        whole_result.reshape(sequence_count, sequence_length, KEY_VALUE_HEADS, HEAD_SIZE)
        .transpose(0, 2, 1, 3)
        .reshape(sequence_count * KEY_VALUE_HEADS, sequence_length, HEAD_SIZE)
    )


def per_device(
    tokens,
    prefix,
    gain_one,
    w_query,
    w_key,
    value_weight,
    w_out,
    gain_two,
    w_gate,
    w_up,
    w_down,
    cotangent,
):
    sequence_count, token_local, model_width = tokens.shape
    sequence_length = token_local * lax.axis_size("ctx")
    number_of_rows = sequence_count * token_local
    queries_per_key_head = QUERY_HEADS // KEY_VALUE_HEADS
    score_scale = HEAD_SIZE ** (-0.5)
    gathered = gather_weights(
        w_query, w_key, value_weight, w_out, w_gate, w_up, w_down, gain_one, gain_two
    )
    full_query, full_key, full_value, full_out, full_gate, full_up, full_down = gathered[:7]
    first_norm = gathered[7].astype(jnp.float32)
    second_norm = gathered[8].astype(jnp.float32)
    input_rows = tokens.reshape(number_of_rows, model_width).astype(jnp.float32)
    first_factor = lax.rsqrt(jnp.mean(input_rows * input_rows, axis=-1, keepdims=True) + EPSILON)
    first_normalized_input = input_rows * first_factor
    normalized_rows = (first_normalized_input * first_norm).astype(jnp.bfloat16)
    query_pre = jnp.dot(normalized_rows, full_query, preferred_element_type=jnp.float32)
    key_prerotation = jnp.dot(normalized_rows, full_key, preferred_element_type=jnp.float32)
    value_reduced = jnp.dot(normalized_rows, full_value, preferred_element_type=jnp.float32).astype(
        jnp.bfloat16
    )
    positions = lax.axis_index("ctx") * token_local + jnp.arange(token_local, dtype=jnp.int32)
    cosine_table, sine_values = rotary_tables(positions, HEAD_SIZE)
    query_rows = apply_rotation(
        query_pre.reshape(sequence_count, token_local, QUERY_HEADS, HEAD_SIZE),
        cosine_table,
        sine_values,
    ).astype(jnp.bfloat16)
    key_rotated = apply_rotation(
        key_prerotation.reshape(sequence_count, token_local, KEY_VALUE_HEADS, HEAD_SIZE),
        cosine_table,
        sine_values,
    ).astype(jnp.bfloat16)
    key_rotated = key_rotated.reshape(sequence_count, token_local, KEY_VALUE_HEADS * HEAD_SIZE)
    value_reduced = value_reduced.reshape(sequence_count, token_local, KEY_VALUE_HEADS * HEAD_SIZE)
    keys_all, values_all = gather_pairs(key_rotated, value_reduced)
    query_block_list = query_rows.reshape(
        sequence_count, token_local, KEY_VALUE_HEADS, queries_per_key_head, HEAD_SIZE
    ).transpose(0, 2, 3, 1, 4)
    query_block_list = query_block_list.reshape(
        sequence_count * KEY_VALUE_HEADS, queries_per_key_head, token_local, HEAD_SIZE
    )
    key_blocks = head_major(keys_all, sequence_count)
    value_blocks = head_major(values_all, sequence_count)
    prefix_repeated = jnp.repeat(prefix, KEY_VALUE_HEADS)
    key_place = jnp.arange(sequence_length, dtype=jnp.int32)

    def visible_for(prefix_len):
        return (key_place[None, :] <= positions[:, None]) | (key_place[None, :] < prefix_len)

    def attend(block_item):
        query_block, key_block, value_block, prefix_len = block_item
        scores = (
            jnp.einsum("gqd,kd->gqk", query_block, key_block, preferred_element_type=jnp.float32)
            * score_scale
        )
        scores = jnp.where(visible_for(prefix_len)[None], scores, -1e30)
        row_max = jnp.max(scores, axis=-1, keepdims=True)
        expo = jnp.exp(scores - row_max)
        total = jnp.sum(expo, axis=-1, keepdims=True)
        probs_low = (expo / total).astype(jnp.bfloat16)
        result = jnp.einsum(
            "gqk,kd->gqd", probs_low, value_block, preferred_element_type=jnp.float32
        )
        return (result.astype(jnp.bfloat16), (row_max + jnp.log(total))[..., 0])

    attention_result_blocks, log_totals = lax.map(
        attend, (query_block_list, key_blocks, value_blocks, prefix_repeated)
    )
    attention_result = attention_result_blocks.reshape(
        sequence_count, KEY_VALUE_HEADS, queries_per_key_head, token_local, HEAD_SIZE
    ).transpose(0, 3, 1, 2, 4)
    attention_result = attention_result.reshape(number_of_rows, QUERY_HEADS * HEAD_SIZE)
    mixed_output = input_rows + jnp.dot(
        attention_result, full_out, preferred_element_type=jnp.float32
    )
    second_factor = lax.rsqrt(
        jnp.mean(mixed_output * mixed_output, axis=-1, keepdims=True) + EPSILON
    )
    second_normalized_input = mixed_output * second_factor
    normalized_second = (second_normalized_input * second_norm).astype(jnp.bfloat16)
    gate = jnp.dot(normalized_second, full_gate, preferred_element_type=jnp.float32)
    up_part = jnp.dot(normalized_second, full_up, preferred_element_type=jnp.float32)
    sigmoid_gate = jax.nn.sigmoid(gate)
    activated = gate * sigmoid_gate
    hidden = (activated * up_part).astype(jnp.bfloat16)
    result_rows = mixed_output + jnp.dot(hidden, full_down, preferred_element_type=jnp.float32)
    output = result_rows.astype(jnp.bfloat16).reshape(sequence_count, token_local, model_width)
    gathered = gather_weights(
        w_query, w_key, value_weight, w_out, w_gate, w_up, w_down, gain_one, gain_two
    )
    full_query, full_key, full_value, full_out, full_gate, full_up, full_down = gathered[:7]
    grad_rows_in = cotangent.reshape(number_of_rows, model_width)
    grad_down = jnp.dot(hidden.T, grad_rows_in, preferred_element_type=jnp.float32)
    dhidden = jnp.dot(grad_rows_in, full_down.T, preferred_element_type=jnp.float32)
    dgate = (dhidden * up_part * sigmoid_gate * (1.0 + gate * (1.0 - sigmoid_gate))).astype(
        jnp.bfloat16
    )
    dup_part = (dhidden * activated).astype(jnp.bfloat16)
    grad_gate = jnp.dot(normalized_second.T, dgate, preferred_element_type=jnp.float32)
    grad_up = jnp.dot(normalized_second.T, dup_part, preferred_element_type=jnp.float32)
    normalized_second_grad = jnp.dot(dgate, full_gate.T, preferred_element_type=jnp.float32)
    normalized_second_grad = normalized_second_grad + jnp.dot(
        dup_part, full_up.T, preferred_element_type=jnp.float32
    )
    second_gain_gradient = jnp.sum(normalized_second_grad * second_normalized_input, axis=0)
    second_scaled = normalized_second_grad * second_norm
    dmixed = grad_rows_in.astype(jnp.float32) + second_factor * (
        second_scaled
        - second_normalized_input
        * jnp.mean(second_scaled * second_normalized_input, axis=-1, keepdims=True)
    )
    dproj = dmixed.astype(jnp.bfloat16)
    grad_out = jnp.dot(attention_result.T, dproj, preferred_element_type=jnp.float32)
    attention_result_grad = jnp.dot(dproj, full_out.T, preferred_element_type=jnp.float32).astype(
        jnp.bfloat16
    )
    attention_result_block_grads = attention_result_grad.reshape(
        sequence_count, token_local, KEY_VALUE_HEADS, queries_per_key_head, HEAD_SIZE
    ).transpose(0, 2, 3, 1, 4)
    attention_result_block_grads = attention_result_block_grads.reshape(
        sequence_count * KEY_VALUE_HEADS, queries_per_key_head, token_local, HEAD_SIZE
    )
    keys_all, values_all = gather_pairs(key_rotated, value_reduced)
    key_blocks = head_major(keys_all, sequence_count)
    value_blocks = head_major(values_all, sequence_count)

    def attend_back(block_item):
        query_block, key_block, value_block, prefix_len, log_total, dout_block = block_item
        scores = (
            jnp.einsum("gqd,kd->gqk", query_block, key_block, preferred_element_type=jnp.float32)
            * score_scale
        )
        visible = visible_for(prefix_len)[None]
        probs = jnp.where(
            visible, jnp.exp(jnp.where(visible, scores, -1e30) - log_total[..., None]), 0.0
        )
        dvalues = jnp.einsum(
            "gqk,gqd->kd",
            probs.astype(jnp.bfloat16),
            dout_block,
            preferred_element_type=jnp.float32,
        )
        dprobs = jnp.einsum(
            "gqd,kd->gqk", dout_block, value_block, preferred_element_type=jnp.float32
        )
        dscores = (probs * (dprobs - jnp.sum(probs * dprobs, axis=-1, keepdims=True))).astype(
            jnp.bfloat16
        )
        dquery = (
            jnp.einsum("gqk,kd->gqd", dscores, key_block, preferred_element_type=jnp.float32)
            * score_scale
        )
        dkeys = (
            jnp.einsum("gqk,gqd->kd", dscores, query_block, preferred_element_type=jnp.float32)
            * score_scale
        )
        return (dquery, dkeys, dvalues)

    query_block_grads, key_block_grads, value_block_grads = lax.map(
        attend_back,
        (
            query_block_list,
            key_blocks,
            value_blocks,
            prefix_repeated,
            log_totals,
            attention_result_block_grads,
        ),
    )
    key_grads_combined = key_block_grads.reshape(
        sequence_count, KEY_VALUE_HEADS, sequence_length, HEAD_SIZE
    ).transpose(0, 2, 1, 3)
    key_grads_combined = key_grads_combined.reshape(
        sequence_count, sequence_length, KEY_VALUE_HEADS * HEAD_SIZE
    )
    value_grads_combined = value_block_grads.reshape(
        sequence_count, KEY_VALUE_HEADS, sequence_length, HEAD_SIZE
    ).transpose(0, 2, 1, 3)
    value_grads_combined = value_grads_combined.reshape(
        sequence_count, sequence_length, KEY_VALUE_HEADS * HEAD_SIZE
    )
    key_grads_local, value_grads_local = (
        lax.psum_scatter(
            key_grads_combined.astype(jnp.bfloat16), "ctx", scatter_dimension=1, tiled=True
        ).astype(jnp.float32),
        lax.psum_scatter(
            value_grads_combined.astype(jnp.bfloat16), "ctx", scatter_dimension=1, tiled=True
        ).astype(jnp.float32),
    )
    key_prerotation_grad = inverse_rotation(
        key_grads_local.reshape(sequence_count, token_local, KEY_VALUE_HEADS, HEAD_SIZE),
        cosine_table,
        sine_values,
    )
    key_prerotation_grad = key_prerotation_grad.astype(jnp.bfloat16).reshape(
        number_of_rows, KEY_VALUE_HEADS * HEAD_SIZE
    )
    value_reduced_grad = value_grads_local.astype(jnp.bfloat16).reshape(
        number_of_rows, KEY_VALUE_HEADS * HEAD_SIZE
    )
    query_row_grads = query_block_grads.reshape(
        sequence_count, KEY_VALUE_HEADS, queries_per_key_head, token_local, HEAD_SIZE
    ).transpose(0, 3, 1, 2, 4)
    query_row_grads = query_row_grads.reshape(sequence_count, token_local, QUERY_HEADS, HEAD_SIZE)
    dquery_pre = (
        inverse_rotation(query_row_grads, cosine_table, sine_values)
        .astype(jnp.bfloat16)
        .reshape(number_of_rows, QUERY_HEADS * HEAD_SIZE)
    )
    grad_query = jnp.dot(normalized_rows.T, dquery_pre, preferred_element_type=jnp.float32)
    grad_key = jnp.dot(normalized_rows.T, key_prerotation_grad, preferred_element_type=jnp.float32)
    grad_value = jnp.dot(normalized_rows.T, value_reduced_grad, preferred_element_type=jnp.float32)
    normalized_grad = jnp.dot(dquery_pre, full_query.T, preferred_element_type=jnp.float32)
    normalized_grad = normalized_grad + jnp.dot(
        key_prerotation_grad, full_key.T, preferred_element_type=jnp.float32
    )
    normalized_grad = normalized_grad + jnp.dot(
        value_reduced_grad, full_value.T, preferred_element_type=jnp.float32
    )
    first_gain_gradient = jnp.sum(normalized_grad * first_normalized_input, axis=0)
    first_scaled = normalized_grad * first_norm
    input_grad = dmixed + first_factor * (
        first_scaled
        - first_normalized_input
        * jnp.mean(first_scaled * first_normalized_input, axis=-1, keepdims=True)
    )
    input_grad = input_grad.reshape(sequence_count, token_local, model_width)
    partial_value = (
        lax.psum_scatter(
            grad_query.astype(jnp.bfloat16), "seq", scatter_dimension=0, tiled=True
        ).astype(jnp.float32),
        lax.psum_scatter(
            grad_key.astype(jnp.bfloat16), "seq", scatter_dimension=0, tiled=True
        ).astype(jnp.float32),
        lax.psum_scatter(
            grad_value.astype(jnp.bfloat16), "seq", scatter_dimension=0, tiled=True
        ).astype(jnp.float32),
        lax.psum_scatter(
            grad_out.astype(jnp.bfloat16), "seq", scatter_dimension=0, tiled=True
        ).astype(jnp.float32),
        lax.psum_scatter(
            grad_gate.astype(jnp.bfloat16), "seq", scatter_dimension=0, tiled=True
        ).astype(jnp.float32),
        lax.psum_scatter(
            grad_up.astype(jnp.bfloat16), "seq", scatter_dimension=0, tiled=True
        ).astype(jnp.float32),
        lax.psum_scatter(
            grad_down.astype(jnp.bfloat16), "seq", scatter_dimension=0, tiled=True
        ).astype(jnp.float32),
        lax.psum_scatter(
            first_gain_gradient.astype(jnp.bfloat16), "seq", scatter_dimension=0, tiled=True
        ).astype(jnp.float32),
        lax.psum_scatter(
            second_gain_gradient.astype(jnp.bfloat16), "seq", scatter_dimension=0, tiled=True
        ).astype(jnp.float32),
    )
    owned = (
        lax.psum_scatter(
            partial_value[0].astype(jnp.bfloat16), "ctx", scatter_dimension=1, tiled=True
        ).astype(jnp.float32),
        lax.psum_scatter(
            partial_value[1].astype(jnp.bfloat16), "ctx", scatter_dimension=1, tiled=True
        ).astype(jnp.float32),
        lax.psum_scatter(
            partial_value[2].astype(jnp.bfloat16), "ctx", scatter_dimension=1, tiled=True
        ).astype(jnp.float32),
        lax.psum_scatter(
            partial_value[3].astype(jnp.bfloat16), "ctx", scatter_dimension=1, tiled=True
        ).astype(jnp.float32),
        lax.psum_scatter(
            partial_value[4].astype(jnp.bfloat16), "ctx", scatter_dimension=1, tiled=True
        ).astype(jnp.float32),
        lax.psum_scatter(
            partial_value[5].astype(jnp.bfloat16), "ctx", scatter_dimension=1, tiled=True
        ).astype(jnp.float32),
        lax.psum_scatter(
            partial_value[6].astype(jnp.bfloat16), "ctx", scatter_dimension=1, tiled=True
        ).astype(jnp.float32),
    )
    gains_owned = lax.psum((partial_value[7], partial_value[8]), "ctx")
    final_grads = owned + gains_owned
    return (
        output,
        input_grad,
        final_grads[7],
        final_grads[0],
        final_grads[1],
        final_grads[2],
        final_grads[3],
        final_grads[8],
        final_grads[4],
        final_grads[5],
        final_grads[6],
    )


def permute_pairs(axis, step):
    pairs = []
    for seq_at in range(4):
        for ctx_at in range(8):
            target_seq, target_ctx = seq_at, ctx_at
            if axis == "core":
                target_seq = seq_at ^ 1
            elif axis == "y":
                target_seq = seq_at ^ 2
            elif axis == "x":
                target_ctx = ctx_at ^ 1
            elif axis == "z":
                target_ctx = (ctx_at + 2 * step) % 8
            elif axis == "z_flip":
                target_ctx = ctx_at ^ (2 * step)
            pairs.append((seq_at * 8 + ctx_at, target_seq * 8 + target_ctx))
    return pairs


def hop(array, axis, step=1):
    return lax.ppermute(array, ("seq", "ctx"), permute_pairs(axis, step))


def add_pair(left, right):
    return (left.astype(F32) + right.astype(F32)).astype(BF16)


def scatter_ring(array):
    total = array[Z_SIZE - 1]
    for t in range(Z_SIZE - 2, -1, -1):
        arrived = hop(total, "z", -1)
        if t:
            total = add_pair(array[t], arrived)
        else:
            total = array[0].astype(F32) + arrived.astype(F32)
    return total


def scatter_rest(near, far, first):
    second = "x" if first == "y" else "y"
    arrived = hop(far, first)
    far_two = add_pair(near[:, 1], arrived[:, 1])
    near_two = add_pair(near[:, 0], arrived[:, 0])
    return scatter_ring(add_pair(near_two, hop(far_two, second)))


def sum_everywhere(vector):
    for axis, step in (("core", 1), ("y", 1), ("x", 1), ("z_flip", 1), ("z_flip", 2)):
        vector = vector + hop(vector, axis, step)
    return vector


def my_place():
    seq_at, ctx_at = lax.axis_index("seq"), lax.axis_index("ctx")
    return ctx_at // 2, lax.rem(ctx_at, 2), seq_at // 2, lax.rem(seq_at, 2)


def flipped(at, flip):
    return 1 - at if flip else at


def lane_ids(rows):
    return lax.broadcasted_iota(jnp.int32, (rows, LANES), 1)


def rotate_halves(tile, cosine, sine):
    lower = lax.rem(lane_ids(tile.shape[0]), HEAD_SIZE) < HEAD_SIZE // 2
    swapped = jnp.where(
        lower, pltpu.roll(tile, LANES - HEAD_SIZE // 2, 1), pltpu.roll(tile, HEAD_SIZE // 2, 1)
    )
    return tile * cosine + swapped * sine


def pair_tiles(natural):
    lower = lane_ids(natural[0].shape[0]) < HEAD_SIZE
    tiles = []
    for pair in range(3):
        for member in range(3):
            one, two = 6 * pair + member, 6 * pair + 3 + member
            left, right = natural[one // 2], natural[two // 2]
            if one % 2:
                left, right = pltpu.roll(left, HEAD_SIZE, 1), pltpu.roll(right, HEAD_SIZE, 1)
            tiles.append(jnp.where(lower, left, right))
    return tiles


def natural_tiles(paired):
    lower = lane_ids(paired[0].shape[0]) < HEAD_SIZE
    tiles = []
    for at in range(9):
        sides = []
        for side in range(2):
            head = 2 * at + side
            tile = paired[head // 6 * 3 + head % 3]
            if (head % 6) // 3 != side:
                tile = pltpu.roll(tile, HEAD_SIZE, 1)
            sides.append(tile)
        tiles.append(jnp.where(lower, sides[0], sides[1]))
    return tiles


def normalized(rows):
    factor = lax.rsqrt(jnp.mean(rows * rows, axis=-1, keepdims=True) + EPSILON)
    return factor, rows * factor


def vmem_specs(count):
    return [pl.BlockSpec(memory_space=pltpu.VMEM)] * count


def any_specs(count):
    return [pl.BlockSpec(memory_space=pl.ANY)] * count


def cost(flops, moved, transcendentals=0):
    return pl.CostEstimate(flops=int(flops), bytes_accessed=int(moved), transcendentals=int(transcendentals))


def params():
    return pltpu.CompilerParams(vmem_limit_bytes=VMEM_LIMIT)


def masked_pair(block, half, other):
    inside = (lane_ids(block.shape[0]) < HEAD_SIZE) == (half == 0)
    return jnp.where(inside, block.astype(F32), other)


class Gathering:
    def __init__(self, own, full, block, sends, arrivals, corner_over_x):
        self.own, self.full, self.block, self.sends, self.arrivals = own, full, block, sends, arrivals
        self.corner_over_x = corner_over_x
        self.started = []

    def place(self, t, dx, dy, dcore=0):
        z, x, y, core = my_place()
        ctx_block = lax.rem(z - t + Z_SIZE, Z_SIZE) * 2 + flipped(x, dx)
        return self.full.at[self.block(ctx_block, flipped(y, dy) * 2 + flipped(core, dcore))]

    def copy(self, source, target, number, axis):
        return pltpu.make_async_remote_copy(
            src_ref=source,
            dst_ref=target,
            send_sem=self.sends.at[number],
            recv_sem=self.arrivals.at[number],
            device_id=neighbour(axis),
            device_id_type=pl.DeviceIdType.MESH,
        )

    def send(self, piece, number, axis):
        place = self.place(*piece)
        copy = self.copy(self.own if piece == (0, 0, 0) else place, place, number, axis)
        copy.start()
        self.started.append(copy)

    def wait(self, piece, number, dcore=0):
        place = self.place(*piece, dcore)
        self.copy(place, place, number, "core").wait_recv()

    def to_core(self, piece):
        t, dx, dy = piece
        self.send(piece, 15 + 4 * t + 2 * dx + dy, "core")

    def over_z(self, t):
        if t < Z_SIZE - 1:
            self.send((t, 0, 0), t, "z")

    def over_plane(self, t):
        self.send((t, 0, 0), 3 + t, "x")
        self.send((t, 0, 0), 7 + t, "y")

    def begin(self):
        self.over_z(0)
        self.over_plane(0)
        self.to_core((0, 0, 0))

    def pass_on(self, t):
        self.wait((t, 0, 0), t - 1)
        self.over_z(t)
        self.over_plane(t)
        self.to_core((t, 0, 0))

    def sides(self, t):
        self.wait((t, 1, 0), 3 + t)
        if t not in self.corner_over_x:
            self.send((t, 1, 0), 11 + t, "y")
        self.to_core((t, 1, 0))
        self.wait((t, 0, 1), 7 + t)
        if t in self.corner_over_x:
            self.send((t, 0, 1), 11 + t, "x")
        self.to_core((t, 0, 1))

    def corner(self, t):
        self.wait((t, 1, 1), 11 + t)
        self.to_core((t, 1, 1))

    def finish(self):
        for t in range(Z_SIZE):
            for dx in range(2):
                for dy in range(2):
                    self.wait((t, dx, dy), 15 + 4 * t + 2 * dx + dy, 1)

    def drain(self):
        for copy in self.started:
            copy.wait_send()


def neighbour(axis):
    z, x, y, core = my_place()
    if axis == "z":
        z = lax.rem(z + 1, Z_SIZE)
    elif axis == "z_back":
        z = lax.rem(z + Z_SIZE - 1, Z_SIZE)
    elif axis == "x":
        x = 1 - x
    elif axis == "y":
        y = 1 - y
    elif axis == "core":
        core = 1 - core
    elif axis == "y_core":
        y, core = 1 - y, 1 - core
    return (y * 2 + core, z * 2 + x)


def meet(axes):
    barrier = pltpu.get_barrier_semaphore()
    for axis in axes:
        pl.semaphore_signal(barrier, inc=1, device_id=neighbour(axis), device_id_type=pl.DeviceIdType.MESH)
    pl.semaphore_wait(barrier, len(axes))


def front_kernel(
    qkv_own,
    down_own,
    up_own,
    gains_own,
    tokens,
    cosine,
    sine,
    limit,
    qkv,
    down,
    up,
    pairs,
    query_out,
    attended,
    log_total,
    gain_out,
    pieces,
    wide,
    keys,
    values,
    scores,
    gains,
    qkv_sends,
    qkv_arrivals,
    down_sends,
    down_arrivals,
    up_sends,
    up_arrivals,
    pair_sends,
    pair_arrivals,
    gain_sends,
    gain_arrivals,
    own_sems,
):
    z, x, y, core = my_place()
    seq_at, ctx_at = y * 2 + core, z * 2 + x
    by_ctx, by_seq = (lambda ctx, seq: (ctx, seq)), (lambda ctx, seq: (seq, ctx))
    first = Gathering(qkv_own, qkv, by_ctx, qkv_sends, qkv_arrivals, (1, 3))
    rest = (
        Gathering(down_own, down, by_seq, down_sends, down_arrivals, (3,)),
        Gathering(up_own, up, by_ctx, up_sends, up_arrivals, (3,)),
    )
    meet(("z", "z_back", "x", "y", "core", "y_core"))
    first.begin()
    gain_copies = []
    for number, axis in enumerate(("core", "y", "y_core")):
        copy = pltpu.make_async_remote_copy(
            src_ref=gains_own,
            dst_ref=gains.at[seq_at],
            send_sem=gain_sends.at[number],
            recv_sem=gain_arrivals.at[number],
            device_id=neighbour(axis),
            device_id_type=pl.DeviceIdType.MESH,
        )
        copy.start()
        gain_copies.append(copy)
    own_copies = [
        pltpu.make_async_copy(source, target, own_sems.at[number])
        for number, (source, target) in enumerate(
            (
                (qkv_own, first.place(0, 0, 0)),
                (down_own, rest[0].place(0, 0, 0)),
                (up_own, rest[1].place(0, 0, 0)),
                (gains_own, gains.at[seq_at]),
            )
        )
    ]
    for copy in own_copies:
        copy.start()
    for t in range(1, Z_SIZE):
        first.pass_on(t)
        if t == Z_SIZE - 2:
            for group in rest:
                group.over_z(0)
        first.sides(t - 1)
    first.sides(Z_SIZE - 1)
    for group in rest:
        group.over_plane(0)
        group.to_core((0, 0, 0))
    for number, flips in enumerate(((0, 1), (1, 0), (1, 1))):
        place = gains.at[flipped(y, flips[0]) * 2 + flipped(core, flips[1])]
        pltpu.make_async_remote_copy(
            src_ref=place,
            dst_ref=place,
            send_sem=gain_sends.at[number],
            recv_sem=gain_arrivals.at[number],
            device_id=neighbour("core"),
            device_id_type=pl.DeviceIdType.MESH,
        ).wait_recv()
    for copy in own_copies:
        copy.wait()
    for row in range(4):
        gain_out[:, row * 288 : (row + 1) * 288] = gains[row]
    _, hat = normalized(tokens[...].astype(F32))
    rows = (hat * gain_out[0:1, :]).astype(BF16)
    for t in range(Z_SIZE):
        first.corner(t)
    first.finish()

    def multiply(ctx_block, carry):
        matrix = qkv[ctx_block].reshape(tokens.shape[1], 240)
        pieces[ctx_block] = jnp.dot(rows, matrix, preferred_element_type=F32)
        return carry

    lax.fori_loop(0, 8, multiply, 0)
    for group in rest:
        group.pass_on(1)
    q_part, kv_part = 144, 48
    for at in range(8):
        wide[:, at * q_part : (at + 1) * q_part] = pieces[at, :, :q_part]
        wide[:, 1152 + at * kv_part : 1152 + (at + 1) * kv_part] = pieces[at, :, q_part : q_part + kv_part]
        wide[:, 1536 + at * kv_part : 1536 + (at + 1) * kv_part] = pieces[at, :, q_part + kv_part :]
    cos_tile, sin_tile = cosine[...], sine[...]
    for pair in range(3):
        key_tile = wide[:, 1152 + pair * LANES : 1152 + (pair + 1) * LANES]
        pairs[ctx_at, :, 2 * pair * LANES : (2 * pair + 1) * LANES] = rotate_halves(
            key_tile, cos_tile, sin_tile
        ).astype(BF16)
        pairs[ctx_at, :, (2 * pair + 1) * LANES : (2 * pair + 2) * LANES] = wide[
            :, 1536 + pair * LANES : 1536 + (pair + 1) * LANES
        ].astype(BF16)
    natural = [
        rotate_halves(wide[:, at * LANES : (at + 1) * LANES], cos_tile, sin_tile) * HEAD_SIZE**-0.5
        for at in range(9)
    ]
    for at, tile in enumerate(pair_tiles(natural)):
        query_out[at] = tile.astype(BF16)

    pair_copies = []

    def pair_place(t, dx):
        return pairs.at[lax.rem(z - t + Z_SIZE, Z_SIZE) * 2 + flipped(x, dx)]

    def pair_copy(place, number, axis):
        return pltpu.make_async_remote_copy(
            src_ref=place,
            dst_ref=place,
            send_sem=pair_sends.at[number],
            recv_sem=pair_arrivals.at[number],
            device_id=neighbour(axis),
            device_id_type=pl.DeviceIdType.MESH,
        )

    def pair_pass(t):
        if t:
            pair_copy(pair_place(t, 0), t - 1, "z").wait_recv()
        for number, axis in ((t, "z"), (3 + t, "x")):
            if axis == "x" or t < Z_SIZE - 1:
                copy = pair_copy(pair_place(t, 0), number, axis)
                copy.start()
                pair_copies.append(copy)

    def in_rest(step):
        for group in rest:
            step(group)

    pair_pass(0)
    pair_pass(1)
    in_rest(lambda group: group.pass_on(2))
    pair_pass(2)
    in_rest(lambda group: group.sides(0))
    pair_pass(3)
    in_rest(lambda group: group.sides(1))
    in_rest(lambda group: group.pass_on(3))
    for t in range(Z_SIZE):
        pair_copy(pair_place(t, 1), 3 + t, "x").wait_recv()

    key_ids = lax.broadcasted_iota(jnp.int32, (256, tokens.shape[0]), 0)

    def attend_pair(pair):
        for at in range(8):
            for half in range(2):
                block = pairs[at, :, 2 * pair * LANES : (2 * pair + 1) * LANES]
                keys[half, at] = masked_pair(block, half, 0.0).astype(BF16)
                block = pairs[at, :, (2 * pair + 1) * LANES : (2 * pair + 2) * LANES]
                values[half, at] = masked_pair(block, half, 1.0).T.astype(BF16)

        def attend_member(member, carry):
            tile = query_out[3 * pair + member]
            parts = []
            for half in range(2):
                top = None
                for at in range(8):
                    part = lax.dot_general(keys[half, at], tile, NT, preferred_element_type=F32)
                    part = jnp.where(key_ids < limit[...] - at * 256, part, -1e30)
                    scores[at] = part
                    block_top = jnp.max(part, axis=0, keepdims=True)
                    top = block_top if top is None else jnp.maximum(top, block_top)
                total = jnp.zeros((LANES, tile.shape[0]), F32)
                for at in range(8):
                    weight = jnp.exp(scores[at] - top).astype(BF16)
                    total = total + jnp.dot(values[half, at], weight, preferred_element_type=F32)
                norm = total[HEAD_SIZE : HEAD_SIZE + 1] if half == 0 else total[:1]
                log_total[3 * pair + member, half : half + 1, :] = top + jnp.log(norm)
                own = total[:HEAD_SIZE] if half == 0 else total[HEAD_SIZE:]
                parts.append(own / norm)
            attended[3 * pair + member] = jnp.concatenate(parts, axis=0).T.astype(BF16)
            return carry

        lax.fori_loop(0, 3, attend_member, 0)

    attend_pair(0)
    in_rest(lambda group: group.sides(2))
    attend_pair(1)
    in_rest(lambda group: group.sides(3))
    attend_pair(2)
    for t in range(Z_SIZE):
        in_rest(lambda group: group.corner(t))
    in_rest(lambda group: group.finish())
    for group in (first,) + rest:
        group.drain()
    for copy in pair_copies + gain_copies:
        copy.wait_send()


def front(qkv_own, down_own, up_own, gains_own, tokens, cosine, sine, limit):
    rows, width = tokens.shape
    dma = pltpu.SemaphoreType.DMA
    return pl.pallas_call(
        front_kernel,
        out_shape=(
            jax.ShapeDtypeStruct((8, 4) + qkv_own.shape, BF16),
            jax.ShapeDtypeStruct((4, 8) + down_own.shape, BF16),
            jax.ShapeDtypeStruct((8, 4) + up_own.shape, BF16),
            jax.ShapeDtypeStruct((8, rows, 768), BF16),
            jax.ShapeDtypeStruct((9, rows, LANES), BF16),
            jax.ShapeDtypeStruct((9, rows, LANES), BF16),
            jax.ShapeDtypeStruct((9, 2, rows), F32),
            jax.ShapeDtypeStruct((8, width), F32),
        ),
        in_specs=vmem_specs(1) + any_specs(2) + vmem_specs(5),
        out_specs=tuple(vmem_specs(1) + any_specs(2) + vmem_specs(5)),
        scratch_shapes=[
            pltpu.VMEM((8, rows, 240), F32),
            pltpu.VMEM((rows, 1920), F32),
            pltpu.VMEM((2, 8, 256, LANES), BF16),
            pltpu.VMEM((2, 8, LANES, 256), BF16),
            pltpu.VMEM((8, 256, rows), F32),
            pltpu.VMEM((4, 8, 288), F32),
        ]
        + [dma((31,))] * 6
        + [dma((7,))] * 2
        + [dma((3,))] * 2
        + [dma((4,))],
        compiler_params=pltpu.CompilerParams(
            vmem_limit_bytes=VMEM_LIMIT, collective_id=1, has_side_effects=True
        ),
        cost_estimate=cost(4 * 18 * rows * 2048 * 128 * 4, 4e8, 18 * rows * 2048),
        name="front",
    )(qkv_own, down_own, up_own, gains_own, tokens, cosine, sine, limit)


def attend_back_kernel(query, attended, grad, log_total, limit, cosine, sine, *refs):
    pairs, near, far = refs[0], refs[1], refs[2:6]
    query_grad, keys, keys_turned, values, key_sum, value_sum = refs[6:]

    @pl.when(pl.program_id(1) == 0)
    def _():
        key_sum[...] = jnp.zeros_like(key_sum)
        value_sum[...] = jnp.zeros_like(value_sum)
        for at in range(8):
            for half in range(2):
                masked = masked_pair(pairs[at, :, :LANES], half, 0.0)
                keys[half, at] = masked.astype(BF16)
                keys_turned[half, at] = masked.T.astype(BF16)
                values[half, at] = masked_pair(pairs[at, :, LANES:], half, 0.0).astype(BF16)

    rows = query.shape[1]
    tile, grad_tile = query[0], grad[0]
    product = (attended[0].astype(F32) * grad_tile.astype(F32)).T
    key_ids = lax.broadcasted_iota(jnp.int32, (256, rows), 0)
    turned = jnp.zeros((LANES, rows), F32)
    for half in range(2):
        own = slice(half * HEAD_SIZE, (half + 1) * HEAD_SIZE)
        shift = jnp.sum(product[own], axis=0, keepdims=True)
        log_row = log_total[0, half : half + 1, :]
        query_half = masked_pair(tile, half, 0.0).astype(BF16)
        grad_half = masked_pair(grad_tile, half, 0.0).astype(BF16)
        for at in range(8):
            part = lax.dot_general(keys[half, at], tile, NT, preferred_element_type=F32)
            part = jnp.where(key_ids < limit[...] - at * 256, part, -1e30)
            probs = jnp.exp(part - log_row)
            back = lax.dot_general(values[half, at], grad_tile, NT, preferred_element_type=F32)
            scored = (probs * (back - shift)).astype(BF16)
            value_sum[at] += jnp.dot(probs.astype(BF16), grad_half, preferred_element_type=F32)
            key_sum[at] += jnp.dot(scored, query_half, preferred_element_type=F32)
            turned = turned + jnp.dot(keys_turned[half, at], scored, preferred_element_type=F32)
    query_grad[0] = rotate_halves(turned.T * HEAD_SIZE**-0.5, cosine[...], -sine[...]).astype(BF16)

    @pl.when(pl.program_id(1) == 2)
    def _():
        z, x, _, _ = my_place()
        for at in range(8):
            block = lax.rem(z - at // 2 + Z_SIZE, Z_SIZE) * 2 + flipped(x, at % 2)
            ref = far[at // 2] if at % 2 else near.at[at // 2]
            ref[:, :LANES] = key_sum[block].astype(BF16)
            ref[:, LANES:] = value_sum[block].astype(BF16)


def attend_back(query, attended, grad, log_total, limit, cosine, sine, pairs):
    rows = query.shape[1]
    tile_spec = pl.BlockSpec((1, rows, LANES), lambda p, g: (3 * p + g, 0, 0))
    pair_spec = pl.BlockSpec((256, 2 * LANES), lambda p, g: (0, p))
    table_spec = pl.BlockSpec((rows, LANES), lambda p, g: (0, 0))
    return pl.pallas_call(
        attend_back_kernel,
        grid=(3, 3),
        out_shape=(jax.ShapeDtypeStruct((4, 256, 768), BF16),)
        + (jax.ShapeDtypeStruct((256, 768), BF16),) * 4
        + (jax.ShapeDtypeStruct((9, rows, LANES), BF16),),
        in_specs=[
            tile_spec,
            tile_spec,
            tile_spec,
            pl.BlockSpec((1, 2, rows), lambda p, g: (3 * p + g, 0, 0)),
            pl.BlockSpec((1, rows), lambda p, g: (0, 0)),
            table_spec,
            table_spec,
        ]
        + [pl.BlockSpec((8, 256, 2 * LANES), lambda p, g: (0, 0, p))],
        out_specs=(pl.BlockSpec((4, 256, 2 * LANES), lambda p, g: (0, 0, p)),) + (pair_spec,) * 4 + (tile_spec,),
        scratch_shapes=[
            pltpu.VMEM((2, 8, 256, LANES), BF16),
            pltpu.VMEM((2, 8, LANES, 256), BF16),
            pltpu.VMEM((2, 8, 256, LANES), BF16),
            pltpu.VMEM((8, 256, LANES), F32),
            pltpu.VMEM((8, 256, LANES), F32),
        ],
        compiler_params=params(),
        cost_estimate=cost(4 * 18 * rows * 2048 * 128 * 10, 12e6, 18 * rows * 2048),
        name="attend_back",
    )(query, attended, grad, log_total, limit, cosine, sine, pairs)


def middle_kernel(tokens, attended, cotangent, gain, *refs):
    down_in, up_in = refs[:2]
    (output, hidden, gate_grad, up_grad, rows_two, mixed_grad, proj_grad, attended_out, attended_grad, gain_grad) = refs[2:12]
    down, up_w, gates, ups, wide, down_sems, up_sems = refs[12:]
    down_copies = [pltpu.make_async_copy(down_in.at[at], down.at[at], down_sems.at[at]) for at in range(4)]
    up_copies = [pltpu.make_async_copy(up_in.at[at], up_w.at[at], up_sems.at[at]) for at in range(8)]
    for copy in down_copies + up_copies:
        copy.start()
    width = tokens.shape[1]
    for at, tile in enumerate(natural_tiles([attended[at].astype(F32) for at in range(9)])):
        wide[:, at * LANES : (at + 1) * LANES] = tile
    for copy in down_copies:
        copy.wait()

    def out_block(row):
        return down[row, :, :, 768:].reshape(width, 288)

    def down_block(row):
        return down[row, :, :, :768].reshape(width, 768)

    def gate_block(block):
        return up_w[block, :, :, :384].reshape(width, 384)

    def up_block(block):
        return up_w[block, :, :, 384:].reshape(width, 384)

    mixed_grad[...] = tokens[...].astype(F32)
    for row in range(4):
        part = wide[:, row * 288 : (row + 1) * 288].astype(BF16)
        attended_out[row] = part
        mixed_grad[...] += lax.dot_general(part, out_block(row), NT, preferred_element_type=F32)
    factor, hat = normalized(mixed_grad[...])
    gains = gain[...]
    wide[...] = hat
    rows_two[...] = (hat * gains).astype(BF16)
    for block in range(8):
        up_copies[block].wait()
        gates[block] = jnp.dot(rows_two[...], gate_block(block), preferred_element_type=F32)
        ups[block] = jnp.dot(rows_two[...], up_block(block), preferred_element_type=F32)
    for row in range(4):
        for side in range(2):
            gate, up = gates[2 * row + side], ups[2 * row + side]
            sigmoid = 1.0 / (1.0 + jnp.exp(-gate))
            hidden[row, :, side * 384 : (side + 1) * 384] = (gate * sigmoid * up).astype(BF16)
        mixed_grad[...] += lax.dot_general(hidden[row], down_block(row), NT, preferred_element_type=F32)
        back = jnp.dot(cotangent[...], down_block(row), preferred_element_type=F32)
        for side in range(2):
            gate, up = gates[2 * row + side], ups[2 * row + side]
            sigmoid = 1.0 / (1.0 + jnp.exp(-gate))
            part = back[:, side * 384 : (side + 1) * 384]
            gate_grad[2 * row + side] = (part * up * sigmoid * (1.0 + gate * (1.0 - sigmoid))).astype(BF16)
            up_grad[2 * row + side] = (part * (gate * sigmoid)).astype(BF16)
    output[...] = mixed_grad[...].astype(BF16)
    for block in range(8):
        grad_two = lax.dot_general(
            gate_grad[block], gate_block(block), NT, preferred_element_type=F32
        )
        grad_two = grad_two + lax.dot_general(
            up_grad[block], up_block(block), NT, preferred_element_type=F32
        )
        mixed_grad[...] = grad_two if block == 0 else mixed_grad[...] + grad_two
    grad_two, hat = mixed_grad[...], wide[...]
    gain_grad[...] = jnp.sum(grad_two * hat, axis=0, keepdims=True)
    scaled = grad_two * gains
    total = cotangent[...].astype(F32) + factor * (
        scaled - hat * jnp.mean(scaled * hat, axis=-1, keepdims=True)
    )
    mixed_grad[...] = total
    proj_grad[...] = total.astype(BF16)
    for row in range(4):
        wide[:, row * 288 : (row + 1) * 288] = jnp.dot(
            proj_grad[...], out_block(row), preferred_element_type=F32
        )
    tiles = pair_tiles([wide[:, at * LANES : (at + 1) * LANES] for at in range(9)])
    for at, tile in enumerate(tiles):
        attended_grad[at] = tile.astype(BF16)


def middle(tokens, attended, cotangent, gain, down, up):
    rows, width = tokens.shape
    return pl.pallas_call(
        middle_kernel,
        out_shape=(
            jax.ShapeDtypeStruct((rows, width), BF16),
            jax.ShapeDtypeStruct((4, rows, 768), BF16),
            jax.ShapeDtypeStruct((8, rows, 384), BF16),
            jax.ShapeDtypeStruct((8, rows, 384), BF16),
            jax.ShapeDtypeStruct((rows, width), BF16),
            jax.ShapeDtypeStruct((rows, width), F32),
            jax.ShapeDtypeStruct((rows, width), BF16),
            jax.ShapeDtypeStruct((4, rows, 288), BF16),
            jax.ShapeDtypeStruct((9, rows, LANES), BF16),
            jax.ShapeDtypeStruct((1, width), F32),
        ),
        in_specs=vmem_specs(4) + any_specs(2),
        out_specs=tuple(vmem_specs(10)),
        scratch_shapes=[
            pltpu.VMEM(down.shape, BF16),
            pltpu.VMEM(up.shape, BF16),
            pltpu.VMEM((8, rows, 384), F32),
            pltpu.VMEM((8, rows, 384), F32),
            pltpu.VMEM((rows, width), F32),
            pltpu.SemaphoreType.DMA((4,)),
            pltpu.SemaphoreType.DMA((8,)),
        ],
        compiler_params=params(),
        cost_estimate=cost(2 * rows * width * (6 * 3072 + 2 * 1152), 4e7),
        name="middle",
    )(tokens, attended, cotangent, gain, down, up)


def turned_rows(matrix, parts):
    flat = matrix.astype(F32).T.astype(BF16)
    return flat.reshape(parts, flat.shape[0] // parts, flat.shape[1])


def weight_grad_kernel(keep, first, rows_two, gate_grad, up_grad, hidden, cotangent, proj_grad, attended, *refs):
    if keep:
        arrived, refs = refs[:3], refs[3:]
        near, far, turned = refs[:3], refs[3:6], refs[6:]
    else:
        outs, turned = refs[:3], refs[3:]
    rows_turned, cot_turned, proj_turned = turned
    z, x, y, core = my_place()
    t = pl.program_id(0)

    @pl.when(t == 0)
    def _():
        rows_turned[...] = turned_rows(rows_two[...], 4)
        cot_turned[...] = turned_rows(cotangent[...], 8)
        proj_turned[...] = turned_rows(proj_grad[...], 8)

    target_core = core if keep else 1 - core
    z_at = lax.rem(z - t + Z_SIZE, Z_SIZE)

    def put(group, dx, dy, value):
        if not keep:
            outs[group][0, dx, dy] = value.astype(BF16)
            return
        value = (value + arrived[group][0, dx, dy].astype(F32)).astype(BF16)
        flip, other = (dy, dx) if first[group] == "y" else (dx, dy)
        (far if flip else near)[group][0, other] = value

    for dx in range(2):
        ctx_block = z_at * 2 + flipped(x, dx)
        for dy in range(2):
            row = flipped(y, dy) * 2 + target_core
            left = rows_turned[row]
            put(1, dx, dy, jnp.dot(left, gate_grad[ctx_block], preferred_element_type=F32))
            put(2, dx, dy, jnp.dot(left, up_grad[ctx_block], preferred_element_type=F32))
            value = jnp.concatenate(
                [
                    jnp.dot(cot_turned[ctx_block], hidden[row], preferred_element_type=F32),
                    jnp.dot(proj_turned[ctx_block], attended[row], preferred_element_type=F32),
                ],
                axis=1,
            )
            put(0, dx, dy, value)


def weight_grads(keep, first, rows_two, gate_grad, up_grad, hidden, cotangent, proj_grad, attended, arrived=()):
    rows, width = rows_two.shape
    shapes = ((144, 1056), (288, 384), (288, 384))
    both = [(Z_SIZE, 2, 2) + shape for shape in shapes]
    half = [(Z_SIZE, 2) + shape for shape in shapes]

    def spec(shape):
        return pl.BlockSpec((1,) + shape[1:], lambda t: (t,) + (0,) * (len(shape) - 1))

    whole = [rows_two, gate_grad, up_grad, hidden, cotangent, proj_grad, attended]
    out = half + half if keep else both
    return pl.pallas_call(
        functools.partial(weight_grad_kernel, keep, first),
        grid=(Z_SIZE,),
        out_shape=tuple(jax.ShapeDtypeStruct(shape, BF16) for shape in out),
        in_specs=[
            pl.BlockSpec(array.shape, lambda t, rank=array.ndim: (0,) * rank) for array in whole
        ]
        + [spec(shape) for shape in (both if keep else [])],
        out_specs=tuple(spec(shape) for shape in out),
        scratch_shapes=[
            pltpu.VMEM((4, 288, rows), BF16),
            pltpu.VMEM((8, 144, rows), BF16),
            pltpu.VMEM((8, 144, rows), BF16),
        ],
        compiler_params=params(),
        cost_estimate=cost(rows * width * (3 * 3072 + 1152), 3e7),
        name="weight_grads_keep" if keep else "weight_grads_send",
    )(*whole, *arrived)


def project_back_kernel(tokens, gain, query_grad, pair_grad, mixed_grad, cosine, sine, *refs):
    weights, input_grad, gain_grad, send, kept, buffer, pieces, wide, rows_turned, sem = refs
    z, x, y, core = my_place()
    copy = pltpu.make_async_copy(weights, buffer, sem)
    copy.start()
    width = tokens.shape[1]
    factor, hat = normalized(tokens[...].astype(F32))
    gains = gain[...]
    rows_turned[...] = turned_rows((hat * gains).astype(BF16), 4)
    for at, tile in enumerate(natural_tiles([query_grad[at].astype(F32) for at in range(9)])):
        wide[:, at * LANES : (at + 1) * LANES] = tile
    cos_tile, sin_tile = cosine[...], -sine[...]
    for pair in range(3):
        key_tile = pair_grad[:, 2 * pair * LANES : (2 * pair + 1) * LANES].astype(F32)
        wide[:, 1152 + pair * LANES : 1152 + (pair + 1) * LANES] = rotate_halves(key_tile, cos_tile, sin_tile)
        wide[:, 1536 + pair * LANES : 1536 + (pair + 1) * LANES] = pair_grad[
            :, (2 * pair + 1) * LANES : (2 * pair + 2) * LANES
        ].astype(F32)
    q_part, kv_part = 144, 48
    for at in range(8):
        pieces[at] = jnp.concatenate(
            [
                wide[:, at * q_part : (at + 1) * q_part],
                wide[:, 1152 + at * kv_part : 1152 + (at + 1) * kv_part],
                wide[:, 1536 + at * kv_part : 1536 + (at + 1) * kv_part],
            ],
            axis=1,
        ).astype(BF16)
    for t in range(Z_SIZE):
        for dx in range(2):
            block = lax.rem(z - t + Z_SIZE, Z_SIZE) * 2 + flipped(x, dx)
            for dy in range(2):
                for keep in range(2):
                    row = flipped(y, dy) * 2 + (core if keep else 1 - core)
                    value = jnp.dot(rows_turned[row], pieces[block], preferred_element_type=F32)
                    (kept if keep else send)[t, dx, dy] = value.astype(BF16)
    copy.wait()
    grad_one = jnp.zeros_like(hat)
    for block in range(8):
        grad_one = grad_one + lax.dot_general(
            pieces[block], buffer[block].reshape(width, 240), NT, preferred_element_type=F32
        )
    gain_grad[...] = jnp.sum(grad_one * hat, axis=0, keepdims=True)
    scaled = grad_one * gains
    input_grad[...] = mixed_grad[...] + factor * (
        scaled - hat * jnp.mean(scaled * hat, axis=-1, keepdims=True)
    )


def project_back(tokens, gain, query_grad, pair_grad, mixed_grad, cosine, sine, weights):
    rows, width = tokens.shape
    piece = weights.shape[2:]
    return pl.pallas_call(
        project_back_kernel,
        out_shape=(
            jax.ShapeDtypeStruct((rows, width), F32),
            jax.ShapeDtypeStruct((1, width), F32),
            jax.ShapeDtypeStruct((Z_SIZE, 2, 2) + piece, BF16),
            jax.ShapeDtypeStruct((Z_SIZE, 2, 2) + piece, BF16),
        ),
        in_specs=vmem_specs(7) + any_specs(1),
        out_specs=tuple(vmem_specs(4)),
        scratch_shapes=[
            pltpu.VMEM((8, 4) + piece, BF16),
            pltpu.VMEM((8, rows, 240), BF16),
            pltpu.VMEM((rows, 1920), F32),
            pltpu.VMEM((4, 288, rows), BF16),
            pltpu.SemaphoreType.DMA,
        ],
        compiler_params=params(),
        cost_estimate=cost(4 * rows * width * 1920, 1.4e7),
        name="project_back",
    )(tokens, gain, query_grad, pair_grad, mixed_grad, cosine, sine, weights)


def lane_tables(first, rows):
    half = HEAD_SIZE // 2
    frequency = ROTARY_BASE ** (-jnp.arange(half, dtype=F32) * 2.0 / HEAD_SIZE)
    angles = (first + jnp.arange(rows, dtype=jnp.int32)).astype(F32)[:, None] * frequency[None, :]
    cosine, sine = jnp.cos(angles), jnp.sin(angles)
    return jnp.tile(cosine, (1, 4)), jnp.tile(jnp.concatenate([-sine, sine], axis=1), (1, 2))


def permuted_device(
    tokens, prefix, gain_one, w_query, w_key, value_weight, w_out, gain_two, w_gate, w_up, w_down, cotangent
):
    _, rows, width = tokens.shape
    tokens, cotangent = tokens[0], cotangent[0]
    ctx_at, seq_at = lax.axis_index("ctx"), lax.axis_index("seq")
    gains = jnp.zeros((8, gain_one.shape[0]), F32).at[0].set(gain_one.astype(F32)).at[1].set(gain_two.astype(F32))
    cosine, sine = lane_tables(ctx_at * rows, rows)
    limit = jnp.maximum(ctx_at * rows + jnp.arange(rows, dtype=jnp.int32) + 1, prefix[0])[None, :]
    qkv, down, up, pairs, query, attended, log_total, gains = front(
        jnp.concatenate([w_query, w_key, value_weight], axis=1),
        jnp.concatenate([w_down.T, w_out.T], axis=1),
        jnp.concatenate([w_gate, w_up], axis=1),
        gains,
        tokens,
        cosine,
        sine,
        limit,
    )
    first_norm, second_norm = gains[0:1], gains[1:2]
    (
        output,
        hidden,
        gate_grad,
        up_grad,
        rows_two,
        mixed_grad,
        proj_grad,
        attended_rows,
        attended_grad,
        second_gain_part,
    ) = middle(tokens, attended, cotangent, second_norm, down, up)

    first = ("x", "y", "x")
    factors = (rows_two, gate_grad, up_grad, hidden, cotangent, proj_grad, attended_rows)
    sent = weight_grads(False, first, *factors)
    attended_grad, sent = lax.optimization_barrier((attended_grad, sent))
    arrived = [hop(array, "core") for array in sent]
    near, *far, query_grad = attend_back(
        query, attended, attended_grad, log_total, limit, cosine, sine, pairs
    )
    arrived, near, far = lax.optimization_barrier((arrived, near, far))
    parts = weight_grads(True, first, *factors, arrived)
    grad_down_out, grad_gate, grad_up = [
        scatter_rest(parts[at], parts[3 + at], first[at]) for at in range(3)
    ]
    second_gain_gradient = sum_everywhere(second_gain_part)

    total = add_pair(near[3], hop(far[3], "x"))
    for t in (2, 1, 0):
        local = near[t].astype(F32) + hop(far[t], "x").astype(F32)
        total = (local + hop(total, "z", -1).astype(F32)).astype(BF16)
    input_grad, first_gain_part, qkv_send, qkv_keep = project_back(
        tokens, first_norm, query_grad, total, mixed_grad, cosine, sine, qkv
    )
    qkv_sum = add_pair(qkv_keep, hop(qkv_send, "core"))
    grad_qkv = scatter_rest(qkv_sum[:, :, 0], qkv_sum[:, :, 1], "y")
    first_gain_gradient = sum_everywhere(first_gain_part)

    def own_gain(vector):
        return lax.dynamic_slice(vector[0], (seq_at * 288,), (288,))

    return (
        output[None],
        input_grad[None],
        own_gain(first_gain_gradient),
        grad_qkv[:, :144],
        grad_qkv[:, 144:192],
        grad_qkv[:, 192:],
        grad_down_out[:, 768:].T,
        own_gain(second_gain_gradient),
        grad_gate,
        grad_up,
        grad_down_out[:, :768].T,
    )


def permute_plan_fits(mesh, tokens):
    return dict(mesh.shape) == {"seq": 4, "ctx": 8} and tokens.shape == (4, 2048, 1152)


def solution(mesh):
    placed = (
        P("seq", "ctx", None),
        P("seq"),
        P("seq"),
        P("seq", "ctx"),
        P("seq", "ctx"),
        P("seq", "ctx"),
        P("seq", "ctx"),
        P("seq"),
        P("seq", "ctx"),
        P("seq", "ctx"),
        P("seq", "ctx"),
        P("seq", "ctx", None),
    )

    def mapped(device_function):
        return jax.shard_map(
            device_function,
            mesh=mesh,
            in_specs=placed,
            out_specs=(
                P("seq", "ctx", None),
                P("seq", "ctx", None),
                P("seq"),
                P("seq", "ctx"),
                P("seq", "ctx"),
                P("seq", "ctx"),
                P("seq", "ctx"),
                P("seq"),
                P("seq", "ctx"),
                P("seq", "ctx"),
                P("seq", "ctx"),
            ),
            check_vma=False,
        )

    def layer(tokens, *rest):
        return mapped(permuted_device if permute_plan_fits(mesh, tokens) else per_device)(tokens, *rest)

    return layer
```

```python
import functools

import jax
import jax.numpy as jnp
from jax import lax
from jax.experimental import pallas as pl
from jax.experimental.pallas import tpu as pltpu
from jax.sharding import PartitionSpec as P

QUERY_HEADS = 18
KEY_VALUE_HEADS = 6
HEAD_SIZE = 64


EPSILON = 1e-05
ROTARY_BASE = 10000.0

LANES = 128
Z_SIZE = 4
VMEM_LIMIT = 66_000_000
F32 = jnp.float32
BF16 = jnp.bfloat16
NT = (((1,), (1,)), ((), ()))


def rotary_tables(positions, head_width):
    half_width = head_width // 2
    frequency = ROTARY_BASE ** (-jnp.arange(half_width, dtype=jnp.float32) * 2.0 / head_width)
    angles = positions.astype(jnp.float32)[:, None] * frequency[None, :]
    return (jnp.cos(angles)[:, None, :], jnp.sin(angles)[:, None, :])


def apply_rotation(values_in, cosine_table, sine_values):
    half_width = values_in.shape[-1] // 2
    first = values_in[..., :half_width]
    second = values_in[..., half_width:]
    return jnp.concatenate(
        [first * cosine_table - second * sine_values, second * cosine_table + first * sine_values],
        axis=-1,
    )


def inverse_rotation(grads_in, cosine_table, sine_values):
    half_width = grads_in.shape[-1] // 2
    first = grads_in[..., :half_width]
    second = grads_in[..., half_width:]
    return jnp.concatenate(
        [first * cosine_table + second * sine_values, second * cosine_table - first * sine_values],
        axis=-1,
    )


def gather_weights(w_query, w_key, value_weight, w_out, w_gate, w_up, w_down, gain_one, gain_two):
    columns = (
        lax.all_gather(w_query, "ctx", axis=1, tiled=True),
        lax.all_gather(w_key, "ctx", axis=1, tiled=True),
        lax.all_gather(value_weight, "ctx", axis=1, tiled=True),
        lax.all_gather(w_out, "ctx", axis=1, tiled=True),
        lax.all_gather(w_gate, "ctx", axis=1, tiled=True),
        lax.all_gather(w_up, "ctx", axis=1, tiled=True),
        lax.all_gather(w_down, "ctx", axis=1, tiled=True),
    )
    return (
        lax.all_gather(columns[0], "seq", axis=0, tiled=True),
        lax.all_gather(columns[1], "seq", axis=0, tiled=True),
        lax.all_gather(columns[2], "seq", axis=0, tiled=True),
        lax.all_gather(columns[3], "seq", axis=0, tiled=True),
        lax.all_gather(columns[4], "seq", axis=0, tiled=True),
        lax.all_gather(columns[5], "seq", axis=0, tiled=True),
        lax.all_gather(columns[6], "seq", axis=0, tiled=True),
        lax.all_gather(gain_one, "seq", axis=0, tiled=True),
        lax.all_gather(gain_two, "seq", axis=0, tiled=True),
    )


def gather_pairs(key_rotated, value_reduced):
    return (
        lax.all_gather(key_rotated, "ctx", axis=1, tiled=True),
        lax.all_gather(value_reduced, "ctx", axis=1, tiled=True),
    )


def head_major(whole_result, sequence_count):
    sequence_length = whole_result.shape[1]
    return (
        whole_result.reshape(sequence_count, sequence_length, KEY_VALUE_HEADS, HEAD_SIZE)
        .transpose(0, 2, 1, 3)
        .reshape(sequence_count * KEY_VALUE_HEADS, sequence_length, HEAD_SIZE)
    )


def per_device(
    tokens,
    prefix,
    gain_one,
    w_query,
    w_key,
    value_weight,
    w_out,
    gain_two,
    w_gate,
    w_up,
    w_down,
    cotangent,
):
    sequence_count, token_local, model_width = tokens.shape
    sequence_length = token_local * lax.axis_size("ctx")
    number_of_rows = sequence_count * token_local
    queries_per_key_head = QUERY_HEADS // KEY_VALUE_HEADS
    score_scale = HEAD_SIZE ** (-0.5)
    gathered = gather_weights(
        w_query, w_key, value_weight, w_out, w_gate, w_up, w_down, gain_one, gain_two
    )
    full_query, full_key, full_value, full_out, full_gate, full_up, full_down = gathered[:7]
    first_norm = gathered[7].astype(jnp.float32)
    second_norm = gathered[8].astype(jnp.float32)
    input_rows = tokens.reshape(number_of_rows, model_width).astype(jnp.float32)
    first_factor = lax.rsqrt(jnp.mean(input_rows * input_rows, axis=-1, keepdims=True) + EPSILON)
    first_normalized_input = input_rows * first_factor
    normalized_rows = (first_normalized_input * first_norm).astype(jnp.bfloat16)
    query_pre = jnp.dot(normalized_rows, full_query, preferred_element_type=jnp.float32)
    key_prerotation = jnp.dot(normalized_rows, full_key, preferred_element_type=jnp.float32)
    value_reduced = jnp.dot(normalized_rows, full_value, preferred_element_type=jnp.float32).astype(
        jnp.bfloat16
    )
    positions = lax.axis_index("ctx") * token_local + jnp.arange(token_local, dtype=jnp.int32)
    cosine_table, sine_values = rotary_tables(positions, HEAD_SIZE)
    query_rows = apply_rotation(
        query_pre.reshape(sequence_count, token_local, QUERY_HEADS, HEAD_SIZE),
        cosine_table,
        sine_values,
    ).astype(jnp.bfloat16)
    key_rotated = apply_rotation(
        key_prerotation.reshape(sequence_count, token_local, KEY_VALUE_HEADS, HEAD_SIZE),
        cosine_table,
        sine_values,
    ).astype(jnp.bfloat16)
    key_rotated = key_rotated.reshape(sequence_count, token_local, KEY_VALUE_HEADS * HEAD_SIZE)
    value_reduced = value_reduced.reshape(sequence_count, token_local, KEY_VALUE_HEADS * HEAD_SIZE)
    keys_all, values_all = gather_pairs(key_rotated, value_reduced)
    query_block_list = query_rows.reshape(
        sequence_count, token_local, KEY_VALUE_HEADS, queries_per_key_head, HEAD_SIZE
    ).transpose(0, 2, 3, 1, 4)
    query_block_list = query_block_list.reshape(
        sequence_count * KEY_VALUE_HEADS, queries_per_key_head, token_local, HEAD_SIZE
    )
    key_blocks = head_major(keys_all, sequence_count)
    value_blocks = head_major(values_all, sequence_count)
    prefix_repeated = jnp.repeat(prefix, KEY_VALUE_HEADS)
    key_place = jnp.arange(sequence_length, dtype=jnp.int32)

    def visible_for(prefix_len):
        return (key_place[None, :] <= positions[:, None]) | (key_place[None, :] < prefix_len)

    def attend(block_item):
        query_block, key_block, value_block, prefix_len = block_item
        scores = (
            jnp.einsum("gqd,kd->gqk", query_block, key_block, preferred_element_type=jnp.float32)
            * score_scale
        )
        scores = jnp.where(visible_for(prefix_len)[None], scores, -1e30)
        row_max = jnp.max(scores, axis=-1, keepdims=True)
        expo = jnp.exp(scores - row_max)
        total = jnp.sum(expo, axis=-1, keepdims=True)
        probs_low = (expo / total).astype(jnp.bfloat16)
        result = jnp.einsum(
            "gqk,kd->gqd", probs_low, value_block, preferred_element_type=jnp.float32
        )
        return (result.astype(jnp.bfloat16), (row_max + jnp.log(total))[..., 0])

    attention_result_blocks, log_totals = lax.map(
        attend, (query_block_list, key_blocks, value_blocks, prefix_repeated)
    )
    attention_result = attention_result_blocks.reshape(
        sequence_count, KEY_VALUE_HEADS, queries_per_key_head, token_local, HEAD_SIZE
    ).transpose(0, 3, 1, 2, 4)
    attention_result = attention_result.reshape(number_of_rows, QUERY_HEADS * HEAD_SIZE)
    mixed_output = input_rows + jnp.dot(
        attention_result, full_out, preferred_element_type=jnp.float32
    )
    second_factor = lax.rsqrt(
        jnp.mean(mixed_output * mixed_output, axis=-1, keepdims=True) + EPSILON
    )
    second_normalized_input = mixed_output * second_factor
    normalized_second = (second_normalized_input * second_norm).astype(jnp.bfloat16)
    gate = jnp.dot(normalized_second, full_gate, preferred_element_type=jnp.float32)
    up_part = jnp.dot(normalized_second, full_up, preferred_element_type=jnp.float32)
    sigmoid_gate = jax.nn.sigmoid(gate)
    activated = gate * sigmoid_gate
    hidden = (activated * up_part).astype(jnp.bfloat16)
    result_rows = mixed_output + jnp.dot(hidden, full_down, preferred_element_type=jnp.float32)
    output = result_rows.astype(jnp.bfloat16).reshape(sequence_count, token_local, model_width)
    gathered = gather_weights(
        w_query, w_key, value_weight, w_out, w_gate, w_up, w_down, gain_one, gain_two
    )
    full_query, full_key, full_value, full_out, full_gate, full_up, full_down = gathered[:7]
    grad_rows_in = cotangent.reshape(number_of_rows, model_width)
    grad_down = jnp.dot(hidden.T, grad_rows_in, preferred_element_type=jnp.float32)
    dhidden = jnp.dot(grad_rows_in, full_down.T, preferred_element_type=jnp.float32)
    dgate = (dhidden * up_part * sigmoid_gate * (1.0 + gate * (1.0 - sigmoid_gate))).astype(
        jnp.bfloat16
    )
    dup_part = (dhidden * activated).astype(jnp.bfloat16)
    grad_gate = jnp.dot(normalized_second.T, dgate, preferred_element_type=jnp.float32)
    grad_up = jnp.dot(normalized_second.T, dup_part, preferred_element_type=jnp.float32)
    normalized_second_grad = jnp.dot(dgate, full_gate.T, preferred_element_type=jnp.float32)
    normalized_second_grad = normalized_second_grad + jnp.dot(
        dup_part, full_up.T, preferred_element_type=jnp.float32
    )
    second_gain_gradient = jnp.sum(normalized_second_grad * second_normalized_input, axis=0)
    second_scaled = normalized_second_grad * second_norm
    dmixed = grad_rows_in.astype(jnp.float32) + second_factor * (
        second_scaled
        - second_normalized_input
        * jnp.mean(second_scaled * second_normalized_input, axis=-1, keepdims=True)
    )
    dproj = dmixed.astype(jnp.bfloat16)
    grad_out = jnp.dot(attention_result.T, dproj, preferred_element_type=jnp.float32)
    attention_result_grad = jnp.dot(dproj, full_out.T, preferred_element_type=jnp.float32).astype(
        jnp.bfloat16
    )
    attention_result_block_grads = attention_result_grad.reshape(
        sequence_count, token_local, KEY_VALUE_HEADS, queries_per_key_head, HEAD_SIZE
    ).transpose(0, 2, 3, 1, 4)
    attention_result_block_grads = attention_result_block_grads.reshape(
        sequence_count * KEY_VALUE_HEADS, queries_per_key_head, token_local, HEAD_SIZE
    )
    keys_all, values_all = gather_pairs(key_rotated, value_reduced)
    key_blocks = head_major(keys_all, sequence_count)
    value_blocks = head_major(values_all, sequence_count)

    def attend_back(block_item):
        query_block, key_block, value_block, prefix_len, log_total, dout_block = block_item
        scores = (
            jnp.einsum("gqd,kd->gqk", query_block, key_block, preferred_element_type=jnp.float32)
            * score_scale
        )
        visible = visible_for(prefix_len)[None]
        probs = jnp.where(
            visible, jnp.exp(jnp.where(visible, scores, -1e30) - log_total[..., None]), 0.0
        )
        dvalues = jnp.einsum(
            "gqk,gqd->kd",
            probs.astype(jnp.bfloat16),
            dout_block,
            preferred_element_type=jnp.float32,
        )
        dprobs = jnp.einsum(
            "gqd,kd->gqk", dout_block, value_block, preferred_element_type=jnp.float32
        )
        dscores = (probs * (dprobs - jnp.sum(probs * dprobs, axis=-1, keepdims=True))).astype(
            jnp.bfloat16
        )
        dquery = (
            jnp.einsum("gqk,kd->gqd", dscores, key_block, preferred_element_type=jnp.float32)
            * score_scale
        )
        dkeys = (
            jnp.einsum("gqk,gqd->kd", dscores, query_block, preferred_element_type=jnp.float32)
            * score_scale
        )
        return (dquery, dkeys, dvalues)

    query_block_grads, key_block_grads, value_block_grads = lax.map(
        attend_back,
        (
            query_block_list,
            key_blocks,
            value_blocks,
            prefix_repeated,
            log_totals,
            attention_result_block_grads,
        ),
    )
    key_grads_combined = key_block_grads.reshape(
        sequence_count, KEY_VALUE_HEADS, sequence_length, HEAD_SIZE
    ).transpose(0, 2, 1, 3)
    key_grads_combined = key_grads_combined.reshape(
        sequence_count, sequence_length, KEY_VALUE_HEADS * HEAD_SIZE
    )
    value_grads_combined = value_block_grads.reshape(
        sequence_count, KEY_VALUE_HEADS, sequence_length, HEAD_SIZE
    ).transpose(0, 2, 1, 3)
    value_grads_combined = value_grads_combined.reshape(
        sequence_count, sequence_length, KEY_VALUE_HEADS * HEAD_SIZE
    )
    key_grads_local, value_grads_local = (
        lax.psum_scatter(
            key_grads_combined.astype(jnp.bfloat16), "ctx", scatter_dimension=1, tiled=True
        ).astype(jnp.float32),
        lax.psum_scatter(
            value_grads_combined.astype(jnp.bfloat16), "ctx", scatter_dimension=1, tiled=True
        ).astype(jnp.float32),
    )
    key_prerotation_grad = inverse_rotation(
        key_grads_local.reshape(sequence_count, token_local, KEY_VALUE_HEADS, HEAD_SIZE),
        cosine_table,
        sine_values,
    )
    key_prerotation_grad = key_prerotation_grad.astype(jnp.bfloat16).reshape(
        number_of_rows, KEY_VALUE_HEADS * HEAD_SIZE
    )
    value_reduced_grad = value_grads_local.astype(jnp.bfloat16).reshape(
        number_of_rows, KEY_VALUE_HEADS * HEAD_SIZE
    )
    query_row_grads = query_block_grads.reshape(
        sequence_count, KEY_VALUE_HEADS, queries_per_key_head, token_local, HEAD_SIZE
    ).transpose(0, 3, 1, 2, 4)
    query_row_grads = query_row_grads.reshape(sequence_count, token_local, QUERY_HEADS, HEAD_SIZE)
    dquery_pre = (
        inverse_rotation(query_row_grads, cosine_table, sine_values)
        .astype(jnp.bfloat16)
        .reshape(number_of_rows, QUERY_HEADS * HEAD_SIZE)
    )
    grad_query = jnp.dot(normalized_rows.T, dquery_pre, preferred_element_type=jnp.float32)
    grad_key = jnp.dot(normalized_rows.T, key_prerotation_grad, preferred_element_type=jnp.float32)
    grad_value = jnp.dot(normalized_rows.T, value_reduced_grad, preferred_element_type=jnp.float32)
    normalized_grad = jnp.dot(dquery_pre, full_query.T, preferred_element_type=jnp.float32)
    normalized_grad = normalized_grad + jnp.dot(
        key_prerotation_grad, full_key.T, preferred_element_type=jnp.float32
    )
    normalized_grad = normalized_grad + jnp.dot(
        value_reduced_grad, full_value.T, preferred_element_type=jnp.float32
    )
    first_gain_gradient = jnp.sum(normalized_grad * first_normalized_input, axis=0)
    first_scaled = normalized_grad * first_norm
    input_grad = dmixed + first_factor * (
        first_scaled
        - first_normalized_input
        * jnp.mean(first_scaled * first_normalized_input, axis=-1, keepdims=True)
    )
    input_grad = input_grad.reshape(sequence_count, token_local, model_width)
    partial_value = (
        lax.psum_scatter(
            grad_query.astype(jnp.bfloat16), "seq", scatter_dimension=0, tiled=True
        ).astype(jnp.float32),
        lax.psum_scatter(
            grad_key.astype(jnp.bfloat16), "seq", scatter_dimension=0, tiled=True
        ).astype(jnp.float32),
        lax.psum_scatter(
            grad_value.astype(jnp.bfloat16), "seq", scatter_dimension=0, tiled=True
        ).astype(jnp.float32),
        lax.psum_scatter(
            grad_out.astype(jnp.bfloat16), "seq", scatter_dimension=0, tiled=True
        ).astype(jnp.float32),
        lax.psum_scatter(
            grad_gate.astype(jnp.bfloat16), "seq", scatter_dimension=0, tiled=True
        ).astype(jnp.float32),
        lax.psum_scatter(
            grad_up.astype(jnp.bfloat16), "seq", scatter_dimension=0, tiled=True
        ).astype(jnp.float32),
        lax.psum_scatter(
            grad_down.astype(jnp.bfloat16), "seq", scatter_dimension=0, tiled=True
        ).astype(jnp.float32),
        lax.psum_scatter(
            first_gain_gradient.astype(jnp.bfloat16), "seq", scatter_dimension=0, tiled=True
        ).astype(jnp.float32),
        lax.psum_scatter(
            second_gain_gradient.astype(jnp.bfloat16), "seq", scatter_dimension=0, tiled=True
        ).astype(jnp.float32),
    )
    owned = (
        lax.psum_scatter(
            partial_value[0].astype(jnp.bfloat16), "ctx", scatter_dimension=1, tiled=True
        ).astype(jnp.float32),
        lax.psum_scatter(
            partial_value[1].astype(jnp.bfloat16), "ctx", scatter_dimension=1, tiled=True
        ).astype(jnp.float32),
        lax.psum_scatter(
            partial_value[2].astype(jnp.bfloat16), "ctx", scatter_dimension=1, tiled=True
        ).astype(jnp.float32),
        lax.psum_scatter(
            partial_value[3].astype(jnp.bfloat16), "ctx", scatter_dimension=1, tiled=True
        ).astype(jnp.float32),
        lax.psum_scatter(
            partial_value[4].astype(jnp.bfloat16), "ctx", scatter_dimension=1, tiled=True
        ).astype(jnp.float32),
        lax.psum_scatter(
            partial_value[5].astype(jnp.bfloat16), "ctx", scatter_dimension=1, tiled=True
        ).astype(jnp.float32),
        lax.psum_scatter(
            partial_value[6].astype(jnp.bfloat16), "ctx", scatter_dimension=1, tiled=True
        ).astype(jnp.float32),
    )
    gains_owned = lax.psum((partial_value[7], partial_value[8]), "ctx")
    final_grads = owned + gains_owned
    return (
        output,
        input_grad,
        final_grads[7],
        final_grads[0],
        final_grads[1],
        final_grads[2],
        final_grads[3],
        final_grads[8],
        final_grads[4],
        final_grads[5],
        final_grads[6],
    )


def my_place():
    seq_at, ctx_at = lax.axis_index("seq"), lax.axis_index("ctx")
    return ctx_at // 2, lax.rem(ctx_at, 2), seq_at // 2, lax.rem(seq_at, 2)


def flipped(at, flip):
    return 1 - at if flip else at


def lane_ids(rows):
    return lax.broadcasted_iota(jnp.int32, (rows, LANES), 1)


def rotate_halves(tile, cosine, sine):
    lower = lax.rem(lane_ids(tile.shape[0]), HEAD_SIZE) < HEAD_SIZE // 2
    swapped = jnp.where(
        lower, pltpu.roll(tile, LANES - HEAD_SIZE // 2, 1), pltpu.roll(tile, HEAD_SIZE // 2, 1)
    )
    return tile * cosine + swapped * sine


def pair_tiles(natural):
    lower = lane_ids(natural[0].shape[0]) < HEAD_SIZE
    tiles = []
    for pair in range(3):
        for member in range(3):
            one, two = 6 * pair + member, 6 * pair + 3 + member
            left, right = natural[one // 2], natural[two // 2]
            if one % 2:
                left, right = pltpu.roll(left, HEAD_SIZE, 1), pltpu.roll(right, HEAD_SIZE, 1)
            tiles.append(jnp.where(lower, left, right))
    return tiles


def natural_tiles(paired):
    lower = lane_ids(paired[0].shape[0]) < HEAD_SIZE
    tiles = []
    for at in range(9):
        sides = []
        for side in range(2):
            head = 2 * at + side
            tile = paired[head // 6 * 3 + head % 3]
            if (head % 6) // 3 != side:
                tile = pltpu.roll(tile, HEAD_SIZE, 1)
            sides.append(tile)
        tiles.append(jnp.where(lower, sides[0], sides[1]))
    return tiles


def normalized(rows):
    factor = lax.rsqrt(jnp.mean(rows * rows, axis=-1, keepdims=True) + EPSILON)
    return factor, rows * factor


def vmem_specs(count):
    return [pl.BlockSpec(memory_space=pltpu.VMEM)] * count


def any_specs(count):
    return [pl.BlockSpec(memory_space=pl.ANY)] * count


def cost(flops, moved, transcendentals=0):
    return pl.CostEstimate(flops=int(flops), bytes_accessed=int(moved), transcendentals=int(transcendentals))


def params():
    return pltpu.CompilerParams(vmem_limit_bytes=VMEM_LIMIT)


def masked_pair(block, half, other):
    inside = (lane_ids(block.shape[0]) < HEAD_SIZE) == (half == 0)
    return jnp.where(inside, block.astype(F32), other)


class Gathering:
    def __init__(self, own, full, block, sends, arrivals, corner_over_x):
        self.own, self.full, self.block, self.sends, self.arrivals = own, full, block, sends, arrivals
        self.corner_over_x = corner_over_x
        self.started = []

    def place(self, t, dx, dy, dcore=0):
        z, x, y, core = my_place()
        ctx_block = lax.rem(z - t + Z_SIZE, Z_SIZE) * 2 + flipped(x, dx)
        return self.full.at[self.block(ctx_block, flipped(y, dy) * 2 + flipped(core, dcore))]

    def copy(self, source, target, number, axis):
        return pltpu.make_async_remote_copy(
            src_ref=source,
            dst_ref=target,
            send_sem=self.sends.at[number],
            recv_sem=self.arrivals.at[number],
            device_id=neighbour(axis),
            device_id_type=pl.DeviceIdType.MESH,
        )

    def send(self, piece, number, axis):
        place = self.place(*piece)
        copy = self.copy(self.own if piece == (0, 0, 0) else place, place, number, axis)
        copy.start()
        self.started.append(copy)

    def wait(self, piece, number, dcore=0):
        place = self.place(*piece, dcore)
        self.copy(place, place, number, "core").wait_recv()

    def to_core(self, piece):
        t, dx, dy = piece
        self.send(piece, 15 + 4 * t + 2 * dx + dy, "core")

    def over_z(self, t):
        if t < Z_SIZE - 1:
            self.send((t, 0, 0), t, "z")

    def over_plane(self, t):
        self.send((t, 0, 0), 3 + t, "x")
        self.send((t, 0, 0), 7 + t, "y")

    def begin(self):
        self.over_z(0)
        self.over_plane(0)
        self.to_core((0, 0, 0))

    def pass_on(self, t):
        self.wait((t, 0, 0), t - 1)
        self.over_z(t)
        self.over_plane(t)
        self.to_core((t, 0, 0))

    def sides(self, t):
        self.wait((t, 1, 0), 3 + t)
        if t not in self.corner_over_x:
            self.send((t, 1, 0), 11 + t, "y")
        self.to_core((t, 1, 0))
        self.wait((t, 0, 1), 7 + t)
        if t in self.corner_over_x:
            self.send((t, 0, 1), 11 + t, "x")
        self.to_core((t, 0, 1))

    def corner(self, t):
        self.wait((t, 1, 1), 11 + t)
        self.to_core((t, 1, 1))

    def finish(self):
        for t in range(Z_SIZE):
            for dx in range(2):
                for dy in range(2):
                    self.wait((t, dx, dy), 15 + 4 * t + 2 * dx + dy, 1)

    def drain(self):
        for copy in self.started:
            copy.wait_send()


def neighbour(axis):
    z, x, y, core = my_place()
    if axis == "z":
        z = lax.rem(z + 1, Z_SIZE)
    elif axis == "z_back":
        z = lax.rem(z + Z_SIZE - 1, Z_SIZE)
    elif axis == "z_two":
        z = lax.rem(z + 2, Z_SIZE)
    elif axis == "x":
        x = 1 - x
    elif axis == "y":
        y = 1 - y
    elif axis == "core":
        core = 1 - core
    elif axis == "y_core":
        y, core = 1 - y, 1 - core
    return (y * 2 + core, z * 2 + x)


def meet(axes):
    barrier = pltpu.get_barrier_semaphore()
    for axis in axes:
        pl.semaphore_signal(barrier, inc=1, device_id=neighbour(axis), device_id_type=pl.DeviceIdType.MESH)
    pl.semaphore_wait(barrier, len(axes))


def front_kernel(
    qkv_own,
    down_own,
    up_own,
    gains_own,
    tokens,
    cosine,
    sine,
    limit,
    qkv,
    down,
    up,
    pairs,
    query_out,
    attended,
    log_total,
    gain_out,
    pieces,
    wide,
    keys,
    values,
    scores,
    gains,
    qkv_sends,
    qkv_arrivals,
    down_sends,
    down_arrivals,
    up_sends,
    up_arrivals,
    pair_sends,
    pair_arrivals,
    gain_sends,
    gain_arrivals,
    own_sems,
):
    z, x, y, core = my_place()
    seq_at, ctx_at = y * 2 + core, z * 2 + x
    by_ctx, by_seq = (lambda ctx, seq: (ctx, seq)), (lambda ctx, seq: (seq, ctx))
    first = Gathering(qkv_own, qkv, by_ctx, qkv_sends, qkv_arrivals, (1, 3))
    rest = (
        Gathering(down_own, down, by_seq, down_sends, down_arrivals, (3,)),
        Gathering(up_own, up, by_ctx, up_sends, up_arrivals, (3,)),
    )
    meet(("z", "z_back", "x", "y", "core", "y_core"))
    first.begin()
    gain_copies = []
    for number, axis in enumerate(("core", "y", "y_core")):
        copy = pltpu.make_async_remote_copy(
            src_ref=gains_own,
            dst_ref=gains.at[seq_at],
            send_sem=gain_sends.at[number],
            recv_sem=gain_arrivals.at[number],
            device_id=neighbour(axis),
            device_id_type=pl.DeviceIdType.MESH,
        )
        copy.start()
        gain_copies.append(copy)
    own_copies = [
        pltpu.make_async_copy(source, target, own_sems.at[number])
        for number, (source, target) in enumerate(
            (
                (qkv_own, first.place(0, 0, 0)),
                (down_own, rest[0].place(0, 0, 0)),
                (up_own, rest[1].place(0, 0, 0)),
                (gains_own, gains.at[seq_at]),
            )
        )
    ]
    for copy in own_copies:
        copy.start()
    for t in range(1, Z_SIZE):
        first.pass_on(t)
        if t == Z_SIZE - 2:
            for group in rest:
                group.over_z(0)
        first.sides(t - 1)
    first.sides(Z_SIZE - 1)
    for group in rest:
        group.over_plane(0)
        group.to_core((0, 0, 0))
    for number, flips in enumerate(((0, 1), (1, 0), (1, 1))):
        place = gains.at[flipped(y, flips[0]) * 2 + flipped(core, flips[1])]
        pltpu.make_async_remote_copy(
            src_ref=place,
            dst_ref=place,
            send_sem=gain_sends.at[number],
            recv_sem=gain_arrivals.at[number],
            device_id=neighbour("core"),
            device_id_type=pl.DeviceIdType.MESH,
        ).wait_recv()
    for copy in own_copies:
        copy.wait()
    for row in range(4):
        gain_out[:, row * 288 : (row + 1) * 288] = gains[row]
    _, hat = normalized(tokens[...].astype(F32))
    rows = (hat * gain_out[0:1, :]).astype(BF16)
    for t in range(Z_SIZE):
        first.corner(t)
    first.finish()

    def multiply(ctx_block, carry):
        matrix = qkv[ctx_block].reshape(tokens.shape[1], 240)
        pieces[ctx_block] = jnp.dot(rows, matrix, preferred_element_type=F32)
        return carry

    lax.fori_loop(0, 8, multiply, 0)
    for group in rest:
        group.pass_on(1)
    q_part, kv_part = 144, 48
    for at in range(8):
        wide[:, at * q_part : (at + 1) * q_part] = pieces[at, :, :q_part]
        wide[:, 1152 + at * kv_part : 1152 + (at + 1) * kv_part] = pieces[at, :, q_part : q_part + kv_part]
        wide[:, 1536 + at * kv_part : 1536 + (at + 1) * kv_part] = pieces[at, :, q_part + kv_part :]
    cos_tile, sin_tile = cosine[...], sine[...]
    for pair in range(3):
        key_tile = wide[:, 1152 + pair * LANES : 1152 + (pair + 1) * LANES]
        pairs[ctx_at, :, 2 * pair * LANES : (2 * pair + 1) * LANES] = rotate_halves(
            key_tile, cos_tile, sin_tile
        ).astype(BF16)
        pairs[ctx_at, :, (2 * pair + 1) * LANES : (2 * pair + 2) * LANES] = wide[
            :, 1536 + pair * LANES : 1536 + (pair + 1) * LANES
        ].astype(BF16)
    natural = [
        rotate_halves(wide[:, at * LANES : (at + 1) * LANES], cos_tile, sin_tile) * HEAD_SIZE**-0.5
        for at in range(9)
    ]
    for at, tile in enumerate(pair_tiles(natural)):
        query_out[at] = tile.astype(BF16)

    pair_copies = []

    def pair_place(t, dx):
        return pairs.at[lax.rem(z - t + Z_SIZE, Z_SIZE) * 2 + flipped(x, dx)]

    def pair_copy(place, number, axis):
        return pltpu.make_async_remote_copy(
            src_ref=place,
            dst_ref=place,
            send_sem=pair_sends.at[number],
            recv_sem=pair_arrivals.at[number],
            device_id=neighbour(axis),
            device_id_type=pl.DeviceIdType.MESH,
        )

    def pair_pass(t):
        if t:
            pair_copy(pair_place(t, 0), t - 1, "z").wait_recv()
        for number, axis in ((t, "z"), (3 + t, "x")):
            if axis == "x" or t < Z_SIZE - 1:
                copy = pair_copy(pair_place(t, 0), number, axis)
                copy.start()
                pair_copies.append(copy)

    def in_rest(step):
        for group in rest:
            step(group)

    pair_pass(0)
    pair_pass(1)
    in_rest(lambda group: group.pass_on(2))
    pair_pass(2)
    in_rest(lambda group: group.sides(0))
    pair_pass(3)
    in_rest(lambda group: group.sides(1))
    in_rest(lambda group: group.pass_on(3))
    for t in range(Z_SIZE):
        pair_copy(pair_place(t, 1), 3 + t, "x").wait_recv()

    key_ids = lax.broadcasted_iota(jnp.int32, (256, tokens.shape[0]), 0)

    def attend_pair(pair):
        for at in range(8):
            for half in range(2):
                block = pairs[at, :, 2 * pair * LANES : (2 * pair + 1) * LANES]
                keys[half, at] = masked_pair(block, half, 0.0).astype(BF16)
                block = pairs[at, :, (2 * pair + 1) * LANES : (2 * pair + 2) * LANES]
                values[half, at] = masked_pair(block, half, 1.0).T.astype(BF16)

        def attend_member(member, carry):
            tile = query_out[3 * pair + member]
            parts = []
            for half in range(2):
                top = None
                for at in range(8):
                    part = lax.dot_general(keys[half, at], tile, NT, preferred_element_type=F32)
                    part = jnp.where(key_ids < limit[...] - at * 256, part, -1e30)
                    scores[at] = part
                    block_top = jnp.max(part, axis=0, keepdims=True)
                    top = block_top if top is None else jnp.maximum(top, block_top)
                total = jnp.zeros((LANES, tile.shape[0]), F32)
                for at in range(8):
                    weight = jnp.exp(scores[at] - top).astype(BF16)
                    total = total + jnp.dot(values[half, at], weight, preferred_element_type=F32)
                norm = total[HEAD_SIZE : HEAD_SIZE + 1] if half == 0 else total[:1]
                log_total[3 * pair + member, half : half + 1, :] = top + jnp.log(norm)
                own = total[:HEAD_SIZE] if half == 0 else total[HEAD_SIZE:]
                parts.append(own / norm)
            attended[3 * pair + member] = jnp.concatenate(parts, axis=0).T.astype(BF16)
            return carry

        lax.fori_loop(0, 3, attend_member, 0)

    attend_pair(0)
    in_rest(lambda group: group.sides(2))
    attend_pair(1)
    in_rest(lambda group: group.sides(3))
    attend_pair(2)
    for t in range(Z_SIZE):
        in_rest(lambda group: group.corner(t))
    in_rest(lambda group: group.finish())
    for group in (first,) + rest:
        group.drain()
    for copy in pair_copies + gain_copies:
        copy.wait_send()


def front(qkv_own, down_own, up_own, gains_own, tokens, cosine, sine, limit):
    rows, width = tokens.shape
    dma = pltpu.SemaphoreType.DMA
    return pl.pallas_call(
        front_kernel,
        out_shape=(
            jax.ShapeDtypeStruct((8, 4) + qkv_own.shape, BF16),
            jax.ShapeDtypeStruct((4, 8) + down_own.shape, BF16),
            jax.ShapeDtypeStruct((8, 4) + up_own.shape, BF16),
            jax.ShapeDtypeStruct((8, rows, 768), BF16),
            jax.ShapeDtypeStruct((9, rows, LANES), BF16),
            jax.ShapeDtypeStruct((9, rows, LANES), BF16),
            jax.ShapeDtypeStruct((9, 2, rows), F32),
            jax.ShapeDtypeStruct((8, width), F32),
        ),
        in_specs=vmem_specs(1) + any_specs(2) + vmem_specs(5),
        out_specs=tuple(vmem_specs(1) + any_specs(2) + vmem_specs(5)),
        scratch_shapes=[
            pltpu.VMEM((8, rows, 240), F32),
            pltpu.VMEM((rows, 1920), F32),
            pltpu.VMEM((2, 8, 256, LANES), BF16),
            pltpu.VMEM((2, 8, LANES, 256), BF16),
            pltpu.VMEM((8, 256, rows), F32),
            pltpu.VMEM((4, 8, 288), F32),
        ]
        + [dma((31,))] * 6
        + [dma((7,))] * 2
        + [dma((3,))] * 2
        + [dma((4,))],
        compiler_params=pltpu.CompilerParams(
            vmem_limit_bytes=VMEM_LIMIT, collective_id=1, has_side_effects=True
        ),
        cost_estimate=cost(4 * 18 * rows * 2048 * 128 * 4, 4e8, 18 * rows * 2048),
        name="front",
    )(qkv_own, down_own, up_own, gains_own, tokens, cosine, sine, limit)


def core_rows(core):
    return pl.ds(pl.multiple_of(core * 256, 256), 256)


def turned_blocks(matrix, parts):
    flat = matrix.astype(F32).T.astype(BF16)
    return flat.reshape(parts, flat.shape[0] // parts, flat.shape[1])


def middle_kernel(
    tokens,
    attended,
    cotangent,
    gain,
    down_in,
    up_in,
    output,
    mixed_grad,
    attended_grad,
    gain_grad,
    rows_turned,
    both_grads,
    hidden_both,
    attended_both,
    cot_turned,
    proj_turned,
    down,
    up_w,
    gates,
    ups,
    wide,
    rows_two,
    rows_stage,
    hidden,
    attended_rows,
    proj_grad,
    down_sems,
    up_sems,
    sends,
    arrivals,
    own_sems,
):
    _, _, _, core = my_place()
    mine, width = core_rows(core), tokens.shape[1]
    down_copies = [pltpu.make_async_copy(down_in.at[at], down.at[at], down_sems.at[at]) for at in range(4)]
    up_copies = [pltpu.make_async_copy(up_in.at[at], up_w.at[at], up_sems.at[at]) for at in range(8)]
    for copy in down_copies + up_copies:
        copy.start()
    meet(("core",))
    started, own_copies = [], []

    def share(source, target, number):
        copy = pltpu.make_async_remote_copy(
            src_ref=source,
            dst_ref=target,
            send_sem=sends.at[number],
            recv_sem=arrivals.at[number],
            device_id=neighbour("core"),
            device_id_type=pl.DeviceIdType.MESH,
        )
        copy.start()
        started.append(copy)

    def deal(stage, target_of, number):
        for y_at in range(2):
            copy = pltpu.make_async_copy(
                stage.at[y_at * 2 + core], target_of(y_at), own_sems.at[number - 9 + y_at]
            )
            copy.start()
            own_copies.append(copy)
            share(stage.at[y_at * 2 + 1 - core], target_of(y_at), number + y_at)

    cot_turned[:, :, mine] = turned_blocks(cotangent[...], 8)
    for at, tile in enumerate(natural_tiles([attended[at].astype(F32) for at in range(9)])):
        wide[:, at * LANES : (at + 1) * LANES] = tile
    for row in range(4):
        attended_rows[row] = wide[:, row * 288 : (row + 1) * 288].astype(BF16)
    share(cot_turned.at[:, :, mine], cot_turned.at[:, :, mine], 8)
    for copy in down_copies:
        copy.wait()

    def out_block(row):
        return down[row, :, :, 768:].reshape(width, 288)

    def down_block(row):
        return down[row, :, :, :768].reshape(width, 768)

    def gate_block(block):
        return up_w[block, :, :, :384].reshape(width, 384)

    def up_block(block):
        return up_w[block, :, :, 384:].reshape(width, 384)

    mixed_grad[...] = tokens[...].astype(F32)
    for row in range(4):
        mixed_grad[...] += lax.dot_general(attended_rows[row], out_block(row), NT, preferred_element_type=F32)
    deal(attended_rows, lambda y_at: attended_both.at[y_at, mine], 9)
    factor, hat = normalized(mixed_grad[...])
    gains = gain[...]
    wide[...] = hat
    rows_two[...] = (hat * gains).astype(BF16)
    rows_stage[...] = turned_blocks(rows_two[...], 4)
    for block in range(8):
        up_copies[block].wait()
        gates[block] = jnp.dot(rows_two[...], gate_block(block), preferred_element_type=F32)
        ups[block] = jnp.dot(rows_two[...], up_block(block), preferred_element_type=F32)
    deal(rows_stage, lambda y_at: rows_turned.at[y_at, :, mine], 11)
    for row in range(4):
        for side in range(2):
            gate, up = gates[2 * row + side], ups[2 * row + side]
            sigmoid = 1.0 / (1.0 + jnp.exp(-gate))
            hidden[row, :, side * 384 : (side + 1) * 384] = (gate * sigmoid * up).astype(BF16)
        mixed_grad[...] += lax.dot_general(hidden[row], down_block(row), NT, preferred_element_type=F32)
        back = jnp.dot(cotangent[...], down_block(row), preferred_element_type=F32)
        for side in range(2):
            block = 2 * row + side
            gate, up = gates[block], ups[block]
            sigmoid = 1.0 / (1.0 + jnp.exp(-gate))
            part = back[:, side * 384 : (side + 1) * 384]
            both_grads[block, mine, :384] = (
                part * up * sigmoid * (1.0 + gate * (1.0 - sigmoid))
            ).astype(BF16)
            both_grads[block, mine, 384:] = (part * (gate * sigmoid)).astype(BF16)
    output[...] = mixed_grad[...].astype(BF16)
    for block in range(8):
        share(both_grads.at[block, mine], both_grads.at[block, mine], block)
    deal(hidden, lambda y_at: hidden_both.at[y_at, mine], 13)
    for block in range(8):
        grad_two = lax.dot_general(
            both_grads[block, mine, :384], gate_block(block), NT, preferred_element_type=F32
        )
        grad_two = grad_two + lax.dot_general(
            both_grads[block, mine, 384:], up_block(block), NT, preferred_element_type=F32
        )
        mixed_grad[...] = grad_two if block == 0 else mixed_grad[...] + grad_two
    grad_two, hat = mixed_grad[...], wide[...]
    gain_grad[...] = jnp.sum(grad_two * hat, axis=0, keepdims=True)
    scaled = grad_two * gains
    total = cotangent[...].astype(F32) + factor * (
        scaled - hat * jnp.mean(scaled * hat, axis=-1, keepdims=True)
    )
    mixed_grad[...] = total
    proj_grad[...] = total.astype(BF16)
    proj_turned[:, :, mine] = turned_blocks(proj_grad[...], 8)
    for row in range(4):
        wide[:, row * 288 : (row + 1) * 288] = jnp.dot(
            proj_grad[...], out_block(row), preferred_element_type=F32
        )
    share(proj_turned.at[:, :, mine], proj_turned.at[:, :, mine], 17)
    tiles = pair_tiles([wide[:, at * LANES : (at + 1) * LANES] for at in range(9)])
    for at, tile in enumerate(tiles):
        attended_grad[at] = tile.astype(BF16)
    theirs = core_rows(1 - core)

    def arrive(place, number):
        pltpu.make_async_remote_copy(
            src_ref=place,
            dst_ref=place,
            send_sem=sends.at[number],
            recv_sem=arrivals.at[number],
            device_id=neighbour("core"),
            device_id_type=pl.DeviceIdType.MESH,
        ).wait_recv()

    for block in range(8):
        arrive(both_grads.at[block, theirs], block)
    arrive(cot_turned.at[:, :, theirs], 8)
    for y_at in range(2):
        arrive(attended_both.at[y_at, theirs], 9 + y_at)
        arrive(rows_turned.at[y_at, :, theirs], 11 + y_at)
        arrive(hidden_both.at[y_at, theirs], 13 + y_at)
    arrive(proj_turned.at[:, :, theirs], 17)
    for copy in started:
        copy.wait_send()
    for copy in own_copies:
        copy.wait()


def middle(tokens, attended, cotangent, gain, down, up):
    rows, width = tokens.shape
    return pl.pallas_call(
        middle_kernel,
        out_shape=(
            jax.ShapeDtypeStruct((rows, width), BF16),
            jax.ShapeDtypeStruct((rows, width), F32),
            jax.ShapeDtypeStruct((9, rows, LANES), BF16),
            jax.ShapeDtypeStruct((1, width), F32),
            jax.ShapeDtypeStruct((2, 288, 2 * rows), BF16),
            jax.ShapeDtypeStruct((8, 2 * rows, 768), BF16),
            jax.ShapeDtypeStruct((2, 2 * rows, 768), BF16),
            jax.ShapeDtypeStruct((2, 2 * rows, 288), BF16),
            jax.ShapeDtypeStruct((8, 144, 2 * rows), BF16),
            jax.ShapeDtypeStruct((8, 144, 2 * rows), BF16),
        ),
        in_specs=vmem_specs(4) + any_specs(2),
        out_specs=tuple(vmem_specs(10)),
        scratch_shapes=[
            pltpu.VMEM(down.shape, BF16),
            pltpu.VMEM(up.shape, BF16),
            pltpu.VMEM((8, rows, 384), F32),
            pltpu.VMEM((8, rows, 384), F32),
            pltpu.VMEM((rows, width), F32),
            pltpu.VMEM((rows, width), BF16),
            pltpu.VMEM((4, 288, rows), BF16),
            pltpu.VMEM((4, rows, 768), BF16),
            pltpu.VMEM((4, rows, 288), BF16),
            pltpu.VMEM((rows, width), BF16),
            pltpu.SemaphoreType.DMA((4,)),
            pltpu.SemaphoreType.DMA((8,)),
            pltpu.SemaphoreType.DMA((18,)),
            pltpu.SemaphoreType.DMA((18,)),
            pltpu.SemaphoreType.DMA((6,)),
        ],
        compiler_params=pltpu.CompilerParams(
            vmem_limit_bytes=VMEM_LIMIT, collective_id=2, has_side_effects=True
        ),
        cost_estimate=cost(2 * rows * width * (6 * 3072 + 2 * 1152), 4e7),
        name="middle",
    )(tokens, attended, cotangent, gain, down, up)


class Scattering:
    def __init__(self, buffers, sends, arrivals, out, piece, corners):
        self.corner, self.side_x, self.side_y, self.near_x, self.near_y, self.ring = buffers
        self.sends, self.arrivals, self.out, self.piece, self.corners = sends, arrivals, out, piece, corners

    def copy(self, source, target, number, axis):
        return pltpu.make_async_remote_copy(
            src_ref=source,
            dst_ref=target,
            send_sem=self.sends.at[number],
            recv_sem=self.arrivals.at[number],
            device_id=neighbour(axis),
            device_id_type=pl.DeviceIdType.MESH,
        )

    def corner_copies(self, t, axes=("x", "y")):
        for number, (axis, lanes) in enumerate(self.corners):
            if axis in axes:
                target = self.side_x if axis == "y" else self.side_y
                yield self.copy(self.corner.at[t, :, lanes], target.at[t, :, lanes], 4 * number + t, axis)

    def side_copy(self, t, axis):
        source, target, first = (self.side_x, self.near_x, 8) if axis == "x" else (self.side_y, self.near_y, 12)
        return self.copy(source.at[t], target.at[t], first + t, axis)

    def ring_copy(self, t):
        return self.copy(self.near_x.at[t], self.ring.at[t - 1], 15 + t, "z_back")

    def corner_step(self, t):
        self.piece(t, 1, 1, self.corner.at[t], lambda lanes: [])
        for copy in self.corner_copies(t):
            copy.start()

    def side_step(self, t, axis):
        came = "y" if axis == "x" else "x"
        for copy in self.corner_copies(t, (came,)):
            copy.wait_recv()
        side = (self.side_x if axis == "x" else self.side_y).at[t]
        ranges = [lanes for at, lanes in self.corners if at == came]

        def addend(lanes):
            return [side[:, lanes]] if any(at.start <= lanes.start and lanes.stop <= at.stop for at in ranges) else []

        self.piece(t, int(axis == "x"), int(axis == "y"), side, addend)
        self.side_copy(t, axis).start()

    def near_step(self, t):
        self.side_copy(t, "x").wait_recv()
        self.side_copy(t, "y").wait_recv()
        if t < Z_SIZE - 1:
            self.ring_copy(t + 1).wait_recv()

        def addend(lanes):
            parts = [self.near_x[t, :, lanes], self.near_y[t, :, lanes]]
            return parts + ([self.ring[t, :, lanes]] if t < Z_SIZE - 1 else [])

        self.piece(t, 0, 0, self.near_x.at[t] if t else self.out, addend)
        if t:
            self.ring_copy(t).start()

    def drain(self):
        for t in range(Z_SIZE):
            for copy in self.corner_copies(t):
                copy.wait_send()
            self.side_copy(t, "x").wait_send()
            self.side_copy(t, "y").wait_send()
            if t:
                self.ring_copy(t).wait_send()


def back_kernel(
    rows_turned,
    both_grads,
    hidden,
    attended_rows,
    cot_turned,
    proj_turned,
    query,
    attended,
    grad,
    log_total,
    limit,
    cosine,
    sine,
    pairs,
    tokens,
    gains,
    second_gain,
    weights,
    mixed_grad,
    down_out,
    up_out,
    qkv_out,
    input_grad,
    gain_out,
    *refs,
):
    down_buffers, up_buffers, qkv_buffers = refs[:6], refs[6:12], refs[12:18]
    (
        keys,
        keys_turned,
        values,
        key_sum,
        value_sum,
        pair_far,
        pair_own,
        pair_near,
        pair_ring,
        query_grad,
        wide,
        pieces,
        first_stage,
        first_turned,
        weight_slots,
        gain_sum,
        gain_came,
    ) = refs[18:35]
    (
        down_sends,
        down_arrivals,
        up_sends,
        up_arrivals,
        qkv_sends,
        qkv_arrivals,
        pair_sends,
        pair_arrivals,
        core_sends,
        core_arrivals,
        gain_sends,
        gain_arrivals,
        own_sems,
        weight_sems,
    ) = refs[35:]
    z, x, y, core = my_place()
    mine, theirs = core_rows(core), core_rows(1 - core)
    rows, width = tokens.shape

    def ctx_of(t, dx):
        return lax.rem(z - t + Z_SIZE, Z_SIZE) * 2 + flipped(x, dx)

    def put(target, lanes, value, addend):
        for part in addend(lanes):
            value = value + part.astype(F32)
        target[:, lanes] = value.astype(target.dtype)

    def down_piece(t, dx, dy, target, addend):
        block, row = ctx_of(t, dx), flipped(y, dy)
        for lanes in (slice(0, 384), slice(384, 768)):
            value = jnp.dot(cot_turned[block], hidden[row, :, lanes], preferred_element_type=F32)
            put(target, lanes, value, addend)
        value = jnp.dot(proj_turned[block], attended_rows[row], preferred_element_type=F32)
        put(target, slice(768, 1056), value, addend)

    def up_piece(t, dx, dy, target, addend):
        block, row = ctx_of(t, dx), flipped(y, dy)
        for lanes in (slice(0, 384), slice(384, 768)):
            value = jnp.dot(rows_turned[row], both_grads[block, :, lanes], preferred_element_type=F32)
            put(target, lanes, value, addend)

    def qkv_piece(t, dx, dy, target, addend):
        block, row = ctx_of(t, dx), flipped(y, dy)
        value = jnp.dot(first_turned[row], pieces[block], preferred_element_type=F32)
        put(target, slice(0, 240), value, addend)

    down = Scattering(down_buffers, down_sends, down_arrivals, down_out, down_piece, (("y", slice(0, 1056)),))
    up = Scattering(
        up_buffers, up_sends, up_arrivals, up_out, up_piece, (("y", slice(0, 384)), ("x", slice(384, 768)))
    )
    qkv = Scattering(qkv_buffers, qkv_sends, qkv_arrivals, qkv_out, qkv_piece, (("x", slice(0, 240)),))

    meet(("z", "z_back", "x", "y", "core", "z_two"))
    residual = pltpu.make_async_copy(mixed_grad, input_grad, own_sems.at[2])
    residual.start()

    def corners(number, carry):
        t = Z_SIZE - 1 - number
        down.corner_step(t)
        up.corner_step(t)
        return carry

    lax.fori_loop(0, Z_SIZE, corners, 0)

    factor, hat = normalized(tokens[...].astype(F32))
    first_stage[...] = turned_blocks((hat * gains[0:1, :]).astype(BF16), 4)

    def core_copy(source, target, number):
        return pltpu.make_async_remote_copy(
            src_ref=source,
            dst_ref=target,
            send_sem=core_sends.at[number],
            recv_sem=core_arrivals.at[number],
            device_id=neighbour("core"),
            device_id_type=pl.DeviceIdType.MESH,
        )

    def pair_copy(pair, t, axis):
        if axis == "x":
            source, target, number = pair_far.at[pair, t], pair_near.at[pair, t], 4 * pair + t
        else:
            source, target, number = pair_own.at[pair, t], pair_ring.at[pair, t - 1], 11 + 3 * pair + t
        return pltpu.make_async_remote_copy(
            src_ref=source,
            dst_ref=target,
            send_sem=pair_sends.at[number],
            recv_sem=pair_arrivals.at[number],
            device_id=neighbour(axis),
            device_id_type=pl.DeviceIdType.MESH,
        )

    key_ids = lax.broadcasted_iota(jnp.int32, (256, rows), 0)

    def attend_pair_back(pair):
        key_lanes = pl.ds(pl.multiple_of(pair * 256, 256), LANES)
        value_lanes = pl.ds(pl.multiple_of(pair * 256 + LANES, LANES), LANES)
        key_sum[...] = jnp.zeros_like(key_sum)
        value_sum[...] = jnp.zeros_like(value_sum)
        for at in range(8):
            key_block, value_block = pairs[at, :, key_lanes], pairs[at, :, value_lanes]
            for half in range(2):
                masked = masked_pair(key_block, half, 0.0)
                keys[half, at] = masked.astype(BF16)
                keys_turned[half, at] = masked.T.astype(BF16)
                values[half, at] = masked_pair(value_block, half, 0.0).astype(BF16)

        def member_step(member, carry):
            number = 3 * pair + member
            tile, grad_tile = query[number], grad[number]
            product = (attended[number].astype(F32) * grad_tile.astype(F32)).T
            turned = jnp.zeros((LANES, rows), F32)
            for half in range(2):
                own = slice(half * HEAD_SIZE, (half + 1) * HEAD_SIZE)
                shift = jnp.sum(product[own], axis=0, keepdims=True)
                log_row = log_total[number, half : half + 1, :]
                query_half = masked_pair(tile, half, 0.0).astype(BF16)
                grad_half = masked_pair(grad_tile, half, 0.0).astype(BF16)
                for at in range(8):
                    part = lax.dot_general(keys[half, at], tile, NT, preferred_element_type=F32)
                    part = jnp.where(key_ids < limit[...] - at * 256, part, -1e30)
                    probs = jnp.exp(part - log_row)
                    back = lax.dot_general(values[half, at], grad_tile, NT, preferred_element_type=F32)
                    scored = (probs * (back - shift)).astype(BF16)
                    value_sum[at] += jnp.dot(probs.astype(BF16), grad_half, preferred_element_type=F32)
                    key_sum[at] += jnp.dot(scored, query_half, preferred_element_type=F32)
                    turned = turned + jnp.dot(keys_turned[half, at], scored, preferred_element_type=F32)
            turned = rotate_halves(turned.T * HEAD_SIZE**-0.5, cosine[...], -sine[...])
            query_grad[number] = turned.astype(BF16)
            return carry

        lax.fori_loop(0, 3, member_step, 0)
        for t in range(Z_SIZE):
            for dx, place in ((0, pair_own), (1, pair_far)):
                block = ctx_of(t, dx)
                place[pair, t, :, :LANES] = key_sum[block].astype(BF16)
                place[pair, t, :, LANES:] = value_sum[block].astype(BF16)
        for t in range(Z_SIZE - 1, -1, -1):
            pair_copy(pair, t, "x").start()

    def attend_and_sides(number, carry):
        @pl.when(number < 3)
        def _():
            attend_pair_back(number)

        t = Z_SIZE - 1 - number
        for axis in ("y", "x"):
            down.side_step(t, axis)
            up.side_step(t, axis)
        return carry

    lax.fori_loop(0, 4, attend_and_sides, 0)

    first_copies = []
    for y_at in range(2):
        place = first_turned.at[y_at, :, mine]
        own = pltpu.make_async_copy(first_stage.at[y_at * 2 + core], place, own_sems.at[y_at])
        own.start()
        copy = core_copy(first_stage.at[y_at * 2 + 1 - core], place, 1 + y_at)
        copy.start()
        first_copies.append((own, copy))

    def pair_step(t):
        for pair in range(3):
            pair_copy(pair, t, "x").wait_recv()
            total = pair_own[pair, t].astype(F32) + pair_near[pair, t].astype(F32)
            if t < Z_SIZE - 1:
                pair_copy(pair, t + 1, "z_back").wait_recv()
                total = total + pair_ring[pair, t].astype(F32)
            if t:
                pair_own[pair, t] = total.astype(BF16)
                pair_copy(pair, t, "z_back").start()
            else:
                key_tile = rotate_halves(total[:, :LANES], cosine[...], -sine[...])
                wide[:, 1152 + pair * LANES : 1152 + (pair + 1) * LANES] = key_tile
                wide[:, 1536 + pair * LANES : 1536 + (pair + 1) * LANES] = total[:, LANES:]

    pair_step(3)
    for at, tile in enumerate(natural_tiles([query_grad[at].astype(F32) for at in range(9)])):
        wide[:, at * LANES : (at + 1) * LANES] = tile
    pair_step(2)
    pair_step(1)
    down.near_step(3)
    up.near_step(3)
    pair_step(0)
    q_part, kv_part = 144, 48
    for at in range(8):
        pieces[at, mine, :] = jnp.concatenate(
            [
                wide[:, at * q_part : (at + 1) * q_part],
                wide[:, 1152 + at * kv_part : 1152 + (at + 1) * kv_part],
                wide[:, 1536 + at * kv_part : 1536 + (at + 1) * kv_part],
            ],
            axis=1,
        ).astype(BF16)

    def weight_copy(at):
        return pltpu.make_async_copy(weights.at[at], weight_slots.at[at % 2], weight_sems.at[at % 2])

    weight_copy(0).start()
    weight_copy(1).start()
    piece_copy = core_copy(pieces.at[:, mine, :], pieces.at[:, mine, :], 0)
    piece_copy.start()
    grad_one = wide.at[:, :1152]
    for at in range(8):
        weight_copy(at).wait()
        part = lax.dot_general(
            pieces[at, mine, :], weight_slots[at % 2].reshape(width, 240), NT, preferred_element_type=F32
        )
        grad_one[...] = part if at == 0 else grad_one[...] + part
        if at < 6:
            weight_copy(at + 2).start()
    core_copy(pieces.at[:, theirs, :], pieces.at[:, theirs, :], 0).wait_recv()
    for y_at, (own, _) in enumerate(first_copies):
        place = first_turned.at[y_at, :, theirs]
        core_copy(place, place, 1 + y_at).wait_recv()
        own.wait()

    def qkv_corners(number, carry):
        qkv.corner_step(Z_SIZE - 1 - number)
        return carry

    lax.fori_loop(0, Z_SIZE, qkv_corners, 0)
    down.near_step(2)
    up.near_step(2)

    def qkv_sides(number, carry):
        for axis in ("x", "y"):
            qkv.side_step(Z_SIZE - 1 - number, axis)
        return carry

    lax.fori_loop(0, Z_SIZE, qkv_sides, 0)
    residual.wait()
    grad_rows = grad_one[...]
    _, hat = normalized(tokens[...].astype(F32))
    first_gain = jnp.sum(grad_rows * hat, axis=0, keepdims=True)
    scaled = grad_rows * gains[0:1, :]
    input_grad[...] += factor * (scaled - hat * jnp.mean(scaled * hat, axis=-1, keepdims=True))
    both = jnp.concatenate([first_gain, second_gain[...], jnp.zeros((6, width), F32)], axis=0)
    for row in range(4):
        gain_sum[0, row] = both[:, row * 288 : (row + 1) * 288]
    gain_copies = []

    def gain_send(source, number, axis):
        copy = pltpu.make_async_remote_copy(
            src_ref=gain_sum.at[source],
            dst_ref=gain_came.at[number],
            send_sem=gain_sends.at[number],
            recv_sem=gain_arrivals.at[number],
            device_id=neighbour(axis),
            device_id_type=pl.DeviceIdType.MESH,
        )
        copy.start()
        gain_copies.append(copy)
        return copy

    down.near_step(1)
    up.near_step(1)
    for number, axis in enumerate(("core", "y", "x")):
        gain_send(number, number, axis).wait_recv()
        gain_sum[number + 1] = gain_sum[number] + gain_came[number]
        if number < 3:
            qkv.near_step(Z_SIZE - 1 - number)
    ends = [gain_send(3, 3 + number, axis) for number, axis in enumerate(("z", "z_two", "z_back"))]
    down.near_step(0)
    up.near_step(0)
    qkv.near_step(0)
    for copy in ends:
        copy.wait_recv()
    seq_at = y * 2 + core
    gain_out[...] = (gain_sum[3, seq_at] + gain_came[3, seq_at]) + (gain_came[4, seq_at] + gain_came[5, seq_at])
    for group in (down, up, qkv):
        group.drain()
    for pair in range(3):
        for t in range(Z_SIZE):
            pair_copy(pair, t, "x").wait_send()
            if t:
                pair_copy(pair, t, "z_back").wait_send()
    for copy in gain_copies + [piece_copy] + [copy for _, copy in first_copies]:
        copy.wait_send()


def back(weight_inputs, attention_inputs, tokens, gains, second_gain, weights, mixed_grad):
    rows, width = tokens.shape
    dma, arrays = pltpu.SemaphoreType.DMA, []
    for shape in ((144, 1056), (288, 768), (288, 240)):
        arrays += [pltpu.VMEM((Z_SIZE,) + shape, BF16)] * 5 + [pltpu.VMEM((Z_SIZE - 1,) + shape, BF16)]
    return pl.pallas_call(
        back_kernel,
        out_shape=(
            jax.ShapeDtypeStruct((144, 1056), F32),
            jax.ShapeDtypeStruct((288, 768), F32),
            jax.ShapeDtypeStruct((288, 240), F32),
            jax.ShapeDtypeStruct((rows, width), F32),
            jax.ShapeDtypeStruct((8, 288), F32),
        ),
        in_specs=vmem_specs(17) + any_specs(2),
        out_specs=tuple(vmem_specs(5)),
        scratch_shapes=arrays
        + [
            pltpu.VMEM((2, 8, 256, LANES), BF16),
            pltpu.VMEM((2, 8, LANES, 256), BF16),
            pltpu.VMEM((2, 8, 256, LANES), BF16),
            pltpu.VMEM((8, 256, LANES), F32),
            pltpu.VMEM((8, 256, LANES), F32),
            pltpu.VMEM((3, Z_SIZE, 256, 2 * LANES), BF16),
            pltpu.VMEM((3, Z_SIZE, 256, 2 * LANES), BF16),
            pltpu.VMEM((3, Z_SIZE, 256, 2 * LANES), BF16),
            pltpu.VMEM((3, Z_SIZE - 1, 256, 2 * LANES), BF16),
            pltpu.VMEM((9, rows, LANES), BF16),
            pltpu.VMEM((rows, 1920), F32),
            pltpu.VMEM((8, 2 * rows, 240), BF16),
            pltpu.VMEM((4, 288, rows), BF16),
            pltpu.VMEM((2, 288, 2 * rows), BF16),
            pltpu.VMEM((2, 4, 288, 240), BF16),
            pltpu.VMEM((4, 4, 8, 288), F32),
            pltpu.VMEM((6, 4, 8, 288), F32),
        ]
        + [dma((19,))] * 6
        + [dma((21,))] * 2
        + [dma((3,))] * 2
        + [dma((6,))] * 2
        + [dma((3,)), dma((2,))],
        compiler_params=pltpu.CompilerParams(
            vmem_limit_bytes=VMEM_LIMIT, collective_id=3, has_side_effects=True
        ),
        cost_estimate=cost(4 * 18 * rows * 2048 * 128 * 10, 4e8, 18 * rows * 2048),
        name="back",
    )(*weight_inputs, *attention_inputs, tokens, gains, second_gain, weights, mixed_grad)


def lane_tables(first, rows):
    half = HEAD_SIZE // 2
    frequency = ROTARY_BASE ** (-jnp.arange(half, dtype=F32) * 2.0 / HEAD_SIZE)
    angles = (first + jnp.arange(rows, dtype=jnp.int32)).astype(F32)[:, None] * frequency[None, :]
    cosine, sine = jnp.cos(angles), jnp.sin(angles)
    return jnp.tile(cosine, (1, 4)), jnp.tile(jnp.concatenate([-sine, sine], axis=1), (1, 2))


def permuted_device(
    tokens, prefix, gain_one, w_query, w_key, value_weight, w_out, gain_two, w_gate, w_up, w_down, cotangent
):
    _, rows, width = tokens.shape
    tokens, cotangent = tokens[0], cotangent[0]
    ctx_at = lax.axis_index("ctx")
    gains = jnp.zeros((8, gain_one.shape[0]), F32).at[0].set(gain_one.astype(F32)).at[1].set(gain_two.astype(F32))
    cosine, sine = lane_tables(ctx_at * rows, rows)
    limit = jnp.maximum(ctx_at * rows + jnp.arange(rows, dtype=jnp.int32) + 1, prefix[0])[None, :]
    qkv, down, up, pairs, query, attended, log_total, gains = front(
        jnp.concatenate([w_query, w_key, value_weight], axis=1),
        jnp.concatenate([w_down.T, w_out.T], axis=1),
        jnp.concatenate([w_gate, w_up], axis=1),
        gains,
        tokens,
        cosine,
        sine,
        limit,
    )
    output, mixed_grad, attended_grad, second_gain, *weight_inputs = middle(
        tokens, attended, cotangent, gains[1:2], down, up
    )
    grad_down_out, grad_up, grad_qkv, input_grad, gain_grads = back(
        weight_inputs,
        (query, attended, attended_grad, log_total, limit, cosine, sine, pairs),
        tokens,
        gains,
        second_gain,
        qkv,
        mixed_grad,
    )
    return (
        output[None],
        input_grad[None],
        gain_grads[0],
        grad_qkv[:, :144],
        grad_qkv[:, 144:192],
        grad_qkv[:, 192:],
        grad_down_out[:, 768:].T,
        gain_grads[1],
        grad_up[:, :384],
        grad_up[:, 384:],
        grad_down_out[:, :768].T,
    )


def permute_plan_fits(mesh, tokens):
    return dict(mesh.shape) == {"seq": 4, "ctx": 8} and tokens.shape == (4, 2048, 1152)


def solution(mesh):
    placed = (
        P("seq", "ctx", None),
        P("seq"),
        P("seq"),
        P("seq", "ctx"),
        P("seq", "ctx"),
        P("seq", "ctx"),
        P("seq", "ctx"),
        P("seq"),
        P("seq", "ctx"),
        P("seq", "ctx"),
        P("seq", "ctx"),
        P("seq", "ctx", None),
    )

    def mapped(device_function):
        return jax.shard_map(
            device_function,
            mesh=mesh,
            in_specs=placed,
            out_specs=(
                P("seq", "ctx", None),
                P("seq", "ctx", None),
                P("seq"),
                P("seq", "ctx"),
                P("seq", "ctx"),
                P("seq", "ctx"),
                P("seq", "ctx"),
                P("seq"),
                P("seq", "ctx"),
                P("seq", "ctx"),
                P("seq", "ctx"),
            ),
            check_vma=False,
        )

    def layer(tokens, *rest):
        return mapped(permuted_device if permute_plan_fits(mesh, tokens) else per_device)(tokens, *rest)

    return layer
```

```python
import functools

import jax
import jax.numpy as jnp
from jax import lax
from jax.experimental import pallas as pl
from jax.experimental.pallas import tpu as pltpu
from jax.sharding import PartitionSpec as P

QUERY_HEADS = 18
KEY_VALUE_HEADS = 6
HEAD_SIZE = 64


EPSILON = 1e-05
ROTARY_BASE = 10000.0

LANES = 128
Z_SIZE = 4
VMEM_LIMIT = 66_000_000
PLANE_LANES = 640
F32 = jnp.float32
BF16 = jnp.bfloat16
NT = (((1,), (1,)), ((), ()))


def rotary_tables(positions, head_width):
    half_width = head_width // 2
    frequency = ROTARY_BASE ** (-jnp.arange(half_width, dtype=jnp.float32) * 2.0 / head_width)
    angles = positions.astype(jnp.float32)[:, None] * frequency[None, :]
    return (jnp.cos(angles)[:, None, :], jnp.sin(angles)[:, None, :])


def apply_rotation(values_in, cosine_table, sine_values):
    half_width = values_in.shape[-1] // 2
    first = values_in[..., :half_width]
    second = values_in[..., half_width:]
    return jnp.concatenate(
        [first * cosine_table - second * sine_values, second * cosine_table + first * sine_values],
        axis=-1,
    )


def inverse_rotation(grads_in, cosine_table, sine_values):
    half_width = grads_in.shape[-1] // 2
    first = grads_in[..., :half_width]
    second = grads_in[..., half_width:]
    return jnp.concatenate(
        [first * cosine_table + second * sine_values, second * cosine_table - first * sine_values],
        axis=-1,
    )


def gather_weights(w_query, w_key, value_weight, w_out, w_gate, w_up, w_down, gain_one, gain_two):
    columns = (
        lax.all_gather(w_query, "ctx", axis=1, tiled=True),
        lax.all_gather(w_key, "ctx", axis=1, tiled=True),
        lax.all_gather(value_weight, "ctx", axis=1, tiled=True),
        lax.all_gather(w_out, "ctx", axis=1, tiled=True),
        lax.all_gather(w_gate, "ctx", axis=1, tiled=True),
        lax.all_gather(w_up, "ctx", axis=1, tiled=True),
        lax.all_gather(w_down, "ctx", axis=1, tiled=True),
    )
    return (
        lax.all_gather(columns[0], "seq", axis=0, tiled=True),
        lax.all_gather(columns[1], "seq", axis=0, tiled=True),
        lax.all_gather(columns[2], "seq", axis=0, tiled=True),
        lax.all_gather(columns[3], "seq", axis=0, tiled=True),
        lax.all_gather(columns[4], "seq", axis=0, tiled=True),
        lax.all_gather(columns[5], "seq", axis=0, tiled=True),
        lax.all_gather(columns[6], "seq", axis=0, tiled=True),
        lax.all_gather(gain_one, "seq", axis=0, tiled=True),
        lax.all_gather(gain_two, "seq", axis=0, tiled=True),
    )


def gather_pairs(key_rotated, value_reduced):
    return (
        lax.all_gather(key_rotated, "ctx", axis=1, tiled=True),
        lax.all_gather(value_reduced, "ctx", axis=1, tiled=True),
    )


def head_major(whole_result, sequence_count):
    sequence_length = whole_result.shape[1]
    return (
        whole_result.reshape(sequence_count, sequence_length, KEY_VALUE_HEADS, HEAD_SIZE)
        .transpose(0, 2, 1, 3)
        .reshape(sequence_count * KEY_VALUE_HEADS, sequence_length, HEAD_SIZE)
    )


def per_device(
    tokens,
    prefix,
    gain_one,
    w_query,
    w_key,
    value_weight,
    w_out,
    gain_two,
    w_gate,
    w_up,
    w_down,
    cotangent,
):
    sequence_count, token_local, model_width = tokens.shape
    sequence_length = token_local * lax.axis_size("ctx")
    number_of_rows = sequence_count * token_local
    queries_per_key_head = QUERY_HEADS // KEY_VALUE_HEADS
    score_scale = HEAD_SIZE ** (-0.5)
    gathered = gather_weights(
        w_query, w_key, value_weight, w_out, w_gate, w_up, w_down, gain_one, gain_two
    )
    full_query, full_key, full_value, full_out, full_gate, full_up, full_down = gathered[:7]
    first_norm = gathered[7].astype(jnp.float32)
    second_norm = gathered[8].astype(jnp.float32)
    input_rows = tokens.reshape(number_of_rows, model_width).astype(jnp.float32)
    first_factor = lax.rsqrt(jnp.mean(input_rows * input_rows, axis=-1, keepdims=True) + EPSILON)
    first_normalized_input = input_rows * first_factor
    normalized_rows = (first_normalized_input * first_norm).astype(jnp.bfloat16)
    query_pre = jnp.dot(normalized_rows, full_query, preferred_element_type=jnp.float32)
    key_prerotation = jnp.dot(normalized_rows, full_key, preferred_element_type=jnp.float32)
    value_reduced = jnp.dot(normalized_rows, full_value, preferred_element_type=jnp.float32).astype(
        jnp.bfloat16
    )
    positions = lax.axis_index("ctx") * token_local + jnp.arange(token_local, dtype=jnp.int32)
    cosine_table, sine_values = rotary_tables(positions, HEAD_SIZE)
    query_rows = apply_rotation(
        query_pre.reshape(sequence_count, token_local, QUERY_HEADS, HEAD_SIZE),
        cosine_table,
        sine_values,
    ).astype(jnp.bfloat16)
    key_rotated = apply_rotation(
        key_prerotation.reshape(sequence_count, token_local, KEY_VALUE_HEADS, HEAD_SIZE),
        cosine_table,
        sine_values,
    ).astype(jnp.bfloat16)
    key_rotated = key_rotated.reshape(sequence_count, token_local, KEY_VALUE_HEADS * HEAD_SIZE)
    value_reduced = value_reduced.reshape(sequence_count, token_local, KEY_VALUE_HEADS * HEAD_SIZE)
    keys_all, values_all = gather_pairs(key_rotated, value_reduced)
    query_block_list = query_rows.reshape(
        sequence_count, token_local, KEY_VALUE_HEADS, queries_per_key_head, HEAD_SIZE
    ).transpose(0, 2, 3, 1, 4)
    query_block_list = query_block_list.reshape(
        sequence_count * KEY_VALUE_HEADS, queries_per_key_head, token_local, HEAD_SIZE
    )
    key_blocks = head_major(keys_all, sequence_count)
    value_blocks = head_major(values_all, sequence_count)
    prefix_repeated = jnp.repeat(prefix, KEY_VALUE_HEADS)
    key_place = jnp.arange(sequence_length, dtype=jnp.int32)

    def visible_for(prefix_len):
        return (key_place[None, :] <= positions[:, None]) | (key_place[None, :] < prefix_len)

    def attend(block_item):
        query_block, key_block, value_block, prefix_len = block_item
        scores = (
            jnp.einsum("gqd,kd->gqk", query_block, key_block, preferred_element_type=jnp.float32)
            * score_scale
        )
        scores = jnp.where(visible_for(prefix_len)[None], scores, -1e30)
        row_max = jnp.max(scores, axis=-1, keepdims=True)
        expo = jnp.exp(scores - row_max)
        total = jnp.sum(expo, axis=-1, keepdims=True)
        probs_low = (expo / total).astype(jnp.bfloat16)
        result = jnp.einsum(
            "gqk,kd->gqd", probs_low, value_block, preferred_element_type=jnp.float32
        )
        return (result.astype(jnp.bfloat16), (row_max + jnp.log(total))[..., 0])

    attention_result_blocks, log_totals = lax.map(
        attend, (query_block_list, key_blocks, value_blocks, prefix_repeated)
    )
    attention_result = attention_result_blocks.reshape(
        sequence_count, KEY_VALUE_HEADS, queries_per_key_head, token_local, HEAD_SIZE
    ).transpose(0, 3, 1, 2, 4)
    attention_result = attention_result.reshape(number_of_rows, QUERY_HEADS * HEAD_SIZE)
    mixed_output = input_rows + jnp.dot(
        attention_result, full_out, preferred_element_type=jnp.float32
    )
    second_factor = lax.rsqrt(
        jnp.mean(mixed_output * mixed_output, axis=-1, keepdims=True) + EPSILON
    )
    second_normalized_input = mixed_output * second_factor
    normalized_second = (second_normalized_input * second_norm).astype(jnp.bfloat16)
    gate = jnp.dot(normalized_second, full_gate, preferred_element_type=jnp.float32)
    up_part = jnp.dot(normalized_second, full_up, preferred_element_type=jnp.float32)
    sigmoid_gate = jax.nn.sigmoid(gate)
    activated = gate * sigmoid_gate
    hidden = (activated * up_part).astype(jnp.bfloat16)
    result_rows = mixed_output + jnp.dot(hidden, full_down, preferred_element_type=jnp.float32)
    output = result_rows.astype(jnp.bfloat16).reshape(sequence_count, token_local, model_width)
    gathered = gather_weights(
        w_query, w_key, value_weight, w_out, w_gate, w_up, w_down, gain_one, gain_two
    )
    full_query, full_key, full_value, full_out, full_gate, full_up, full_down = gathered[:7]
    grad_rows_in = cotangent.reshape(number_of_rows, model_width)
    grad_down = jnp.dot(hidden.T, grad_rows_in, preferred_element_type=jnp.float32)
    dhidden = jnp.dot(grad_rows_in, full_down.T, preferred_element_type=jnp.float32)
    dgate = (dhidden * up_part * sigmoid_gate * (1.0 + gate * (1.0 - sigmoid_gate))).astype(
        jnp.bfloat16
    )
    dup_part = (dhidden * activated).astype(jnp.bfloat16)
    grad_gate = jnp.dot(normalized_second.T, dgate, preferred_element_type=jnp.float32)
    grad_up = jnp.dot(normalized_second.T, dup_part, preferred_element_type=jnp.float32)
    normalized_second_grad = jnp.dot(dgate, full_gate.T, preferred_element_type=jnp.float32)
    normalized_second_grad = normalized_second_grad + jnp.dot(
        dup_part, full_up.T, preferred_element_type=jnp.float32
    )
    second_gain_gradient = jnp.sum(normalized_second_grad * second_normalized_input, axis=0)
    second_scaled = normalized_second_grad * second_norm
    dmixed = grad_rows_in.astype(jnp.float32) + second_factor * (
        second_scaled
        - second_normalized_input
        * jnp.mean(second_scaled * second_normalized_input, axis=-1, keepdims=True)
    )
    dproj = dmixed.astype(jnp.bfloat16)
    grad_out = jnp.dot(attention_result.T, dproj, preferred_element_type=jnp.float32)
    attention_result_grad = jnp.dot(dproj, full_out.T, preferred_element_type=jnp.float32).astype(
        jnp.bfloat16
    )
    attention_result_block_grads = attention_result_grad.reshape(
        sequence_count, token_local, KEY_VALUE_HEADS, queries_per_key_head, HEAD_SIZE
    ).transpose(0, 2, 3, 1, 4)
    attention_result_block_grads = attention_result_block_grads.reshape(
        sequence_count * KEY_VALUE_HEADS, queries_per_key_head, token_local, HEAD_SIZE
    )
    keys_all, values_all = gather_pairs(key_rotated, value_reduced)
    key_blocks = head_major(keys_all, sequence_count)
    value_blocks = head_major(values_all, sequence_count)

    def attend_back(block_item):
        query_block, key_block, value_block, prefix_len, log_total, dout_block = block_item
        scores = (
            jnp.einsum("gqd,kd->gqk", query_block, key_block, preferred_element_type=jnp.float32)
            * score_scale
        )
        visible = visible_for(prefix_len)[None]
        probs = jnp.where(
            visible, jnp.exp(jnp.where(visible, scores, -1e30) - log_total[..., None]), 0.0
        )
        dvalues = jnp.einsum(
            "gqk,gqd->kd",
            probs.astype(jnp.bfloat16),
            dout_block,
            preferred_element_type=jnp.float32,
        )
        dprobs = jnp.einsum(
            "gqd,kd->gqk", dout_block, value_block, preferred_element_type=jnp.float32
        )
        dscores = (probs * (dprobs - jnp.sum(probs * dprobs, axis=-1, keepdims=True))).astype(
            jnp.bfloat16
        )
        dquery = (
            jnp.einsum("gqk,kd->gqd", dscores, key_block, preferred_element_type=jnp.float32)
            * score_scale
        )
        dkeys = (
            jnp.einsum("gqk,gqd->kd", dscores, query_block, preferred_element_type=jnp.float32)
            * score_scale
        )
        return (dquery, dkeys, dvalues)

    query_block_grads, key_block_grads, value_block_grads = lax.map(
        attend_back,
        (
            query_block_list,
            key_blocks,
            value_blocks,
            prefix_repeated,
            log_totals,
            attention_result_block_grads,
        ),
    )
    key_grads_combined = key_block_grads.reshape(
        sequence_count, KEY_VALUE_HEADS, sequence_length, HEAD_SIZE
    ).transpose(0, 2, 1, 3)
    key_grads_combined = key_grads_combined.reshape(
        sequence_count, sequence_length, KEY_VALUE_HEADS * HEAD_SIZE
    )
    value_grads_combined = value_block_grads.reshape(
        sequence_count, KEY_VALUE_HEADS, sequence_length, HEAD_SIZE
    ).transpose(0, 2, 1, 3)
    value_grads_combined = value_grads_combined.reshape(
        sequence_count, sequence_length, KEY_VALUE_HEADS * HEAD_SIZE
    )
    key_grads_local, value_grads_local = (
        lax.psum_scatter(
            key_grads_combined.astype(jnp.bfloat16), "ctx", scatter_dimension=1, tiled=True
        ).astype(jnp.float32),
        lax.psum_scatter(
            value_grads_combined.astype(jnp.bfloat16), "ctx", scatter_dimension=1, tiled=True
        ).astype(jnp.float32),
    )
    key_prerotation_grad = inverse_rotation(
        key_grads_local.reshape(sequence_count, token_local, KEY_VALUE_HEADS, HEAD_SIZE),
        cosine_table,
        sine_values,
    )
    key_prerotation_grad = key_prerotation_grad.astype(jnp.bfloat16).reshape(
        number_of_rows, KEY_VALUE_HEADS * HEAD_SIZE
    )
    value_reduced_grad = value_grads_local.astype(jnp.bfloat16).reshape(
        number_of_rows, KEY_VALUE_HEADS * HEAD_SIZE
    )
    query_row_grads = query_block_grads.reshape(
        sequence_count, KEY_VALUE_HEADS, queries_per_key_head, token_local, HEAD_SIZE
    ).transpose(0, 3, 1, 2, 4)
    query_row_grads = query_row_grads.reshape(sequence_count, token_local, QUERY_HEADS, HEAD_SIZE)
    dquery_pre = (
        inverse_rotation(query_row_grads, cosine_table, sine_values)
        .astype(jnp.bfloat16)
        .reshape(number_of_rows, QUERY_HEADS * HEAD_SIZE)
    )
    grad_query = jnp.dot(normalized_rows.T, dquery_pre, preferred_element_type=jnp.float32)
    grad_key = jnp.dot(normalized_rows.T, key_prerotation_grad, preferred_element_type=jnp.float32)
    grad_value = jnp.dot(normalized_rows.T, value_reduced_grad, preferred_element_type=jnp.float32)
    normalized_grad = jnp.dot(dquery_pre, full_query.T, preferred_element_type=jnp.float32)
    normalized_grad = normalized_grad + jnp.dot(
        key_prerotation_grad, full_key.T, preferred_element_type=jnp.float32
    )
    normalized_grad = normalized_grad + jnp.dot(
        value_reduced_grad, full_value.T, preferred_element_type=jnp.float32
    )
    first_gain_gradient = jnp.sum(normalized_grad * first_normalized_input, axis=0)
    first_scaled = normalized_grad * first_norm
    input_grad = dmixed + first_factor * (
        first_scaled
        - first_normalized_input
        * jnp.mean(first_scaled * first_normalized_input, axis=-1, keepdims=True)
    )
    input_grad = input_grad.reshape(sequence_count, token_local, model_width)
    partial_value = (
        lax.psum_scatter(
            grad_query.astype(jnp.bfloat16), "seq", scatter_dimension=0, tiled=True
        ).astype(jnp.float32),
        lax.psum_scatter(
            grad_key.astype(jnp.bfloat16), "seq", scatter_dimension=0, tiled=True
        ).astype(jnp.float32),
        lax.psum_scatter(
            grad_value.astype(jnp.bfloat16), "seq", scatter_dimension=0, tiled=True
        ).astype(jnp.float32),
        lax.psum_scatter(
            grad_out.astype(jnp.bfloat16), "seq", scatter_dimension=0, tiled=True
        ).astype(jnp.float32),
        lax.psum_scatter(
            grad_gate.astype(jnp.bfloat16), "seq", scatter_dimension=0, tiled=True
        ).astype(jnp.float32),
        lax.psum_scatter(
            grad_up.astype(jnp.bfloat16), "seq", scatter_dimension=0, tiled=True
        ).astype(jnp.float32),
        lax.psum_scatter(
            grad_down.astype(jnp.bfloat16), "seq", scatter_dimension=0, tiled=True
        ).astype(jnp.float32),
        lax.psum_scatter(
            first_gain_gradient.astype(jnp.bfloat16), "seq", scatter_dimension=0, tiled=True
        ).astype(jnp.float32),
        lax.psum_scatter(
            second_gain_gradient.astype(jnp.bfloat16), "seq", scatter_dimension=0, tiled=True
        ).astype(jnp.float32),
    )
    owned = (
        lax.psum_scatter(
            partial_value[0].astype(jnp.bfloat16), "ctx", scatter_dimension=1, tiled=True
        ).astype(jnp.float32),
        lax.psum_scatter(
            partial_value[1].astype(jnp.bfloat16), "ctx", scatter_dimension=1, tiled=True
        ).astype(jnp.float32),
        lax.psum_scatter(
            partial_value[2].astype(jnp.bfloat16), "ctx", scatter_dimension=1, tiled=True
        ).astype(jnp.float32),
        lax.psum_scatter(
            partial_value[3].astype(jnp.bfloat16), "ctx", scatter_dimension=1, tiled=True
        ).astype(jnp.float32),
        lax.psum_scatter(
            partial_value[4].astype(jnp.bfloat16), "ctx", scatter_dimension=1, tiled=True
        ).astype(jnp.float32),
        lax.psum_scatter(
            partial_value[5].astype(jnp.bfloat16), "ctx", scatter_dimension=1, tiled=True
        ).astype(jnp.float32),
        lax.psum_scatter(
            partial_value[6].astype(jnp.bfloat16), "ctx", scatter_dimension=1, tiled=True
        ).astype(jnp.float32),
    )
    gains_owned = lax.psum((partial_value[7], partial_value[8]), "ctx")
    final_grads = owned + gains_owned
    return (
        output,
        input_grad,
        final_grads[7],
        final_grads[0],
        final_grads[1],
        final_grads[2],
        final_grads[3],
        final_grads[8],
        final_grads[4],
        final_grads[5],
        final_grads[6],
    )


def my_place():
    seq_at, ctx_at = lax.axis_index("seq"), lax.axis_index("ctx")
    return ctx_at // 2, lax.rem(ctx_at, 2), seq_at // 2, lax.rem(seq_at, 2)


def flipped(at, flip):
    return 1 - at if flip else at


def lane_ids(rows):
    return lax.broadcasted_iota(jnp.int32, (rows, LANES), 1)


def rotate_halves(tile, cosine, sine):
    lower = lax.rem(lane_ids(tile.shape[0]), HEAD_SIZE) < HEAD_SIZE // 2
    swapped = jnp.where(
        lower, pltpu.roll(tile, LANES - HEAD_SIZE // 2, 1), pltpu.roll(tile, HEAD_SIZE // 2, 1)
    )
    return tile * cosine + swapped * sine


def pair_tiles(natural):
    lower = lane_ids(natural[0].shape[0]) < HEAD_SIZE
    tiles = []
    for pair in range(3):
        for member in range(3):
            one, two = 6 * pair + member, 6 * pair + 3 + member
            left, right = natural[one // 2], natural[two // 2]
            if one % 2:
                left, right = pltpu.roll(left, HEAD_SIZE, 1), pltpu.roll(right, HEAD_SIZE, 1)
            tiles.append(jnp.where(lower, left, right))
    return tiles


def natural_tiles(paired):
    lower = lane_ids(paired[0].shape[0]) < HEAD_SIZE
    tiles = []
    for at in range(9):
        sides = []
        for side in range(2):
            head = 2 * at + side
            tile = paired[head // 6 * 3 + head % 3]
            if (head % 6) // 3 != side:
                tile = pltpu.roll(tile, HEAD_SIZE, 1)
            sides.append(tile)
        tiles.append(jnp.where(lower, sides[0], sides[1]))
    return tiles


def normalized(rows):
    factor = lax.rsqrt(jnp.mean(rows * rows, axis=-1, keepdims=True) + EPSILON)
    return factor, rows * factor


def vmem_specs(count):
    return [pl.BlockSpec(memory_space=pltpu.VMEM)] * count


def any_specs(count):
    return [pl.BlockSpec(memory_space=pl.ANY)] * count


def cost(flops, moved, transcendentals=0):
    return pl.CostEstimate(flops=int(flops), bytes_accessed=int(moved), transcendentals=int(transcendentals))


def params():
    return pltpu.CompilerParams(vmem_limit_bytes=VMEM_LIMIT)


def masked_pair(block, half, other):
    inside = (lane_ids(block.shape[0]) < HEAD_SIZE) == (half == 0)
    return jnp.where(inside, block.astype(F32), other)


def core_rows(core):
    return pl.ds(pl.multiple_of(core * 256, 256), 256)


def turned_blocks(matrix, parts):
    flat = matrix.astype(F32).T.astype(BF16)
    return flat.reshape(parts, flat.shape[0] // parts, flat.shape[1])


class Gathering:
    def __init__(self, own, full, lanes, block, sends, arrivals, corner_over_x=()):
        self.own, self.full, self.block, self.sends, self.arrivals = own, full, block, sends, arrivals
        self.corner_over_x, self.lanes = corner_over_x, lanes
        self.started = []

    def place(self, t, dx, dy, dcore=0):
        z, x, y, core = my_place()
        ctx_block = lax.rem(z - t + Z_SIZE, Z_SIZE) * 2 + flipped(x, dx)
        first, second = self.block(ctx_block, flipped(y, dy) * 2 + flipped(core, dcore))
        return self.full.at[first, second, :, self.lanes]

    def copy(self, source, target, number, axis):
        return pltpu.make_async_remote_copy(
            src_ref=source,
            dst_ref=target,
            send_sem=self.sends.at[number],
            recv_sem=self.arrivals.at[number],
            device_id=neighbour(axis),
            device_id_type=pl.DeviceIdType.MESH,
        )

    def send(self, piece, number, axis):
        place = self.place(*piece)
        source = self.own.at[:, self.lanes] if piece == (0, 0, 0) else place
        copy = self.copy(source, place, number, axis)
        copy.start()
        self.started.append(copy)

    def wait(self, piece, number, dcore=0):
        place = self.place(*piece, dcore)
        self.copy(place, place, number, "core").wait_recv()

    def to_core(self, piece):
        t, dx, dy = piece
        self.send(piece, 15 + 4 * t + 2 * dx + dy, "core")

    def over_z(self, t):
        if t < Z_SIZE - 1:
            self.send((t, 0, 0), t, "z")

    def over_plane(self, t):
        self.send((t, 0, 0), 3 + t, "x")
        self.send((t, 0, 0), 7 + t, "y")

    def begin(self):
        self.over_z(0)
        self.over_plane(0)
        self.to_core((0, 0, 0))

    def pass_on(self, t):
        self.wait((t, 0, 0), t - 1)
        self.over_z(t)
        self.over_plane(t)
        self.to_core((t, 0, 0))

    def sides(self, t):
        self.wait((t, 1, 0), 3 + t)
        if t not in self.corner_over_x:
            self.send((t, 1, 0), 11 + t, "y")
        self.to_core((t, 1, 0))
        self.wait((t, 0, 1), 7 + t)
        if t in self.corner_over_x:
            self.send((t, 0, 1), 11 + t, "x")
        self.to_core((t, 0, 1))

    def corner(self, t):
        self.wait((t, 1, 1), 11 + t)
        self.to_core((t, 1, 1))

    def finish(self, t):
        for dx in range(2):
            for dy in range(2):
                self.wait((t, dx, dy), 15 + 4 * t + 2 * dx + dy, 1)

    def drain(self):
        for copy in self.started:
            copy.wait_send()


class PlaneGathering(Gathering):
    def begin(self):
        self.send((0, 0, 0), 0, "x")
        self.send((0, 0, 0), 1, "y")
        self.to_core((0, 0, 0))

    def plane_sides(self):
        self.wait((0, 1, 0), 0)
        self.send((0, 1, 0), 2, "y")
        self.to_core((0, 1, 0))
        self.wait((0, 0, 1), 1)
        self.to_core((0, 0, 1))

    def plane_corner(self):
        self.wait((0, 1, 1), 2)
        self.to_core((0, 1, 1))

    def ring(self, t):
        for dx in range(2):
            for dy in range(2):
                number = 3 + 4 * t + 2 * dx + dy
                if t:
                    self.wait((t, dx, dy), number - 4)
                if t < Z_SIZE - 1:
                    self.send((t, dx, dy), number, "z")
                if t:
                    self.to_core((t, dx, dy))


def neighbour(axis):
    z, x, y, core = my_place()
    if axis == "z":
        z = lax.rem(z + 1, Z_SIZE)
    elif axis == "z_back":
        z = lax.rem(z + Z_SIZE - 1, Z_SIZE)
    elif axis == "z_two":
        z = lax.rem(z + 2, Z_SIZE)
    elif axis == "x":
        x = 1 - x
    elif axis == "y":
        y = 1 - y
    elif axis == "core":
        core = 1 - core
    elif axis == "y_core":
        y, core = 1 - y, 1 - core
    return (y * 2 + core, z * 2 + x)


def meet(axes):
    barrier = pltpu.get_barrier_semaphore()
    for axis in axes:
        pl.semaphore_signal(barrier, inc=1, device_id=neighbour(axis), device_id_type=pl.DeviceIdType.MESH)
    pl.semaphore_wait(barrier, len(axes))


def front_kernel(
    qkv_own,
    down_own,
    up_own,
    gains_own,
    tokens,
    cosine,
    sine,
    limit,
    cotangent,
    qkv_out,
    pairs_out,
    rows_turned,
    both_grads,
    hidden_both,
    attended_both,
    cot_turned,
    proj_turned,
    query_out,
    attended,
    log_total,
    gain_out,
    output,
    mixed_grad,
    attended_grad,
    gain_grad,
    qkv,
    down,
    up,
    pairs,
    gates,
    ups,
    wide,
    keys,
    values,
    gains,
    rows_two,
    rows_stage,
    hidden,
    attended_rows,
    grads,
    cot_stage,
    proj_stage,
    qkv_sends,
    qkv_arrivals,
    down_sends,
    down_arrivals,
    plane_sends,
    plane_arrivals,
    up_sends,
    up_arrivals,
    pair_sends,
    pair_arrivals,
    gain_sends,
    gain_arrivals,
    own_sems,
    core_sends,
    core_arrivals,
    core_own_sems,
):
    z, x, y, core = my_place()
    seq_at, ctx_at = y * 2 + core, z * 2 + x
    by_ctx, by_seq = (lambda ctx, seq: (ctx, seq)), (lambda ctx, seq: (seq, ctx))
    first = Gathering(qkv_own, qkv, slice(0, 240), by_ctx, qkv_sends, qkv_arrivals, (1, 3))
    plane = PlaneGathering(down_own, down, slice(0, PLANE_LANES), by_seq, plane_sends, plane_arrivals)
    rest = (
        Gathering(down_own, down, slice(PLANE_LANES, 1056), by_seq, down_sends, down_arrivals, (3,)),
        Gathering(up_own, up, slice(0, 768), by_ctx, up_sends, up_arrivals, (3,)),
    )
    mine, theirs, width = core_rows(core), core_rows(1 - core), tokens.shape[1]
    meet(("z", "z_back", "x", "y", "core", "y_core"))
    first.begin()
    gain_copies = []
    for number, axis in enumerate(("core", "y", "y_core")):
        copy = pltpu.make_async_remote_copy(
            src_ref=gains_own,
            dst_ref=gains.at[seq_at],
            send_sem=gain_sends.at[number],
            recv_sem=gain_arrivals.at[number],
            device_id=neighbour(axis),
            device_id_type=pl.DeviceIdType.MESH,
        )
        copy.start()
        gain_copies.append(copy)
    own_copies = [
        pltpu.make_async_copy(source, target, own_sems.at[number])
        for number, (source, target) in enumerate(
            (
                (qkv_own, first.place(0, 0, 0)),
                (down_own, down.at[seq_at, ctx_at]),
                (up_own, up.at[ctx_at, seq_at]),
                (gains_own, gains.at[seq_at]),
            )
        )
    ]
    for copy in own_copies:
        copy.start()
    for t in range(1, Z_SIZE):
        first.pass_on(t)
        if t == 1:
            plane.begin()
        if t == Z_SIZE - 2:
            for group in rest:
                group.over_z(0)
        first.sides(t - 1)
    plane.plane_sides()
    first.sides(Z_SIZE - 1)
    for group in rest:
        group.over_plane(0)
        group.to_core((0, 0, 0))
    plane.plane_corner()
    plane.ring(0)
    for number, flips in enumerate(((0, 1), (1, 0), (1, 1))):
        place = gains.at[flipped(y, flips[0]) * 2 + flipped(core, flips[1])]
        pltpu.make_async_remote_copy(
            src_ref=place,
            dst_ref=place,
            send_sem=gain_sends.at[number],
            recv_sem=gain_arrivals.at[number],
            device_id=neighbour("core"),
            device_id_type=pl.DeviceIdType.MESH,
        ).wait_recv()
    for copy in own_copies:
        copy.wait()
    for row in range(4):
        gain_out[:, row * 288 : (row + 1) * 288] = gains[row]
    _, hat = normalized(tokens[...].astype(F32))
    rows = (hat * gain_out[0:1, :]).astype(BF16)
    for t in range(Z_SIZE):
        first.corner(t)
    for group in rest:
        group.pass_on(1)
    for t in range(Z_SIZE):
        first.finish(t)

    def multiply(ctx_block, carry):
        matrix = qkv[ctx_block].reshape(tokens.shape[1], 240)
        gates[ctx_block, :, :240] = jnp.dot(rows, matrix, preferred_element_type=F32)
        return carry

    lax.fori_loop(0, 8, multiply, 0)
    save_qkv = pltpu.make_async_copy(qkv, qkv_out, own_sems.at[4])
    save_qkv.start()
    q_part, kv_part = 144, 48
    for at in range(8):
        wide[:, at * q_part : (at + 1) * q_part] = gates[at, :, :q_part]
        wide[:, 1152 + at * kv_part : 1152 + (at + 1) * kv_part] = gates[at, :, q_part : q_part + kv_part]
        wide[:, 1536 + at * kv_part : 1536 + (at + 1) * kv_part] = gates[at, :, q_part + kv_part : 240]
    cos_tile, sin_tile = cosine[...], sine[...]
    for pair in range(3):
        key_tile = wide[:, 1152 + pair * LANES : 1152 + (pair + 1) * LANES]
        pairs[ctx_at, :, 2 * pair * LANES : (2 * pair + 1) * LANES] = rotate_halves(
            key_tile, cos_tile, sin_tile
        ).astype(BF16)
        pairs[ctx_at, :, (2 * pair + 1) * LANES : (2 * pair + 2) * LANES] = wide[
            :, 1536 + pair * LANES : 1536 + (pair + 1) * LANES
        ].astype(BF16)
    natural = [
        rotate_halves(wide[:, at * LANES : (at + 1) * LANES], cos_tile, sin_tile) * HEAD_SIZE**-0.5
        for at in range(9)
    ]
    for at, tile in enumerate(pair_tiles(natural)):
        query_out[at] = tile.astype(BF16)

    pair_copies = []

    def pair_place(t, dx):
        return pairs.at[lax.rem(z - t + Z_SIZE, Z_SIZE) * 2 + flipped(x, dx)]

    def pair_copy(place, number, axis):
        return pltpu.make_async_remote_copy(
            src_ref=place,
            dst_ref=place,
            send_sem=pair_sends.at[number],
            recv_sem=pair_arrivals.at[number],
            device_id=neighbour(axis),
            device_id_type=pl.DeviceIdType.MESH,
        )

    def pair_pass(t):
        if t:
            pair_copy(pair_place(t, 0), t - 1, "z").wait_recv()
        for number, axis in ((t, "z"), (3 + t, "x")):
            if axis == "x" or t < Z_SIZE - 1:
                copy = pair_copy(pair_place(t, 0), number, axis)
                copy.start()
                pair_copies.append(copy)

    def in_rest(step):
        for group in rest:
            step(group)

    pair_pass(0)
    in_rest(lambda group: group.pass_on(2))
    pair_pass(1)
    in_rest(lambda group: group.sides(0))
    pair_pass(2)
    plane.ring(1)
    in_rest(lambda group: group.sides(1))
    pair_pass(3)
    cot_stage[...] = turned_blocks(cotangent[...], 8)
    in_rest(lambda group: group.pass_on(3))
    in_rest(lambda group: group.sides(2))
    for t in range(Z_SIZE):
        pair_copy(pair_place(t, 1), 3 + t, "x").wait_recv()
    save_pairs = pltpu.make_async_copy(pairs, pairs_out, own_sems.at[5])
    save_pairs.start()

    key_ids = lax.broadcasted_iota(jnp.int32, (256, tokens.shape[0]), 0)

    def attend_pair(pair):
        for at in range(8):
            for half in range(2):
                block = pairs[at, :, 2 * pair * LANES : (2 * pair + 1) * LANES]
                keys[half, at] = masked_pair(block, half, 0.0).astype(BF16)
                block = pairs[at, :, (2 * pair + 1) * LANES : (2 * pair + 2) * LANES]
                values[half, at] = masked_pair(block, half, 1.0).T.astype(BF16)

        def attend_member(member, carry):
            tile = query_out[3 * pair + member]
            parts = []
            for half in range(2):
                top = None
                for at in range(8):
                    part = lax.dot_general(keys[half, at], tile, NT, preferred_element_type=F32)
                    part = jnp.where(key_ids < limit[...] - at * 256, part, -1e30)
                    ups[at, :, :256] = part
                    block_top = jnp.max(part, axis=0, keepdims=True)
                    top = block_top if top is None else jnp.maximum(top, block_top)
                total = jnp.zeros((LANES, tile.shape[0]), F32)
                for at in range(8):
                    weight = jnp.exp(ups[at, :, :256] - top).astype(BF16)
                    total = total + jnp.dot(values[half, at], weight, preferred_element_type=F32)
                norm = total[HEAD_SIZE : HEAD_SIZE + 1] if half == 0 else total[:1]
                log_total[3 * pair + member, half : half + 1, :] = top + jnp.log(norm)
                own = total[:HEAD_SIZE] if half == 0 else total[HEAD_SIZE:]
                parts.append(own / norm)
            attended[3 * pair + member] = jnp.concatenate(parts, axis=0).T.astype(BF16)
            return carry

        lax.fori_loop(0, 3, attend_member, 0)

    started, own_copies = [], []

    def core_copy(source, target, number):
        return pltpu.make_async_remote_copy(
            src_ref=source,
            dst_ref=target,
            send_sem=core_sends.at[number],
            recv_sem=core_arrivals.at[number],
            device_id=neighbour("core"),
            device_id_type=pl.DeviceIdType.MESH,
        )

    def keep(source, target, number):
        copy = pltpu.make_async_copy(source, target, core_own_sems.at[number])
        copy.start()
        own_copies.append(copy)

    def share(source, target, number):
        copy = core_copy(source, target, number)
        copy.start()
        started.append(copy)

    def deal(stage, target_of, number):
        for y_at in range(2):
            keep(stage.at[y_at * 2 + core], target_of(y_at), number + y_at)
            share(stage.at[y_at * 2 + 1 - core], target_of(y_at), number + y_at)

    attend_pair(0)
    plane.ring(2)
    in_rest(lambda group: group.sides(3))
    attend_pair(1)
    in_rest(lambda group: group.corner(0))
    in_rest(lambda group: group.corner(1))
    attend_pair(2)
    keep(cot_stage, cot_turned.at[:, :, mine], 1)
    share(cot_stage, cot_turned.at[:, :, mine], 1)
    in_rest(lambda group: group.corner(2))
    for at, tile in enumerate(natural_tiles([attended[at].astype(F32) for at in range(9)])):
        wide[:, at * LANES : (at + 1) * LANES] = tile
    for row in range(4):
        attended_rows[row] = wide[:, row * 288 : (row + 1) * 288].astype(BF16)
    rest[0].corner(3)
    for t in range(Z_SIZE):
        rest[0].finish(t)

    def out_block(row):
        return down[row, :, :, 768:].reshape(width, 288)

    def down_block(row):
        return down[row, :, :, :768].reshape(width, 768)

    def gate_block(block):
        return up[block, :, :, :384].reshape(width, 384)

    def up_block(block):
        return up[block, :, :, 384:].reshape(width, 384)

    mixed_grad[...] = tokens[...].astype(F32)
    for row in range(4):
        mixed_grad[...] += lax.dot_general(attended_rows[row], out_block(row), NT, preferred_element_type=F32)
    rest[1].corner(3)
    plane.ring(3)
    deal(attended_rows, lambda y_at: attended_both.at[y_at, mine], 2)
    factor, hat = normalized(mixed_grad[...])
    gain_row = gain_out[1:2, :]
    rows_two[...] = (hat * gain_row).astype(BF16)
    wide[:, :1152] = hat
    for t in range(Z_SIZE):
        rest[1].finish(t)

        def gate_and_up(dx, carry, t=t):
            block = lax.rem(z - t + Z_SIZE, Z_SIZE) * 2 + lax.rem(x + dx, 2)
            gates[block] = jnp.dot(rows_two[...], gate_block(block), preferred_element_type=F32)
            ups[block] = jnp.dot(rows_two[...], up_block(block), preferred_element_type=F32)
            return carry

        lax.fori_loop(0, 2, gate_and_up, 0)
    rows_stage[...] = turned_blocks(rows_two[...], 4)
    for t in range(Z_SIZE):
        plane.finish(t)
    deal(rows_stage, lambda y_at: rows_turned.at[y_at, :, mine], 4)

    def feed_forward(row, carry):
        back = jnp.dot(cotangent[...], down_block(row), preferred_element_type=F32)
        for side in range(2):
            block = 2 * row + side
            gate, up_part = gates[block], ups[block]
            sigmoid = 1.0 / (1.0 + jnp.exp(-gate))
            active = gate * sigmoid
            hidden[row, :, side * 384 : (side + 1) * 384] = (active * up_part).astype(BF16)
            part = back[:, side * 384 : (side + 1) * 384]
            grads[block, :, :384] = (part * up_part * sigmoid * (1.0 + gate * (1.0 - sigmoid))).astype(BF16)
            grads[block, :, 384:] = (part * active).astype(BF16)
        mixed_grad[...] += lax.dot_general(hidden[row], down_block(row), NT, preferred_element_type=F32)
        return carry

    lax.fori_loop(0, 4, feed_forward, 0)
    output[...] = mixed_grad[...].astype(BF16)
    keep(grads, both_grads.at[:, mine, :], 0)
    share(grads, both_grads.at[:, mine, :], 0)
    deal(hidden, lambda y_at: hidden_both.at[y_at, mine], 6)
    mixed_grad[...] = jnp.zeros_like(mixed_grad)

    def rows_back(block, carry):
        part = lax.dot_general(grads[block, :, :384], gate_block(block), NT, preferred_element_type=F32)
        part = part + lax.dot_general(grads[block, :, 384:], up_block(block), NT, preferred_element_type=F32)
        mixed_grad[...] += part
        return carry

    lax.fori_loop(0, 8, rows_back, 0)
    grad_two, hat = mixed_grad[...], wide[:, :1152]
    gain_grad[...] = jnp.sum(grad_two * hat, axis=0, keepdims=True)
    scaled = grad_two * gain_row
    total = cotangent[...].astype(F32) + factor * (
        scaled - hat * jnp.mean(scaled * hat, axis=-1, keepdims=True)
    )
    mixed_grad[...] = total
    rows_two[...] = total.astype(BF16)
    proj_stage[...] = turned_blocks(rows_two[...], 8)
    for row in range(4):
        wide[:, row * 288 : (row + 1) * 288] = jnp.dot(
            rows_two[...], out_block(row), preferred_element_type=F32
        )
    keep(proj_stage, proj_turned.at[:, :, mine], 8)
    share(proj_stage, proj_turned.at[:, :, mine], 8)
    tiles = pair_tiles([wide[:, at * LANES : (at + 1) * LANES] for at in range(9)])
    for at, tile in enumerate(tiles):
        attended_grad[at] = tile.astype(BF16)
    for group in rest + (first, plane):
        group.drain()
    for copy in pair_copies + gain_copies + started:
        copy.wait_send()
    for copy in own_copies + [save_qkv, save_pairs]:
        copy.wait()
    places = [both_grads.at[:, theirs, :], cot_turned.at[:, :, theirs]]
    places += [attended_both.at[y_at, theirs] for y_at in range(2)]
    places += [rows_turned.at[y_at, :, theirs] for y_at in range(2)]
    places += [hidden_both.at[y_at, theirs] for y_at in range(2)]
    places.append(proj_turned.at[:, :, theirs])
    for number, place in enumerate(places):
        core_copy(place, place, number).wait_recv()


def front(qkv_own, down_own, up_own, gains_own, tokens, cosine, sine, limit, cotangent):
    rows, width = tokens.shape
    dma = pltpu.SemaphoreType.DMA
    shape = jax.ShapeDtypeStruct
    return pl.pallas_call(
        front_kernel,
        out_shape=(
            shape((8, 4) + qkv_own.shape, BF16),
            shape((8, rows, 768), BF16),
            shape((2, 288, 2 * rows), BF16),
            shape((8, 2 * rows, 768), BF16),
            shape((2, 2 * rows, 768), BF16),
            shape((2, 2 * rows, 288), BF16),
            shape((8, 144, 2 * rows), BF16),
            shape((8, 144, 2 * rows), BF16),
            shape((9, rows, LANES), BF16),
            shape((9, rows, LANES), BF16),
            shape((9, 2, rows), F32),
            shape((8, width), F32),
            shape((rows, width), BF16),
            shape((rows, width), F32),
            shape((9, rows, LANES), BF16),
            shape((1, width), F32),
        ),
        in_specs=vmem_specs(1) + any_specs(2) + vmem_specs(6),
        out_specs=tuple(any_specs(8) + vmem_specs(8)),
        scratch_shapes=[
            pltpu.VMEM((8, 4) + qkv_own.shape, BF16),
            pltpu.VMEM((4, 8) + down_own.shape, BF16),
            pltpu.VMEM((8, 4) + up_own.shape, BF16),
            pltpu.VMEM((8, rows, 768), BF16),
            pltpu.VMEM((8, rows, 384), F32),
            pltpu.VMEM((8, rows, 384), F32),
            pltpu.VMEM((rows, 1920), F32),
            pltpu.VMEM((2, 8, 256, LANES), BF16),
            pltpu.VMEM((2, 8, LANES, 256), BF16),
            pltpu.VMEM((4, 8, 288), F32),
            pltpu.VMEM((rows, width), BF16),
            pltpu.VMEM((4, 288, rows), BF16),
            pltpu.VMEM((4, rows, 768), BF16),
            pltpu.VMEM((4, rows, 288), BF16),
            pltpu.VMEM((8, rows, 768), BF16),
            pltpu.VMEM((8, 144, rows), BF16),
            pltpu.VMEM((8, 144, rows), BF16),
        ]
        + [dma((31,))] * 8
        + [dma((7,))] * 2
        + [dma((3,))] * 2
        + [dma((6,))]
        + [dma((9,))] * 3,
        compiler_params=pltpu.CompilerParams(
            vmem_limit_bytes=VMEM_LIMIT, collective_id=1, has_side_effects=True
        ),
        cost_estimate=cost(4 * 18 * rows * 2048 * 128 * 4, 4e8, 18 * rows * 2048),
        name="front",
    )(qkv_own, down_own, up_own, gains_own, tokens, cosine, sine, limit, cotangent)


class Scattering:
    def __init__(self, buffers, sends, arrivals, out, piece, corners):
        self.corner, self.side_x, self.side_y, self.near_x, self.near_y, self.ring = buffers
        self.sends, self.arrivals, self.out, self.piece, self.corners = sends, arrivals, out, piece, corners

    def copy(self, source, target, number, axis):
        return pltpu.make_async_remote_copy(
            src_ref=source,
            dst_ref=target,
            send_sem=self.sends.at[number],
            recv_sem=self.arrivals.at[number],
            device_id=neighbour(axis),
            device_id_type=pl.DeviceIdType.MESH,
        )

    def corner_copies(self, t, axes=("x", "y")):
        for number, (axis, lanes) in enumerate(self.corners):
            if axis in axes:
                target = self.side_x if axis == "y" else self.side_y
                yield self.copy(self.corner.at[t, :, lanes], target.at[t, :, lanes], 4 * number + t, axis)

    def side_copy(self, t, axis):
        source, target, first = (self.side_x, self.near_x, 8) if axis == "x" else (self.side_y, self.near_y, 12)
        return self.copy(source.at[t], target.at[t], first + t, axis)

    def ring_copy(self, t):
        return self.copy(self.near_x.at[t], self.ring.at[t - 1], 15 + t, "z_back")

    def corner_step(self, t):
        self.piece(t, 1, 1, self.corner.at[t], lambda lanes: [])
        for copy in self.corner_copies(t):
            copy.start()

    def side_step(self, t, axis):
        came = "y" if axis == "x" else "x"
        for copy in self.corner_copies(t, (came,)):
            copy.wait_recv()
        side = (self.side_x if axis == "x" else self.side_y).at[t]
        ranges = [lanes for at, lanes in self.corners if at == came]

        def addend(lanes):
            return [side[:, lanes]] if any(at.start <= lanes.start and lanes.stop <= at.stop for at in ranges) else []

        self.piece(t, int(axis == "x"), int(axis == "y"), side, addend)
        self.side_copy(t, axis).start()

    def near_step(self, t):
        self.side_copy(t, "x").wait_recv()
        self.side_copy(t, "y").wait_recv()
        if t < Z_SIZE - 1:
            self.ring_copy(t + 1).wait_recv()

        def addend(lanes):
            parts = [self.near_x[t, :, lanes], self.near_y[t, :, lanes]]
            return parts + ([self.ring[t, :, lanes]] if t < Z_SIZE - 1 else [])

        self.piece(t, 0, 0, self.near_x.at[t] if t else self.out, addend)
        if t:
            self.ring_copy(t).start()

    def drain(self):
        for t in range(Z_SIZE):
            for copy in self.corner_copies(t):
                copy.wait_send()
            self.side_copy(t, "x").wait_send()
            self.side_copy(t, "y").wait_send()
            if t:
                self.ring_copy(t).wait_send()


class PlaneScattering:
    def __init__(self, buffers, sends, arrivals, out, piece):
        self.sums, self.corner, self.near_x, self.near_y = buffers
        self.sends, self.arrivals, self.out, self.piece = sends, arrivals, out, piece

    def copy(self, source, target, number, axis):
        return pltpu.make_async_remote_copy(
            src_ref=source,
            dst_ref=target,
            send_sem=self.sends.at[number],
            recv_sem=self.arrivals.at[number],
            device_id=neighbour(axis),
            device_id_type=pl.DeviceIdType.MESH,
        )

    def ring_copy(self, t, dx, dy):
        return self.copy(
            self.sums.at[t, dx, dy], self.sums.at[t - 1, dx, dy], 4 * (t - 1) + 2 * dx + dy, "z_back"
        )

    def plane_copies(self):
        return (
            self.copy(self.sums.at[0, 1, 1], self.corner, 12, "y"),
            self.copy(self.sums.at[0, 1, 0], self.near_x, 13, "x"),
            self.copy(self.sums.at[0, 0, 1], self.near_y, 14, "y"),
        )

    def ring_step(self, t, first=False):
        def one(number, carry):
            dx, dy = number // 2, lax.rem(number, 2)
            target = self.sums.at[t, dx, dy]
            if not first:
                self.ring_copy(t + 1, dx, dy).wait_recv()
            self.piece(t, dx, dy, target, lambda lanes: [] if first else [target[:, lanes]])

            @pl.when(t > 0)
            def _():
                self.ring_copy(t, dx, dy).start()

            return carry

        lax.fori_loop(0, 4, one, 0)

    def plane_start(self):
        corner, _, side_y = self.plane_copies()
        corner.start()
        side_y.start()

    def plane_side(self):
        corner, side_x, _ = self.plane_copies()
        corner.wait_recv()
        side = self.sums.at[0, 1, 0]
        side[...] = (side[...].astype(F32) + self.corner[...].astype(F32)).astype(BF16)
        side_x.start()

    def plane_end(self):
        _, side_x, side_y = self.plane_copies()
        side_x.wait_recv()
        side_y.wait_recv()
        total = self.sums[0, 0, 0].astype(F32) + self.near_x[...].astype(F32)
        self.out[...] = total + self.near_y[...].astype(F32)

    def drain(self):
        for t in range(1, Z_SIZE):
            for dx in range(2):
                for dy in range(2):
                    self.ring_copy(t, dx, dy).wait_send()
        for copy in self.plane_copies():
            copy.wait_send()


def back_kernel(
    rows_turned,
    both_grads,
    hidden,
    attended_rows,
    cot_turned,
    proj_turned,
    query,
    attended,
    grad,
    log_total,
    limit,
    cosine,
    sine,
    pairs,
    tokens,
    gains,
    second_gain,
    weights,
    mixed_grad,
    down_out,
    up_out,
    qkv_out,
    input_grad,
    gain_out,
    *refs,
):
    down_buffers, up_buffers, qkv_buffers, plane_buffers = refs[:6], refs[6:12], refs[12:18], refs[18:22]
    (
        keys,
        keys_turned,
        values,
        key_sum,
        value_sum,
        pair_far,
        pair_own,
        pair_near,
        pair_ring,
        query_grad,
        wide,
        pieces,
        first_stage,
        first_turned,
        weight_slots,
        gain_sum,
        gain_came,
    ) = refs[22:39]
    (
        down_sends,
        down_arrivals,
        up_sends,
        up_arrivals,
        qkv_sends,
        qkv_arrivals,
        plane_sends,
        plane_arrivals,
        pair_sends,
        pair_arrivals,
        core_sends,
        core_arrivals,
        gain_sends,
        gain_arrivals,
        own_sems,
        weight_sems,
    ) = refs[39:]
    z, x, y, core = my_place()
    mine, theirs = core_rows(core), core_rows(1 - core)
    rows, width = tokens.shape

    def flip_if(at, flip):
        return flipped(at, flip) if isinstance(flip, int) else lax.rem(at + flip, 2)

    def ctx_of(t, dx):
        return lax.rem(z - t + Z_SIZE, Z_SIZE) * 2 + flip_if(x, dx)

    def put(target, lanes, value, addend):
        for part in addend(lanes):
            value = value + part.astype(F32)
        target[:, lanes] = value.astype(target.dtype)

    def plane_piece(t, dx, dy, target, addend):
        block, row = ctx_of(t, dx), flip_if(y, dy)
        for lanes in (slice(0, 256), slice(256, PLANE_LANES)):
            value = jnp.dot(cot_turned[block], hidden[row, :, lanes], preferred_element_type=F32)
            put(target, lanes, value, addend)

    def down_piece(t, dx, dy, target, addend):
        block, row = ctx_of(t, dx), flipped(y, dy)
        split = 768 - PLANE_LANES
        value = jnp.dot(cot_turned[block], hidden[row, :, PLANE_LANES:], preferred_element_type=F32)
        put(target, slice(0, split), value, addend)
        value = jnp.dot(proj_turned[block], attended_rows[row], preferred_element_type=F32)
        put(target, slice(split, split + 288), value, addend)

    def up_piece(t, dx, dy, target, addend):
        block, row = ctx_of(t, dx), flipped(y, dy)
        for lanes in (slice(0, 384), slice(384, 768)):
            value = jnp.dot(rows_turned[row], both_grads[block, :, lanes], preferred_element_type=F32)
            put(target, lanes, value, addend)

    def qkv_piece(t, dx, dy, target, addend):
        block, row = ctx_of(t, dx), flipped(y, dy)
        value = jnp.dot(first_turned[row], pieces[block], preferred_element_type=F32)
        put(target, slice(0, 240), value, addend)

    plane = PlaneScattering(
        plane_buffers, plane_sends, plane_arrivals, down_out.at[:, :PLANE_LANES], plane_piece
    )
    down = Scattering(
        down_buffers,
        down_sends,
        down_arrivals,
        down_out.at[:, PLANE_LANES:],
        down_piece,
        (("y", slice(0, 1056 - PLANE_LANES)),),
    )
    up = Scattering(
        up_buffers, up_sends, up_arrivals, up_out, up_piece, (("y", slice(0, 384)), ("x", slice(384, 768)))
    )
    qkv = Scattering(qkv_buffers, qkv_sends, qkv_arrivals, qkv_out, qkv_piece, (("y", slice(0, 240)),))

    meet(("z", "z_back", "x", "y", "core", "z_two"))
    residual = pltpu.make_async_copy(mixed_grad, input_grad, own_sems.at[2])
    residual.start()

    plane.ring_step(Z_SIZE - 1, True)

    def corners(number, carry):
        t = Z_SIZE - 1 - number
        down.corner_step(t)
        up.corner_step(t)
        return carry

    lax.fori_loop(0, Z_SIZE, corners, 0)

    factor, hat = normalized(tokens[...].astype(F32))
    first_stage[...] = turned_blocks((hat * gains[0:1, :]).astype(BF16), 4)

    def core_copy(source, target, number):
        return pltpu.make_async_remote_copy(
            src_ref=source,
            dst_ref=target,
            send_sem=core_sends.at[number],
            recv_sem=core_arrivals.at[number],
            device_id=neighbour("core"),
            device_id_type=pl.DeviceIdType.MESH,
        )

    def pair_copy(pair, t, axis):
        if axis == "x":
            source, target, number = pair_far.at[pair, t], pair_near.at[pair, t], 4 * pair + t
        else:
            source, target, number = pair_own.at[pair, t], pair_ring.at[pair, t - 1], 11 + 3 * pair + t
        return pltpu.make_async_remote_copy(
            src_ref=source,
            dst_ref=target,
            send_sem=pair_sends.at[number],
            recv_sem=pair_arrivals.at[number],
            device_id=neighbour(axis),
            device_id_type=pl.DeviceIdType.MESH,
        )

    key_ids = lax.broadcasted_iota(jnp.int32, (256, rows), 0)

    def attend_pair_back(pair):
        key_lanes = pl.ds(pl.multiple_of(pair * 256, 256), LANES)
        value_lanes = pl.ds(pl.multiple_of(pair * 256 + LANES, LANES), LANES)
        key_sum[...] = jnp.zeros_like(key_sum)
        value_sum[...] = jnp.zeros_like(value_sum)
        for at in range(8):
            key_block, value_block = pairs[at, :, key_lanes], pairs[at, :, value_lanes]
            for half in range(2):
                masked = masked_pair(key_block, half, 0.0)
                keys[half, at] = masked.astype(BF16)
                keys_turned[half, at] = masked.T.astype(BF16)
                values[half, at] = masked_pair(value_block, half, 0.0).astype(BF16)

        def member_step(member, carry):
            number = 3 * pair + member
            tile, grad_tile = query[number], grad[number]
            product = (attended[number].astype(F32) * grad_tile.astype(F32)).T
            turned = jnp.zeros((LANES, rows), F32)
            for half in range(2):
                own = slice(half * HEAD_SIZE, (half + 1) * HEAD_SIZE)
                shift = jnp.sum(product[own], axis=0, keepdims=True)
                log_row = log_total[number, half : half + 1, :]
                query_half = masked_pair(tile, half, 0.0).astype(BF16)
                grad_half = masked_pair(grad_tile, half, 0.0).astype(BF16)
                for at in range(8):
                    part = lax.dot_general(keys[half, at], tile, NT, preferred_element_type=F32)
                    part = jnp.where(key_ids < limit[...] - at * 256, part, -1e30)
                    probs = jnp.exp(part - log_row)
                    back = lax.dot_general(values[half, at], grad_tile, NT, preferred_element_type=F32)
                    scored = (probs * (back - shift)).astype(BF16)
                    value_sum[at] += jnp.dot(probs.astype(BF16), grad_half, preferred_element_type=F32)
                    key_sum[at] += jnp.dot(scored, query_half, preferred_element_type=F32)
                    turned = turned + jnp.dot(keys_turned[half, at], scored, preferred_element_type=F32)
            turned = rotate_halves(turned.T * HEAD_SIZE**-0.5, cosine[...], -sine[...])
            query_grad[number] = turned.astype(BF16)
            return carry

        lax.fori_loop(0, 3, member_step, 0)
        for t in range(Z_SIZE):
            for dx, place in ((0, pair_own), (1, pair_far)):
                block = ctx_of(t, dx)
                place[pair, t, :, :LANES] = key_sum[block].astype(BF16)
                place[pair, t, :, LANES:] = value_sum[block].astype(BF16)
        for t in range(Z_SIZE - 1, -1, -1):
            pair_copy(pair, t, "x").start()

    def attend_and_sides(number, carry):
        @pl.when(number < 3)
        def _():
            attend_pair_back(number)
            plane.ring_step(Z_SIZE - 2 - number)

        t = Z_SIZE - 1 - number
        for axis in ("y", "x"):
            down.side_step(t, axis)
            up.side_step(t, axis)
        return carry

    lax.fori_loop(0, 4, attend_and_sides, 0)
    plane.plane_start()

    first_copies = []
    for y_at in range(2):
        place = first_turned.at[y_at, :, mine]
        own = pltpu.make_async_copy(first_stage.at[y_at * 2 + core], place, own_sems.at[y_at])
        own.start()
        copy = core_copy(first_stage.at[y_at * 2 + 1 - core], place, 1 + y_at)
        copy.start()
        first_copies.append((own, copy))

    def pair_step(t):
        for pair in range(3):
            pair_copy(pair, t, "x").wait_recv()
            total = pair_own[pair, t].astype(F32) + pair_near[pair, t].astype(F32)
            if t < Z_SIZE - 1:
                pair_copy(pair, t + 1, "z_back").wait_recv()
                total = total + pair_ring[pair, t].astype(F32)
            if t:
                pair_own[pair, t] = total.astype(BF16)
                pair_copy(pair, t, "z_back").start()
            else:
                key_tile = rotate_halves(total[:, :LANES], cosine[...], -sine[...])
                wide[:, 1152 + pair * LANES : 1152 + (pair + 1) * LANES] = key_tile
                wide[:, 1536 + pair * LANES : 1536 + (pair + 1) * LANES] = total[:, LANES:]

    pair_step(3)
    for at, tile in enumerate(natural_tiles([query_grad[at].astype(F32) for at in range(9)])):
        wide[:, at * LANES : (at + 1) * LANES] = tile
    pair_step(2)
    pair_step(1)
    plane.plane_side()
    down.near_step(3)
    up.near_step(3)
    pair_step(0)
    q_part, kv_part = 144, 48
    for at in range(8):
        pieces[at, mine, :] = jnp.concatenate(
            [
                wide[:, at * q_part : (at + 1) * q_part],
                wide[:, 1152 + at * kv_part : 1152 + (at + 1) * kv_part],
                wide[:, 1536 + at * kv_part : 1536 + (at + 1) * kv_part],
            ],
            axis=1,
        ).astype(BF16)

    def weight_copy(at):
        return pltpu.make_async_copy(weights.at[at], weight_slots.at[at % 2], weight_sems.at[at % 2])

    weight_copy(0).start()
    weight_copy(1).start()
    piece_copy = core_copy(pieces.at[:, mine, :], pieces.at[:, mine, :], 0)
    piece_copy.start()
    grad_one = wide.at[:, :1152]
    for at in range(8):
        weight_copy(at).wait()
        part = lax.dot_general(
            pieces[at, mine, :], weight_slots[at % 2].reshape(width, 240), NT, preferred_element_type=F32
        )
        grad_one[...] = part if at == 0 else grad_one[...] + part
        if at < 6:
            weight_copy(at + 2).start()
    core_copy(pieces.at[:, theirs, :], pieces.at[:, theirs, :], 0).wait_recv()
    for y_at, (own, _) in enumerate(first_copies):
        place = first_turned.at[y_at, :, theirs]
        core_copy(place, place, 1 + y_at).wait_recv()
        own.wait()

    def qkv_corners(number, carry):
        qkv.corner_step(Z_SIZE - 1 - number)
        return carry

    lax.fori_loop(0, Z_SIZE, qkv_corners, 0)
    down.near_step(2)
    up.near_step(2)

    def qkv_sides(number, carry):
        for axis in ("y", "x"):
            qkv.side_step(Z_SIZE - 1 - number, axis)
        return carry

    lax.fori_loop(0, Z_SIZE, qkv_sides, 0)
    residual.wait()
    grad_rows = grad_one[...]
    _, hat = normalized(tokens[...].astype(F32))
    first_gain = jnp.sum(grad_rows * hat, axis=0, keepdims=True)
    scaled = grad_rows * gains[0:1, :]
    input_grad[...] += factor * (scaled - hat * jnp.mean(scaled * hat, axis=-1, keepdims=True))
    both = jnp.concatenate([first_gain, second_gain[...], jnp.zeros((6, width), F32)], axis=0)
    for row in range(4):
        gain_sum[0, row] = both[:, row * 288 : (row + 1) * 288]
    gain_copies = []

    def gain_send(source, number, axis):
        copy = pltpu.make_async_remote_copy(
            src_ref=gain_sum.at[source],
            dst_ref=gain_came.at[number],
            send_sem=gain_sends.at[number],
            recv_sem=gain_arrivals.at[number],
            device_id=neighbour(axis),
            device_id_type=pl.DeviceIdType.MESH,
        )
        copy.start()
        gain_copies.append(copy)
        return copy

    plane.plane_end()
    down.near_step(1)
    up.near_step(1)
    for number, axis in enumerate(("core", "y", "x")):
        gain_send(number, number, axis).wait_recv()
        gain_sum[number + 1] = gain_sum[number] + gain_came[number]
        if number < 3:
            qkv.near_step(Z_SIZE - 1 - number)
    ends = [gain_send(3, 3 + number, axis) for number, axis in enumerate(("z", "z_two", "z_back"))]
    down.near_step(0)
    up.near_step(0)
    qkv.near_step(0)
    for copy in ends:
        copy.wait_recv()
    seq_at = y * 2 + core
    gain_out[...] = (gain_sum[3, seq_at] + gain_came[3, seq_at]) + (gain_came[4, seq_at] + gain_came[5, seq_at])
    for group in (down, up, qkv, plane):
        group.drain()
    for pair in range(3):
        for t in range(Z_SIZE):
            pair_copy(pair, t, "x").wait_send()
            if t:
                pair_copy(pair, t, "z_back").wait_send()
    for copy in gain_copies + [piece_copy] + [copy for _, copy in first_copies]:
        copy.wait_send()


def back(weight_inputs, attention_inputs, tokens, gains, second_gain, weights, mixed_grad):
    rows, width = tokens.shape
    dma, arrays = pltpu.SemaphoreType.DMA, []
    for shape in ((144, 1056 - PLANE_LANES), (288, 768), (288, 240)):
        arrays += [pltpu.VMEM((Z_SIZE,) + shape, BF16)] * 5 + [pltpu.VMEM((Z_SIZE - 1,) + shape, BF16)]
    arrays.append(pltpu.VMEM((Z_SIZE, 2, 2, 144, PLANE_LANES), BF16))
    arrays += [pltpu.VMEM((144, PLANE_LANES), BF16)] * 3
    return pl.pallas_call(
        back_kernel,
        out_shape=(
            jax.ShapeDtypeStruct((144, 1056), F32),
            jax.ShapeDtypeStruct((288, 768), F32),
            jax.ShapeDtypeStruct((288, 240), F32),
            jax.ShapeDtypeStruct((rows, width), F32),
            jax.ShapeDtypeStruct((8, 288), F32),
        ),
        in_specs=vmem_specs(17) + any_specs(2),
        out_specs=tuple(vmem_specs(5)),
        scratch_shapes=arrays
        + [
            pltpu.VMEM((2, 8, 256, LANES), BF16),
            pltpu.VMEM((2, 8, LANES, 256), BF16),
            pltpu.VMEM((2, 8, 256, LANES), BF16),
            pltpu.VMEM((8, 256, LANES), F32),
            pltpu.VMEM((8, 256, LANES), F32),
            pltpu.VMEM((3, Z_SIZE, 256, 2 * LANES), BF16),
            pltpu.VMEM((3, Z_SIZE, 256, 2 * LANES), BF16),
            pltpu.VMEM((3, Z_SIZE, 256, 2 * LANES), BF16),
            pltpu.VMEM((3, Z_SIZE - 1, 256, 2 * LANES), BF16),
            pltpu.VMEM((9, rows, LANES), BF16),
            pltpu.VMEM((rows, 1920), F32),
            pltpu.VMEM((8, 2 * rows, 240), BF16),
            pltpu.VMEM((4, 288, rows), BF16),
            pltpu.VMEM((2, 288, 2 * rows), BF16),
            pltpu.VMEM((2, 4, 288, 240), BF16),
            pltpu.VMEM((4, 4, 8, 288), F32),
            pltpu.VMEM((6, 4, 8, 288), F32),
        ]
        + [dma((19,))] * 6
        + [dma((15,))] * 2
        + [dma((21,))] * 2
        + [dma((3,))] * 2
        + [dma((6,))] * 2
        + [dma((3,)), dma((2,))],
        compiler_params=pltpu.CompilerParams(
            vmem_limit_bytes=VMEM_LIMIT, collective_id=3, has_side_effects=True
        ),
        cost_estimate=cost(4 * 18 * rows * 2048 * 128 * 10, 4e8, 18 * rows * 2048),
        name="back",
    )(*weight_inputs, *attention_inputs, tokens, gains, second_gain, weights, mixed_grad)


def lane_tables(first, rows):
    half = HEAD_SIZE // 2
    frequency = ROTARY_BASE ** (-jnp.arange(half, dtype=F32) * 2.0 / HEAD_SIZE)
    angles = (first + jnp.arange(rows, dtype=jnp.int32)).astype(F32)[:, None] * frequency[None, :]
    cosine, sine = jnp.cos(angles), jnp.sin(angles)
    return jnp.tile(cosine, (1, 4)), jnp.tile(jnp.concatenate([-sine, sine], axis=1), (1, 2))


def permuted_device(
    tokens, prefix, gain_one, w_query, w_key, value_weight, w_out, gain_two, w_gate, w_up, w_down, cotangent
):
    _, rows, width = tokens.shape
    tokens, cotangent = tokens[0], cotangent[0]
    ctx_at = lax.axis_index("ctx")
    gains = jnp.zeros((8, gain_one.shape[0]), F32).at[0].set(gain_one.astype(F32)).at[1].set(gain_two.astype(F32))
    cosine, sine = lane_tables(ctx_at * rows, rows)
    limit = jnp.maximum(ctx_at * rows + jnp.arange(rows, dtype=jnp.int32) + 1, prefix[0])[None, :]
    (
        qkv,
        pairs,
        *weight_inputs,
        query,
        attended,
        log_total,
        gains,
        output,
        mixed_grad,
        attended_grad,
        second_gain,
    ) = front(
        jnp.concatenate([w_query, w_key, value_weight], axis=1),
        jnp.concatenate([w_down.T, w_out.T], axis=1),
        jnp.concatenate([w_gate, w_up], axis=1),
        gains,
        tokens,
        cosine,
        sine,
        limit,
        cotangent,
    )
    grad_down_out, grad_up, grad_qkv, input_grad, gain_grads = back(
        weight_inputs,
        (query, attended, attended_grad, log_total, limit, cosine, sine, pairs),
        tokens,
        gains,
        second_gain,
        qkv,
        mixed_grad,
    )
    return (
        output[None],
        input_grad[None],
        gain_grads[0],
        grad_qkv[:, :144],
        grad_qkv[:, 144:192],
        grad_qkv[:, 192:],
        grad_down_out[:, 768:].T,
        gain_grads[1],
        grad_up[:, :384],
        grad_up[:, 384:],
        grad_down_out[:, :768].T,
    )


def permute_plan_fits(mesh, tokens):
    return dict(mesh.shape) == {"seq": 4, "ctx": 8} and tokens.shape == (4, 2048, 1152)


def solution(mesh):
    placed = (
        P("seq", "ctx", None),
        P("seq"),
        P("seq"),
        P("seq", "ctx"),
        P("seq", "ctx"),
        P("seq", "ctx"),
        P("seq", "ctx"),
        P("seq"),
        P("seq", "ctx"),
        P("seq", "ctx"),
        P("seq", "ctx"),
        P("seq", "ctx", None),
    )

    def mapped(device_function):
        return jax.shard_map(
            device_function,
            mesh=mesh,
            in_specs=placed,
            out_specs=(
                P("seq", "ctx", None),
                P("seq", "ctx", None),
                P("seq"),
                P("seq", "ctx"),
                P("seq", "ctx"),
                P("seq", "ctx"),
                P("seq", "ctx"),
                P("seq"),
                P("seq", "ctx"),
                P("seq", "ctx"),
                P("seq", "ctx"),
            ),
            check_vma=False,
        )

    def layer(tokens, *rest):
        return mapped(permuted_device if permute_plan_fits(mesh, tokens) else per_device)(tokens, *rest)

    return layer
```

```python
import functools

import jax
import jax.numpy as jnp
from jax import lax
from jax.experimental import pallas as pl
from jax.experimental.pallas import tpu as pltpu
from jax.sharding import PartitionSpec as P

QUERY_HEADS = 18
KEY_VALUE_HEADS = 6
HEAD_SIZE = 64


EPSILON = 1e-05
ROTARY_BASE = 10000.0

LANES = 128
Z_SIZE = 4
VMEM_LIMIT = 66_000_000
PLANE_LANES = 640
F32 = jnp.float32
BF16 = jnp.bfloat16
NT = (((1,), (1,)), ((), ()))


def rotary_tables(positions, head_width):
    half_width = head_width // 2
    frequency = ROTARY_BASE ** (-jnp.arange(half_width, dtype=jnp.float32) * 2.0 / head_width)
    angles = positions.astype(jnp.float32)[:, None] * frequency[None, :]
    return (jnp.cos(angles)[:, None, :], jnp.sin(angles)[:, None, :])


def apply_rotation(values_in, cosine_table, sine_values):
    half_width = values_in.shape[-1] // 2
    first = values_in[..., :half_width]
    second = values_in[..., half_width:]
    return jnp.concatenate(
        [first * cosine_table - second * sine_values, second * cosine_table + first * sine_values],
        axis=-1,
    )


def inverse_rotation(grads_in, cosine_table, sine_values):
    half_width = grads_in.shape[-1] // 2
    first = grads_in[..., :half_width]
    second = grads_in[..., half_width:]
    return jnp.concatenate(
        [first * cosine_table + second * sine_values, second * cosine_table - first * sine_values],
        axis=-1,
    )


def gather_weights(w_query, w_key, value_weight, w_out, w_gate, w_up, w_down, gain_one, gain_two):
    columns = (
        lax.all_gather(w_query, "ctx", axis=1, tiled=True),
        lax.all_gather(w_key, "ctx", axis=1, tiled=True),
        lax.all_gather(value_weight, "ctx", axis=1, tiled=True),
        lax.all_gather(w_out, "ctx", axis=1, tiled=True),
        lax.all_gather(w_gate, "ctx", axis=1, tiled=True),
        lax.all_gather(w_up, "ctx", axis=1, tiled=True),
        lax.all_gather(w_down, "ctx", axis=1, tiled=True),
    )
    return (
        lax.all_gather(columns[0], "seq", axis=0, tiled=True),
        lax.all_gather(columns[1], "seq", axis=0, tiled=True),
        lax.all_gather(columns[2], "seq", axis=0, tiled=True),
        lax.all_gather(columns[3], "seq", axis=0, tiled=True),
        lax.all_gather(columns[4], "seq", axis=0, tiled=True),
        lax.all_gather(columns[5], "seq", axis=0, tiled=True),
        lax.all_gather(columns[6], "seq", axis=0, tiled=True),
        lax.all_gather(gain_one, "seq", axis=0, tiled=True),
        lax.all_gather(gain_two, "seq", axis=0, tiled=True),
    )


def gather_pairs(key_rotated, value_reduced):
    return (
        lax.all_gather(key_rotated, "ctx", axis=1, tiled=True),
        lax.all_gather(value_reduced, "ctx", axis=1, tiled=True),
    )


def head_major(whole_result, sequence_count):
    sequence_length = whole_result.shape[1]
    return (
        whole_result.reshape(sequence_count, sequence_length, KEY_VALUE_HEADS, HEAD_SIZE)
        .transpose(0, 2, 1, 3)
        .reshape(sequence_count * KEY_VALUE_HEADS, sequence_length, HEAD_SIZE)
    )


def per_device(
    tokens,
    prefix,
    gain_one,
    w_query,
    w_key,
    value_weight,
    w_out,
    gain_two,
    w_gate,
    w_up,
    w_down,
    cotangent,
):
    sequence_count, token_local, model_width = tokens.shape
    sequence_length = token_local * lax.axis_size("ctx")
    number_of_rows = sequence_count * token_local
    queries_per_key_head = QUERY_HEADS // KEY_VALUE_HEADS
    score_scale = HEAD_SIZE ** (-0.5)
    gathered = gather_weights(
        w_query, w_key, value_weight, w_out, w_gate, w_up, w_down, gain_one, gain_two
    )
    full_query, full_key, full_value, full_out, full_gate, full_up, full_down = gathered[:7]
    first_norm = gathered[7].astype(jnp.float32)
    second_norm = gathered[8].astype(jnp.float32)
    input_rows = tokens.reshape(number_of_rows, model_width).astype(jnp.float32)
    first_factor = lax.rsqrt(jnp.mean(input_rows * input_rows, axis=-1, keepdims=True) + EPSILON)
    first_normalized_input = input_rows * first_factor
    normalized_rows = (first_normalized_input * first_norm).astype(jnp.bfloat16)
    query_pre = jnp.dot(normalized_rows, full_query, preferred_element_type=jnp.float32)
    key_prerotation = jnp.dot(normalized_rows, full_key, preferred_element_type=jnp.float32)
    value_reduced = jnp.dot(normalized_rows, full_value, preferred_element_type=jnp.float32).astype(
        jnp.bfloat16
    )
    positions = lax.axis_index("ctx") * token_local + jnp.arange(token_local, dtype=jnp.int32)
    cosine_table, sine_values = rotary_tables(positions, HEAD_SIZE)
    query_rows = apply_rotation(
        query_pre.reshape(sequence_count, token_local, QUERY_HEADS, HEAD_SIZE),
        cosine_table,
        sine_values,
    ).astype(jnp.bfloat16)
    key_rotated = apply_rotation(
        key_prerotation.reshape(sequence_count, token_local, KEY_VALUE_HEADS, HEAD_SIZE),
        cosine_table,
        sine_values,
    ).astype(jnp.bfloat16)
    key_rotated = key_rotated.reshape(sequence_count, token_local, KEY_VALUE_HEADS * HEAD_SIZE)
    value_reduced = value_reduced.reshape(sequence_count, token_local, KEY_VALUE_HEADS * HEAD_SIZE)
    keys_all, values_all = gather_pairs(key_rotated, value_reduced)
    query_block_list = query_rows.reshape(
        sequence_count, token_local, KEY_VALUE_HEADS, queries_per_key_head, HEAD_SIZE
    ).transpose(0, 2, 3, 1, 4)
    query_block_list = query_block_list.reshape(
        sequence_count * KEY_VALUE_HEADS, queries_per_key_head, token_local, HEAD_SIZE
    )
    key_blocks = head_major(keys_all, sequence_count)
    value_blocks = head_major(values_all, sequence_count)
    prefix_repeated = jnp.repeat(prefix, KEY_VALUE_HEADS)
    key_place = jnp.arange(sequence_length, dtype=jnp.int32)

    def visible_for(prefix_len):
        return (key_place[None, :] <= positions[:, None]) | (key_place[None, :] < prefix_len)

    def attend(block_item):
        query_block, key_block, value_block, prefix_len = block_item
        scores = (
            jnp.einsum("gqd,kd->gqk", query_block, key_block, preferred_element_type=jnp.float32)
            * score_scale
        )
        scores = jnp.where(visible_for(prefix_len)[None], scores, -1e30)
        row_max = jnp.max(scores, axis=-1, keepdims=True)
        expo = jnp.exp(scores - row_max)
        total = jnp.sum(expo, axis=-1, keepdims=True)
        probs_low = (expo / total).astype(jnp.bfloat16)
        result = jnp.einsum(
            "gqk,kd->gqd", probs_low, value_block, preferred_element_type=jnp.float32
        )
        return (result.astype(jnp.bfloat16), (row_max + jnp.log(total))[..., 0])

    attention_result_blocks, log_totals = lax.map(
        attend, (query_block_list, key_blocks, value_blocks, prefix_repeated)
    )
    attention_result = attention_result_blocks.reshape(
        sequence_count, KEY_VALUE_HEADS, queries_per_key_head, token_local, HEAD_SIZE
    ).transpose(0, 3, 1, 2, 4)
    attention_result = attention_result.reshape(number_of_rows, QUERY_HEADS * HEAD_SIZE)
    mixed_output = input_rows + jnp.dot(
        attention_result, full_out, preferred_element_type=jnp.float32
    )
    second_factor = lax.rsqrt(
        jnp.mean(mixed_output * mixed_output, axis=-1, keepdims=True) + EPSILON
    )
    second_normalized_input = mixed_output * second_factor
    normalized_second = (second_normalized_input * second_norm).astype(jnp.bfloat16)
    gate = jnp.dot(normalized_second, full_gate, preferred_element_type=jnp.float32)
    up_part = jnp.dot(normalized_second, full_up, preferred_element_type=jnp.float32)
    sigmoid_gate = jax.nn.sigmoid(gate)
    activated = gate * sigmoid_gate
    hidden = (activated * up_part).astype(jnp.bfloat16)
    result_rows = mixed_output + jnp.dot(hidden, full_down, preferred_element_type=jnp.float32)
    output = result_rows.astype(jnp.bfloat16).reshape(sequence_count, token_local, model_width)
    gathered = gather_weights(
        w_query, w_key, value_weight, w_out, w_gate, w_up, w_down, gain_one, gain_two
    )
    full_query, full_key, full_value, full_out, full_gate, full_up, full_down = gathered[:7]
    grad_rows_in = cotangent.reshape(number_of_rows, model_width)
    grad_down = jnp.dot(hidden.T, grad_rows_in, preferred_element_type=jnp.float32)
    dhidden = jnp.dot(grad_rows_in, full_down.T, preferred_element_type=jnp.float32)
    dgate = (dhidden * up_part * sigmoid_gate * (1.0 + gate * (1.0 - sigmoid_gate))).astype(
        jnp.bfloat16
    )
    dup_part = (dhidden * activated).astype(jnp.bfloat16)
    grad_gate = jnp.dot(normalized_second.T, dgate, preferred_element_type=jnp.float32)
    grad_up = jnp.dot(normalized_second.T, dup_part, preferred_element_type=jnp.float32)
    normalized_second_grad = jnp.dot(dgate, full_gate.T, preferred_element_type=jnp.float32)
    normalized_second_grad = normalized_second_grad + jnp.dot(
        dup_part, full_up.T, preferred_element_type=jnp.float32
    )
    second_gain_gradient = jnp.sum(normalized_second_grad * second_normalized_input, axis=0)
    second_scaled = normalized_second_grad * second_norm
    dmixed = grad_rows_in.astype(jnp.float32) + second_factor * (
        second_scaled
        - second_normalized_input
        * jnp.mean(second_scaled * second_normalized_input, axis=-1, keepdims=True)
    )
    dproj = dmixed.astype(jnp.bfloat16)
    grad_out = jnp.dot(attention_result.T, dproj, preferred_element_type=jnp.float32)
    attention_result_grad = jnp.dot(dproj, full_out.T, preferred_element_type=jnp.float32).astype(
        jnp.bfloat16
    )
    attention_result_block_grads = attention_result_grad.reshape(
        sequence_count, token_local, KEY_VALUE_HEADS, queries_per_key_head, HEAD_SIZE
    ).transpose(0, 2, 3, 1, 4)
    attention_result_block_grads = attention_result_block_grads.reshape(
        sequence_count * KEY_VALUE_HEADS, queries_per_key_head, token_local, HEAD_SIZE
    )
    keys_all, values_all = gather_pairs(key_rotated, value_reduced)
    key_blocks = head_major(keys_all, sequence_count)
    value_blocks = head_major(values_all, sequence_count)

    def attend_back(block_item):
        query_block, key_block, value_block, prefix_len, log_total, dout_block = block_item
        scores = (
            jnp.einsum("gqd,kd->gqk", query_block, key_block, preferred_element_type=jnp.float32)
            * score_scale
        )
        visible = visible_for(prefix_len)[None]
        probs = jnp.where(
            visible, jnp.exp(jnp.where(visible, scores, -1e30) - log_total[..., None]), 0.0
        )
        dvalues = jnp.einsum(
            "gqk,gqd->kd",
            probs.astype(jnp.bfloat16),
            dout_block,
            preferred_element_type=jnp.float32,
        )
        dprobs = jnp.einsum(
            "gqd,kd->gqk", dout_block, value_block, preferred_element_type=jnp.float32
        )
        dscores = (probs * (dprobs - jnp.sum(probs * dprobs, axis=-1, keepdims=True))).astype(
            jnp.bfloat16
        )
        dquery = (
            jnp.einsum("gqk,kd->gqd", dscores, key_block, preferred_element_type=jnp.float32)
            * score_scale
        )
        dkeys = (
            jnp.einsum("gqk,gqd->kd", dscores, query_block, preferred_element_type=jnp.float32)
            * score_scale
        )
        return (dquery, dkeys, dvalues)

    query_block_grads, key_block_grads, value_block_grads = lax.map(
        attend_back,
        (
            query_block_list,
            key_blocks,
            value_blocks,
            prefix_repeated,
            log_totals,
            attention_result_block_grads,
        ),
    )
    key_grads_combined = key_block_grads.reshape(
        sequence_count, KEY_VALUE_HEADS, sequence_length, HEAD_SIZE
    ).transpose(0, 2, 1, 3)
    key_grads_combined = key_grads_combined.reshape(
        sequence_count, sequence_length, KEY_VALUE_HEADS * HEAD_SIZE
    )
    value_grads_combined = value_block_grads.reshape(
        sequence_count, KEY_VALUE_HEADS, sequence_length, HEAD_SIZE
    ).transpose(0, 2, 1, 3)
    value_grads_combined = value_grads_combined.reshape(
        sequence_count, sequence_length, KEY_VALUE_HEADS * HEAD_SIZE
    )
    key_grads_local, value_grads_local = (
        lax.psum_scatter(
            key_grads_combined.astype(jnp.bfloat16), "ctx", scatter_dimension=1, tiled=True
        ).astype(jnp.float32),
        lax.psum_scatter(
            value_grads_combined.astype(jnp.bfloat16), "ctx", scatter_dimension=1, tiled=True
        ).astype(jnp.float32),
    )
    key_prerotation_grad = inverse_rotation(
        key_grads_local.reshape(sequence_count, token_local, KEY_VALUE_HEADS, HEAD_SIZE),
        cosine_table,
        sine_values,
    )
    key_prerotation_grad = key_prerotation_grad.astype(jnp.bfloat16).reshape(
        number_of_rows, KEY_VALUE_HEADS * HEAD_SIZE
    )
    value_reduced_grad = value_grads_local.astype(jnp.bfloat16).reshape(
        number_of_rows, KEY_VALUE_HEADS * HEAD_SIZE
    )
    query_row_grads = query_block_grads.reshape(
        sequence_count, KEY_VALUE_HEADS, queries_per_key_head, token_local, HEAD_SIZE
    ).transpose(0, 3, 1, 2, 4)
    query_row_grads = query_row_grads.reshape(sequence_count, token_local, QUERY_HEADS, HEAD_SIZE)
    dquery_pre = (
        inverse_rotation(query_row_grads, cosine_table, sine_values)
        .astype(jnp.bfloat16)
        .reshape(number_of_rows, QUERY_HEADS * HEAD_SIZE)
    )
    grad_query = jnp.dot(normalized_rows.T, dquery_pre, preferred_element_type=jnp.float32)
    grad_key = jnp.dot(normalized_rows.T, key_prerotation_grad, preferred_element_type=jnp.float32)
    grad_value = jnp.dot(normalized_rows.T, value_reduced_grad, preferred_element_type=jnp.float32)
    normalized_grad = jnp.dot(dquery_pre, full_query.T, preferred_element_type=jnp.float32)
    normalized_grad = normalized_grad + jnp.dot(
        key_prerotation_grad, full_key.T, preferred_element_type=jnp.float32
    )
    normalized_grad = normalized_grad + jnp.dot(
        value_reduced_grad, full_value.T, preferred_element_type=jnp.float32
    )
    first_gain_gradient = jnp.sum(normalized_grad * first_normalized_input, axis=0)
    first_scaled = normalized_grad * first_norm
    input_grad = dmixed + first_factor * (
        first_scaled
        - first_normalized_input
        * jnp.mean(first_scaled * first_normalized_input, axis=-1, keepdims=True)
    )
    input_grad = input_grad.reshape(sequence_count, token_local, model_width)
    partial_value = (
        lax.psum_scatter(
            grad_query.astype(jnp.bfloat16), "seq", scatter_dimension=0, tiled=True
        ).astype(jnp.float32),
        lax.psum_scatter(
            grad_key.astype(jnp.bfloat16), "seq", scatter_dimension=0, tiled=True
        ).astype(jnp.float32),
        lax.psum_scatter(
            grad_value.astype(jnp.bfloat16), "seq", scatter_dimension=0, tiled=True
        ).astype(jnp.float32),
        lax.psum_scatter(
            grad_out.astype(jnp.bfloat16), "seq", scatter_dimension=0, tiled=True
        ).astype(jnp.float32),
        lax.psum_scatter(
            grad_gate.astype(jnp.bfloat16), "seq", scatter_dimension=0, tiled=True
        ).astype(jnp.float32),
        lax.psum_scatter(
            grad_up.astype(jnp.bfloat16), "seq", scatter_dimension=0, tiled=True
        ).astype(jnp.float32),
        lax.psum_scatter(
            grad_down.astype(jnp.bfloat16), "seq", scatter_dimension=0, tiled=True
        ).astype(jnp.float32),
        lax.psum_scatter(
            first_gain_gradient.astype(jnp.bfloat16), "seq", scatter_dimension=0, tiled=True
        ).astype(jnp.float32),
        lax.psum_scatter(
            second_gain_gradient.astype(jnp.bfloat16), "seq", scatter_dimension=0, tiled=True
        ).astype(jnp.float32),
    )
    owned = (
        lax.psum_scatter(
            partial_value[0].astype(jnp.bfloat16), "ctx", scatter_dimension=1, tiled=True
        ).astype(jnp.float32),
        lax.psum_scatter(
            partial_value[1].astype(jnp.bfloat16), "ctx", scatter_dimension=1, tiled=True
        ).astype(jnp.float32),
        lax.psum_scatter(
            partial_value[2].astype(jnp.bfloat16), "ctx", scatter_dimension=1, tiled=True
        ).astype(jnp.float32),
        lax.psum_scatter(
            partial_value[3].astype(jnp.bfloat16), "ctx", scatter_dimension=1, tiled=True
        ).astype(jnp.float32),
        lax.psum_scatter(
            partial_value[4].astype(jnp.bfloat16), "ctx", scatter_dimension=1, tiled=True
        ).astype(jnp.float32),
        lax.psum_scatter(
            partial_value[5].astype(jnp.bfloat16), "ctx", scatter_dimension=1, tiled=True
        ).astype(jnp.float32),
        lax.psum_scatter(
            partial_value[6].astype(jnp.bfloat16), "ctx", scatter_dimension=1, tiled=True
        ).astype(jnp.float32),
    )
    gains_owned = lax.psum((partial_value[7], partial_value[8]), "ctx")
    final_grads = owned + gains_owned
    return (
        output,
        input_grad,
        final_grads[7],
        final_grads[0],
        final_grads[1],
        final_grads[2],
        final_grads[3],
        final_grads[8],
        final_grads[4],
        final_grads[5],
        final_grads[6],
    )


def my_place():
    seq_at, ctx_at = lax.axis_index("seq"), lax.axis_index("ctx")
    return ctx_at // 2, lax.rem(ctx_at, 2), seq_at // 2, lax.rem(seq_at, 2)


def flipped(at, flip):
    return 1 - at if flip else at


def lane_ids(rows):
    return lax.broadcasted_iota(jnp.int32, (rows, LANES), 1)


def rotate_halves(tile, cosine, sine):
    lower = lax.rem(lane_ids(tile.shape[0]), HEAD_SIZE) < HEAD_SIZE // 2
    swapped = jnp.where(
        lower, pltpu.roll(tile, LANES - HEAD_SIZE // 2, 1), pltpu.roll(tile, HEAD_SIZE // 2, 1)
    )
    return tile * cosine + swapped * sine


def pair_tiles(natural):
    lower = lane_ids(natural[0].shape[0]) < HEAD_SIZE
    tiles = []
    for pair in range(3):
        for member in range(3):
            one, two = 6 * pair + member, 6 * pair + 3 + member
            left, right = natural[one // 2], natural[two // 2]
            if one % 2:
                left, right = pltpu.roll(left, HEAD_SIZE, 1), pltpu.roll(right, HEAD_SIZE, 1)
            tiles.append(jnp.where(lower, left, right))
    return tiles


def natural_tiles(paired):
    lower = lane_ids(paired[0].shape[0]) < HEAD_SIZE
    tiles = []
    for at in range(9):
        sides = []
        for side in range(2):
            head = 2 * at + side
            tile = paired[head // 6 * 3 + head % 3]
            if (head % 6) // 3 != side:
                tile = pltpu.roll(tile, HEAD_SIZE, 1)
            sides.append(tile)
        tiles.append(jnp.where(lower, sides[0], sides[1]))
    return tiles


def normalized(rows):
    factor = lax.rsqrt(jnp.mean(rows * rows, axis=-1, keepdims=True) + EPSILON)
    return factor, rows * factor


def vmem_specs(count):
    return [pl.BlockSpec(memory_space=pltpu.VMEM)] * count


def any_specs(count):
    return [pl.BlockSpec(memory_space=pl.ANY)] * count


def cost(flops, moved, transcendentals=0):
    return pl.CostEstimate(flops=int(flops), bytes_accessed=int(moved), transcendentals=int(transcendentals))


def params():
    return pltpu.CompilerParams(vmem_limit_bytes=VMEM_LIMIT)


def masked_pair(block, half, other):
    inside = (lane_ids(block.shape[0]) < HEAD_SIZE) == (half == 0)
    return jnp.where(inside, block.astype(F32), other)


def core_rows(core):
    return pl.ds(pl.multiple_of(core * 256, 256), 256)


def turned_blocks(matrix, parts):
    flat = matrix.astype(F32).T.astype(BF16)
    return flat.reshape(parts, flat.shape[0] // parts, flat.shape[1])


class Gathering:
    def __init__(self, own, full, lanes, block, sends, arrivals, corner_over_x=()):
        self.own, self.full, self.block, self.sends, self.arrivals = own, full, block, sends, arrivals
        self.corner_over_x, self.lanes = corner_over_x, lanes
        self.started = []

    def place(self, t, dx, dy, dcore=0):
        z, x, y, core = my_place()
        ctx_block = lax.rem(z - t + Z_SIZE, Z_SIZE) * 2 + flipped(x, dx)
        first, second = self.block(ctx_block, flipped(y, dy) * 2 + flipped(core, dcore))
        return self.full.at[first, second, :, self.lanes]

    def copy(self, source, target, number, axis):
        return pltpu.make_async_remote_copy(
            src_ref=source,
            dst_ref=target,
            send_sem=self.sends.at[number],
            recv_sem=self.arrivals.at[number],
            device_id=neighbour(axis),
            device_id_type=pl.DeviceIdType.MESH,
        )

    def send(self, piece, number, axis):
        place = self.place(*piece)
        source = self.own.at[:, self.lanes] if piece == (0, 0, 0) else place
        self.copy(source, place, number, axis).start()
        self.started.append((piece, number))

    def wait(self, piece, number, dcore=0):
        place = self.place(*piece, dcore)
        self.copy(place, place, number, "core").wait_recv()

    def to_core(self, piece):
        t, dx, dy = piece
        self.send(piece, 15 + 4 * t + 2 * dx + dy, "core")

    def over_z(self, t):
        if t < Z_SIZE - 1:
            self.send((t, 0, 0), t, "z")

    def over_plane(self, t):
        self.send((t, 0, 0), 3 + t, "x")
        self.send((t, 0, 0), 7 + t, "y")

    def begin(self):
        self.over_z(0)
        self.over_plane(0)
        self.to_core((0, 0, 0))

    def pass_on(self, t):
        self.wait((t, 0, 0), t - 1)
        self.over_z(t)
        self.over_plane(t)
        self.to_core((t, 0, 0))

    def sides(self, t):
        self.wait((t, 1, 0), 3 + t)
        if t not in self.corner_over_x:
            self.send((t, 1, 0), 11 + t, "y")
        self.to_core((t, 1, 0))
        self.wait((t, 0, 1), 7 + t)
        if t in self.corner_over_x:
            self.send((t, 0, 1), 11 + t, "x")
        self.to_core((t, 0, 1))

    def corner(self, t):
        self.wait((t, 1, 1), 11 + t)
        self.to_core((t, 1, 1))

    def finish(self, t):
        for dx in range(2):
            for dy in range(2):
                self.wait((t, dx, dy), 15 + 4 * t + 2 * dx + dy, 1)

    def drain(self):
        for piece, number in self.started:
            place = self.place(*piece)
            self.copy(place, place, number, "core").wait_send()


class PlaneGathering(Gathering):
    def begin(self):
        self.send((0, 0, 0), 0, "x")
        self.send((0, 0, 0), 1, "y")
        self.to_core((0, 0, 0))

    def plane_sides(self):
        self.wait((0, 1, 0), 0)
        self.send((0, 1, 0), 2, "y")
        self.to_core((0, 1, 0))
        self.wait((0, 0, 1), 1)
        self.to_core((0, 0, 1))

    def plane_corner(self):
        self.wait((0, 1, 1), 2)
        self.to_core((0, 1, 1))

    def ring(self, t):
        for dx in range(2):
            for dy in range(2):
                number = 3 + 4 * t + 2 * dx + dy
                if t:
                    self.wait((t, dx, dy), number - 4)
                if t < Z_SIZE - 1:
                    self.send((t, dx, dy), number, "z")
                if t:
                    self.to_core((t, dx, dy))


def neighbour(axis):
    z, x, y, core = my_place()
    if axis == "z":
        z = lax.rem(z + 1, Z_SIZE)
    elif axis == "z_back":
        z = lax.rem(z + Z_SIZE - 1, Z_SIZE)
    elif axis == "z_two":
        z = lax.rem(z + 2, Z_SIZE)
    elif axis == "x":
        x = 1 - x
    elif axis == "y":
        y = 1 - y
    elif axis == "core":
        core = 1 - core
    elif axis == "y_core":
        y, core = 1 - y, 1 - core
    return (y * 2 + core, z * 2 + x)


def meet(axes):
    barrier = pltpu.get_barrier_semaphore()
    for axis in axes:
        pl.semaphore_signal(barrier, inc=1, device_id=neighbour(axis), device_id_type=pl.DeviceIdType.MESH)
    pl.semaphore_wait(barrier, len(axes))


def front_kernel(
    prefix,
    frequency,
    query_weight,
    key_weight,
    value_weight,
    out_weight,
    gate_weight,
    up_weight,
    down_weight,
    both_gains,
    tokens,
    cotangent,
    qkv_out,
    pairs_out,
    rows_turned,
    both_grads,
    hidden_both,
    attended_both,
    cot_turned,
    proj_turned,
    query_out,
    attended,
    log_total,
    gain_out,
    output,
    mixed_grad,
    attended_grad,
    gain_grad,
    cosine,
    sine,
    limit,
    qkv_own,
    down_own,
    up_own,
    gains_own,
    qkv,
    down,
    up,
    pairs,
    gates,
    ups,
    wide,
    keys,
    values,
    gains,
    rows_two,
    rows_stage,
    hidden,
    attended_rows,
    grads,
    cot_stage,
    proj_stage,
    qkv_sends,
    qkv_arrivals,
    down_sends,
    down_arrivals,
    plane_sends,
    plane_arrivals,
    up_sends,
    up_arrivals,
    pair_sends,
    pair_arrivals,
    gain_sends,
    gain_arrivals,
    own_sems,
    core_sends,
    core_arrivals,
    core_own_sems,
):
    z, x, y, core = my_place()
    seq_at, ctx_at = y * 2 + core, z * 2 + x
    by_ctx, by_seq = (lambda ctx, seq: (ctx, seq)), (lambda ctx, seq: (seq, ctx))
    first = Gathering(qkv_own, qkv, slice(0, 240), by_ctx, qkv_sends, qkv_arrivals, (1, 3))
    plane = PlaneGathering(down_own, down, slice(0, PLANE_LANES), by_seq, plane_sends, plane_arrivals)
    rest = (
        Gathering(down_own, down, slice(PLANE_LANES, 1056), by_seq, down_sends, down_arrivals, (3,)),
        Gathering(up_own, up, slice(0, 768), by_ctx, up_sends, up_arrivals, (3,)),
    )
    mine, theirs, width = core_rows(core), core_rows(1 - core), tokens.shape[1]
    turned = jnp.concatenate([query_weight[...], key_weight[...], value_weight[...]], axis=0)
    qkv_own[...] = turned.astype(F32).T.astype(BF16)
    gains_own[...] = jnp.concatenate([both_gains[...], jnp.zeros((6, 288), F32)], axis=0)
    down_own[:, :768] = down_weight[...]
    down_own[:, 768:] = out_weight[...]
    up_own[:, :384] = gate_weight[...]
    up_own[:, 384:] = up_weight[...]
    meet(("z", "z_back", "x", "y", "core", "y_core"))
    first.begin()
    gain_copies = []
    for number, axis in enumerate(("core", "y", "y_core")):
        copy = pltpu.make_async_remote_copy(
            src_ref=gains_own,
            dst_ref=gains.at[seq_at],
            send_sem=gain_sends.at[number],
            recv_sem=gain_arrivals.at[number],
            device_id=neighbour(axis),
            device_id_type=pl.DeviceIdType.MESH,
        )
        copy.start()
        gain_copies.append(copy)
    own_copies = [
        pltpu.make_async_copy(source, target, own_sems.at[number])
        for number, (source, target) in enumerate(
            (
                (qkv_own, first.place(0, 0, 0)),
                (down_own, down.at[seq_at, ctx_at]),
                (up_own, up.at[ctx_at, seq_at]),
                (gains_own, gains.at[seq_at]),
            )
        )
    ]
    for copy in own_copies:
        copy.start()
    places = ctx_at * 256 + lax.broadcasted_iota(jnp.int32, (256, LANES), 0)
    angles = places.astype(F32) * frequency[...]
    lower = lax.rem(lane_ids(256), HEAD_SIZE) < HEAD_SIZE // 2
    sines = jnp.sin(angles)
    cosine[...] = jnp.cos(angles)
    sine[...] = jnp.where(lower, -sines, sines)
    limit[...] = jnp.maximum(ctx_at * 256 + 1 + lax.broadcasted_iota(jnp.int32, (1, 256), 1), prefix[0])
    for t in range(1, Z_SIZE):
        first.pass_on(t)
        if t == 1:
            plane.begin()
        if t == Z_SIZE - 2:
            for group in rest:
                group.over_z(0)
        first.sides(t - 1)
    plane.plane_sides()
    first.sides(Z_SIZE - 1)
    for group in rest:
        group.over_plane(0)
        group.to_core((0, 0, 0))
    plane.plane_corner()
    plane.ring(0)
    for number, flips in enumerate(((0, 1), (1, 0), (1, 1))):
        place = gains.at[flipped(y, flips[0]) * 2 + flipped(core, flips[1])]
        pltpu.make_async_remote_copy(
            src_ref=place,
            dst_ref=place,
            send_sem=gain_sends.at[number],
            recv_sem=gain_arrivals.at[number],
            device_id=neighbour("core"),
            device_id_type=pl.DeviceIdType.MESH,
        ).wait_recv()
    for copy in own_copies:
        copy.wait()
    for row in range(4):
        gain_out[:, row * 288 : (row + 1) * 288] = gains[row]
    _, hat = normalized(tokens[...].astype(F32))
    rows = (hat * gain_out[0:1, :]).astype(BF16)
    for t in range(Z_SIZE):
        first.corner(t)
    for group in rest:
        group.pass_on(1)
    for t in range(Z_SIZE):
        first.finish(t)

    def multiply(ctx_block, carry):
        matrix = qkv[ctx_block].reshape(tokens.shape[1], 240)
        gates[ctx_block, :, :240] = jnp.dot(rows, matrix, preferred_element_type=F32)
        return carry

    lax.fori_loop(0, 8, multiply, 0)
    save_qkv = pltpu.make_async_copy(qkv, qkv_out, own_sems.at[4])
    save_qkv.start()
    q_part, kv_part = 144, 48
    for at in range(8):
        wide[:, at * q_part : (at + 1) * q_part] = gates[at, :, :q_part]
        wide[:, 1152 + at * kv_part : 1152 + (at + 1) * kv_part] = gates[at, :, q_part : q_part + kv_part]
        wide[:, 1536 + at * kv_part : 1536 + (at + 1) * kv_part] = gates[at, :, q_part + kv_part : 240]
    cos_tile, sin_tile = cosine[...], sine[...]
    for pair in range(3):
        key_tile = wide[:, 1152 + pair * LANES : 1152 + (pair + 1) * LANES]
        pairs[ctx_at, :, 2 * pair * LANES : (2 * pair + 1) * LANES] = rotate_halves(
            key_tile, cos_tile, sin_tile
        ).astype(BF16)
        pairs[ctx_at, :, (2 * pair + 1) * LANES : (2 * pair + 2) * LANES] = wide[
            :, 1536 + pair * LANES : 1536 + (pair + 1) * LANES
        ].astype(BF16)
    natural = [
        rotate_halves(wide[:, at * LANES : (at + 1) * LANES], cos_tile, sin_tile) * HEAD_SIZE**-0.5
        for at in range(9)
    ]
    for at, tile in enumerate(pair_tiles(natural)):
        query_out[at] = tile.astype(BF16)

    pair_copies = []

    def pair_place(t, dx):
        return pairs.at[lax.rem(z - t + Z_SIZE, Z_SIZE) * 2 + flipped(x, dx)]

    def pair_copy(place, number, axis):
        return pltpu.make_async_remote_copy(
            src_ref=place,
            dst_ref=place,
            send_sem=pair_sends.at[number],
            recv_sem=pair_arrivals.at[number],
            device_id=neighbour(axis),
            device_id_type=pl.DeviceIdType.MESH,
        )

    def pair_pass(t):
        if t:
            pair_copy(pair_place(t, 0), t - 1, "z").wait_recv()
        for number, axis in ((t, "z"), (3 + t, "x")):
            if axis == "x" or t < Z_SIZE - 1:
                copy = pair_copy(pair_place(t, 0), number, axis)
                copy.start()
                pair_copies.append(copy)

    def in_rest(step):
        for group in rest:
            step(group)

    pair_pass(0)
    in_rest(lambda group: group.pass_on(2))
    pair_pass(1)
    in_rest(lambda group: group.sides(0))
    pair_pass(2)
    plane.ring(1)
    in_rest(lambda group: group.sides(1))
    pair_pass(3)
    cot_stage[...] = turned_blocks(cotangent[...], 8)
    in_rest(lambda group: group.pass_on(3))
    in_rest(lambda group: group.sides(2))
    for t in range(Z_SIZE):
        pair_copy(pair_place(t, 1), 3 + t, "x").wait_recv()
    save_pairs = pltpu.make_async_copy(pairs, pairs_out, own_sems.at[5])
    save_pairs.start()

    key_ids = lax.broadcasted_iota(jnp.int32, (256, tokens.shape[0]), 0)

    def attend_pair(pair):
        key_lanes = pl.ds(pl.multiple_of(pair * 256, 256), LANES)
        value_lanes = pl.ds(pl.multiple_of(pair * 256 + LANES, LANES), LANES)
        for at in range(8):
            for half in range(2):
                keys[half, at] = masked_pair(pairs[at, :, key_lanes], half, 0.0).astype(BF16)
                values[half, at] = masked_pair(pairs[at, :, value_lanes], half, 1.0).T.astype(BF16)

        def attend_member(member, carry):
            tile = query_out[3 * pair + member]
            parts = []
            for half in range(2):
                top = None
                for at in range(8):
                    part = lax.dot_general(keys[half, at], tile, NT, preferred_element_type=F32)
                    part = jnp.where(key_ids < limit[...] - at * 256, part, -1e30)
                    ups[at, :, :256] = part
                    block_top = jnp.max(part, axis=0, keepdims=True)
                    top = block_top if top is None else jnp.maximum(top, block_top)
                total = jnp.zeros((LANES, tile.shape[0]), F32)
                for at in range(8):
                    weight = jnp.exp(ups[at, :, :256] - top).astype(BF16)
                    total = total + jnp.dot(values[half, at], weight, preferred_element_type=F32)
                norm = total[HEAD_SIZE : HEAD_SIZE + 1] if half == 0 else total[:1]
                log_total[3 * pair + member, half : half + 1, :] = top + jnp.log(norm)
                own = total[:HEAD_SIZE] if half == 0 else total[HEAD_SIZE:]
                parts.append(own / norm)
            attended[3 * pair + member] = jnp.concatenate(parts, axis=0).T.astype(BF16)
            return carry

        lax.fori_loop(0, 3, attend_member, 0)

    started, own_copies = [], []

    def core_copy(source, target, number):
        return pltpu.make_async_remote_copy(
            src_ref=source,
            dst_ref=target,
            send_sem=core_sends.at[number],
            recv_sem=core_arrivals.at[number],
            device_id=neighbour("core"),
            device_id_type=pl.DeviceIdType.MESH,
        )

    def keep(source, target, number):
        copy = pltpu.make_async_copy(source, target, core_own_sems.at[number])
        copy.start()
        own_copies.append(copy)

    def share(source, target, number):
        copy = core_copy(source, target, number)
        copy.start()
        started.append(copy)

    def deal(stage, target_of, number):
        for y_at in range(2):
            keep(stage.at[y_at * 2 + core], target_of(y_at), number + y_at)
            share(stage.at[y_at * 2 + 1 - core], target_of(y_at), number + y_at)

    def attend_and_pass(pair, carry):
        attend_pair(pair)

        @pl.when(pair == 0)
        def _():
            plane.ring(2)
            in_rest(lambda group: group.sides(3))

        @pl.when(pair == 1)
        def _():
            in_rest(lambda group: group.corner(0))
            in_rest(lambda group: group.corner(1))

        return carry

    lax.fori_loop(0, 3, attend_and_pass, 0)
    keep(cot_stage, cot_turned.at[:, :, mine], 1)
    share(cot_stage, cot_turned.at[:, :, mine], 1)
    in_rest(lambda group: group.corner(2))
    for at, tile in enumerate(natural_tiles([attended[at].astype(F32) for at in range(9)])):
        wide[:, at * LANES : (at + 1) * LANES] = tile
    for row in range(4):
        attended_rows[row] = wide[:, row * 288 : (row + 1) * 288].astype(BF16)
    rest[0].corner(3)
    for t in range(Z_SIZE):
        rest[0].finish(t)

    def out_block(row):
        return down[row, :, :, 768:].reshape(width, 288)

    def down_block(row):
        return down[row, :, :, :768].reshape(width, 768)

    def gate_block(block):
        return up[block, :, :, :384].reshape(width, 384)

    def up_block(block):
        return up[block, :, :, 384:].reshape(width, 384)

    mixed_grad[...] = tokens[...].astype(F32)
    for row in range(4):
        mixed_grad[...] += lax.dot_general(attended_rows[row], out_block(row), NT, preferred_element_type=F32)
    rest[1].corner(3)
    plane.ring(3)
    deal(attended_rows, lambda y_at: attended_both.at[y_at, mine], 2)
    factor, hat = normalized(mixed_grad[...])
    gain_row = gain_out[1:2, :]
    rows_two[...] = (hat * gain_row).astype(BF16)
    wide[:, :1152] = hat
    for t in range(Z_SIZE):
        rest[1].finish(t)

        def gate_and_up(dx, carry, t=t):
            block = lax.rem(z - t + Z_SIZE, Z_SIZE) * 2 + lax.rem(x + dx, 2)
            gates[block] = jnp.dot(rows_two[...], gate_block(block), preferred_element_type=F32)
            ups[block] = jnp.dot(rows_two[...], up_block(block), preferred_element_type=F32)
            return carry

        lax.fori_loop(0, 2, gate_and_up, 0)
    rows_stage[...] = turned_blocks(rows_two[...], 4)
    for t in range(Z_SIZE):
        plane.finish(t)
    deal(rows_stage, lambda y_at: rows_turned.at[y_at, :, mine], 4)

    def feed_forward(row, carry):
        back = jnp.dot(cotangent[...], down_block(row), preferred_element_type=F32)
        for side in range(2):
            block = 2 * row + side
            gate, up_part = gates[block], ups[block]
            sigmoid = 1.0 / (1.0 + jnp.exp(-gate))
            active = gate * sigmoid
            hidden[row, :, side * 384 : (side + 1) * 384] = (active * up_part).astype(BF16)
            part = back[:, side * 384 : (side + 1) * 384]
            grads[block, :, :384] = (part * up_part * sigmoid * (1.0 + gate * (1.0 - sigmoid))).astype(BF16)
            grads[block, :, 384:] = (part * active).astype(BF16)
        mixed_grad[...] += lax.dot_general(hidden[row], down_block(row), NT, preferred_element_type=F32)
        return carry

    lax.fori_loop(0, 4, feed_forward, 0)
    output[...] = mixed_grad[...].astype(BF16)
    keep(grads, both_grads.at[:, mine, :], 0)
    share(grads, both_grads.at[:, mine, :], 0)
    deal(hidden, lambda y_at: hidden_both.at[y_at, mine], 6)
    mixed_grad[...] = jnp.zeros_like(mixed_grad)

    def rows_back(block, carry):
        part = lax.dot_general(grads[block, :, :384], gate_block(block), NT, preferred_element_type=F32)
        part = part + lax.dot_general(grads[block, :, 384:], up_block(block), NT, preferred_element_type=F32)
        mixed_grad[...] += part
        return carry

    lax.fori_loop(0, 8, rows_back, 0)
    grad_two, hat = mixed_grad[...], wide[:, :1152]
    gain_grad[...] = jnp.sum(grad_two * hat, axis=0, keepdims=True)
    scaled = grad_two * gain_row
    total = cotangent[...].astype(F32) + factor * (
        scaled - hat * jnp.mean(scaled * hat, axis=-1, keepdims=True)
    )
    mixed_grad[...] = total
    rows_two[...] = total.astype(BF16)
    proj_stage[...] = turned_blocks(rows_two[...], 8)
    for row in range(4):
        wide[:, row * 288 : (row + 1) * 288] = jnp.dot(
            rows_two[...], out_block(row), preferred_element_type=F32
        )
    keep(proj_stage, proj_turned.at[:, :, mine], 8)
    share(proj_stage, proj_turned.at[:, :, mine], 8)
    tiles = pair_tiles([wide[:, at * LANES : (at + 1) * LANES] for at in range(9)])
    for at, tile in enumerate(tiles):
        attended_grad[at] = tile.astype(BF16)
    for group in rest + (first, plane):
        group.drain()
    for copy in pair_copies + gain_copies + started:
        copy.wait_send()
    for copy in own_copies + [save_qkv, save_pairs]:
        copy.wait()
    places = [both_grads.at[:, theirs, :], cot_turned.at[:, :, theirs]]
    places += [attended_both.at[y_at, theirs] for y_at in range(2)]
    places += [rows_turned.at[y_at, :, theirs] for y_at in range(2)]
    places += [hidden_both.at[y_at, theirs] for y_at in range(2)]
    places.append(proj_turned.at[:, :, theirs])
    for number, place in enumerate(places):
        core_copy(place, place, number).wait_recv()


def front(prefix, frequency, weights, gains, tokens, cotangent):
    rows, width = tokens.shape
    dma = pltpu.SemaphoreType.DMA
    shape = jax.ShapeDtypeStruct
    qkv_own, down_own, up_own = (288, 240), (144, 1056), (288, 768)
    return pl.pallas_call(
        front_kernel,
        out_shape=(
            shape((8, 4) + qkv_own, BF16),
            shape((8, rows, 768), BF16),
            shape((2, 288, 2 * rows), BF16),
            shape((8, 2 * rows, 768), BF16),
            shape((2, 2 * rows, 768), BF16),
            shape((2, 2 * rows, 288), BF16),
            shape((8, 144, 2 * rows), BF16),
            shape((8, 144, 2 * rows), BF16),
            shape((9, rows, LANES), BF16),
            shape((9, rows, LANES), BF16),
            shape((9, 2, rows), F32),
            shape((8, width), F32),
            shape((rows, width), BF16),
            shape((rows, width), F32),
            shape((9, rows, LANES), BF16),
            shape((1, width), F32),
            shape((rows, LANES), F32),
            shape((rows, LANES), F32),
            shape((1, rows), jnp.int32),
        ),
        in_specs=[pl.BlockSpec(memory_space=pltpu.SMEM)] + vmem_specs(11),
        out_specs=tuple(any_specs(8) + vmem_specs(11)),
        scratch_shapes=[
            pltpu.VMEM(qkv_own, BF16),
            pltpu.VMEM(down_own, BF16),
            pltpu.VMEM(up_own, BF16),
            pltpu.VMEM((8, 288), F32),
            pltpu.VMEM((8, 4) + qkv_own, BF16),
            pltpu.VMEM((4, 8) + down_own, BF16),
            pltpu.VMEM((8, 4) + up_own, BF16),
            pltpu.VMEM((8, rows, 768), BF16),
            pltpu.VMEM((8, rows, 384), F32),
            pltpu.VMEM((8, rows, 384), F32),
            pltpu.VMEM((rows, 1920), F32),
            pltpu.VMEM((2, 8, 256, LANES), BF16),
            pltpu.VMEM((2, 8, LANES, 256), BF16),
            pltpu.VMEM((4, 8, 288), F32),
            pltpu.VMEM((rows, width), BF16),
            pltpu.VMEM((4, 288, rows), BF16),
            pltpu.VMEM((4, rows, 768), BF16),
            pltpu.VMEM((4, rows, 288), BF16),
            pltpu.VMEM((8, rows, 768), BF16),
            pltpu.VMEM((8, 144, rows), BF16),
            pltpu.VMEM((8, 144, rows), BF16),
        ]
        + [dma((31,))] * 8
        + [dma((7,))] * 2
        + [dma((3,))] * 2
        + [dma((6,))]
        + [dma((9,))] * 3,
        compiler_params=pltpu.CompilerParams(
            vmem_limit_bytes=VMEM_LIMIT, collective_id=1, has_side_effects=True
        ),
        cost_estimate=cost(4 * 18 * rows * 2048 * 128 * 4, 4e8, 18 * rows * 2048),
        name="front",
    )(prefix, frequency, *weights, gains, tokens, cotangent)


class Scattering:
    def __init__(self, buffers, sends, arrivals, out, piece, corners):
        self.corner, self.side_x, self.side_y, self.near_x, self.near_y, self.ring = buffers
        self.sends, self.arrivals, self.out, self.piece, self.corners = sends, arrivals, out, piece, corners

    def copy(self, source, target, number, axis):
        return pltpu.make_async_remote_copy(
            src_ref=source,
            dst_ref=target,
            send_sem=self.sends.at[number],
            recv_sem=self.arrivals.at[number],
            device_id=neighbour(axis),
            device_id_type=pl.DeviceIdType.MESH,
        )

    def corner_copies(self, t, axes=("x", "y")):
        for number, (axis, lanes) in enumerate(self.corners):
            if axis in axes:
                target = self.side_x if axis == "y" else self.side_y
                yield self.copy(self.corner.at[t, :, lanes], target.at[t, :, lanes], 4 * number + t, axis)

    def side_copy(self, t, axis):
        source, target, first = (self.side_x, self.near_x, 8) if axis == "x" else (self.side_y, self.near_y, 12)
        return self.copy(source.at[t], target.at[t], first + t, axis)

    def ring_copy(self, t):
        return self.copy(self.near_x.at[t], self.ring.at[t - 1], 15 + t, "z_back")

    def corner_step(self, t):
        self.piece(t, 1, 1, self.corner.at[t], lambda lanes: [])
        for copy in self.corner_copies(t):
            copy.start()

    def side_step(self, t, axis):
        came = "y" if axis == "x" else "x"
        for copy in self.corner_copies(t, (came,)):
            copy.wait_recv()
        side = (self.side_x if axis == "x" else self.side_y).at[t]
        ranges = [lanes for at, lanes in self.corners if at == came]

        def addend(lanes):
            return [side[:, lanes]] if any(at.start <= lanes.start and lanes.stop <= at.stop for at in ranges) else []

        self.piece(t, int(axis == "x"), int(axis == "y"), side, addend)
        self.side_copy(t, axis).start()

    def near_step(self, t):
        self.side_copy(t, "x").wait_recv()
        self.side_copy(t, "y").wait_recv()
        if t < Z_SIZE - 1:
            self.ring_copy(t + 1).wait_recv()

        def addend(lanes):
            parts = [self.near_x[t, :, lanes], self.near_y[t, :, lanes]]
            return parts + ([self.ring[t, :, lanes]] if t < Z_SIZE - 1 else [])

        self.piece(t, 0, 0, self.near_x.at[t] if t else self.out, addend)
        if t:
            self.ring_copy(t).start()

    def drain(self):
        for t in range(Z_SIZE):
            for copy in self.corner_copies(t):
                copy.wait_send()
            self.side_copy(t, "x").wait_send()
            self.side_copy(t, "y").wait_send()
            if t:
                self.ring_copy(t).wait_send()


class PlaneScattering:
    def __init__(self, buffers, sends, arrivals, out, piece):
        self.sums, self.corner, self.near_x, self.near_y = buffers
        self.sends, self.arrivals, self.out, self.piece = sends, arrivals, out, piece

    def copy(self, source, target, number, axis):
        return pltpu.make_async_remote_copy(
            src_ref=source,
            dst_ref=target,
            send_sem=self.sends.at[number],
            recv_sem=self.arrivals.at[number],
            device_id=neighbour(axis),
            device_id_type=pl.DeviceIdType.MESH,
        )

    def ring_copy(self, t, dx, dy):
        return self.copy(
            self.sums.at[t, dx, dy], self.sums.at[t - 1, dx, dy], 4 * (t - 1) + 2 * dx + dy, "z_back"
        )

    def plane_copies(self):
        return (
            self.copy(self.sums.at[0, 1, 1], self.corner, 12, "y"),
            self.copy(self.sums.at[0, 1, 0], self.near_x, 13, "x"),
            self.copy(self.sums.at[0, 0, 1], self.near_y, 14, "y"),
        )

    def ring_step(self, t, first=False):
        def one(number, carry):
            dx, dy = number // 2, lax.rem(number, 2)
            target = self.sums.at[t, dx, dy]
            if not first:
                self.ring_copy(t + 1, dx, dy).wait_recv()
            self.piece(t, dx, dy, target, lambda lanes: [] if first else [target[:, lanes]])

            @pl.when(t > 0)
            def _():
                self.ring_copy(t, dx, dy).start()

            return carry

        lax.fori_loop(0, 4, one, 0)

    def plane_start(self):
        corner, _, side_y = self.plane_copies()
        corner.start()
        side_y.start()

    def plane_side(self):
        corner, side_x, _ = self.plane_copies()
        corner.wait_recv()
        side = self.sums.at[0, 1, 0]
        side[...] = (side[...].astype(F32) + self.corner[...].astype(F32)).astype(BF16)
        side_x.start()

    def plane_end(self):
        _, side_x, side_y = self.plane_copies()
        side_x.wait_recv()
        side_y.wait_recv()
        total = self.sums[0, 0, 0].astype(F32) + self.near_x[...].astype(F32)
        self.out[...] = total + self.near_y[...].astype(F32)

    def drain(self):
        for t in range(1, Z_SIZE):
            for dx in range(2):
                for dy in range(2):
                    self.ring_copy(t, dx, dy).wait_send()
        for copy in self.plane_copies():
            copy.wait_send()


def back_kernel(
    rows_turned,
    both_grads,
    hidden,
    attended_rows,
    cot_turned,
    proj_turned,
    query,
    attended,
    grad,
    log_total,
    limit,
    cosine,
    sine,
    pairs,
    tokens,
    gains,
    second_gain,
    weights,
    mixed_grad,
    down_out,
    up_out,
    qkv_out,
    input_grad,
    gain_out,
    *refs,
):
    down_buffers, up_buffers, qkv_buffers, plane_buffers = refs[:6], refs[6:12], refs[12:18], refs[18:22]
    (
        keys,
        keys_turned,
        values,
        query_halves,
        grad_halves,
        turned_sum,
        shifts,
        pair_parts,
        pair_near,
        pair_ring,
        query_grad,
        wide,
        pieces,
        first_stage,
        first_turned,
        weight_slots,
        gain_sum,
        gain_came,
    ) = refs[22:40]
    (
        down_sends,
        down_arrivals,
        up_sends,
        up_arrivals,
        qkv_sends,
        qkv_arrivals,
        plane_sends,
        plane_arrivals,
        pair_sends,
        pair_arrivals,
        core_sends,
        core_arrivals,
        gain_sends,
        gain_arrivals,
        own_sems,
        weight_sems,
    ) = refs[40:]
    z, x, y, core = my_place()
    mine, theirs = core_rows(core), core_rows(1 - core)
    rows, width = tokens.shape

    def flip_if(at, flip):
        return flipped(at, flip) if isinstance(flip, int) else lax.rem(at + flip, 2)

    def ctx_of(t, dx):
        return lax.rem(z - t + Z_SIZE, Z_SIZE) * 2 + flip_if(x, dx)

    def put(target, lanes, value, addend):
        for part in addend(lanes):
            value = value + part.astype(F32)
        target[:, lanes] = value.astype(target.dtype)

    def plane_piece(t, dx, dy, target, addend):
        block, row = ctx_of(t, dx), flip_if(y, dy)
        for lanes in (slice(0, 256), slice(256, PLANE_LANES)):
            value = jnp.dot(cot_turned[block], hidden[row, :, lanes], preferred_element_type=F32)
            put(target, lanes, value, addend)

    def down_piece(t, dx, dy, target, addend):
        block, row = ctx_of(t, dx), flipped(y, dy)
        split = 768 - PLANE_LANES
        value = jnp.dot(cot_turned[block], hidden[row, :, PLANE_LANES:], preferred_element_type=F32)
        put(target, slice(0, split), value, addend)
        value = jnp.dot(proj_turned[block], attended_rows[row], preferred_element_type=F32)
        put(target, slice(split, split + 288), value, addend)

    def up_piece(t, dx, dy, target, addend):
        block, row = ctx_of(t, dx), flipped(y, dy)
        for lanes in (slice(0, 384), slice(384, 768)):
            value = jnp.dot(rows_turned[row], both_grads[block, :, lanes], preferred_element_type=F32)
            put(target, lanes, value, addend)

    def qkv_piece(t, dx, dy, target, addend):
        block, row = ctx_of(t, dx), flipped(y, dy)
        value = jnp.dot(first_turned[row], pieces[block], preferred_element_type=F32)
        put(target, slice(0, 240), value, addend)

    plane = PlaneScattering(
        plane_buffers, plane_sends, plane_arrivals, down_out.at[:, :PLANE_LANES], plane_piece
    )
    down = Scattering(
        down_buffers,
        down_sends,
        down_arrivals,
        down_out.at[:, PLANE_LANES:],
        down_piece,
        (("y", slice(0, 1056 - PLANE_LANES)),),
    )
    up = Scattering(
        up_buffers, up_sends, up_arrivals, up_out, up_piece, (("y", slice(0, 384)), ("x", slice(384, 768)))
    )
    qkv = Scattering(qkv_buffers, qkv_sends, qkv_arrivals, qkv_out, qkv_piece, (("y", slice(0, 240)),))

    meet(("z", "z_back", "x", "y", "core", "z_two"))
    residual = pltpu.make_async_copy(mixed_grad, input_grad, own_sems.at[2])
    residual.start()

    plane.ring_step(Z_SIZE - 1, True)

    def corners(number, carry):
        t = Z_SIZE - 1 - number
        down.corner_step(t)
        up.corner_step(t)
        return carry

    lax.fori_loop(0, Z_SIZE, corners, 0)

    factor, hat = normalized(tokens[...].astype(F32))
    first_stage[...] = turned_blocks((hat * gains[0:1, :]).astype(BF16), 4)

    def core_copy(source, target, number):
        return pltpu.make_async_remote_copy(
            src_ref=source,
            dst_ref=target,
            send_sem=core_sends.at[number],
            recv_sem=core_arrivals.at[number],
            device_id=neighbour("core"),
            device_id_type=pl.DeviceIdType.MESH,
        )

    def pair_copy(pair, t, axis):
        if axis == "x":
            source, target, number = pair_parts.at[pair, 1, t], pair_near.at[pair, t], 4 * pair + t
        else:
            source, target, number = pair_parts.at[pair, 0, t], pair_ring.at[pair, t - 1], 11 + 3 * pair + t
        return pltpu.make_async_remote_copy(
            src_ref=source,
            dst_ref=target,
            send_sem=pair_sends.at[number],
            recv_sem=pair_arrivals.at[number],
            device_id=neighbour(axis),
            device_id_type=pl.DeviceIdType.MESH,
        )

    key_ids = lax.broadcasted_iota(jnp.int32, (256, rows), 0)

    def attend_pair_back(pair):
        key_lanes = pl.ds(pl.multiple_of(pair * 256, 256), LANES)
        value_lanes = pl.ds(pl.multiple_of(pair * 256 + LANES, LANES), LANES)
        for at in range(8):
            key_block, value_block = pairs[at, :, key_lanes], pairs[at, :, value_lanes]
            for half in range(2):
                span = slice(256 * half, 256 * (half + 1))
                masked = masked_pair(key_block, half, 0.0)
                keys[at, span] = masked.astype(BF16)
                keys_turned[at, :, span] = masked.T.astype(BF16)
                values[at, span] = masked_pair(value_block, half, 0.0).astype(BF16)
        for member in range(3):
            number = 3 * pair + member
            product = (attended[number].astype(F32) * grad[number].astype(F32)).T
            for half in range(2):
                own = slice(half * HEAD_SIZE, (half + 1) * HEAD_SIZE)
                at = 2 * member + half
                shifts[at] = jnp.sum(product[own], axis=0, keepdims=True)
                query_halves[256 * at : 256 * (at + 1)] = masked_pair(query[number], half, 0.0).astype(BF16)
                grad_halves[256 * at : 256 * (at + 1)] = masked_pair(grad[number], half, 0.0).astype(BF16)
        turned_sum[...] = jnp.zeros_like(turned_sum)

        def block_step(at, carry):
            probs, scores = [], []
            seen = key_ids < limit[...] - at * 256
            for member in range(3):
                number = 3 * pair + member
                parts = lax.dot_general(keys[at], query[number], NT, preferred_element_type=F32)
                backs = lax.dot_general(values[at], grad[number], NT, preferred_element_type=F32)
                for half in range(2):
                    span = slice(256 * half, 256 * (half + 1))
                    part = jnp.where(seen, parts[span], -1e30)
                    prob = jnp.exp(part - log_total[number, half : half + 1, :])
                    scores.append((prob * (backs[span] - shifts[2 * member + half])).astype(BF16))
                    probs.append(prob.astype(BF16))
                turned_sum[member] += jnp.dot(
                    keys_turned[at], jnp.concatenate(scores[-2:], axis=0), preferred_element_type=F32
                )
            t = lax.rem(z - at // 2 + Z_SIZE, Z_SIZE)
            dx = lax.rem(at + x, 2)
            for lanes, left, right in (
                (slice(0, LANES), scores, query_halves),
                (slice(LANES, 2 * LANES), probs, grad_halves),
            ):
                value = jnp.dot(jnp.concatenate(left, axis=1), right[...], preferred_element_type=F32)
                pair_parts[pair, dx, t, :, lanes] = value.astype(BF16)
            return carry

        lax.fori_loop(0, 8, block_step, 0)
        for member in range(3):
            turned = turned_sum[member].T * HEAD_SIZE**-0.5
            query_grad[3 * pair + member] = rotate_halves(turned, cosine[...], -sine[...]).astype(BF16)
        for t in range(Z_SIZE - 1, -1, -1):
            pair_copy(pair, t, "x").start()

    def pair_step(t, pair):
        pair_copy(pair, t, "x").wait_recv()
        total = pair_parts[pair, 0, t].astype(F32) + pair_near[pair, t].astype(F32)
        if t < Z_SIZE - 1:
            pair_copy(pair, t + 1, "z_back").wait_recv()
            total = total + pair_ring[pair, t].astype(F32)
        if t:
            pair_parts[pair, 0, t] = total.astype(BF16)
            pair_copy(pair, t, "z_back").start()
        else:
            key_tile = rotate_halves(total[:, :LANES], cosine[...], -sine[...])
            wide[:, 1152 + pair * LANES : 1152 + (pair + 1) * LANES] = key_tile
            wide[:, 1536 + pair * LANES : 1536 + (pair + 1) * LANES] = total[:, LANES:]

    def side_step(t, axis):
        down.side_step(t, axis)
        up.side_step(t, axis)

    attend_pair_back(0)
    plane.ring_step(2)
    side_step(3, "y")
    side_step(3, "x")
    attend_pair_back(1)
    side_step(2, "y")
    attend_pair_back(2)
    plane.ring_step(1)
    side_step(2, "x")
    side_step(1, "y")
    first_copies = []
    for y_at in range(2):
        place = first_turned.at[y_at, :, mine]
        own = pltpu.make_async_copy(first_stage.at[y_at * 2 + core], place, own_sems.at[y_at])
        own.start()
        copy = core_copy(first_stage.at[y_at * 2 + 1 - core], place, 1 + y_at)
        copy.start()
        first_copies.append((own, copy))

    for at, tile in enumerate(natural_tiles([query_grad[at].astype(F32) for at in range(9)])):
        wide[:, at * LANES : (at + 1) * LANES] = tile
    q_part, kv_part = 144, 48
    for at in range(8):
        pieces[at, mine, :q_part] = wide[:, at * q_part : (at + 1) * q_part].astype(BF16)
    pair_step(3, 0)
    pair_step(3, 1)
    side_step(1, "x")
    side_step(0, "y")
    side_step(0, "x")
    pair_step(2, 0)
    pair_step(3, 2)
    pair_step(2, 1)
    plane.ring_step(0)
    plane.plane_start()
    pair_step(1, 0)
    pair_step(2, 2)
    pair_step(1, 1)
    pair_step(0, 0)
    pair_step(1, 2)
    down.near_step(3)
    up.near_step(3)
    pair_step(0, 1)
    pair_step(0, 2)
    for at in range(8):
        both = jnp.concatenate(
            [
                wide[:, 1152 + at * kv_part : 1152 + (at + 1) * kv_part],
                wide[:, 1536 + at * kv_part : 1536 + (at + 1) * kv_part],
            ],
            axis=1,
        )
        pieces[at, mine, q_part:] = both.astype(BF16)

    def weight_copy(at):
        return pltpu.make_async_copy(weights.at[at], weight_slots.at[at % 2], weight_sems.at[at % 2])

    weight_copy(0).start()
    weight_copy(1).start()
    piece_copy = core_copy(pieces.at[:, mine, :], pieces.at[:, mine, :], 0)
    piece_copy.start()
    grad_one = wide.at[:, :1152]
    for at in range(8):
        weight_copy(at).wait()
        part = lax.dot_general(
            pieces[at, mine, :], weight_slots[at % 2].reshape(width, 240), NT, preferred_element_type=F32
        )
        grad_one[...] = part if at == 0 else grad_one[...] + part
        if at < 6:
            weight_copy(at + 2).start()
    plane.plane_side()
    core_copy(pieces.at[:, theirs, :], pieces.at[:, theirs, :], 0).wait_recv()
    for y_at, (own, _) in enumerate(first_copies):
        place = first_turned.at[y_at, :, theirs]
        core_copy(place, place, 1 + y_at).wait_recv()
        own.wait()
    def qkv_corners(number, carry):
        qkv.corner_step(Z_SIZE - 1 - number)
        return carry

    lax.fori_loop(0, Z_SIZE, qkv_corners, 0)
    down.near_step(2)
    up.near_step(2)
    def qkv_sides(number, carry):
        for axis in ("y", "x"):
            qkv.side_step(Z_SIZE - 1 - number, axis)
        return carry

    lax.fori_loop(0, Z_SIZE, qkv_sides, 0)
    residual.wait()
    grad_rows = grad_one[...]
    _, hat = normalized(tokens[...].astype(F32))
    first_gain = jnp.sum(grad_rows * hat, axis=0, keepdims=True)
    scaled = grad_rows * gains[0:1, :]
    input_grad[...] += factor * (scaled - hat * jnp.mean(scaled * hat, axis=-1, keepdims=True))
    both = jnp.concatenate([first_gain, second_gain[...], jnp.zeros((6, width), F32)], axis=0)
    for row in range(4):
        gain_sum[0, row] = both[:, row * 288 : (row + 1) * 288]
    gain_copies = []

    def gain_send(source, number, axis):
        copy = pltpu.make_async_remote_copy(
            src_ref=gain_sum.at[source],
            dst_ref=gain_came.at[number],
            send_sem=gain_sends.at[number],
            recv_sem=gain_arrivals.at[number],
            device_id=neighbour(axis),
            device_id_type=pl.DeviceIdType.MESH,
        )
        copy.start()
        gain_copies.append(copy)
        return copy

    plane.plane_end()
    down.near_step(1)
    up.near_step(1)
    gain_send(0, 0, "core").wait_recv()
    gain_sum[0+1] = gain_sum[0] + gain_came[0]
    qkv.near_step(3)
    gain_send(1, 1, "y").wait_recv()
    gain_sum[1+1] = gain_sum[1] + gain_came[1]
    qkv.near_step(2)
    gain_send(2, 2, "x").wait_recv()
    gain_sum[2+1] = gain_sum[2] + gain_came[2]
    qkv.near_step(1)
    ends = [gain_send(3, 3 + number, axis) for number, axis in enumerate(("z", "z_two", "z_back"))]
    down.near_step(0)
    up.near_step(0)
    qkv.near_step(0)
    for copy in ends:
        copy.wait_recv()
    seq_at = y * 2 + core
    gain_out[...] = (gain_sum[3, seq_at] + gain_came[3, seq_at]) + (gain_came[4, seq_at] + gain_came[5, seq_at])
    for group in (down, up, qkv, plane):
        group.drain()
    for pair in range(3):
        for t in range(Z_SIZE):
            pair_copy(pair, t, "x").wait_send()
            if t:
                pair_copy(pair, t, "z_back").wait_send()
    for copy in gain_copies + [piece_copy] + [copy for _, copy in first_copies]:
        copy.wait_send()


def back(weight_inputs, attention_inputs, tokens, gains, second_gain, weights, mixed_grad):
    rows, width = tokens.shape
    dma, arrays = pltpu.SemaphoreType.DMA, []
    for shape in ((144, 1056 - PLANE_LANES), (288, 768), (288, 240)):
        arrays += [pltpu.VMEM((Z_SIZE,) + shape, BF16)] * 5 + [pltpu.VMEM((Z_SIZE - 1,) + shape, BF16)]
    arrays.append(pltpu.VMEM((Z_SIZE, 2, 2, 144, PLANE_LANES), BF16))
    arrays += [pltpu.VMEM((144, PLANE_LANES), BF16)] * 3
    return pl.pallas_call(
        back_kernel,
        out_shape=(
            jax.ShapeDtypeStruct((144, 1056), F32),
            jax.ShapeDtypeStruct((288, 768), F32),
            jax.ShapeDtypeStruct((288, 240), F32),
            jax.ShapeDtypeStruct((rows, width), F32),
            jax.ShapeDtypeStruct((8, 288), F32),
        ),
        in_specs=vmem_specs(17) + any_specs(2),
        out_specs=tuple(vmem_specs(5)),
        scratch_shapes=arrays
        + [
            pltpu.VMEM((8, 512, LANES), BF16),
            pltpu.VMEM((8, LANES, 512), BF16),
            pltpu.VMEM((8, 512, LANES), BF16),
            pltpu.VMEM((6 * rows, LANES), BF16),
            pltpu.VMEM((6 * rows, LANES), BF16),
            pltpu.VMEM((3, LANES, rows), F32),
            pltpu.VMEM((6, 1, rows), F32),
            pltpu.VMEM((3, 2, Z_SIZE, 256, 2 * LANES), BF16),
            pltpu.VMEM((3, Z_SIZE, 256, 2 * LANES), BF16),
            pltpu.VMEM((3, Z_SIZE - 1, 256, 2 * LANES), BF16),
            pltpu.VMEM((9, rows, LANES), BF16),
            pltpu.VMEM((rows, 1920), F32),
            pltpu.VMEM((8, 2 * rows, 240), BF16),
            pltpu.VMEM((4, 288, rows), BF16),
            pltpu.VMEM((2, 288, 2 * rows), BF16),
            pltpu.VMEM((2, 4, 288, 240), BF16),
            pltpu.VMEM((4, 4, 8, 288), F32),
            pltpu.VMEM((6, 4, 8, 288), F32),
        ]
        + [dma((19,))] * 6
        + [dma((15,))] * 2
        + [dma((21,))] * 2
        + [dma((3,))] * 2
        + [dma((6,))] * 2
        + [dma((3,)), dma((2,))],
        compiler_params=pltpu.CompilerParams(
            vmem_limit_bytes=VMEM_LIMIT, collective_id=3, has_side_effects=True
        ),
        cost_estimate=cost(4 * 18 * rows * 2048 * 128 * 10, 4e8, 18 * rows * 2048),
        name="back",
    )(*weight_inputs, *attention_inputs, tokens, gains, second_gain, weights, mixed_grad)


def finish_kernel(output, input_grad, gains, qkv, down, up, *outs):
    turned = qkv[...].T
    outs[0][...] = output[...]
    outs[1][...] = input_grad[...]
    outs[2][...] = gains[...]
    outs[3][...] = turned[:144]
    outs[4][...] = turned[144:192]
    outs[5][...] = turned[192:]
    outs[6][...] = down[:, 768:]
    outs[7][...] = down[:, :768]
    outs[8][...] = up[:, :384]
    outs[9][...] = up[:, 384:]


def finish(*parts):
    rows, width = parts[0].shape
    shapes = ((8, 288), (144, 288), (48, 288), (48, 288), (144, 288), (144, 768), (288, 384), (288, 384))
    return pl.pallas_call(
        finish_kernel,
        out_shape=(jax.ShapeDtypeStruct((rows, width), BF16), jax.ShapeDtypeStruct((rows, width), F32))
        + tuple(jax.ShapeDtypeStruct(shape, F32) for shape in shapes),
        in_specs=vmem_specs(6),
        out_specs=tuple(vmem_specs(10)),
        cost_estimate=cost(1e6, 8e6),
        name="finish",
    )(*parts)


def permuted_device(
    tokens, prefix, gain_one, w_query, w_key, value_weight, w_out, gain_two, w_gate, w_up, w_down, cotangent
):
    tokens, cotangent = tokens[0], cotangent[0]
    half = HEAD_SIZE // 2
    frequency = ROTARY_BASE ** (-jnp.arange(half, dtype=F32) * 2.0 / HEAD_SIZE)
    (
        qkv,
        pairs,
        *weight_inputs,
        query,
        attended,
        log_total,
        gains,
        output,
        mixed_grad,
        attended_grad,
        second_gain,
        cosine,
        sine,
        limit,
    ) = front(
        prefix,
        jnp.tile(frequency, 4)[None, :],
        (w_query.T, w_key.T, value_weight.T, w_out.T, w_gate, w_up, w_down.T),
        jnp.stack([gain_one, gain_two]).astype(F32),
        tokens,
        cotangent,
    )
    grad_down_out, grad_up, grad_qkv, input_grad, gain_grads = back(
        weight_inputs,
        (query, attended, attended_grad, log_total, limit, cosine, sine, pairs),
        tokens,
        gains,
        second_gain,
        qkv,
        mixed_grad,
    )
    output, input_grad, gain_grads, query_t, key_t, value_t, out_t, down_t, gate, up = finish(
        output, input_grad, gain_grads, grad_qkv, grad_down_out, grad_up
    )
    return (
        output[None],
        input_grad[None],
        gain_grads[0],
        query_t.T,
        key_t.T,
        value_t.T,
        out_t.T,
        gain_grads[1],
        gate,
        up,
        down_t.T,
    )


def permute_plan_fits(mesh, tokens):
    return dict(mesh.shape) == {"seq": 4, "ctx": 8} and tokens.shape == (4, 2048, 1152)


def solution(mesh):
    placed = (
        P("seq", "ctx", None),
        P("seq"),
        P("seq"),
        P("seq", "ctx"),
        P("seq", "ctx"),
        P("seq", "ctx"),
        P("seq", "ctx"),
        P("seq"),
        P("seq", "ctx"),
        P("seq", "ctx"),
        P("seq", "ctx"),
        P("seq", "ctx", None),
    )

    def mapped(device_function):
        return jax.shard_map(
            device_function,
            mesh=mesh,
            in_specs=placed,
            out_specs=(
                P("seq", "ctx", None),
                P("seq", "ctx", None),
                P("seq"),
                P("seq", "ctx"),
                P("seq", "ctx"),
                P("seq", "ctx"),
                P("seq", "ctx"),
                P("seq"),
                P("seq", "ctx"),
                P("seq", "ctx"),
                P("seq", "ctx"),
            ),
            check_vma=False,
        )

    def layer(tokens, *rest):
        return mapped(permuted_device if permute_plan_fits(mesh, tokens) else per_device)(tokens, *rest)

    return layer
```

```python
import functools

import jax
import jax.numpy as jnp
from jax import lax
from jax.experimental import pallas as pl
from jax.experimental.pallas import tpu as pltpu
from jax.sharding import PartitionSpec as P

QUERY_HEADS = 18
KEY_VALUE_HEADS = 6
HEAD_SIZE = 64


EPSILON = 1e-05
ROTARY_BASE = 10000.0

LANES = 128
Z_SIZE = 4
VMEM_LIMIT = 66_000_000
PLANE_LANES = 640
F32 = jnp.float32
BF16 = jnp.bfloat16
NT = (((1,), (1,)), ((), ()))


def rotary_tables(positions, head_width):
    half_width = head_width // 2
    frequency = ROTARY_BASE ** (-jnp.arange(half_width, dtype=jnp.float32) * 2.0 / head_width)
    angles = positions.astype(jnp.float32)[:, None] * frequency[None, :]
    return (jnp.cos(angles)[:, None, :], jnp.sin(angles)[:, None, :])


def apply_rotation(values_in, cosine_table, sine_values):
    half_width = values_in.shape[-1] // 2
    first = values_in[..., :half_width]
    second = values_in[..., half_width:]
    return jnp.concatenate(
        [first * cosine_table - second * sine_values, second * cosine_table + first * sine_values],
        axis=-1,
    )


def inverse_rotation(grads_in, cosine_table, sine_values):
    half_width = grads_in.shape[-1] // 2
    first = grads_in[..., :half_width]
    second = grads_in[..., half_width:]
    return jnp.concatenate(
        [first * cosine_table + second * sine_values, second * cosine_table - first * sine_values],
        axis=-1,
    )


def gather_weights(w_query, w_key, value_weight, w_out, w_gate, w_up, w_down, gain_one, gain_two):
    columns = (
        lax.all_gather(w_query, "ctx", axis=1, tiled=True),
        lax.all_gather(w_key, "ctx", axis=1, tiled=True),
        lax.all_gather(value_weight, "ctx", axis=1, tiled=True),
        lax.all_gather(w_out, "ctx", axis=1, tiled=True),
        lax.all_gather(w_gate, "ctx", axis=1, tiled=True),
        lax.all_gather(w_up, "ctx", axis=1, tiled=True),
        lax.all_gather(w_down, "ctx", axis=1, tiled=True),
    )
    return (
        lax.all_gather(columns[0], "seq", axis=0, tiled=True),
        lax.all_gather(columns[1], "seq", axis=0, tiled=True),
        lax.all_gather(columns[2], "seq", axis=0, tiled=True),
        lax.all_gather(columns[3], "seq", axis=0, tiled=True),
        lax.all_gather(columns[4], "seq", axis=0, tiled=True),
        lax.all_gather(columns[5], "seq", axis=0, tiled=True),
        lax.all_gather(columns[6], "seq", axis=0, tiled=True),
        lax.all_gather(gain_one, "seq", axis=0, tiled=True),
        lax.all_gather(gain_two, "seq", axis=0, tiled=True),
    )


def gather_pairs(key_rotated, value_reduced):
    return (
        lax.all_gather(key_rotated, "ctx", axis=1, tiled=True),
        lax.all_gather(value_reduced, "ctx", axis=1, tiled=True),
    )


def head_major(whole_result, sequence_count):
    sequence_length = whole_result.shape[1]
    return (
        whole_result.reshape(sequence_count, sequence_length, KEY_VALUE_HEADS, HEAD_SIZE)
        .transpose(0, 2, 1, 3)
        .reshape(sequence_count * KEY_VALUE_HEADS, sequence_length, HEAD_SIZE)
    )


def per_device(
    tokens,
    prefix,
    gain_one,
    w_query,
    w_key,
    value_weight,
    w_out,
    gain_two,
    w_gate,
    w_up,
    w_down,
    cotangent,
):
    sequence_count, token_local, model_width = tokens.shape
    sequence_length = token_local * lax.axis_size("ctx")
    number_of_rows = sequence_count * token_local
    queries_per_key_head = QUERY_HEADS // KEY_VALUE_HEADS
    score_scale = HEAD_SIZE ** (-0.5)
    gathered = gather_weights(
        w_query, w_key, value_weight, w_out, w_gate, w_up, w_down, gain_one, gain_two
    )
    full_query, full_key, full_value, full_out, full_gate, full_up, full_down = gathered[:7]
    first_norm = gathered[7].astype(jnp.float32)
    second_norm = gathered[8].astype(jnp.float32)
    input_rows = tokens.reshape(number_of_rows, model_width).astype(jnp.float32)
    first_factor = lax.rsqrt(jnp.mean(input_rows * input_rows, axis=-1, keepdims=True) + EPSILON)
    first_normalized_input = input_rows * first_factor
    normalized_rows = (first_normalized_input * first_norm).astype(jnp.bfloat16)
    query_pre = jnp.dot(normalized_rows, full_query, preferred_element_type=jnp.float32)
    key_prerotation = jnp.dot(normalized_rows, full_key, preferred_element_type=jnp.float32)
    value_reduced = jnp.dot(normalized_rows, full_value, preferred_element_type=jnp.float32).astype(
        jnp.bfloat16
    )
    positions = lax.axis_index("ctx") * token_local + jnp.arange(token_local, dtype=jnp.int32)
    cosine_table, sine_values = rotary_tables(positions, HEAD_SIZE)
    query_rows = apply_rotation(
        query_pre.reshape(sequence_count, token_local, QUERY_HEADS, HEAD_SIZE),
        cosine_table,
        sine_values,
    ).astype(jnp.bfloat16)
    key_rotated = apply_rotation(
        key_prerotation.reshape(sequence_count, token_local, KEY_VALUE_HEADS, HEAD_SIZE),
        cosine_table,
        sine_values,
    ).astype(jnp.bfloat16)
    key_rotated = key_rotated.reshape(sequence_count, token_local, KEY_VALUE_HEADS * HEAD_SIZE)
    value_reduced = value_reduced.reshape(sequence_count, token_local, KEY_VALUE_HEADS * HEAD_SIZE)
    keys_all, values_all = gather_pairs(key_rotated, value_reduced)
    query_block_list = query_rows.reshape(
        sequence_count, token_local, KEY_VALUE_HEADS, queries_per_key_head, HEAD_SIZE
    ).transpose(0, 2, 3, 1, 4)
    query_block_list = query_block_list.reshape(
        sequence_count * KEY_VALUE_HEADS, queries_per_key_head, token_local, HEAD_SIZE
    )
    key_blocks = head_major(keys_all, sequence_count)
    value_blocks = head_major(values_all, sequence_count)
    prefix_repeated = jnp.repeat(prefix, KEY_VALUE_HEADS)
    key_place = jnp.arange(sequence_length, dtype=jnp.int32)

    def visible_for(prefix_len):
        return (key_place[None, :] <= positions[:, None]) | (key_place[None, :] < prefix_len)

    def attend(block_item):
        query_block, key_block, value_block, prefix_len = block_item
        scores = (
            jnp.einsum("gqd,kd->gqk", query_block, key_block, preferred_element_type=jnp.float32)
            * score_scale
        )
        scores = jnp.where(visible_for(prefix_len)[None], scores, -1e30)
        row_max = jnp.max(scores, axis=-1, keepdims=True)
        expo = jnp.exp(scores - row_max)
        total = jnp.sum(expo, axis=-1, keepdims=True)
        probs_low = (expo / total).astype(jnp.bfloat16)
        result = jnp.einsum(
            "gqk,kd->gqd", probs_low, value_block, preferred_element_type=jnp.float32
        )
        return (result.astype(jnp.bfloat16), (row_max + jnp.log(total))[..., 0])

    attention_result_blocks, log_totals = lax.map(
        attend, (query_block_list, key_blocks, value_blocks, prefix_repeated)
    )
    attention_result = attention_result_blocks.reshape(
        sequence_count, KEY_VALUE_HEADS, queries_per_key_head, token_local, HEAD_SIZE
    ).transpose(0, 3, 1, 2, 4)
    attention_result = attention_result.reshape(number_of_rows, QUERY_HEADS * HEAD_SIZE)
    mixed_output = input_rows + jnp.dot(
        attention_result, full_out, preferred_element_type=jnp.float32
    )
    second_factor = lax.rsqrt(
        jnp.mean(mixed_output * mixed_output, axis=-1, keepdims=True) + EPSILON
    )
    second_normalized_input = mixed_output * second_factor
    normalized_second = (second_normalized_input * second_norm).astype(jnp.bfloat16)
    gate = jnp.dot(normalized_second, full_gate, preferred_element_type=jnp.float32)
    up_part = jnp.dot(normalized_second, full_up, preferred_element_type=jnp.float32)
    sigmoid_gate = jax.nn.sigmoid(gate)
    activated = gate * sigmoid_gate
    hidden = (activated * up_part).astype(jnp.bfloat16)
    result_rows = mixed_output + jnp.dot(hidden, full_down, preferred_element_type=jnp.float32)
    output = result_rows.astype(jnp.bfloat16).reshape(sequence_count, token_local, model_width)
    gathered = gather_weights(
        w_query, w_key, value_weight, w_out, w_gate, w_up, w_down, gain_one, gain_two
    )
    full_query, full_key, full_value, full_out, full_gate, full_up, full_down = gathered[:7]
    grad_rows_in = cotangent.reshape(number_of_rows, model_width)
    grad_down = jnp.dot(hidden.T, grad_rows_in, preferred_element_type=jnp.float32)
    dhidden = jnp.dot(grad_rows_in, full_down.T, preferred_element_type=jnp.float32)
    dgate = (dhidden * up_part * sigmoid_gate * (1.0 + gate * (1.0 - sigmoid_gate))).astype(
        jnp.bfloat16
    )
    dup_part = (dhidden * activated).astype(jnp.bfloat16)
    grad_gate = jnp.dot(normalized_second.T, dgate, preferred_element_type=jnp.float32)
    grad_up = jnp.dot(normalized_second.T, dup_part, preferred_element_type=jnp.float32)
    normalized_second_grad = jnp.dot(dgate, full_gate.T, preferred_element_type=jnp.float32)
    normalized_second_grad = normalized_second_grad + jnp.dot(
        dup_part, full_up.T, preferred_element_type=jnp.float32
    )
    second_gain_gradient = jnp.sum(normalized_second_grad * second_normalized_input, axis=0)
    second_scaled = normalized_second_grad * second_norm
    dmixed = grad_rows_in.astype(jnp.float32) + second_factor * (
        second_scaled
        - second_normalized_input
        * jnp.mean(second_scaled * second_normalized_input, axis=-1, keepdims=True)
    )
    dproj = dmixed.astype(jnp.bfloat16)
    grad_out = jnp.dot(attention_result.T, dproj, preferred_element_type=jnp.float32)
    attention_result_grad = jnp.dot(dproj, full_out.T, preferred_element_type=jnp.float32).astype(
        jnp.bfloat16
    )
    attention_result_block_grads = attention_result_grad.reshape(
        sequence_count, token_local, KEY_VALUE_HEADS, queries_per_key_head, HEAD_SIZE
    ).transpose(0, 2, 3, 1, 4)
    attention_result_block_grads = attention_result_block_grads.reshape(
        sequence_count * KEY_VALUE_HEADS, queries_per_key_head, token_local, HEAD_SIZE
    )
    keys_all, values_all = gather_pairs(key_rotated, value_reduced)
    key_blocks = head_major(keys_all, sequence_count)
    value_blocks = head_major(values_all, sequence_count)

    def attend_back(block_item):
        query_block, key_block, value_block, prefix_len, log_total, dout_block = block_item
        scores = (
            jnp.einsum("gqd,kd->gqk", query_block, key_block, preferred_element_type=jnp.float32)
            * score_scale
        )
        visible = visible_for(prefix_len)[None]
        probs = jnp.where(
            visible, jnp.exp(jnp.where(visible, scores, -1e30) - log_total[..., None]), 0.0
        )
        dvalues = jnp.einsum(
            "gqk,gqd->kd",
            probs.astype(jnp.bfloat16),
            dout_block,
            preferred_element_type=jnp.float32,
        )
        dprobs = jnp.einsum(
            "gqd,kd->gqk", dout_block, value_block, preferred_element_type=jnp.float32
        )
        dscores = (probs * (dprobs - jnp.sum(probs * dprobs, axis=-1, keepdims=True))).astype(
            jnp.bfloat16
        )
        dquery = (
            jnp.einsum("gqk,kd->gqd", dscores, key_block, preferred_element_type=jnp.float32)
            * score_scale
        )
        dkeys = (
            jnp.einsum("gqk,gqd->kd", dscores, query_block, preferred_element_type=jnp.float32)
            * score_scale
        )
        return (dquery, dkeys, dvalues)

    query_block_grads, key_block_grads, value_block_grads = lax.map(
        attend_back,
        (
            query_block_list,
            key_blocks,
            value_blocks,
            prefix_repeated,
            log_totals,
            attention_result_block_grads,
        ),
    )
    key_grads_combined = key_block_grads.reshape(
        sequence_count, KEY_VALUE_HEADS, sequence_length, HEAD_SIZE
    ).transpose(0, 2, 1, 3)
    key_grads_combined = key_grads_combined.reshape(
        sequence_count, sequence_length, KEY_VALUE_HEADS * HEAD_SIZE
    )
    value_grads_combined = value_block_grads.reshape(
        sequence_count, KEY_VALUE_HEADS, sequence_length, HEAD_SIZE
    ).transpose(0, 2, 1, 3)
    value_grads_combined = value_grads_combined.reshape(
        sequence_count, sequence_length, KEY_VALUE_HEADS * HEAD_SIZE
    )
    key_grads_local, value_grads_local = (
        lax.psum_scatter(
            key_grads_combined.astype(jnp.bfloat16), "ctx", scatter_dimension=1, tiled=True
        ).astype(jnp.float32),
        lax.psum_scatter(
            value_grads_combined.astype(jnp.bfloat16), "ctx", scatter_dimension=1, tiled=True
        ).astype(jnp.float32),
    )
    key_prerotation_grad = inverse_rotation(
        key_grads_local.reshape(sequence_count, token_local, KEY_VALUE_HEADS, HEAD_SIZE),
        cosine_table,
        sine_values,
    )
    key_prerotation_grad = key_prerotation_grad.astype(jnp.bfloat16).reshape(
        number_of_rows, KEY_VALUE_HEADS * HEAD_SIZE
    )
    value_reduced_grad = value_grads_local.astype(jnp.bfloat16).reshape(
        number_of_rows, KEY_VALUE_HEADS * HEAD_SIZE
    )
    query_row_grads = query_block_grads.reshape(
        sequence_count, KEY_VALUE_HEADS, queries_per_key_head, token_local, HEAD_SIZE
    ).transpose(0, 3, 1, 2, 4)
    query_row_grads = query_row_grads.reshape(sequence_count, token_local, QUERY_HEADS, HEAD_SIZE)
    dquery_pre = (
        inverse_rotation(query_row_grads, cosine_table, sine_values)
        .astype(jnp.bfloat16)
        .reshape(number_of_rows, QUERY_HEADS * HEAD_SIZE)
    )
    grad_query = jnp.dot(normalized_rows.T, dquery_pre, preferred_element_type=jnp.float32)
    grad_key = jnp.dot(normalized_rows.T, key_prerotation_grad, preferred_element_type=jnp.float32)
    grad_value = jnp.dot(normalized_rows.T, value_reduced_grad, preferred_element_type=jnp.float32)
    normalized_grad = jnp.dot(dquery_pre, full_query.T, preferred_element_type=jnp.float32)
    normalized_grad = normalized_grad + jnp.dot(
        key_prerotation_grad, full_key.T, preferred_element_type=jnp.float32
    )
    normalized_grad = normalized_grad + jnp.dot(
        value_reduced_grad, full_value.T, preferred_element_type=jnp.float32
    )
    first_gain_gradient = jnp.sum(normalized_grad * first_normalized_input, axis=0)
    first_scaled = normalized_grad * first_norm
    input_grad = dmixed + first_factor * (
        first_scaled
        - first_normalized_input
        * jnp.mean(first_scaled * first_normalized_input, axis=-1, keepdims=True)
    )
    input_grad = input_grad.reshape(sequence_count, token_local, model_width)
    partial_value = (
        lax.psum_scatter(
            grad_query.astype(jnp.bfloat16), "seq", scatter_dimension=0, tiled=True
        ).astype(jnp.float32),
        lax.psum_scatter(
            grad_key.astype(jnp.bfloat16), "seq", scatter_dimension=0, tiled=True
        ).astype(jnp.float32),
        lax.psum_scatter(
            grad_value.astype(jnp.bfloat16), "seq", scatter_dimension=0, tiled=True
        ).astype(jnp.float32),
        lax.psum_scatter(
            grad_out.astype(jnp.bfloat16), "seq", scatter_dimension=0, tiled=True
        ).astype(jnp.float32),
        lax.psum_scatter(
            grad_gate.astype(jnp.bfloat16), "seq", scatter_dimension=0, tiled=True
        ).astype(jnp.float32),
        lax.psum_scatter(
            grad_up.astype(jnp.bfloat16), "seq", scatter_dimension=0, tiled=True
        ).astype(jnp.float32),
        lax.psum_scatter(
            grad_down.astype(jnp.bfloat16), "seq", scatter_dimension=0, tiled=True
        ).astype(jnp.float32),
        lax.psum_scatter(
            first_gain_gradient.astype(jnp.bfloat16), "seq", scatter_dimension=0, tiled=True
        ).astype(jnp.float32),
        lax.psum_scatter(
            second_gain_gradient.astype(jnp.bfloat16), "seq", scatter_dimension=0, tiled=True
        ).astype(jnp.float32),
    )
    owned = (
        lax.psum_scatter(
            partial_value[0].astype(jnp.bfloat16), "ctx", scatter_dimension=1, tiled=True
        ).astype(jnp.float32),
        lax.psum_scatter(
            partial_value[1].astype(jnp.bfloat16), "ctx", scatter_dimension=1, tiled=True
        ).astype(jnp.float32),
        lax.psum_scatter(
            partial_value[2].astype(jnp.bfloat16), "ctx", scatter_dimension=1, tiled=True
        ).astype(jnp.float32),
        lax.psum_scatter(
            partial_value[3].astype(jnp.bfloat16), "ctx", scatter_dimension=1, tiled=True
        ).astype(jnp.float32),
        lax.psum_scatter(
            partial_value[4].astype(jnp.bfloat16), "ctx", scatter_dimension=1, tiled=True
        ).astype(jnp.float32),
        lax.psum_scatter(
            partial_value[5].astype(jnp.bfloat16), "ctx", scatter_dimension=1, tiled=True
        ).astype(jnp.float32),
        lax.psum_scatter(
            partial_value[6].astype(jnp.bfloat16), "ctx", scatter_dimension=1, tiled=True
        ).astype(jnp.float32),
    )
    gains_owned = lax.psum((partial_value[7], partial_value[8]), "ctx")
    final_grads = owned + gains_owned
    return (
        output,
        input_grad,
        final_grads[7],
        final_grads[0],
        final_grads[1],
        final_grads[2],
        final_grads[3],
        final_grads[8],
        final_grads[4],
        final_grads[5],
        final_grads[6],
    )


def my_place():
    seq_at, ctx_at = lax.axis_index("seq"), lax.axis_index("ctx")
    return ctx_at // 2, lax.rem(ctx_at, 2), seq_at // 2, lax.rem(seq_at, 2)


def flipped(at, flip):
    return 1 - at if flip else at


def lane_ids(rows):
    return lax.broadcasted_iota(jnp.int32, (rows, LANES), 1)


def rotate_halves(tile, cosine, sine):
    lower = lax.rem(lane_ids(tile.shape[0]), HEAD_SIZE) < HEAD_SIZE // 2
    swapped = jnp.where(
        lower, pltpu.roll(tile, LANES - HEAD_SIZE // 2, 1), pltpu.roll(tile, HEAD_SIZE // 2, 1)
    )
    return tile * cosine + swapped * sine


def pair_tiles(natural):
    lower = lane_ids(natural[0].shape[0]) < HEAD_SIZE
    tiles = []
    for pair in range(3):
        for member in range(3):
            one, two = 6 * pair + member, 6 * pair + 3 + member
            left, right = natural[one // 2], natural[two // 2]
            if one % 2:
                left, right = pltpu.roll(left, HEAD_SIZE, 1), pltpu.roll(right, HEAD_SIZE, 1)
            tiles.append(jnp.where(lower, left, right))
    return tiles


def natural_tiles(paired):
    lower = lane_ids(paired[0].shape[0]) < HEAD_SIZE
    tiles = []
    for at in range(9):
        sides = []
        for side in range(2):
            head = 2 * at + side
            tile = paired[head // 6 * 3 + head % 3]
            if (head % 6) // 3 != side:
                tile = pltpu.roll(tile, HEAD_SIZE, 1)
            sides.append(tile)
        tiles.append(jnp.where(lower, sides[0], sides[1]))
    return tiles


def normalized(rows):
    factor = lax.rsqrt(jnp.mean(rows * rows, axis=-1, keepdims=True) + EPSILON)
    return factor, rows * factor


def vmem_specs(count):
    return [pl.BlockSpec(memory_space=pltpu.VMEM)] * count


def any_specs(count):
    return [pl.BlockSpec(memory_space=pl.ANY)] * count


def cost(flops, moved, transcendentals=0):
    return pl.CostEstimate(flops=int(flops), bytes_accessed=int(moved), transcendentals=int(transcendentals))


def params():
    return pltpu.CompilerParams(vmem_limit_bytes=VMEM_LIMIT)


def masked_pair(block, half, other):
    inside = (lane_ids(block.shape[0]) < HEAD_SIZE) == (half == 0)
    return jnp.where(inside, block.astype(F32), other)


def core_rows(core):
    return pl.ds(pl.multiple_of(core * 256, 256), 256)


def turned_blocks(matrix, parts):
    flat = matrix.astype(F32).T.astype(BF16)
    return flat.reshape(parts, flat.shape[0] // parts, flat.shape[1])


class Gathering:
    def __init__(self, own, full, lanes, block, sends, arrivals, corner_over_x=()):
        self.own, self.full, self.block, self.sends, self.arrivals = own, full, block, sends, arrivals
        self.corner_over_x, self.lanes = corner_over_x, lanes
        self.started = []

    def place(self, t, dx, dy, dcore=0):
        z, x, y, core = my_place()
        ctx_block = lax.rem(z - t + Z_SIZE, Z_SIZE) * 2 + flipped(x, dx)
        first, second = self.block(ctx_block, flipped(y, dy) * 2 + flipped(core, dcore))
        return self.full.at[first, second, :, self.lanes]

    def copy(self, source, target, number, axis):
        return pltpu.make_async_remote_copy(
            src_ref=source,
            dst_ref=target,
            send_sem=self.sends.at[number],
            recv_sem=self.arrivals.at[number],
            device_id=neighbour(axis),
            device_id_type=pl.DeviceIdType.MESH,
        )

    def send(self, piece, number, axis):
        place = self.place(*piece)
        source = self.own.at[:, self.lanes] if piece == (0, 0, 0) else place
        self.copy(source, place, number, axis).start()
        self.started.append((piece, number))

    def wait(self, piece, number, dcore=0):
        place = self.place(*piece, dcore)
        self.copy(place, place, number, "core").wait_recv()

    def to_core(self, piece):
        t, dx, dy = piece
        self.send(piece, 15 + 4 * t + 2 * dx + dy, "core")

    def over_z(self, t):
        if t < Z_SIZE - 1:
            self.send((t, 0, 0), t, "z")

    def over_plane(self, t):
        self.send((t, 0, 0), 3 + t, "x")
        self.send((t, 0, 0), 7 + t, "y")

    def begin(self):
        self.over_z(0)
        self.over_plane(0)
        self.to_core((0, 0, 0))

    def pass_on(self, t):
        self.wait((t, 0, 0), t - 1)
        self.over_z(t)
        self.over_plane(t)
        self.to_core((t, 0, 0))

    def sides(self, t):
        self.wait((t, 1, 0), 3 + t)
        if t not in self.corner_over_x:
            self.send((t, 1, 0), 11 + t, "y")
        self.to_core((t, 1, 0))
        self.wait((t, 0, 1), 7 + t)
        if t in self.corner_over_x:
            self.send((t, 0, 1), 11 + t, "x")
        self.to_core((t, 0, 1))

    def corner(self, t):
        self.wait((t, 1, 1), 11 + t)
        self.to_core((t, 1, 1))

    def finish(self, t):
        for dx in range(2):
            for dy in range(2):
                self.wait((t, dx, dy), 15 + 4 * t + 2 * dx + dy, 1)

    def drain(self):
        for piece, number in self.started:
            place = self.place(*piece)
            self.copy(place, place, number, "core").wait_send()


class PlaneGathering(Gathering):
    def begin(self):
        self.send((0, 0, 0), 0, "x")
        self.send((0, 0, 0), 1, "y")
        self.to_core((0, 0, 0))

    def plane_sides(self):
        self.wait((0, 1, 0), 0)
        self.send((0, 1, 0), 2, "y")
        self.to_core((0, 1, 0))
        self.wait((0, 0, 1), 1)
        self.to_core((0, 0, 1))

    def plane_corner(self):
        self.wait((0, 1, 1), 2)
        self.to_core((0, 1, 1))

    def ring(self, t):
        for dx in range(2):
            for dy in range(2):
                number = 3 + 4 * t + 2 * dx + dy
                if t:
                    self.wait((t, dx, dy), number - 4)
                if t < Z_SIZE - 1:
                    self.send((t, dx, dy), number, "z")
                if t:
                    self.to_core((t, dx, dy))


def neighbour(axis):
    z, x, y, core = my_place()
    if axis == "z":
        z = lax.rem(z + 1, Z_SIZE)
    elif axis == "z_back":
        z = lax.rem(z + Z_SIZE - 1, Z_SIZE)
    elif axis == "z_two":
        z = lax.rem(z + 2, Z_SIZE)
    elif axis == "x":
        x = 1 - x
    elif axis == "y":
        y = 1 - y
    elif axis == "core":
        core = 1 - core
    elif axis == "y_core":
        y, core = 1 - y, 1 - core
    return (y * 2 + core, z * 2 + x)


def meet(axes):
    barrier = pltpu.get_barrier_semaphore()
    for axis in axes:
        pl.semaphore_signal(barrier, inc=1, device_id=neighbour(axis), device_id_type=pl.DeviceIdType.MESH)
    pl.semaphore_wait(barrier, len(axes))


def front_kernel(
    prefix,
    frequency,
    query_weight,
    key_weight,
    value_weight,
    out_weight,
    gate_weight,
    up_weight,
    down_weight,
    both_gains,
    tokens,
    cotangent,
    qkv_out,
    pairs_out,
    rows_turned,
    both_grads,
    hidden_both,
    attended_both,
    cot_turned,
    proj_turned,
    query_out,
    attended,
    log_total,
    gain_out,
    output,
    mixed_grad,
    attended_grad,
    gain_grad,
    cosine,
    sine,
    limit,
    qkv_own,
    down_own,
    up_own,
    gains_own,
    qkv,
    down,
    up,
    pairs,
    gates,
    ups,
    wide,
    keys,
    values,
    gains,
    rows_two,
    rows_stage,
    hidden,
    attended_rows,
    grads,
    cot_stage,
    proj_stage,
    qkv_sends,
    qkv_arrivals,
    down_sends,
    down_arrivals,
    plane_sends,
    plane_arrivals,
    up_sends,
    up_arrivals,
    pair_sends,
    pair_arrivals,
    gain_sends,
    gain_arrivals,
    own_sems,
    core_sends,
    core_arrivals,
    core_own_sems,
):
    z, x, y, core = my_place()
    seq_at, ctx_at = y * 2 + core, z * 2 + x
    by_ctx, by_seq = (lambda ctx, seq: (ctx, seq)), (lambda ctx, seq: (seq, ctx))
    first = Gathering(qkv_own, qkv, slice(0, 240), by_ctx, qkv_sends, qkv_arrivals, (1, 3))
    plane = PlaneGathering(down_own, down, slice(0, PLANE_LANES), by_seq, plane_sends, plane_arrivals)
    rest = (
        Gathering(down_own, down, slice(PLANE_LANES, 1056), by_seq, down_sends, down_arrivals, (3,)),
        Gathering(up_own, up, slice(0, 768), by_ctx, up_sends, up_arrivals, (3,)),
    )
    mine, theirs, width = core_rows(core), core_rows(1 - core), tokens.shape[1]
    turned = jnp.concatenate([query_weight[...], key_weight[...], value_weight[...]], axis=0)
    qkv_own[...] = turned.astype(F32).T.astype(BF16)
    gains_own[...] = jnp.concatenate([both_gains[...], jnp.zeros((6, 288), F32)], axis=0)
    down_own[:, :768] = down_weight[...]
    down_own[:, 768:] = out_weight[...]
    up_own[:, :384] = gate_weight[...]
    up_own[:, 384:] = up_weight[...]
    meet(("z", "z_back", "x", "y", "core", "y_core"))
    first.begin()
    gain_copies = []
    for number, axis in enumerate(("core", "y", "y_core")):
        copy = pltpu.make_async_remote_copy(
            src_ref=gains_own,
            dst_ref=gains.at[seq_at],
            send_sem=gain_sends.at[number],
            recv_sem=gain_arrivals.at[number],
            device_id=neighbour(axis),
            device_id_type=pl.DeviceIdType.MESH,
        )
        copy.start()
        gain_copies.append(copy)
    own_copies = [
        pltpu.make_async_copy(source, target, own_sems.at[number])
        for number, (source, target) in enumerate(
            (
                (qkv_own, first.place(0, 0, 0)),
                (down_own, down.at[seq_at, ctx_at]),
                (up_own, up.at[ctx_at, seq_at]),
                (gains_own, gains.at[seq_at]),
            )
        )
    ]
    for copy in own_copies:
        copy.start()
    places = ctx_at * 256 + lax.broadcasted_iota(jnp.int32, (256, LANES), 0)
    angles = places.astype(F32) * frequency[...]
    lower = lax.rem(lane_ids(256), HEAD_SIZE) < HEAD_SIZE // 2
    sines = jnp.sin(angles)
    cosine[...] = jnp.cos(angles)
    sine[...] = jnp.where(lower, -sines, sines)
    limit[...] = jnp.maximum(ctx_at * 256 + 1 + lax.broadcasted_iota(jnp.int32, (1, 256), 1), prefix[0])
    for t in range(1, Z_SIZE):
        first.pass_on(t)
        if t == 1:
            plane.begin()
        if t == Z_SIZE - 2:
            for group in rest:
                group.over_z(0)
        first.sides(t - 1)
    plane.plane_sides()
    first.sides(Z_SIZE - 1)
    for group in rest:
        group.over_plane(0)
        group.to_core((0, 0, 0))
    plane.plane_corner()
    plane.ring(0)
    for number, flips in enumerate(((0, 1), (1, 0), (1, 1))):
        place = gains.at[flipped(y, flips[0]) * 2 + flipped(core, flips[1])]
        pltpu.make_async_remote_copy(
            src_ref=place,
            dst_ref=place,
            send_sem=gain_sends.at[number],
            recv_sem=gain_arrivals.at[number],
            device_id=neighbour("core"),
            device_id_type=pl.DeviceIdType.MESH,
        ).wait_recv()
    for copy in own_copies:
        copy.wait()
    for row in range(4):
        gain_out[:, row * 288 : (row + 1) * 288] = gains[row]
    _, hat = normalized(tokens[...].astype(F32))
    rows = (hat * gain_out[0:1, :]).astype(BF16)
    for t in range(Z_SIZE):
        first.corner(t)
    for group in rest:
        group.pass_on(1)
    for t in range(Z_SIZE):
        first.finish(t)

    def multiply(ctx_block, carry):
        matrix = qkv[ctx_block].reshape(tokens.shape[1], 240)
        gates[ctx_block, :, :240] = jnp.dot(rows, matrix, preferred_element_type=F32)
        return carry

    lax.fori_loop(0, 8, multiply, 0)
    save_qkv = pltpu.make_async_copy(qkv, qkv_out, own_sems.at[4])
    save_qkv.start()
    q_part, kv_part = 144, 48
    for at in range(8):
        wide[:, at * q_part : (at + 1) * q_part] = gates[at, :, :q_part]
        wide[:, 1152 + at * kv_part : 1152 + (at + 1) * kv_part] = gates[at, :, q_part : q_part + kv_part]
        wide[:, 1536 + at * kv_part : 1536 + (at + 1) * kv_part] = gates[at, :, q_part + kv_part : 240]
    cos_tile, sin_tile = cosine[...], sine[...]
    for pair in range(3):
        key_tile = wide[:, 1152 + pair * LANES : 1152 + (pair + 1) * LANES]
        pairs[ctx_at, :, 2 * pair * LANES : (2 * pair + 1) * LANES] = rotate_halves(
            key_tile, cos_tile, sin_tile
        ).astype(BF16)
        pairs[ctx_at, :, (2 * pair + 1) * LANES : (2 * pair + 2) * LANES] = wide[
            :, 1536 + pair * LANES : 1536 + (pair + 1) * LANES
        ].astype(BF16)
    natural = [
        rotate_halves(wide[:, at * LANES : (at + 1) * LANES], cos_tile, sin_tile) * HEAD_SIZE**-0.5
        for at in range(9)
    ]
    for at, tile in enumerate(pair_tiles(natural)):
        query_out[at] = tile.astype(BF16)

    pair_copies = []

    def pair_place(t, dx):
        return pairs.at[lax.rem(z - t + Z_SIZE, Z_SIZE) * 2 + flipped(x, dx)]

    def pair_copy(place, number, axis):
        return pltpu.make_async_remote_copy(
            src_ref=place,
            dst_ref=place,
            send_sem=pair_sends.at[number],
            recv_sem=pair_arrivals.at[number],
            device_id=neighbour(axis),
            device_id_type=pl.DeviceIdType.MESH,
        )

    def pair_pass(t):
        if t:
            pair_copy(pair_place(t, 0), t - 1, "z").wait_recv()
        for number, axis in ((t, "z"), (3 + t, "x")):
            if axis == "x" or t < Z_SIZE - 1:
                copy = pair_copy(pair_place(t, 0), number, axis)
                copy.start()
                pair_copies.append(copy)

    def in_rest(step):
        for group in rest:
            step(group)

    pair_pass(0)
    in_rest(lambda group: group.pass_on(2))
    pair_pass(1)
    in_rest(lambda group: group.sides(0))
    pair_pass(2)
    plane.ring(1)
    in_rest(lambda group: group.sides(1))
    pair_pass(3)
    cot_stage[...] = turned_blocks(cotangent[...], 8)
    in_rest(lambda group: group.pass_on(3))
    in_rest(lambda group: group.sides(2))
    for t in range(Z_SIZE):
        pair_copy(pair_place(t, 1), 3 + t, "x").wait_recv()
    save_pairs = pltpu.make_async_copy(pairs, pairs_out, own_sems.at[5])
    save_pairs.start()

    key_ids = lax.broadcasted_iota(jnp.int32, (256, tokens.shape[0]), 0)

    def attend_pair(pair):
        key_lanes = pl.ds(pl.multiple_of(pair * 256, 256), LANES)
        value_lanes = pl.ds(pl.multiple_of(pair * 256 + LANES, LANES), LANES)
        for at in range(8):
            for half in range(2):
                keys[half, at] = masked_pair(pairs[at, :, key_lanes], half, 0.0).astype(BF16)
                values[half, at] = masked_pair(pairs[at, :, value_lanes], half, 1.0).T.astype(BF16)

        def attend_member(member, carry):
            tile = query_out[3 * pair + member]
            parts = []
            for half in range(2):
                top = None
                for at in range(8):
                    part = lax.dot_general(keys[half, at], tile, NT, preferred_element_type=F32)
                    part = jnp.where(key_ids < limit[...] - at * 256, part, -1e30)
                    ups[at, :, :256] = part
                    block_top = jnp.max(part, axis=0, keepdims=True)
                    top = block_top if top is None else jnp.maximum(top, block_top)
                total = jnp.zeros((LANES, tile.shape[0]), F32)
                for at in range(8):
                    weight = jnp.exp(ups[at, :, :256] - top).astype(BF16)
                    total = total + jnp.dot(values[half, at], weight, preferred_element_type=F32)
                norm = total[HEAD_SIZE : HEAD_SIZE + 1] if half == 0 else total[:1]
                log_total[3 * pair + member, half : half + 1, :] = top + jnp.log(norm)
                own = total[:HEAD_SIZE] if half == 0 else total[HEAD_SIZE:]
                parts.append(own / norm)
            attended[3 * pair + member] = jnp.concatenate(parts, axis=0).T.astype(BF16)
            return carry

        lax.fori_loop(0, 3, attend_member, 0)

    started, own_copies = [], []

    def core_copy(source, target, number):
        return pltpu.make_async_remote_copy(
            src_ref=source,
            dst_ref=target,
            send_sem=core_sends.at[number],
            recv_sem=core_arrivals.at[number],
            device_id=neighbour("core"),
            device_id_type=pl.DeviceIdType.MESH,
        )

    def keep(source, target, number):
        copy = pltpu.make_async_copy(source, target, core_own_sems.at[number])
        copy.start()
        own_copies.append(copy)

    def share(source, target, number):
        copy = core_copy(source, target, number)
        copy.start()
        started.append(copy)

    def deal(stage, target_of, number):
        for y_at in range(2):
            keep(stage.at[y_at * 2 + core], target_of(y_at), number + y_at)
            share(stage.at[y_at * 2 + 1 - core], target_of(y_at), number + y_at)

    def attend_and_pass(pair, carry):
        attend_pair(pair)

        @pl.when(pair == 0)
        def _():
            plane.ring(2)
            in_rest(lambda group: group.sides(3))

        @pl.when(pair == 1)
        def _():
            in_rest(lambda group: group.corner(0))
            in_rest(lambda group: group.corner(1))

        return carry

    lax.fori_loop(0, 3, attend_and_pass, 0)
    keep(cot_stage, cot_turned.at[:, :, mine], 1)
    share(cot_stage, cot_turned.at[:, :, mine], 1)
    in_rest(lambda group: group.corner(2))
    for at, tile in enumerate(natural_tiles([attended[at].astype(F32) for at in range(9)])):
        wide[:, at * LANES : (at + 1) * LANES] = tile
    for row in range(4):
        attended_rows[row] = wide[:, row * 288 : (row + 1) * 288].astype(BF16)
    rest[0].corner(3)
    for t in range(Z_SIZE):
        rest[0].finish(t)

    def out_block(row):
        return down[row, :, :, 768:].reshape(width, 288)

    def down_block(row):
        return down[row, :, :, :768].reshape(width, 768)

    def gate_block(block):
        return up[block, :, :, :384].reshape(width, 384)

    def up_block(block):
        return up[block, :, :, 384:].reshape(width, 384)

    mixed_grad[...] = tokens[...].astype(F32)
    for row in range(4):
        mixed_grad[...] += lax.dot_general(attended_rows[row], out_block(row), NT, preferred_element_type=F32)
    rest[1].corner(3)
    plane.ring(3)
    deal(attended_rows, lambda y_at: attended_both.at[y_at, mine], 2)
    factor, hat = normalized(mixed_grad[...])
    gain_row = gain_out[1:2, :]
    rows_two[...] = (hat * gain_row).astype(BF16)
    wide[:, :1152] = hat
    for t in range(Z_SIZE):
        rest[1].finish(t)

        def gate_and_up(dx, carry, t=t):
            block = lax.rem(z - t + Z_SIZE, Z_SIZE) * 2 + lax.rem(x + dx, 2)
            gates[block] = jnp.dot(rows_two[...], gate_block(block), preferred_element_type=F32)
            ups[block] = jnp.dot(rows_two[...], up_block(block), preferred_element_type=F32)
            return carry

        lax.fori_loop(0, 2, gate_and_up, 0)
    rows_stage[...] = turned_blocks(rows_two[...], 4)
    for t in range(Z_SIZE):
        plane.finish(t)
    deal(rows_stage, lambda y_at: rows_turned.at[y_at, :, mine], 4)

    def feed_forward(row, carry):
        back = jnp.dot(cotangent[...], down_block(row), preferred_element_type=F32)
        for side in range(2):
            block = 2 * row + side
            gate, up_part = gates[block], ups[block]
            sigmoid = 1.0 / (1.0 + jnp.exp(-gate))
            active = gate * sigmoid
            hidden[row, :, side * 384 : (side + 1) * 384] = (active * up_part).astype(BF16)
            part = back[:, side * 384 : (side + 1) * 384]
            grads[block, :, :384] = (part * up_part * sigmoid * (1.0 + gate * (1.0 - sigmoid))).astype(BF16)
            grads[block, :, 384:] = (part * active).astype(BF16)
        mixed_grad[...] += lax.dot_general(hidden[row], down_block(row), NT, preferred_element_type=F32)
        return carry

    lax.fori_loop(0, 4, feed_forward, 0)
    output[...] = mixed_grad[...].astype(BF16)
    keep(grads, both_grads.at[:, mine, :], 0)
    share(grads, both_grads.at[:, mine, :], 0)
    deal(hidden, lambda y_at: hidden_both.at[y_at, mine], 6)
    mixed_grad[...] = jnp.zeros_like(mixed_grad)

    def rows_back(block, carry):
        part = lax.dot_general(grads[block, :, :384], gate_block(block), NT, preferred_element_type=F32)
        part = part + lax.dot_general(grads[block, :, 384:], up_block(block), NT, preferred_element_type=F32)
        mixed_grad[...] += part
        return carry

    lax.fori_loop(0, 8, rows_back, 0)
    grad_two, hat = mixed_grad[...], wide[:, :1152]
    gain_grad[...] = jnp.sum(grad_two * hat, axis=0, keepdims=True)
    scaled = grad_two * gain_row
    total = cotangent[...].astype(F32) + factor * (
        scaled - hat * jnp.mean(scaled * hat, axis=-1, keepdims=True)
    )
    mixed_grad[...] = total
    rows_two[...] = total.astype(BF16)
    proj_stage[...] = turned_blocks(rows_two[...], 8)
    for row in range(4):
        wide[:, row * 288 : (row + 1) * 288] = jnp.dot(
            rows_two[...], out_block(row), preferred_element_type=F32
        )
    keep(proj_stage, proj_turned.at[:, :, mine], 8)
    share(proj_stage, proj_turned.at[:, :, mine], 8)
    tiles = pair_tiles([wide[:, at * LANES : (at + 1) * LANES] for at in range(9)])
    for at, tile in enumerate(tiles):
        attended_grad[at] = tile.astype(BF16)
    for group in rest + (first, plane):
        group.drain()
    for copy in pair_copies + gain_copies + started:
        copy.wait_send()
    for copy in own_copies + [save_qkv, save_pairs]:
        copy.wait()
    places = [both_grads.at[:, theirs, :], cot_turned.at[:, :, theirs]]
    places += [attended_both.at[y_at, theirs] for y_at in range(2)]
    places += [rows_turned.at[y_at, :, theirs] for y_at in range(2)]
    places += [hidden_both.at[y_at, theirs] for y_at in range(2)]
    places.append(proj_turned.at[:, :, theirs])
    for number, place in enumerate(places):
        core_copy(place, place, number).wait_recv()


def front(prefix, frequency, weights, gains, tokens, cotangent):
    rows, width = tokens.shape
    dma = pltpu.SemaphoreType.DMA
    shape = jax.ShapeDtypeStruct
    qkv_own, down_own, up_own = (288, 240), (144, 1056), (288, 768)
    return pl.pallas_call(
        front_kernel,
        out_shape=(
            shape((8, 4) + qkv_own, BF16),
            shape((8, rows, 768), BF16),
            shape((2, 288, 2 * rows), BF16),
            shape((8, 2 * rows, 768), BF16),
            shape((2, 2 * rows, 768), BF16),
            shape((2, 2 * rows, 288), BF16),
            shape((8, 144, 2 * rows), BF16),
            shape((8, 144, 2 * rows), BF16),
            shape((9, rows, LANES), BF16),
            shape((9, rows, LANES), BF16),
            shape((9, 2, rows), F32),
            shape((8, width), F32),
            shape((rows, width), BF16),
            shape((rows, width), F32),
            shape((9, rows, LANES), BF16),
            shape((1, width), F32),
            shape((rows, LANES), F32),
            shape((rows, LANES), F32),
            shape((1, rows), jnp.int32),
        ),
        in_specs=[pl.BlockSpec(memory_space=pltpu.SMEM)] + vmem_specs(11),
        out_specs=tuple(any_specs(8) + vmem_specs(11)),
        scratch_shapes=[
            pltpu.VMEM(qkv_own, BF16),
            pltpu.VMEM(down_own, BF16),
            pltpu.VMEM(up_own, BF16),
            pltpu.VMEM((8, 288), F32),
            pltpu.VMEM((8, 4) + qkv_own, BF16),
            pltpu.VMEM((4, 8) + down_own, BF16),
            pltpu.VMEM((8, 4) + up_own, BF16),
            pltpu.VMEM((8, rows, 768), BF16),
            pltpu.VMEM((8, rows, 384), F32),
            pltpu.VMEM((8, rows, 384), F32),
            pltpu.VMEM((rows, 1920), F32),
            pltpu.VMEM((2, 8, 256, LANES), BF16),
            pltpu.VMEM((2, 8, LANES, 256), BF16),
            pltpu.VMEM((4, 8, 288), F32),
            pltpu.VMEM((rows, width), BF16),
            pltpu.VMEM((4, 288, rows), BF16),
            pltpu.VMEM((4, rows, 768), BF16),
            pltpu.VMEM((4, rows, 288), BF16),
            pltpu.VMEM((8, rows, 768), BF16),
            pltpu.VMEM((8, 144, rows), BF16),
            pltpu.VMEM((8, 144, rows), BF16),
        ]
        + [dma((31,))] * 8
        + [dma((7,))] * 2
        + [dma((3,))] * 2
        + [dma((6,))]
        + [dma((9,))] * 3,
        compiler_params=pltpu.CompilerParams(
            vmem_limit_bytes=VMEM_LIMIT, collective_id=1, has_side_effects=True
        ),
        cost_estimate=cost(4 * 18 * rows * 2048 * 128 * 4, 4e8, 18 * rows * 2048),
        name="front",
    )(prefix, frequency, *weights, gains, tokens, cotangent)


class Scattering:
    def __init__(self, buffers, sends, arrivals, out, piece, corners):
        self.corner, self.side_x, self.side_y, self.near_x, self.near_y, self.ring = buffers
        self.sends, self.arrivals, self.out, self.piece, self.corners = sends, arrivals, out, piece, corners

    def copy(self, source, target, number, axis):
        return pltpu.make_async_remote_copy(
            src_ref=source,
            dst_ref=target,
            send_sem=self.sends.at[number],
            recv_sem=self.arrivals.at[number],
            device_id=neighbour(axis),
            device_id_type=pl.DeviceIdType.MESH,
        )

    def corner_copies(self, t, axes=("x", "y")):
        for number, (axis, lanes) in enumerate(self.corners):
            if axis in axes:
                target = self.side_x if axis == "y" else self.side_y
                yield self.copy(self.corner.at[t, :, lanes], target.at[t, :, lanes], 4 * number + t, axis)

    def side_copy(self, t, axis):
        source, target, first = (self.side_x, self.near_x, 8) if axis == "x" else (self.side_y, self.near_y, 12)
        return self.copy(source.at[t], target.at[t], first + t, axis)

    def ring_copy(self, t):
        return self.copy(self.near_x.at[t], self.ring.at[t - 1], 15 + t, "z_back")

    def corner_step(self, t):
        self.piece(t, 1, 1, self.corner.at[t], lambda lanes: [])
        for copy in self.corner_copies(t):
            copy.start()

    def side_step(self, t, axis):
        came = "y" if axis == "x" else "x"
        for copy in self.corner_copies(t, (came,)):
            copy.wait_recv()
        side = (self.side_x if axis == "x" else self.side_y).at[t]
        ranges = [lanes for at, lanes in self.corners if at == came]

        def addend(lanes):
            return [side[:, lanes]] if any(at.start <= lanes.start and lanes.stop <= at.stop for at in ranges) else []

        self.piece(t, int(axis == "x"), int(axis == "y"), side, addend)
        self.side_copy(t, axis).start()

    def near_step(self, t):
        self.side_copy(t, "x").wait_recv()
        self.side_copy(t, "y").wait_recv()
        if t < Z_SIZE - 1:
            self.ring_copy(t + 1).wait_recv()

        def addend(lanes):
            parts = [self.near_x[t, :, lanes], self.near_y[t, :, lanes]]
            return parts + ([self.ring[t, :, lanes]] if t < Z_SIZE - 1 else [])

        self.piece(t, 0, 0, self.near_x.at[t] if t else self.out, addend)
        if t:
            self.ring_copy(t).start()

    def drain(self):
        for t in range(Z_SIZE):
            for copy in self.corner_copies(t):
                copy.wait_send()
            self.side_copy(t, "x").wait_send()
            self.side_copy(t, "y").wait_send()
            if t:
                self.ring_copy(t).wait_send()


class PlaneScattering:
    def __init__(self, buffers, sends, arrivals, out, piece):
        self.sums, self.corner, self.near_x, self.near_y = buffers
        self.sends, self.arrivals, self.out, self.piece = sends, arrivals, out, piece

    def copy(self, source, target, number, axis):
        return pltpu.make_async_remote_copy(
            src_ref=source,
            dst_ref=target,
            send_sem=self.sends.at[number],
            recv_sem=self.arrivals.at[number],
            device_id=neighbour(axis),
            device_id_type=pl.DeviceIdType.MESH,
        )

    def ring_copy(self, t, dx, dy):
        return self.copy(
            self.sums.at[t, dx, dy], self.sums.at[t - 1, dx, dy], 4 * (t - 1) + 2 * dx + dy, "z_back"
        )

    def plane_copies(self):
        return (
            self.copy(self.sums.at[0, 1, 1], self.corner, 12, "y"),
            self.copy(self.sums.at[0, 1, 0], self.near_x, 13, "x"),
            self.copy(self.sums.at[0, 0, 1], self.near_y, 14, "y"),
        )

    def ring_step(self, t, first=False):
        def one(number, carry):
            dx, dy = number // 2, lax.rem(number, 2)
            target = self.sums.at[t, dx, dy]
            if not first:
                self.ring_copy(t + 1, dx, dy).wait_recv()
            self.piece(t, dx, dy, target, lambda lanes: [] if first else [target[:, lanes]])

            @pl.when(t > 0)
            def _():
                self.ring_copy(t, dx, dy).start()

            return carry

        lax.fori_loop(0, 4, one, 0)

    def plane_start(self):
        corner, _, side_y = self.plane_copies()
        corner.start()
        side_y.start()

    def plane_side(self):
        corner, side_x, _ = self.plane_copies()
        corner.wait_recv()
        side = self.sums.at[0, 1, 0]
        side[...] = (side[...].astype(F32) + self.corner[...].astype(F32)).astype(BF16)
        side_x.start()

    def plane_end(self):
        _, side_x, side_y = self.plane_copies()
        side_x.wait_recv()
        side_y.wait_recv()
        total = self.sums[0, 0, 0].astype(F32) + self.near_x[...].astype(F32)
        self.out[...] = total + self.near_y[...].astype(F32)

    def drain(self):
        for t in range(1, Z_SIZE):
            for dx in range(2):
                for dy in range(2):
                    self.ring_copy(t, dx, dy).wait_send()
        for copy in self.plane_copies():
            copy.wait_send()


def back_kernel(
    rows_turned,
    both_grads,
    hidden,
    attended_rows,
    cot_turned,
    proj_turned,
    query,
    attended,
    grad,
    log_total,
    limit,
    cosine,
    sine,
    pairs,
    tokens,
    gains,
    second_gain,
    weights,
    mixed_grad,
    down_out,
    up_out,
    qkv_out,
    input_grad,
    gain_out,
    *refs,
):
    down_buffers, up_buffers, qkv_buffers, plane_buffers = refs[:6], refs[6:12], refs[12:18], refs[18:22]
    (
        keys,
        keys_turned,
        values,
        query_halves,
        grad_halves,
        turned_sum,
        shifts,
        pair_parts,
        pair_near,
        pair_ring,
        query_grad,
        wide,
        pieces,
        first_stage,
        first_turned,
        weight_slots,
        gain_sum,
        gain_came,
    ) = refs[22:40]
    (
        down_sends,
        down_arrivals,
        up_sends,
        up_arrivals,
        qkv_sends,
        qkv_arrivals,
        plane_sends,
        plane_arrivals,
        pair_sends,
        pair_arrivals,
        core_sends,
        core_arrivals,
        gain_sends,
        gain_arrivals,
        own_sems,
        weight_sems,
    ) = refs[40:]
    z, x, y, core = my_place()
    mine, theirs = core_rows(core), core_rows(1 - core)
    rows, width = tokens.shape

    def flip_if(at, flip):
        return flipped(at, flip) if isinstance(flip, int) else lax.rem(at + flip, 2)

    def ctx_of(t, dx):
        return lax.rem(z - t + Z_SIZE, Z_SIZE) * 2 + flip_if(x, dx)

    def put(target, lanes, value, addend):
        for part in addend(lanes):
            value = value + part.astype(F32)
        target[:, lanes] = value.astype(target.dtype)

    def plane_piece(t, dx, dy, target, addend):
        block, row = ctx_of(t, dx), flip_if(y, dy)
        for lanes in (slice(0, 256), slice(256, PLANE_LANES)):
            value = jnp.dot(cot_turned[block], hidden[row, :, lanes], preferred_element_type=F32)
            put(target, lanes, value, addend)

    def down_piece(t, dx, dy, target, addend):
        block, row = ctx_of(t, dx), flipped(y, dy)
        split = 768 - PLANE_LANES
        value = jnp.dot(cot_turned[block], hidden[row, :, PLANE_LANES:], preferred_element_type=F32)
        put(target, slice(0, split), value, addend)
        value = jnp.dot(proj_turned[block], attended_rows[row], preferred_element_type=F32)
        put(target, slice(split, split + 288), value, addend)

    def up_piece(t, dx, dy, target, addend):
        block, row = ctx_of(t, dx), flipped(y, dy)
        for lanes in (slice(0, 384), slice(384, 768)):
            value = jnp.dot(rows_turned[row], both_grads[block, :, lanes], preferred_element_type=F32)
            put(target, lanes, value, addend)

    def qkv_piece(t, dx, dy, target, addend):
        block, row = ctx_of(t, dx), flipped(y, dy)
        value = jnp.dot(first_turned[row], pieces[block], preferred_element_type=F32)
        put(target, slice(0, 240), value, addend)

    plane = PlaneScattering(
        plane_buffers, plane_sends, plane_arrivals, down_out.at[:, :PLANE_LANES], plane_piece
    )
    down = Scattering(
        down_buffers,
        down_sends,
        down_arrivals,
        down_out.at[:, PLANE_LANES:],
        down_piece,
        (("y", slice(0, 1056 - PLANE_LANES)),),
    )
    up = Scattering(
        up_buffers, up_sends, up_arrivals, up_out, up_piece, (("y", slice(0, 384)), ("x", slice(384, 768)))
    )
    qkv = Scattering(qkv_buffers, qkv_sends, qkv_arrivals, qkv_out, qkv_piece, (("y", slice(0, 240)),))

    meet(("z", "z_back", "x", "y", "core", "z_two"))
    residual = pltpu.make_async_copy(mixed_grad, input_grad, own_sems.at[2])
    residual.start()

    plane.ring_step(Z_SIZE - 1, True)

    def corners(number, carry):
        t = Z_SIZE - 1 - number
        down.corner_step(t)
        up.corner_step(t)
        return carry

    lax.fori_loop(0, Z_SIZE, corners, 0)

    factor, hat = normalized(tokens[...].astype(F32))
    first_stage[...] = turned_blocks((hat * gains[0:1, :]).astype(BF16), 4)

    def core_copy(source, target, number):
        return pltpu.make_async_remote_copy(
            src_ref=source,
            dst_ref=target,
            send_sem=core_sends.at[number],
            recv_sem=core_arrivals.at[number],
            device_id=neighbour("core"),
            device_id_type=pl.DeviceIdType.MESH,
        )

    def pair_copy(pair, t, axis):
        if axis == "x":
            source, target, number = pair_parts.at[pair, 1, t], pair_near.at[pair, t], 4 * pair + t
        else:
            source, target, number = pair_parts.at[pair, 0, t], pair_ring.at[pair, t - 1], 11 + 3 * pair + t
        return pltpu.make_async_remote_copy(
            src_ref=source,
            dst_ref=target,
            send_sem=pair_sends.at[number],
            recv_sem=pair_arrivals.at[number],
            device_id=neighbour(axis),
            device_id_type=pl.DeviceIdType.MESH,
        )

    key_ids = lax.broadcasted_iota(jnp.int32, (256, rows), 0)

    def attend_pair_back(pair):
        key_lanes = pl.ds(pl.multiple_of(pair * 256, 256), LANES)
        value_lanes = pl.ds(pl.multiple_of(pair * 256 + LANES, LANES), LANES)
        for at in range(8):
            key_block, value_block = pairs[at, :, key_lanes], pairs[at, :, value_lanes]
            for half in range(2):
                span = slice(256 * half, 256 * (half + 1))
                masked = masked_pair(key_block, half, 0.0)
                keys[at, span] = masked.astype(BF16)
                keys_turned[at, :, span] = masked.T.astype(BF16)
                values[at, span] = masked_pair(value_block, half, 0.0).astype(BF16)
        for member in range(3):
            number = 3 * pair + member
            product = (attended[number].astype(F32) * grad[number].astype(F32)).T
            for half in range(2):
                own = slice(half * HEAD_SIZE, (half + 1) * HEAD_SIZE)
                at = 2 * member + half
                shifts[at] = jnp.sum(product[own], axis=0, keepdims=True)
                query_halves[256 * at : 256 * (at + 1)] = masked_pair(query[number], half, 0.0).astype(BF16)
                grad_halves[256 * at : 256 * (at + 1)] = masked_pair(grad[number], half, 0.0).astype(BF16)
        turned_sum[...] = jnp.zeros_like(turned_sum)

        def block_step(at, carry):
            probs, scores = [], []
            seen = key_ids < limit[...] - at * 256
            for member in range(3):
                number = 3 * pair + member
                parts = lax.dot_general(keys[at], query[number], NT, preferred_element_type=F32)
                backs = lax.dot_general(values[at], grad[number], NT, preferred_element_type=F32)
                for half in range(2):
                    span = slice(256 * half, 256 * (half + 1))
                    part = jnp.where(seen, parts[span], -1e30)
                    prob = jnp.exp(part - log_total[number, half : half + 1, :])
                    scores.append((prob * (backs[span] - shifts[2 * member + half])).astype(BF16))
                    probs.append(prob.astype(BF16))
                turned_sum[member] += jnp.dot(
                    keys_turned[at], jnp.concatenate(scores[-2:], axis=0), preferred_element_type=F32
                )
            t = lax.rem(z - at // 2 + Z_SIZE, Z_SIZE)
            dx = lax.rem(at + x, 2)
            for lanes, left, right in (
                (slice(0, LANES), scores, query_halves),
                (slice(LANES, 2 * LANES), probs, grad_halves),
            ):
                value = jnp.dot(jnp.concatenate(left, axis=1), right[...], preferred_element_type=F32)
                pair_parts[pair, dx, t, :, lanes] = value.astype(BF16)
            return carry

        lax.fori_loop(0, 8, block_step, 0)
        for member in range(3):
            turned = turned_sum[member].T * HEAD_SIZE**-0.5
            query_grad[3 * pair + member] = rotate_halves(turned, cosine[...], -sine[...]).astype(BF16)
        for t in range(Z_SIZE - 1, -1, -1):
            pair_copy(pair, t, "x").start()

    def pair_step(t, pair):
        pair_copy(pair, t, "x").wait_recv()
        total = pair_parts[pair, 0, t].astype(F32) + pair_near[pair, t].astype(F32)
        if t < Z_SIZE - 1:
            pair_copy(pair, t + 1, "z_back").wait_recv()
            total = total + pair_ring[pair, t].astype(F32)
        if t:
            pair_parts[pair, 0, t] = total.astype(BF16)
            pair_copy(pair, t, "z_back").start()
        else:
            key_tile = rotate_halves(total[:, :LANES], cosine[...], -sine[...])
            wide[:, 1152 + pair * LANES : 1152 + (pair + 1) * LANES] = key_tile
            wide[:, 1536 + pair * LANES : 1536 + (pair + 1) * LANES] = total[:, LANES:]

    def side_step(t, axis):
        down.side_step(t, axis)
        up.side_step(t, axis)

    def attend_step(pair, carry):
        attend_pair_back(pair)

        @pl.when(pair == 0)
        def _():
            plane.ring_step(2)
            side_step(3, "y")
            side_step(3, "x")

        @pl.when(pair == 1)
        def _():
            side_step(2, "y")

        return carry

    lax.fori_loop(0, 3, attend_step, 0)
    plane.ring_step(1)
    side_step(2, "x")
    side_step(1, "y")
    first_copies = []
    for y_at in range(2):
        place = first_turned.at[y_at, :, mine]
        own = pltpu.make_async_copy(first_stage.at[y_at * 2 + core], place, own_sems.at[y_at])
        own.start()
        copy = core_copy(first_stage.at[y_at * 2 + 1 - core], place, 1 + y_at)
        copy.start()
        first_copies.append((own, copy))

    for at, tile in enumerate(natural_tiles([query_grad[at].astype(F32) for at in range(9)])):
        wide[:, at * LANES : (at + 1) * LANES] = tile
    q_part, kv_part = 144, 48
    for at in range(8):
        pieces[at, mine, :q_part] = wide[:, at * q_part : (at + 1) * q_part].astype(BF16)
    pair_step(3, 0)
    pair_step(3, 1)
    side_step(1, "x")
    side_step(0, "y")
    side_step(0, "x")
    pair_step(2, 0)
    pair_step(3, 2)
    pair_step(2, 1)
    plane.ring_step(0)
    plane.plane_start()
    pair_step(1, 0)
    pair_step(2, 2)
    pair_step(1, 1)
    pair_step(0, 0)
    pair_step(1, 2)
    down.near_step(3)
    up.near_step(3)
    pair_step(0, 1)
    pair_step(0, 2)
    for at in range(8):
        both = jnp.concatenate(
            [
                wide[:, 1152 + at * kv_part : 1152 + (at + 1) * kv_part],
                wide[:, 1536 + at * kv_part : 1536 + (at + 1) * kv_part],
            ],
            axis=1,
        )
        pieces[at, mine, q_part:] = both.astype(BF16)

    def weight_copy(at):
        return pltpu.make_async_copy(weights.at[at], weight_slots.at[at % 2], weight_sems.at[at % 2])

    weight_copy(0).start()
    weight_copy(1).start()
    piece_copy = core_copy(pieces.at[:, mine, :], pieces.at[:, mine, :], 0)
    piece_copy.start()
    grad_one = wide.at[:, :1152]
    for at in range(8):
        weight_copy(at).wait()
        part = lax.dot_general(
            pieces[at, mine, :], weight_slots[at % 2].reshape(width, 240), NT, preferred_element_type=F32
        )
        grad_one[...] = part if at == 0 else grad_one[...] + part
        if at < 6:
            weight_copy(at + 2).start()
    plane.plane_side()
    core_copy(pieces.at[:, theirs, :], pieces.at[:, theirs, :], 0).wait_recv()
    for y_at, (own, _) in enumerate(first_copies):
        place = first_turned.at[y_at, :, theirs]
        core_copy(place, place, 1 + y_at).wait_recv()
        own.wait()
    def qkv_corners(number, carry):
        qkv.corner_step(Z_SIZE - 1 - number)
        return carry

    lax.fori_loop(0, Z_SIZE, qkv_corners, 0)
    down.near_step(2)
    up.near_step(2)
    def qkv_sides(number, carry):
        for axis in ("y", "x"):
            qkv.side_step(Z_SIZE - 1 - number, axis)
        return carry

    lax.fori_loop(0, Z_SIZE, qkv_sides, 0)
    residual.wait()
    grad_rows = grad_one[...]
    _, hat = normalized(tokens[...].astype(F32))
    first_gain = jnp.sum(grad_rows * hat, axis=0, keepdims=True)
    scaled = grad_rows * gains[0:1, :]
    input_grad[...] += factor * (scaled - hat * jnp.mean(scaled * hat, axis=-1, keepdims=True))
    both = jnp.concatenate([first_gain, second_gain[...], jnp.zeros((6, width), F32)], axis=0)
    for row in range(4):
        gain_sum[0, row] = both[:, row * 288 : (row + 1) * 288]
    gain_copies = []

    def gain_send(source, number, axis):
        copy = pltpu.make_async_remote_copy(
            src_ref=gain_sum.at[source],
            dst_ref=gain_came.at[number],
            send_sem=gain_sends.at[number],
            recv_sem=gain_arrivals.at[number],
            device_id=neighbour(axis),
            device_id_type=pl.DeviceIdType.MESH,
        )
        copy.start()
        gain_copies.append(copy)
        return copy

    plane.plane_end()
    down.near_step(1)
    up.near_step(1)
    gain_send(0, 0, "core").wait_recv()
    gain_sum[0+1] = gain_sum[0] + gain_came[0]
    qkv.near_step(3)
    gain_send(1, 1, "y").wait_recv()
    gain_sum[1+1] = gain_sum[1] + gain_came[1]
    qkv.near_step(2)
    gain_send(2, 2, "x").wait_recv()
    gain_sum[2+1] = gain_sum[2] + gain_came[2]
    qkv.near_step(1)
    ends = [gain_send(3, 3 + number, axis) for number, axis in enumerate(("z", "z_two", "z_back"))]
    down.near_step(0)
    up.near_step(0)
    qkv.near_step(0)
    for copy in ends:
        copy.wait_recv()
    seq_at = y * 2 + core
    gain_out[...] = (gain_sum[3, seq_at] + gain_came[3, seq_at]) + (gain_came[4, seq_at] + gain_came[5, seq_at])
    for group in (down, up, qkv, plane):
        group.drain()
    for pair in range(3):
        for t in range(Z_SIZE):
            pair_copy(pair, t, "x").wait_send()
            if t:
                pair_copy(pair, t, "z_back").wait_send()
    for copy in gain_copies + [piece_copy] + [copy for _, copy in first_copies]:
        copy.wait_send()


def back(weight_inputs, attention_inputs, tokens, gains, second_gain, weights, mixed_grad):
    rows, width = tokens.shape
    dma, arrays = pltpu.SemaphoreType.DMA, []
    for shape in ((144, 1056 - PLANE_LANES), (288, 768), (288, 240)):
        arrays += [pltpu.VMEM((Z_SIZE,) + shape, BF16)] * 5 + [pltpu.VMEM((Z_SIZE - 1,) + shape, BF16)]
    arrays.append(pltpu.VMEM((Z_SIZE, 2, 2, 144, PLANE_LANES), BF16))
    arrays += [pltpu.VMEM((144, PLANE_LANES), BF16)] * 3
    return pl.pallas_call(
        back_kernel,
        out_shape=(
            jax.ShapeDtypeStruct((144, 1056), F32),
            jax.ShapeDtypeStruct((288, 768), F32),
            jax.ShapeDtypeStruct((288, 240), F32),
            jax.ShapeDtypeStruct((rows, width), F32),
            jax.ShapeDtypeStruct((8, 288), F32),
        ),
        in_specs=vmem_specs(17) + any_specs(2),
        out_specs=tuple(vmem_specs(5)),
        scratch_shapes=arrays
        + [
            pltpu.VMEM((8, 512, LANES), BF16),
            pltpu.VMEM((8, LANES, 512), BF16),
            pltpu.VMEM((8, 512, LANES), BF16),
            pltpu.VMEM((6 * rows, LANES), BF16),
            pltpu.VMEM((6 * rows, LANES), BF16),
            pltpu.VMEM((3, LANES, rows), F32),
            pltpu.VMEM((6, 1, rows), F32),
            pltpu.VMEM((3, 2, Z_SIZE, 256, 2 * LANES), BF16),
            pltpu.VMEM((3, Z_SIZE, 256, 2 * LANES), BF16),
            pltpu.VMEM((3, Z_SIZE - 1, 256, 2 * LANES), BF16),
            pltpu.VMEM((9, rows, LANES), BF16),
            pltpu.VMEM((rows, 1920), F32),
            pltpu.VMEM((8, 2 * rows, 240), BF16),
            pltpu.VMEM((4, 288, rows), BF16),
            pltpu.VMEM((2, 288, 2 * rows), BF16),
            pltpu.VMEM((2, 4, 288, 240), BF16),
            pltpu.VMEM((4, 4, 8, 288), F32),
            pltpu.VMEM((6, 4, 8, 288), F32),
        ]
        + [dma((19,))] * 6
        + [dma((15,))] * 2
        + [dma((21,))] * 2
        + [dma((3,))] * 2
        + [dma((6,))] * 2
        + [dma((3,)), dma((2,))],
        compiler_params=pltpu.CompilerParams(
            vmem_limit_bytes=VMEM_LIMIT, collective_id=3, has_side_effects=True
        ),
        cost_estimate=cost(4 * 18 * rows * 2048 * 128 * 10, 4e8, 18 * rows * 2048),
        name="back",
    )(*weight_inputs, *attention_inputs, tokens, gains, second_gain, weights, mixed_grad)


def finish_kernel(output, input_grad, gains, qkv, down, up, *outs):
    turned = qkv[...].T
    outs[0][...] = output[...]
    outs[1][...] = input_grad[...]
    outs[2][...] = gains[...]
    outs[3][...] = turned[:144]
    outs[4][...] = turned[144:192]
    outs[5][...] = turned[192:]
    outs[6][...] = down[:, 768:]
    outs[7][...] = down[:, :768]
    outs[8][...] = up[:, :384]
    outs[9][...] = up[:, 384:]


def finish(*parts):
    rows, width = parts[0].shape
    shapes = ((8, 288), (144, 288), (48, 288), (48, 288), (144, 288), (144, 768), (288, 384), (288, 384))
    return pl.pallas_call(
        finish_kernel,
        out_shape=(jax.ShapeDtypeStruct((rows, width), BF16), jax.ShapeDtypeStruct((rows, width), F32))
        + tuple(jax.ShapeDtypeStruct(shape, F32) for shape in shapes),
        in_specs=vmem_specs(6),
        out_specs=tuple(vmem_specs(10)),
        cost_estimate=cost(1e6, 8e6),
        name="finish",
    )(*parts)


def permuted_device(
    tokens, prefix, gain_one, w_query, w_key, value_weight, w_out, gain_two, w_gate, w_up, w_down, cotangent
):
    tokens, cotangent = tokens[0], cotangent[0]
    half = HEAD_SIZE // 2
    frequency = ROTARY_BASE ** (-jnp.arange(half, dtype=F32) * 2.0 / HEAD_SIZE)
    (
        qkv,
        pairs,
        *weight_inputs,
        query,
        attended,
        log_total,
        gains,
        output,
        mixed_grad,
        attended_grad,
        second_gain,
        cosine,
        sine,
        limit,
    ) = front(
        prefix,
        jnp.tile(frequency, 4)[None, :],
        (w_query.T, w_key.T, value_weight.T, w_out.T, w_gate, w_up, w_down.T),
        jnp.stack([gain_one, gain_two]).astype(F32),
        tokens,
        cotangent,
    )
    grad_down_out, grad_up, grad_qkv, input_grad, gain_grads = back(
        weight_inputs,
        (query, attended, attended_grad, log_total, limit, cosine, sine, pairs),
        tokens,
        gains,
        second_gain,
        qkv,
        mixed_grad,
    )
    output, input_grad, gain_grads, query_t, key_t, value_t, out_t, down_t, gate, up = finish(
        output, input_grad, gain_grads, grad_qkv, grad_down_out, grad_up
    )
    return (
        output[None],
        input_grad[None],
        gain_grads[0],
        query_t.T,
        key_t.T,
        value_t.T,
        out_t.T,
        gain_grads[1],
        gate,
        up,
        down_t.T,
    )


def permute_plan_fits(mesh, tokens):
    return dict(mesh.shape) == {"seq": 4, "ctx": 8} and tokens.shape == (4, 2048, 1152)


def solution(mesh):
    placed = (
        P("seq", "ctx", None),
        P("seq"),
        P("seq"),
        P("seq", "ctx"),
        P("seq", "ctx"),
        P("seq", "ctx"),
        P("seq", "ctx"),
        P("seq"),
        P("seq", "ctx"),
        P("seq", "ctx"),
        P("seq", "ctx"),
        P("seq", "ctx", None),
    )

    def mapped(device_function):
        return jax.shard_map(
            device_function,
            mesh=mesh,
            in_specs=placed,
            out_specs=(
                P("seq", "ctx", None),
                P("seq", "ctx", None),
                P("seq"),
                P("seq", "ctx"),
                P("seq", "ctx"),
                P("seq", "ctx"),
                P("seq", "ctx"),
                P("seq"),
                P("seq", "ctx"),
                P("seq", "ctx"),
                P("seq", "ctx"),
            ),
            check_vma=False,
        )

    def layer(tokens, *rest):
        return mapped(permuted_device if permute_plan_fits(mesh, tokens) else per_device)(tokens, *rest)

    return layer
```

```python
import functools

import jax
import jax.numpy as jnp
from jax import lax
from jax.experimental import pallas as pl
from jax.experimental.pallas import tpu as pltpu
from jax.sharding import PartitionSpec as P

QUERY_HEADS = 18
KEY_VALUE_HEADS = 6
HEAD_SIZE = 64


EPSILON = 1e-05
ROTARY_BASE = 10000.0

LANES = 128
Z_SIZE = 4
VMEM_LIMIT = 66_000_000
PLANE_LANES = 512
F32 = jnp.float32
BF16 = jnp.bfloat16
NT = (((1,), (1,)), ((), ()))


def rotary_tables(positions, head_width):
    half_width = head_width // 2
    frequency = ROTARY_BASE ** (-jnp.arange(half_width, dtype=jnp.float32) * 2.0 / head_width)
    angles = positions.astype(jnp.float32)[:, None] * frequency[None, :]
    return (jnp.cos(angles)[:, None, :], jnp.sin(angles)[:, None, :])


def apply_rotation(values_in, cosine_table, sine_values):
    half_width = values_in.shape[-1] // 2
    first = values_in[..., :half_width]
    second = values_in[..., half_width:]
    return jnp.concatenate(
        [first * cosine_table - second * sine_values, second * cosine_table + first * sine_values],
        axis=-1,
    )


def inverse_rotation(grads_in, cosine_table, sine_values):
    half_width = grads_in.shape[-1] // 2
    first = grads_in[..., :half_width]
    second = grads_in[..., half_width:]
    return jnp.concatenate(
        [first * cosine_table + second * sine_values, second * cosine_table - first * sine_values],
        axis=-1,
    )


def gather_weights(w_query, w_key, value_weight, w_out, w_gate, w_up, w_down, gain_one, gain_two):
    columns = (
        lax.all_gather(w_query, "ctx", axis=1, tiled=True),
        lax.all_gather(w_key, "ctx", axis=1, tiled=True),
        lax.all_gather(value_weight, "ctx", axis=1, tiled=True),
        lax.all_gather(w_out, "ctx", axis=1, tiled=True),
        lax.all_gather(w_gate, "ctx", axis=1, tiled=True),
        lax.all_gather(w_up, "ctx", axis=1, tiled=True),
        lax.all_gather(w_down, "ctx", axis=1, tiled=True),
    )
    return (
        lax.all_gather(columns[0], "seq", axis=0, tiled=True),
        lax.all_gather(columns[1], "seq", axis=0, tiled=True),
        lax.all_gather(columns[2], "seq", axis=0, tiled=True),
        lax.all_gather(columns[3], "seq", axis=0, tiled=True),
        lax.all_gather(columns[4], "seq", axis=0, tiled=True),
        lax.all_gather(columns[5], "seq", axis=0, tiled=True),
        lax.all_gather(columns[6], "seq", axis=0, tiled=True),
        lax.all_gather(gain_one, "seq", axis=0, tiled=True),
        lax.all_gather(gain_two, "seq", axis=0, tiled=True),
    )


def gather_pairs(key_rotated, value_reduced):
    return (
        lax.all_gather(key_rotated, "ctx", axis=1, tiled=True),
        lax.all_gather(value_reduced, "ctx", axis=1, tiled=True),
    )


def head_major(whole_result, sequence_count):
    sequence_length = whole_result.shape[1]
    return (
        whole_result.reshape(sequence_count, sequence_length, KEY_VALUE_HEADS, HEAD_SIZE)
        .transpose(0, 2, 1, 3)
        .reshape(sequence_count * KEY_VALUE_HEADS, sequence_length, HEAD_SIZE)
    )


def per_device(
    tokens,
    prefix,
    gain_one,
    w_query,
    w_key,
    value_weight,
    w_out,
    gain_two,
    w_gate,
    w_up,
    w_down,
    cotangent,
):
    sequence_count, token_local, model_width = tokens.shape
    sequence_length = token_local * lax.axis_size("ctx")
    number_of_rows = sequence_count * token_local
    queries_per_key_head = QUERY_HEADS // KEY_VALUE_HEADS
    score_scale = HEAD_SIZE ** (-0.5)
    gathered = gather_weights(
        w_query, w_key, value_weight, w_out, w_gate, w_up, w_down, gain_one, gain_two
    )
    full_query, full_key, full_value, full_out, full_gate, full_up, full_down = gathered[:7]
    first_norm = gathered[7].astype(jnp.float32)
    second_norm = gathered[8].astype(jnp.float32)
    input_rows = tokens.reshape(number_of_rows, model_width).astype(jnp.float32)
    first_factor = lax.rsqrt(jnp.mean(input_rows * input_rows, axis=-1, keepdims=True) + EPSILON)
    first_normalized_input = input_rows * first_factor
    normalized_rows = (first_normalized_input * first_norm).astype(jnp.bfloat16)
    query_pre = jnp.dot(normalized_rows, full_query, preferred_element_type=jnp.float32)
    key_prerotation = jnp.dot(normalized_rows, full_key, preferred_element_type=jnp.float32)
    value_reduced = jnp.dot(normalized_rows, full_value, preferred_element_type=jnp.float32).astype(
        jnp.bfloat16
    )
    positions = lax.axis_index("ctx") * token_local + jnp.arange(token_local, dtype=jnp.int32)
    cosine_table, sine_values = rotary_tables(positions, HEAD_SIZE)
    query_rows = apply_rotation(
        query_pre.reshape(sequence_count, token_local, QUERY_HEADS, HEAD_SIZE),
        cosine_table,
        sine_values,
    ).astype(jnp.bfloat16)
    key_rotated = apply_rotation(
        key_prerotation.reshape(sequence_count, token_local, KEY_VALUE_HEADS, HEAD_SIZE),
        cosine_table,
        sine_values,
    ).astype(jnp.bfloat16)
    key_rotated = key_rotated.reshape(sequence_count, token_local, KEY_VALUE_HEADS * HEAD_SIZE)
    value_reduced = value_reduced.reshape(sequence_count, token_local, KEY_VALUE_HEADS * HEAD_SIZE)
    keys_all, values_all = gather_pairs(key_rotated, value_reduced)
    query_block_list = query_rows.reshape(
        sequence_count, token_local, KEY_VALUE_HEADS, queries_per_key_head, HEAD_SIZE
    ).transpose(0, 2, 3, 1, 4)
    query_block_list = query_block_list.reshape(
        sequence_count * KEY_VALUE_HEADS, queries_per_key_head, token_local, HEAD_SIZE
    )
    key_blocks = head_major(keys_all, sequence_count)
    value_blocks = head_major(values_all, sequence_count)
    prefix_repeated = jnp.repeat(prefix, KEY_VALUE_HEADS)
    key_place = jnp.arange(sequence_length, dtype=jnp.int32)

    def visible_for(prefix_len):
        return (key_place[None, :] <= positions[:, None]) | (key_place[None, :] < prefix_len)

    def attend(block_item):
        query_block, key_block, value_block, prefix_len = block_item
        scores = (
            jnp.einsum("gqd,kd->gqk", query_block, key_block, preferred_element_type=jnp.float32)
            * score_scale
        )
        scores = jnp.where(visible_for(prefix_len)[None], scores, -1e30)
        row_max = jnp.max(scores, axis=-1, keepdims=True)
        expo = jnp.exp(scores - row_max)
        total = jnp.sum(expo, axis=-1, keepdims=True)
        probs_low = (expo / total).astype(jnp.bfloat16)
        result = jnp.einsum(
            "gqk,kd->gqd", probs_low, value_block, preferred_element_type=jnp.float32
        )
        return (result.astype(jnp.bfloat16), (row_max + jnp.log(total))[..., 0])

    attention_result_blocks, log_totals = lax.map(
        attend, (query_block_list, key_blocks, value_blocks, prefix_repeated)
    )
    attention_result = attention_result_blocks.reshape(
        sequence_count, KEY_VALUE_HEADS, queries_per_key_head, token_local, HEAD_SIZE
    ).transpose(0, 3, 1, 2, 4)
    attention_result = attention_result.reshape(number_of_rows, QUERY_HEADS * HEAD_SIZE)
    mixed_output = input_rows + jnp.dot(
        attention_result, full_out, preferred_element_type=jnp.float32
    )
    second_factor = lax.rsqrt(
        jnp.mean(mixed_output * mixed_output, axis=-1, keepdims=True) + EPSILON
    )
    second_normalized_input = mixed_output * second_factor
    normalized_second = (second_normalized_input * second_norm).astype(jnp.bfloat16)
    gate = jnp.dot(normalized_second, full_gate, preferred_element_type=jnp.float32)
    up_part = jnp.dot(normalized_second, full_up, preferred_element_type=jnp.float32)
    sigmoid_gate = jax.nn.sigmoid(gate)
    activated = gate * sigmoid_gate
    hidden = (activated * up_part).astype(jnp.bfloat16)
    result_rows = mixed_output + jnp.dot(hidden, full_down, preferred_element_type=jnp.float32)
    output = result_rows.astype(jnp.bfloat16).reshape(sequence_count, token_local, model_width)
    gathered = gather_weights(
        w_query, w_key, value_weight, w_out, w_gate, w_up, w_down, gain_one, gain_two
    )
    full_query, full_key, full_value, full_out, full_gate, full_up, full_down = gathered[:7]
    grad_rows_in = cotangent.reshape(number_of_rows, model_width)
    grad_down = jnp.dot(hidden.T, grad_rows_in, preferred_element_type=jnp.float32)
    dhidden = jnp.dot(grad_rows_in, full_down.T, preferred_element_type=jnp.float32)
    dgate = (dhidden * up_part * sigmoid_gate * (1.0 + gate * (1.0 - sigmoid_gate))).astype(
        jnp.bfloat16
    )
    dup_part = (dhidden * activated).astype(jnp.bfloat16)
    grad_gate = jnp.dot(normalized_second.T, dgate, preferred_element_type=jnp.float32)
    grad_up = jnp.dot(normalized_second.T, dup_part, preferred_element_type=jnp.float32)
    normalized_second_grad = jnp.dot(dgate, full_gate.T, preferred_element_type=jnp.float32)
    normalized_second_grad = normalized_second_grad + jnp.dot(
        dup_part, full_up.T, preferred_element_type=jnp.float32
    )
    second_gain_gradient = jnp.sum(normalized_second_grad * second_normalized_input, axis=0)
    second_scaled = normalized_second_grad * second_norm
    dmixed = grad_rows_in.astype(jnp.float32) + second_factor * (
        second_scaled
        - second_normalized_input
        * jnp.mean(second_scaled * second_normalized_input, axis=-1, keepdims=True)
    )
    dproj = dmixed.astype(jnp.bfloat16)
    grad_out = jnp.dot(attention_result.T, dproj, preferred_element_type=jnp.float32)
    attention_result_grad = jnp.dot(dproj, full_out.T, preferred_element_type=jnp.float32).astype(
        jnp.bfloat16
    )
    attention_result_block_grads = attention_result_grad.reshape(
        sequence_count, token_local, KEY_VALUE_HEADS, queries_per_key_head, HEAD_SIZE
    ).transpose(0, 2, 3, 1, 4)
    attention_result_block_grads = attention_result_block_grads.reshape(
        sequence_count * KEY_VALUE_HEADS, queries_per_key_head, token_local, HEAD_SIZE
    )
    keys_all, values_all = gather_pairs(key_rotated, value_reduced)
    key_blocks = head_major(keys_all, sequence_count)
    value_blocks = head_major(values_all, sequence_count)

    def attend_back(block_item):
        query_block, key_block, value_block, prefix_len, log_total, dout_block = block_item
        scores = (
            jnp.einsum("gqd,kd->gqk", query_block, key_block, preferred_element_type=jnp.float32)
            * score_scale
        )
        visible = visible_for(prefix_len)[None]
        probs = jnp.where(
            visible, jnp.exp(jnp.where(visible, scores, -1e30) - log_total[..., None]), 0.0
        )
        dvalues = jnp.einsum(
            "gqk,gqd->kd",
            probs.astype(jnp.bfloat16),
            dout_block,
            preferred_element_type=jnp.float32,
        )
        dprobs = jnp.einsum(
            "gqd,kd->gqk", dout_block, value_block, preferred_element_type=jnp.float32
        )
        dscores = (probs * (dprobs - jnp.sum(probs * dprobs, axis=-1, keepdims=True))).astype(
            jnp.bfloat16
        )
        dquery = (
            jnp.einsum("gqk,kd->gqd", dscores, key_block, preferred_element_type=jnp.float32)
            * score_scale
        )
        dkeys = (
            jnp.einsum("gqk,gqd->kd", dscores, query_block, preferred_element_type=jnp.float32)
            * score_scale
        )
        return (dquery, dkeys, dvalues)

    query_block_grads, key_block_grads, value_block_grads = lax.map(
        attend_back,
        (
            query_block_list,
            key_blocks,
            value_blocks,
            prefix_repeated,
            log_totals,
            attention_result_block_grads,
        ),
    )
    key_grads_combined = key_block_grads.reshape(
        sequence_count, KEY_VALUE_HEADS, sequence_length, HEAD_SIZE
    ).transpose(0, 2, 1, 3)
    key_grads_combined = key_grads_combined.reshape(
        sequence_count, sequence_length, KEY_VALUE_HEADS * HEAD_SIZE
    )
    value_grads_combined = value_block_grads.reshape(
        sequence_count, KEY_VALUE_HEADS, sequence_length, HEAD_SIZE
    ).transpose(0, 2, 1, 3)
    value_grads_combined = value_grads_combined.reshape(
        sequence_count, sequence_length, KEY_VALUE_HEADS * HEAD_SIZE
    )
    key_grads_local, value_grads_local = (
        lax.psum_scatter(
            key_grads_combined.astype(jnp.bfloat16), "ctx", scatter_dimension=1, tiled=True
        ).astype(jnp.float32),
        lax.psum_scatter(
            value_grads_combined.astype(jnp.bfloat16), "ctx", scatter_dimension=1, tiled=True
        ).astype(jnp.float32),
    )
    key_prerotation_grad = inverse_rotation(
        key_grads_local.reshape(sequence_count, token_local, KEY_VALUE_HEADS, HEAD_SIZE),
        cosine_table,
        sine_values,
    )
    key_prerotation_grad = key_prerotation_grad.astype(jnp.bfloat16).reshape(
        number_of_rows, KEY_VALUE_HEADS * HEAD_SIZE
    )
    value_reduced_grad = value_grads_local.astype(jnp.bfloat16).reshape(
        number_of_rows, KEY_VALUE_HEADS * HEAD_SIZE
    )
    query_row_grads = query_block_grads.reshape(
        sequence_count, KEY_VALUE_HEADS, queries_per_key_head, token_local, HEAD_SIZE
    ).transpose(0, 3, 1, 2, 4)
    query_row_grads = query_row_grads.reshape(sequence_count, token_local, QUERY_HEADS, HEAD_SIZE)
    dquery_pre = (
        inverse_rotation(query_row_grads, cosine_table, sine_values)
        .astype(jnp.bfloat16)
        .reshape(number_of_rows, QUERY_HEADS * HEAD_SIZE)
    )
    grad_query = jnp.dot(normalized_rows.T, dquery_pre, preferred_element_type=jnp.float32)
    grad_key = jnp.dot(normalized_rows.T, key_prerotation_grad, preferred_element_type=jnp.float32)
    grad_value = jnp.dot(normalized_rows.T, value_reduced_grad, preferred_element_type=jnp.float32)
    normalized_grad = jnp.dot(dquery_pre, full_query.T, preferred_element_type=jnp.float32)
    normalized_grad = normalized_grad + jnp.dot(
        key_prerotation_grad, full_key.T, preferred_element_type=jnp.float32
    )
    normalized_grad = normalized_grad + jnp.dot(
        value_reduced_grad, full_value.T, preferred_element_type=jnp.float32
    )
    first_gain_gradient = jnp.sum(normalized_grad * first_normalized_input, axis=0)
    first_scaled = normalized_grad * first_norm
    input_grad = dmixed + first_factor * (
        first_scaled
        - first_normalized_input
        * jnp.mean(first_scaled * first_normalized_input, axis=-1, keepdims=True)
    )
    input_grad = input_grad.reshape(sequence_count, token_local, model_width)
    partial_value = (
        lax.psum_scatter(
            grad_query.astype(jnp.bfloat16), "seq", scatter_dimension=0, tiled=True
        ).astype(jnp.float32),
        lax.psum_scatter(
            grad_key.astype(jnp.bfloat16), "seq", scatter_dimension=0, tiled=True
        ).astype(jnp.float32),
        lax.psum_scatter(
            grad_value.astype(jnp.bfloat16), "seq", scatter_dimension=0, tiled=True
        ).astype(jnp.float32),
        lax.psum_scatter(
            grad_out.astype(jnp.bfloat16), "seq", scatter_dimension=0, tiled=True
        ).astype(jnp.float32),
        lax.psum_scatter(
            grad_gate.astype(jnp.bfloat16), "seq", scatter_dimension=0, tiled=True
        ).astype(jnp.float32),
        lax.psum_scatter(
            grad_up.astype(jnp.bfloat16), "seq", scatter_dimension=0, tiled=True
        ).astype(jnp.float32),
        lax.psum_scatter(
            grad_down.astype(jnp.bfloat16), "seq", scatter_dimension=0, tiled=True
        ).astype(jnp.float32),
        lax.psum_scatter(
            first_gain_gradient.astype(jnp.bfloat16), "seq", scatter_dimension=0, tiled=True
        ).astype(jnp.float32),
        lax.psum_scatter(
            second_gain_gradient.astype(jnp.bfloat16), "seq", scatter_dimension=0, tiled=True
        ).astype(jnp.float32),
    )
    owned = (
        lax.psum_scatter(
            partial_value[0].astype(jnp.bfloat16), "ctx", scatter_dimension=1, tiled=True
        ).astype(jnp.float32),
        lax.psum_scatter(
            partial_value[1].astype(jnp.bfloat16), "ctx", scatter_dimension=1, tiled=True
        ).astype(jnp.float32),
        lax.psum_scatter(
            partial_value[2].astype(jnp.bfloat16), "ctx", scatter_dimension=1, tiled=True
        ).astype(jnp.float32),
        lax.psum_scatter(
            partial_value[3].astype(jnp.bfloat16), "ctx", scatter_dimension=1, tiled=True
        ).astype(jnp.float32),
        lax.psum_scatter(
            partial_value[4].astype(jnp.bfloat16), "ctx", scatter_dimension=1, tiled=True
        ).astype(jnp.float32),
        lax.psum_scatter(
            partial_value[5].astype(jnp.bfloat16), "ctx", scatter_dimension=1, tiled=True
        ).astype(jnp.float32),
        lax.psum_scatter(
            partial_value[6].astype(jnp.bfloat16), "ctx", scatter_dimension=1, tiled=True
        ).astype(jnp.float32),
    )
    gains_owned = lax.psum((partial_value[7], partial_value[8]), "ctx")
    final_grads = owned + gains_owned
    return (
        output,
        input_grad,
        final_grads[7],
        final_grads[0],
        final_grads[1],
        final_grads[2],
        final_grads[3],
        final_grads[8],
        final_grads[4],
        final_grads[5],
        final_grads[6],
    )


def my_place():
    seq_at, ctx_at = lax.axis_index("seq"), lax.axis_index("ctx")
    return ctx_at // 2, lax.rem(ctx_at, 2), seq_at // 2, lax.rem(seq_at, 2)


def flipped(at, flip):
    return 1 - at if flip else at


def lane_ids(rows):
    return lax.broadcasted_iota(jnp.int32, (rows, LANES), 1)


def rotate_halves(tile, cosine, sine):
    lower = lax.rem(lane_ids(tile.shape[0]), HEAD_SIZE) < HEAD_SIZE // 2
    swapped = jnp.where(
        lower, pltpu.roll(tile, LANES - HEAD_SIZE // 2, 1), pltpu.roll(tile, HEAD_SIZE // 2, 1)
    )
    return tile * cosine + swapped * sine


def pair_tiles(natural):
    lower = lane_ids(natural[0].shape[0]) < HEAD_SIZE
    tiles = []
    for pair in range(3):
        for member in range(3):
            one, two = 6 * pair + member, 6 * pair + 3 + member
            left, right = natural[one // 2], natural[two // 2]
            if one % 2:
                left, right = pltpu.roll(left, HEAD_SIZE, 1), pltpu.roll(right, HEAD_SIZE, 1)
            tiles.append(jnp.where(lower, left, right))
    return tiles


def natural_tiles(paired):
    lower = lane_ids(paired[0].shape[0]) < HEAD_SIZE
    tiles = []
    for at in range(9):
        sides = []
        for side in range(2):
            head = 2 * at + side
            tile = paired[head // 6 * 3 + head % 3]
            if (head % 6) // 3 != side:
                tile = pltpu.roll(tile, HEAD_SIZE, 1)
            sides.append(tile)
        tiles.append(jnp.where(lower, sides[0], sides[1]))
    return tiles


def normalized(rows):
    factor = lax.rsqrt(jnp.mean(rows * rows, axis=-1, keepdims=True) + EPSILON)
    return factor, rows * factor


def vmem_specs(count):
    return [pl.BlockSpec(memory_space=pltpu.VMEM)] * count


def any_specs(count):
    return [pl.BlockSpec(memory_space=pl.ANY)] * count


def cost(flops, moved, transcendentals=0):
    return pl.CostEstimate(flops=int(flops), bytes_accessed=int(moved), transcendentals=int(transcendentals))


def params():
    return pltpu.CompilerParams(vmem_limit_bytes=VMEM_LIMIT)


def masked_pair(block, half, other):
    inside = (lane_ids(block.shape[0]) < HEAD_SIZE) == (half == 0)
    return jnp.where(inside, block.astype(F32), other)


def core_rows(core):
    return pl.ds(pl.multiple_of(core * 256, 256), 256)


def turned_blocks(matrix, parts):
    flat = matrix.astype(F32).T.astype(BF16)
    return flat.reshape(parts, flat.shape[0] // parts, flat.shape[1])


class Gathering:
    def __init__(self, own, full, lanes, block, sends, arrivals, corner_over_x=()):
        self.own, self.full, self.block, self.sends, self.arrivals = own, full, block, sends, arrivals
        self.corner_over_x, self.lanes = corner_over_x, lanes
        self.started = []

    def place(self, t, dx, dy, dcore=0):
        z, x, y, core = my_place()
        ctx_block = lax.rem(z - t + Z_SIZE, Z_SIZE) * 2 + flipped(x, dx)
        first, second = self.block(ctx_block, flipped(y, dy) * 2 + flipped(core, dcore))
        return self.full.at[first, second, :, self.lanes]

    def copy(self, source, target, number, axis):
        return pltpu.make_async_remote_copy(
            src_ref=source,
            dst_ref=target,
            send_sem=self.sends.at[number],
            recv_sem=self.arrivals.at[number],
            device_id=neighbour(axis),
            device_id_type=pl.DeviceIdType.MESH,
        )

    def send(self, piece, number, axis):
        place = self.place(*piece)
        source = self.own.at[:, self.lanes] if piece == (0, 0, 0) else place
        self.copy(source, place, number, axis).start()
        self.started.append((piece, number))

    def wait(self, piece, number, dcore=0):
        place = self.place(*piece, dcore)
        self.copy(place, place, number, "core").wait_recv()

    def to_core(self, piece):
        t, dx, dy = piece
        self.send(piece, 15 + 4 * t + 2 * dx + dy, "core")

    def over_z(self, t):
        if t < Z_SIZE - 1:
            self.send((t, 0, 0), t, "z")

    def over_plane(self, t):
        self.send((t, 0, 0), 3 + t, "x")
        self.send((t, 0, 0), 7 + t, "y")

    def begin(self):
        self.over_z(0)
        self.over_plane(0)
        self.to_core((0, 0, 0))

    def pass_on(self, t):
        self.wait((t, 0, 0), t - 1)
        self.over_z(t)
        self.over_plane(t)
        self.to_core((t, 0, 0))

    def sides(self, t):
        self.wait((t, 1, 0), 3 + t)
        if t not in self.corner_over_x:
            self.send((t, 1, 0), 11 + t, "y")
        self.to_core((t, 1, 0))
        self.wait((t, 0, 1), 7 + t)
        if t in self.corner_over_x:
            self.send((t, 0, 1), 11 + t, "x")
        self.to_core((t, 0, 1))

    def corner(self, t):
        self.wait((t, 1, 1), 11 + t)
        self.to_core((t, 1, 1))

    def finish(self, t):
        for dx in range(2):
            for dy in range(2):
                self.wait((t, dx, dy), 15 + 4 * t + 2 * dx + dy, 1)

    def drain(self):
        for piece, number in self.started:
            place = self.place(*piece)
            self.copy(place, place, number, "core").wait_send()


class PlaneGathering(Gathering):
    def begin(self):
        self.send((0, 0, 0), 0, "x")
        self.send((0, 0, 0), 1, "y")
        self.to_core((0, 0, 0))

    def plane_sides(self):
        self.wait((0, 1, 0), 0)
        self.send((0, 1, 0), 2, "y")
        self.to_core((0, 1, 0))
        self.wait((0, 0, 1), 1)
        self.to_core((0, 0, 1))

    def plane_corner(self):
        self.wait((0, 1, 1), 2)
        self.to_core((0, 1, 1))

    def ring(self, t):
        for dx in range(2):
            for dy in range(2):
                number = 3 + 4 * t + 2 * dx + dy
                if t:
                    self.wait((t, dx, dy), number - 4)
                if t < Z_SIZE - 1:
                    self.send((t, dx, dy), number, "z")
                if t:
                    self.to_core((t, dx, dy))


def neighbour(axis):
    z, x, y, core = my_place()
    if axis == "z":
        z = lax.rem(z + 1, Z_SIZE)
    elif axis == "z_back":
        z = lax.rem(z + Z_SIZE - 1, Z_SIZE)
    elif axis == "z_two":
        z = lax.rem(z + 2, Z_SIZE)
    elif axis == "x":
        x = 1 - x
    elif axis == "y":
        y = 1 - y
    elif axis == "core":
        core = 1 - core
    elif axis == "y_core":
        y, core = 1 - y, 1 - core
    return (y * 2 + core, z * 2 + x)


def meet(axes):
    barrier = pltpu.get_barrier_semaphore()
    for axis in axes:
        pl.semaphore_signal(barrier, inc=1, device_id=neighbour(axis), device_id_type=pl.DeviceIdType.MESH)
    pl.semaphore_wait(barrier, len(axes))


def front_kernel(
    prefix,
    frequency,
    query_weight,
    key_weight,
    value_weight,
    out_weight,
    gate_weight,
    up_weight,
    down_weight,
    both_gains,
    tokens,
    cotangent,
    qkv_out,
    pairs_out,
    rows_turned,
    both_grads,
    hidden_both,
    attended_both,
    cot_turned,
    proj_turned,
    query_out,
    attended,
    log_total,
    gain_out,
    output,
    mixed_grad,
    attended_grad,
    gain_grad,
    cosine,
    sine,
    limit,
    qkv_own,
    down_own,
    up_own,
    gains_own,
    qkv,
    down,
    up,
    pairs,
    gates,
    ups,
    wide,
    keys,
    values,
    gains,
    rows_two,
    rows_stage,
    hidden,
    attended_rows,
    grads,
    cot_stage,
    proj_stage,
    qkv_sends,
    qkv_arrivals,
    down_sends,
    down_arrivals,
    plane_sends,
    plane_arrivals,
    up_sends,
    up_arrivals,
    pair_sends,
    pair_arrivals,
    gain_sends,
    gain_arrivals,
    own_sems,
    core_sends,
    core_arrivals,
    core_own_sems,
):
    z, x, y, core = my_place()
    seq_at, ctx_at = y * 2 + core, z * 2 + x
    by_ctx, by_seq = (lambda ctx, seq: (ctx, seq)), (lambda ctx, seq: (seq, ctx))
    first = Gathering(qkv_own, qkv, slice(0, 240), by_ctx, qkv_sends, qkv_arrivals, (1, 3))
    plane = PlaneGathering(down_own, down, slice(0, PLANE_LANES), by_seq, plane_sends, plane_arrivals)
    rest = (
        Gathering(down_own, down, slice(PLANE_LANES, 1056), by_seq, down_sends, down_arrivals, (3,)),
        Gathering(up_own, up, slice(0, 768), by_ctx, up_sends, up_arrivals, (3,)),
    )
    mine, theirs, width = core_rows(core), core_rows(1 - core), tokens.shape[1]
    turned = jnp.concatenate([query_weight[...], key_weight[...], value_weight[...]], axis=0)
    qkv_own[...] = turned.astype(F32).T.astype(BF16)
    gains_own[...] = jnp.concatenate([both_gains[...], jnp.zeros((6, 288), F32)], axis=0)
    down_own[:, :768] = down_weight[...]
    down_own[:, 768:] = out_weight[...]
    up_own[:, :384] = gate_weight[...]
    up_own[:, 384:] = up_weight[...]
    meet(("z", "z_back", "x", "y", "core", "y_core"))
    first.begin()
    gain_copies = []
    for number, axis in enumerate(("core", "y", "y_core")):
        copy = pltpu.make_async_remote_copy(
            src_ref=gains_own,
            dst_ref=gains.at[seq_at],
            send_sem=gain_sends.at[number],
            recv_sem=gain_arrivals.at[number],
            device_id=neighbour(axis),
            device_id_type=pl.DeviceIdType.MESH,
        )
        copy.start()
        gain_copies.append(copy)
    own_copies = [
        pltpu.make_async_copy(source, target, own_sems.at[number])
        for number, (source, target) in enumerate(
            (
                (qkv_own, first.place(0, 0, 0)),
                (down_own, down.at[seq_at, ctx_at]),
                (up_own, up.at[ctx_at, seq_at]),
                (gains_own, gains.at[seq_at]),
            )
        )
    ]
    for copy in own_copies:
        copy.start()
    places = ctx_at * 256 + lax.broadcasted_iota(jnp.int32, (256, LANES), 0)
    angles = places.astype(F32) * frequency[...]
    lower = lax.rem(lane_ids(256), HEAD_SIZE) < HEAD_SIZE // 2
    sines = jnp.sin(angles)
    cosine[...] = jnp.cos(angles)
    sine[...] = jnp.where(lower, -sines, sines)
    limit[...] = jnp.maximum(ctx_at * 256 + 1 + lax.broadcasted_iota(jnp.int32, (1, 256), 1), prefix[0])
    for t in range(1, Z_SIZE):
        first.pass_on(t)
        if t == 1:
            plane.begin()
        if t == Z_SIZE - 2:
            for group in rest:
                group.over_z(0)
        first.sides(t - 1)
    plane.plane_sides()
    first.sides(Z_SIZE - 1)
    for group in rest:
        group.over_plane(0)
        group.to_core((0, 0, 0))
    plane.plane_corner()
    plane.ring(0)
    for number, flips in enumerate(((0, 1), (1, 0), (1, 1))):
        place = gains.at[flipped(y, flips[0]) * 2 + flipped(core, flips[1])]
        pltpu.make_async_remote_copy(
            src_ref=place,
            dst_ref=place,
            send_sem=gain_sends.at[number],
            recv_sem=gain_arrivals.at[number],
            device_id=neighbour("core"),
            device_id_type=pl.DeviceIdType.MESH,
        ).wait_recv()
    for copy in own_copies:
        copy.wait()
    for row in range(4):
        gain_out[:, row * 288 : (row + 1) * 288] = gains[row]
    _, hat = normalized(tokens[...].astype(F32))
    rows = (hat * gain_out[0:1, :]).astype(BF16)
    for t in range(Z_SIZE):
        first.corner(t)
    for group in rest:
        group.pass_on(1)
    for t in range(Z_SIZE):
        first.finish(t)

    def multiply(ctx_block, carry):
        matrix = qkv[ctx_block].reshape(tokens.shape[1], 240)
        gates[ctx_block, :, :240] = jnp.dot(rows, matrix, preferred_element_type=F32)
        return carry

    lax.fori_loop(0, 8, multiply, 0)
    save_qkv = pltpu.make_async_copy(qkv, qkv_out, own_sems.at[4])
    save_qkv.start()
    q_part, kv_part = 144, 48
    for at in range(8):
        wide[:, at * q_part : (at + 1) * q_part] = gates[at, :, :q_part]
        wide[:, 1152 + at * kv_part : 1152 + (at + 1) * kv_part] = gates[at, :, q_part : q_part + kv_part]
        wide[:, 1536 + at * kv_part : 1536 + (at + 1) * kv_part] = gates[at, :, q_part + kv_part : 240]
    cos_tile, sin_tile = cosine[...], sine[...]
    for pair in range(3):
        key_tile = wide[:, 1152 + pair * LANES : 1152 + (pair + 1) * LANES]
        pairs[ctx_at, :, 2 * pair * LANES : (2 * pair + 1) * LANES] = rotate_halves(
            key_tile, cos_tile, sin_tile
        ).astype(BF16)
        pairs[ctx_at, :, (2 * pair + 1) * LANES : (2 * pair + 2) * LANES] = wide[
            :, 1536 + pair * LANES : 1536 + (pair + 1) * LANES
        ].astype(BF16)
    natural = [
        rotate_halves(wide[:, at * LANES : (at + 1) * LANES], cos_tile, sin_tile) * HEAD_SIZE**-0.5
        for at in range(9)
    ]
    for at, tile in enumerate(pair_tiles(natural)):
        query_out[at] = tile.astype(BF16)

    pair_copies = []

    def pair_place(t, dx):
        return pairs.at[lax.rem(z - t + Z_SIZE, Z_SIZE) * 2 + flipped(x, dx)]

    def pair_copy(place, number, axis):
        return pltpu.make_async_remote_copy(
            src_ref=place,
            dst_ref=place,
            send_sem=pair_sends.at[number],
            recv_sem=pair_arrivals.at[number],
            device_id=neighbour(axis),
            device_id_type=pl.DeviceIdType.MESH,
        )

    def pair_pass(t):
        if t:
            pair_copy(pair_place(t, 0), t - 1, "z").wait_recv()
        for number, axis in ((t, "z"), (3 + t, "x")):
            if axis == "x" or t < Z_SIZE - 1:
                copy = pair_copy(pair_place(t, 0), number, axis)
                copy.start()
                pair_copies.append(copy)

    def in_rest(step):
        for group in rest:
            step(group)

    pair_pass(0)
    in_rest(lambda group: group.pass_on(2))
    pair_pass(1)
    in_rest(lambda group: group.sides(0))
    pair_pass(2)
    plane.ring(1)
    in_rest(lambda group: group.sides(1))
    pair_pass(3)
    cot_stage[...] = turned_blocks(cotangent[...], 8)
    in_rest(lambda group: group.pass_on(3))
    in_rest(lambda group: group.sides(2))
    for t in range(Z_SIZE):
        pair_copy(pair_place(t, 1), 3 + t, "x").wait_recv()
    save_pairs = pltpu.make_async_copy(pairs, pairs_out, own_sems.at[5])
    save_pairs.start()

    key_ids = lax.broadcasted_iota(jnp.int32, (256, tokens.shape[0]), 0)

    def attend_pair(pair):
        key_lanes = pl.ds(pl.multiple_of(pair * 256, 256), LANES)
        value_lanes = pl.ds(pl.multiple_of(pair * 256 + LANES, LANES), LANES)
        for at in range(8):
            for half in range(2):
                keys[half, at] = masked_pair(pairs[at, :, key_lanes], half, 0.0).astype(BF16)
                values[half, at] = masked_pair(pairs[at, :, value_lanes], half, 1.0).T.astype(BF16)

        def attend_member(member, carry):
            tile = query_out[3 * pair + member]
            parts = []
            for half in range(2):
                top = None
                for at in range(8):
                    part = lax.dot_general(keys[half, at], tile, NT, preferred_element_type=F32)
                    part = jnp.where(key_ids < limit[...] - at * 256, part, -1e30)
                    ups[at, :, :256] = part
                    block_top = jnp.max(part, axis=0, keepdims=True)
                    top = block_top if top is None else jnp.maximum(top, block_top)
                total = jnp.zeros((LANES, tile.shape[0]), F32)
                for at in range(8):
                    weight = jnp.exp(ups[at, :, :256] - top).astype(BF16)
                    total = total + jnp.dot(values[half, at], weight, preferred_element_type=F32)
                norm = total[HEAD_SIZE : HEAD_SIZE + 1] if half == 0 else total[:1]
                log_total[3 * pair + member, half : half + 1, :] = top + jnp.log(norm)
                own = total[:HEAD_SIZE] if half == 0 else total[HEAD_SIZE:]
                parts.append(own / norm)
            attended[3 * pair + member] = jnp.concatenate(parts, axis=0).T.astype(BF16)
            return carry

        lax.fori_loop(0, 3, attend_member, 0)

    started, own_copies = [], []

    def core_copy(source, target, number):
        return pltpu.make_async_remote_copy(
            src_ref=source,
            dst_ref=target,
            send_sem=core_sends.at[number],
            recv_sem=core_arrivals.at[number],
            device_id=neighbour("core"),
            device_id_type=pl.DeviceIdType.MESH,
        )

    def keep(source, target, number):
        copy = pltpu.make_async_copy(source, target, core_own_sems.at[number])
        copy.start()
        own_copies.append(copy)

    def share(source, target, number):
        copy = core_copy(source, target, number)
        copy.start()
        started.append(copy)

    def deal(stage, target_of, number):
        for y_at in range(2):
            keep(stage.at[y_at * 2 + core], target_of(y_at), number + y_at)
            share(stage.at[y_at * 2 + 1 - core], target_of(y_at), number + y_at)

    def attend_and_pass(pair, carry):
        attend_pair(pair)

        @pl.when(pair == 0)
        def _():
            plane.ring(2)
            in_rest(lambda group: group.sides(3))

        @pl.when(pair == 1)
        def _():
            in_rest(lambda group: group.corner(0))
            in_rest(lambda group: group.corner(1))

        return carry

    lax.fori_loop(0, 3, attend_and_pass, 0)
    keep(cot_stage, cot_turned.at[:, :, mine], 1)
    share(cot_stage, cot_turned.at[:, :, mine], 1)
    in_rest(lambda group: group.corner(2))
    for at, tile in enumerate(natural_tiles([attended[at].astype(F32) for at in range(9)])):
        wide[:, at * LANES : (at + 1) * LANES] = tile
    for row in range(4):
        attended_rows[row] = wide[:, row * 288 : (row + 1) * 288].astype(BF16)
    rest[0].corner(3)
    for t in range(Z_SIZE):
        rest[0].finish(t)

    def out_block(row):
        return down[row, :, :, 768:].reshape(width, 288)

    def down_block(row):
        return down[row, :, :, :768].reshape(width, 768)

    def gate_block(block):
        return up[block, :, :, :384].reshape(width, 384)

    def up_block(block):
        return up[block, :, :, 384:].reshape(width, 384)

    mixed_grad[...] = tokens[...].astype(F32)
    for row in range(4):
        mixed_grad[...] += lax.dot_general(attended_rows[row], out_block(row), NT, preferred_element_type=F32)
    rest[1].corner(3)
    plane.ring(3)
    deal(attended_rows, lambda y_at: attended_both.at[y_at, mine], 2)
    factor, hat = normalized(mixed_grad[...])
    gain_row = gain_out[1:2, :]
    rows_two[...] = (hat * gain_row).astype(BF16)
    wide[:, :1152] = hat
    for t in range(Z_SIZE):
        rest[1].finish(t)

        def gate_and_up(dx, carry, t=t):
            block = lax.rem(z - t + Z_SIZE, Z_SIZE) * 2 + lax.rem(x + dx, 2)
            gates[block] = jnp.dot(rows_two[...], gate_block(block), preferred_element_type=F32)
            ups[block] = jnp.dot(rows_two[...], up_block(block), preferred_element_type=F32)
            return carry

        lax.fori_loop(0, 2, gate_and_up, 0)
    rows_stage[...] = turned_blocks(rows_two[...], 4)
    for t in range(Z_SIZE):
        plane.finish(t)
    deal(rows_stage, lambda y_at: rows_turned.at[y_at, :, mine], 4)

    def feed_forward(row, carry):
        back = jnp.dot(cotangent[...], down_block(row), preferred_element_type=F32)
        for side in range(2):
            block = 2 * row + side
            gate, up_part = gates[block], ups[block]
            sigmoid = 1.0 / (1.0 + jnp.exp(-gate))
            active = gate * sigmoid
            hidden[row, :, side * 384 : (side + 1) * 384] = (active * up_part).astype(BF16)
            part = back[:, side * 384 : (side + 1) * 384]
            grads[block, :, :384] = (part * up_part * sigmoid * (1.0 + gate * (1.0 - sigmoid))).astype(BF16)
            grads[block, :, 384:] = (part * active).astype(BF16)
        mixed_grad[...] += lax.dot_general(hidden[row], down_block(row), NT, preferred_element_type=F32)
        return carry

    lax.fori_loop(0, 4, feed_forward, 0)
    output[...] = mixed_grad[...].astype(BF16)
    keep(grads, both_grads.at[:, mine, :], 0)
    share(grads, both_grads.at[:, mine, :], 0)
    deal(hidden, lambda y_at: hidden_both.at[y_at, mine], 6)
    mixed_grad[...] = jnp.zeros_like(mixed_grad)

    def rows_back(block, carry):
        part = lax.dot_general(grads[block, :, :384], gate_block(block), NT, preferred_element_type=F32)
        part = part + lax.dot_general(grads[block, :, 384:], up_block(block), NT, preferred_element_type=F32)
        mixed_grad[...] += part
        return carry

    lax.fori_loop(0, 8, rows_back, 0)
    grad_two, hat = mixed_grad[...], wide[:, :1152]
    gain_grad[...] = jnp.sum(grad_two * hat, axis=0, keepdims=True)
    scaled = grad_two * gain_row
    total = cotangent[...].astype(F32) + factor * (
        scaled - hat * jnp.mean(scaled * hat, axis=-1, keepdims=True)
    )
    mixed_grad[...] = total
    rows_two[...] = total.astype(BF16)
    proj_stage[...] = turned_blocks(rows_two[...], 8)
    for row in range(4):
        wide[:, row * 288 : (row + 1) * 288] = jnp.dot(
            rows_two[...], out_block(row), preferred_element_type=F32
        )
    keep(proj_stage, proj_turned.at[:, :, mine], 8)
    share(proj_stage, proj_turned.at[:, :, mine], 8)
    tiles = pair_tiles([wide[:, at * LANES : (at + 1) * LANES] for at in range(9)])
    for at, tile in enumerate(tiles):
        attended_grad[at] = tile.astype(BF16)
    for group in rest + (first, plane):
        group.drain()
    for copy in pair_copies + gain_copies + started:
        copy.wait_send()
    for copy in own_copies + [save_qkv, save_pairs]:
        copy.wait()
    places = [both_grads.at[:, theirs, :], cot_turned.at[:, :, theirs]]
    places += [attended_both.at[y_at, theirs] for y_at in range(2)]
    places += [rows_turned.at[y_at, :, theirs] for y_at in range(2)]
    places += [hidden_both.at[y_at, theirs] for y_at in range(2)]
    places.append(proj_turned.at[:, :, theirs])
    for number, place in enumerate(places):
        core_copy(place, place, number).wait_recv()


def front(prefix, frequency, weights, gains, tokens, cotangent):
    rows, width = tokens.shape
    dma = pltpu.SemaphoreType.DMA
    shape = jax.ShapeDtypeStruct
    qkv_own, down_own, up_own = (288, 240), (144, 1056), (288, 768)
    return pl.pallas_call(
        front_kernel,
        out_shape=(
            shape((8, 4) + qkv_own, BF16),
            shape((8, rows, 768), BF16),
            shape((2, 288, 2 * rows), BF16),
            shape((8, 2 * rows, 768), BF16),
            shape((2, 2 * rows, 768), BF16),
            shape((2, 2 * rows, 288), BF16),
            shape((8, 144, 2 * rows), BF16),
            shape((8, 144, 2 * rows), BF16),
            shape((9, rows, LANES), BF16),
            shape((9, rows, LANES), BF16),
            shape((9, 2, rows), F32),
            shape((8, width), F32),
            shape((rows, width), BF16),
            shape((rows, width), F32),
            shape((9, rows, LANES), BF16),
            shape((1, width), F32),
            shape((rows, LANES), F32),
            shape((rows, LANES), F32),
            shape((1, rows), jnp.int32),
        ),
        in_specs=[pl.BlockSpec(memory_space=pltpu.SMEM)] + vmem_specs(11),
        out_specs=tuple(any_specs(8) + vmem_specs(11)),
        scratch_shapes=[
            pltpu.VMEM(qkv_own, BF16),
            pltpu.VMEM(down_own, BF16),
            pltpu.VMEM(up_own, BF16),
            pltpu.VMEM((8, 288), F32),
            pltpu.VMEM((8, 4) + qkv_own, BF16),
            pltpu.VMEM((4, 8) + down_own, BF16),
            pltpu.VMEM((8, 4) + up_own, BF16),
            pltpu.VMEM((8, rows, 768), BF16),
            pltpu.VMEM((8, rows, 384), F32),
            pltpu.VMEM((8, rows, 384), F32),
            pltpu.VMEM((rows, 1920), F32),
            pltpu.VMEM((2, 8, 256, LANES), BF16),
            pltpu.VMEM((2, 8, LANES, 256), BF16),
            pltpu.VMEM((4, 8, 288), F32),
            pltpu.VMEM((rows, width), BF16),
            pltpu.VMEM((4, 288, rows), BF16),
            pltpu.VMEM((4, rows, 768), BF16),
            pltpu.VMEM((4, rows, 288), BF16),
            pltpu.VMEM((8, rows, 768), BF16),
            pltpu.VMEM((8, 144, rows), BF16),
            pltpu.VMEM((8, 144, rows), BF16),
        ]
        + [dma((31,))] * 8
        + [dma((7,))] * 2
        + [dma((3,))] * 2
        + [dma((6,))]
        + [dma((9,))] * 3,
        compiler_params=pltpu.CompilerParams(
            vmem_limit_bytes=VMEM_LIMIT, collective_id=1, has_side_effects=True
        ),
        cost_estimate=cost(4 * 18 * rows * 2048 * 128 * 4, 4e8, 18 * rows * 2048),
        name="front",
    )(prefix, frequency, *weights, gains, tokens, cotangent)


class Scattering:
    def __init__(self, buffers, sends, arrivals, out, piece, corners):
        self.corner, self.side_x, self.side_y, self.near_x, self.near_y, self.ring = buffers
        self.sends, self.arrivals, self.out, self.piece, self.corners = sends, arrivals, out, piece, corners

    def copy(self, source, target, number, axis):
        return pltpu.make_async_remote_copy(
            src_ref=source,
            dst_ref=target,
            send_sem=self.sends.at[number],
            recv_sem=self.arrivals.at[number],
            device_id=neighbour(axis),
            device_id_type=pl.DeviceIdType.MESH,
        )

    def corner_copies(self, t, axes=("x", "y")):
        for number, (axis, lanes) in enumerate(self.corners):
            if axis in axes:
                target = self.side_x if axis == "y" else self.side_y
                yield self.copy(self.corner.at[t, :, lanes], target.at[t, :, lanes], 4 * number + t, axis)

    def side_copy(self, t, axis):
        source, target, first = (self.side_x, self.near_x, 8) if axis == "x" else (self.side_y, self.near_y, 12)
        return self.copy(source.at[t], target.at[t], first + t, axis)

    def ring_copy(self, t):
        return self.copy(self.near_x.at[t], self.ring.at[t - 1], 15 + t, "z_back")

    def corner_step(self, t):
        self.piece(t, 1, 1, self.corner.at[t], lambda lanes: [])
        for copy in self.corner_copies(t):
            copy.start()

    def side_step(self, t, axis):
        came = "y" if axis == "x" else "x"
        for copy in self.corner_copies(t, (came,)):
            copy.wait_recv()
        side = (self.side_x if axis == "x" else self.side_y).at[t]
        ranges = [lanes for at, lanes in self.corners if at == came]

        def addend(lanes):
            return [side[:, lanes]] if any(at.start <= lanes.start and lanes.stop <= at.stop for at in ranges) else []

        self.piece(t, int(axis == "x"), int(axis == "y"), side, addend)
        self.side_copy(t, axis).start()

    def near_step(self, t):
        self.side_copy(t, "x").wait_recv()
        self.side_copy(t, "y").wait_recv()
        if t < Z_SIZE - 1:
            self.ring_copy(t + 1).wait_recv()

        def addend(lanes):
            parts = [self.near_x[t, :, lanes], self.near_y[t, :, lanes]]
            return parts + ([self.ring[t, :, lanes]] if t < Z_SIZE - 1 else [])

        self.piece(t, 0, 0, self.near_x.at[t] if t else self.out, addend)
        if t:
            self.ring_copy(t).start()

    def drain(self):
        for t in range(Z_SIZE):
            for copy in self.corner_copies(t):
                copy.wait_send()
            self.side_copy(t, "x").wait_send()
            self.side_copy(t, "y").wait_send()
            if t:
                self.ring_copy(t).wait_send()


class PlaneScattering:
    def __init__(self, buffers, sends, arrivals, out, piece):
        self.sums, self.corner, self.near_x, self.near_y = buffers
        self.sends, self.arrivals, self.out, self.piece = sends, arrivals, out, piece

    def copy(self, source, target, number, axis):
        return pltpu.make_async_remote_copy(
            src_ref=source,
            dst_ref=target,
            send_sem=self.sends.at[number],
            recv_sem=self.arrivals.at[number],
            device_id=neighbour(axis),
            device_id_type=pl.DeviceIdType.MESH,
        )

    def ring_copy(self, t, dx, dy):
        return self.copy(
            self.sums.at[t, dx, dy], self.sums.at[t - 1, dx, dy], 4 * (t - 1) + 2 * dx + dy, "z_back"
        )

    def plane_copies(self):
        return (
            self.copy(self.sums.at[0, 1, 1], self.corner, 12, "y"),
            self.copy(self.sums.at[0, 1, 0], self.near_x, 13, "x"),
            self.copy(self.sums.at[0, 0, 1], self.near_y, 14, "y"),
        )

    def ring_step(self, t, first=False):
        def one(number, carry):
            dx, dy = number // 2, lax.rem(number, 2)
            target = self.sums.at[t, dx, dy]
            if not first:
                self.ring_copy(t + 1, dx, dy).wait_recv()
            self.piece(t, dx, dy, target, lambda lanes: [] if first else [target[:, lanes]])

            @pl.when(t > 0)
            def _():
                self.ring_copy(t, dx, dy).start()

            return carry

        lax.fori_loop(0, 4, one, 0)

    def plane_start(self):
        corner, _, side_y = self.plane_copies()
        corner.start()
        side_y.start()

    def plane_side(self):
        corner, side_x, _ = self.plane_copies()
        corner.wait_recv()
        side = self.sums.at[0, 1, 0]
        side[...] = (side[...].astype(F32) + self.corner[...].astype(F32)).astype(BF16)
        side_x.start()

    def plane_end(self):
        _, side_x, side_y = self.plane_copies()
        side_x.wait_recv()
        side_y.wait_recv()
        total = self.sums[0, 0, 0].astype(F32) + self.near_x[...].astype(F32)
        self.out[...] = total + self.near_y[...].astype(F32)

    def drain(self):
        for t in range(1, Z_SIZE):
            for dx in range(2):
                for dy in range(2):
                    self.ring_copy(t, dx, dy).wait_send()
        for copy in self.plane_copies():
            copy.wait_send()


def back_kernel(
    rows_turned,
    both_grads,
    hidden,
    attended_rows,
    cot_turned,
    proj_turned,
    query,
    attended,
    grad,
    log_total,
    limit,
    cosine,
    sine,
    pairs,
    tokens,
    gains,
    second_gain,
    weights,
    mixed_grad,
    down_out,
    up_out,
    qkv_out,
    input_grad,
    gain_out,
    *refs,
):
    down_buffers, up_buffers, qkv_buffers, plane_buffers = refs[:6], refs[6:12], refs[12:18], refs[18:22]
    (
        keys,
        keys_turned,
        values,
        query_halves,
        grad_halves,
        turned_sum,
        shifts,
        pair_parts,
        pair_near,
        pair_ring,
        query_grad,
        wide,
        pieces,
        first_stage,
        first_turned,
        weight_slots,
        gain_sum,
        gain_came,
    ) = refs[22:40]
    (
        down_sends,
        down_arrivals,
        up_sends,
        up_arrivals,
        qkv_sends,
        qkv_arrivals,
        plane_sends,
        plane_arrivals,
        pair_sends,
        pair_arrivals,
        core_sends,
        core_arrivals,
        gain_sends,
        gain_arrivals,
        own_sems,
        weight_sems,
    ) = refs[40:]
    z, x, y, core = my_place()
    mine, theirs = core_rows(core), core_rows(1 - core)
    rows, width = tokens.shape

    def flip_if(at, flip):
        return flipped(at, flip) if isinstance(flip, int) else lax.rem(at + flip, 2)

    def ctx_of(t, dx):
        return lax.rem(z - t + Z_SIZE, Z_SIZE) * 2 + flip_if(x, dx)

    def put(target, lanes, value, addend):
        for part in addend(lanes):
            value = value + part.astype(F32)
        target[:, lanes] = value.astype(target.dtype)

    def plane_piece(t, dx, dy, target, addend):
        block, row = ctx_of(t, dx), flip_if(y, dy)
        for lanes in (slice(0, 256), slice(256, PLANE_LANES)):
            value = jnp.dot(cot_turned[block], hidden[row, :, lanes], preferred_element_type=F32)
            put(target, lanes, value, addend)

    def down_piece(t, dx, dy, target, addend):
        block, row = ctx_of(t, dx), flipped(y, dy)
        split = 768 - PLANE_LANES
        value = jnp.dot(cot_turned[block], hidden[row, :, PLANE_LANES:], preferred_element_type=F32)
        put(target, slice(0, split), value, addend)
        value = jnp.dot(proj_turned[block], attended_rows[row], preferred_element_type=F32)
        put(target, slice(split, split + 288), value, addend)

    def up_piece(t, dx, dy, target, addend):
        block, row = ctx_of(t, dx), flipped(y, dy)
        for lanes in (slice(0, 384), slice(384, 768)):
            value = jnp.dot(rows_turned[row], both_grads[block, :, lanes], preferred_element_type=F32)
            put(target, lanes, value, addend)

    def qkv_piece(t, dx, dy, target, addend):
        block, row = ctx_of(t, dx), flipped(y, dy)
        value = jnp.dot(first_turned[row], pieces[block], preferred_element_type=F32)
        put(target, slice(0, 240), value, addend)

    plane = PlaneScattering(
        plane_buffers, plane_sends, plane_arrivals, down_out.at[:, :PLANE_LANES], plane_piece
    )
    down = Scattering(
        down_buffers,
        down_sends,
        down_arrivals,
        down_out.at[:, PLANE_LANES:],
        down_piece,
        (("y", slice(0, 1056 - PLANE_LANES)),),
    )
    up = Scattering(
        up_buffers, up_sends, up_arrivals, up_out, up_piece, (("y", slice(0, 384)), ("x", slice(384, 768)))
    )
    qkv = Scattering(qkv_buffers, qkv_sends, qkv_arrivals, qkv_out, qkv_piece, (("y", slice(0, 240)),))

    meet(("z", "z_back", "x", "y", "core", "z_two"))
    residual = pltpu.make_async_copy(mixed_grad, input_grad, own_sems.at[2])
    residual.start()

    plane.ring_step(Z_SIZE - 1, True)

    def corners(number, carry):
        t = Z_SIZE - 1 - number
        down.corner_step(t)
        up.corner_step(t)
        return carry

    lax.fori_loop(0, Z_SIZE, corners, 0)

    factor, hat = normalized(tokens[...].astype(F32))
    first_stage[...] = turned_blocks((hat * gains[0:1, :]).astype(BF16), 4)

    def core_copy(source, target, number):
        return pltpu.make_async_remote_copy(
            src_ref=source,
            dst_ref=target,
            send_sem=core_sends.at[number],
            recv_sem=core_arrivals.at[number],
            device_id=neighbour("core"),
            device_id_type=pl.DeviceIdType.MESH,
        )

    def pair_copy(pair, t, axis):
        if axis == "x":
            source, target, number = pair_parts.at[pair, 1, t], pair_near.at[pair, t], 4 * pair + t
        else:
            source, target, number = pair_parts.at[pair, 0, t], pair_ring.at[pair, t - 1], 11 + 3 * pair + t
        return pltpu.make_async_remote_copy(
            src_ref=source,
            dst_ref=target,
            send_sem=pair_sends.at[number],
            recv_sem=pair_arrivals.at[number],
            device_id=neighbour(axis),
            device_id_type=pl.DeviceIdType.MESH,
        )

    key_ids = lax.broadcasted_iota(jnp.int32, (256, rows), 0)

    def attend_pair_back(pair):
        key_lanes = pl.ds(pl.multiple_of(pair * 256, 256), LANES)
        value_lanes = pl.ds(pl.multiple_of(pair * 256 + LANES, LANES), LANES)
        for at in range(8):
            key_block, value_block = pairs[at, :, key_lanes], pairs[at, :, value_lanes]
            for half in range(2):
                span = slice(256 * half, 256 * (half + 1))
                masked = masked_pair(key_block, half, 0.0)
                keys[at, span] = masked.astype(BF16)
                keys_turned[at, :, span] = masked.T.astype(BF16)
                values[at, span] = masked_pair(value_block, half, 0.0).astype(BF16)
        for member in range(3):
            number = 3 * pair + member
            product = (attended[number].astype(F32) * grad[number].astype(F32)).T
            for half in range(2):
                own = slice(half * HEAD_SIZE, (half + 1) * HEAD_SIZE)
                at = 2 * member + half
                shifts[at] = jnp.sum(product[own], axis=0, keepdims=True)
                query_halves[256 * at : 256 * (at + 1)] = masked_pair(query[number], half, 0.0).astype(BF16)
                grad_halves[256 * at : 256 * (at + 1)] = masked_pair(grad[number], half, 0.0).astype(BF16)
        turned_sum[...] = jnp.zeros_like(turned_sum)

        def block_step(at, carry):
            probs, scores = [], []
            seen = key_ids < limit[...] - at * 256
            for member in range(3):
                number = 3 * pair + member
                parts = lax.dot_general(keys[at], query[number], NT, preferred_element_type=F32)
                backs = lax.dot_general(values[at], grad[number], NT, preferred_element_type=F32)
                for half in range(2):
                    span = slice(256 * half, 256 * (half + 1))
                    part = jnp.where(seen, parts[span], -1e30)
                    prob = jnp.exp(part - log_total[number, half : half + 1, :])
                    scores.append((prob * (backs[span] - shifts[2 * member + half])).astype(BF16))
                    probs.append(prob.astype(BF16))
                turned_sum[member] += jnp.dot(
                    keys_turned[at], jnp.concatenate(scores[-2:], axis=0), preferred_element_type=F32
                )
            t = lax.rem(z - at // 2 + Z_SIZE, Z_SIZE)
            dx = lax.rem(at + x, 2)
            for lanes, left, right in (
                (slice(0, LANES), scores, query_halves),
                (slice(LANES, 2 * LANES), probs, grad_halves),
            ):
                value = jnp.dot(jnp.concatenate(left, axis=1), right[...], preferred_element_type=F32)
                pair_parts[pair, dx, t, :, lanes] = value.astype(BF16)
            return carry

        lax.fori_loop(0, 8, block_step, 0)
        for member in range(3):
            turned = turned_sum[member].T * HEAD_SIZE**-0.5
            query_grad[3 * pair + member] = rotate_halves(turned, cosine[...], -sine[...]).astype(BF16)
        for t in range(Z_SIZE - 1, -1, -1):
            pair_copy(pair, t, "x").start()

    def pair_step(t, pair):
        pair_copy(pair, t, "x").wait_recv()
        total = pair_parts[pair, 0, t].astype(F32) + pair_near[pair, t].astype(F32)
        if t < Z_SIZE - 1:
            pair_copy(pair, t + 1, "z_back").wait_recv()
            total = total + pair_ring[pair, t].astype(F32)
        if t:
            pair_parts[pair, 0, t] = total.astype(BF16)
            pair_copy(pair, t, "z_back").start()
        else:
            key_tile = rotate_halves(total[:, :LANES], cosine[...], -sine[...])
            wide[:, 1152 + pair * LANES : 1152 + (pair + 1) * LANES] = key_tile
            wide[:, 1536 + pair * LANES : 1536 + (pair + 1) * LANES] = total[:, LANES:]

    def side_step(t, axis):
        down.side_step(t, axis)
        up.side_step(t, axis)

    def attend_step(pair, carry):
        attend_pair_back(pair)

        @pl.when(pair == 0)
        def _():
            plane.ring_step(2)
            side_step(3, "y")
            side_step(3, "x")

        @pl.when(pair == 1)
        def _():
            side_step(2, "y")

        return carry

    lax.fori_loop(0, 3, attend_step, 0)
    plane.ring_step(1)
    side_step(2, "x")
    side_step(1, "y")
    first_copies = []
    for y_at in range(2):
        place = first_turned.at[y_at, :, mine]
        own = pltpu.make_async_copy(first_stage.at[y_at * 2 + core], place, own_sems.at[y_at])
        own.start()
        copy = core_copy(first_stage.at[y_at * 2 + 1 - core], place, 1 + y_at)
        copy.start()
        first_copies.append((own, copy))

    for at, tile in enumerate(natural_tiles([query_grad[at].astype(F32) for at in range(9)])):
        wide[:, at * LANES : (at + 1) * LANES] = tile
    q_part, kv_part = 144, 48
    for at in range(8):
        pieces[at, mine, :q_part] = wide[:, at * q_part : (at + 1) * q_part].astype(BF16)
    pair_step(3, 0)
    pair_step(3, 1)
    side_step(1, "x")
    side_step(0, "y")
    side_step(0, "x")
    pair_step(2, 0)
    pair_step(3, 2)
    pair_step(2, 1)
    plane.ring_step(0)
    plane.plane_start()
    pair_step(1, 0)
    pair_step(2, 2)
    pair_step(1, 1)
    pair_step(0, 0)
    pair_step(1, 2)
    down.near_step(3)
    up.near_step(3)
    pair_step(0, 1)
    pair_step(0, 2)
    for at in range(8):
        both = jnp.concatenate(
            [
                wide[:, 1152 + at * kv_part : 1152 + (at + 1) * kv_part],
                wide[:, 1536 + at * kv_part : 1536 + (at + 1) * kv_part],
            ],
            axis=1,
        )
        pieces[at, mine, q_part:] = both.astype(BF16)

    def weight_copy(at):
        return pltpu.make_async_copy(weights.at[at], weight_slots.at[at % 2], weight_sems.at[at % 2])

    weight_copy(0).start()
    weight_copy(1).start()
    piece_copy = core_copy(pieces.at[:, mine, :], pieces.at[:, mine, :], 0)
    piece_copy.start()
    grad_one = wide.at[:, :1152]
    for at in range(8):
        weight_copy(at).wait()
        part = lax.dot_general(
            pieces[at, mine, :], weight_slots[at % 2].reshape(width, 240), NT, preferred_element_type=F32
        )
        grad_one[...] = part if at == 0 else grad_one[...] + part
        if at < 6:
            weight_copy(at + 2).start()
    plane.plane_side()
    core_copy(pieces.at[:, theirs, :], pieces.at[:, theirs, :], 0).wait_recv()
    for y_at, (own, _) in enumerate(first_copies):
        place = first_turned.at[y_at, :, theirs]
        core_copy(place, place, 1 + y_at).wait_recv()
        own.wait()
    def qkv_corners(number, carry):
        qkv.corner_step(Z_SIZE - 1 - number)
        return carry

    lax.fori_loop(0, Z_SIZE, qkv_corners, 0)
    down.near_step(2)
    up.near_step(2)
    def qkv_sides(number, carry):
        for axis in ("y", "x"):
            qkv.side_step(Z_SIZE - 1 - number, axis)
        return carry

    lax.fori_loop(0, Z_SIZE, qkv_sides, 0)
    residual.wait()
    grad_rows = grad_one[...]
    _, hat = normalized(tokens[...].astype(F32))
    first_gain = jnp.sum(grad_rows * hat, axis=0, keepdims=True)
    scaled = grad_rows * gains[0:1, :]
    input_grad[...] += factor * (scaled - hat * jnp.mean(scaled * hat, axis=-1, keepdims=True))
    both = jnp.concatenate([first_gain, second_gain[...], jnp.zeros((6, width), F32)], axis=0)
    for row in range(4):
        gain_sum[0, row] = both[:, row * 288 : (row + 1) * 288]
    gain_copies = []

    def gain_send(source, number, axis):
        copy = pltpu.make_async_remote_copy(
            src_ref=gain_sum.at[source],
            dst_ref=gain_came.at[number],
            send_sem=gain_sends.at[number],
            recv_sem=gain_arrivals.at[number],
            device_id=neighbour(axis),
            device_id_type=pl.DeviceIdType.MESH,
        )
        copy.start()
        gain_copies.append(copy)
        return copy

    plane.plane_end()
    down.near_step(1)
    up.near_step(1)
    gain_send(0, 0, "core").wait_recv()
    gain_sum[0+1] = gain_sum[0] + gain_came[0]
    qkv.near_step(3)
    gain_send(1, 1, "y").wait_recv()
    gain_sum[1+1] = gain_sum[1] + gain_came[1]
    qkv.near_step(2)
    gain_send(2, 2, "x").wait_recv()
    gain_sum[2+1] = gain_sum[2] + gain_came[2]
    qkv.near_step(1)
    ends = [gain_send(3, 3 + number, axis) for number, axis in enumerate(("z", "z_two", "z_back"))]
    down.near_step(0)
    up.near_step(0)
    qkv.near_step(0)
    for copy in ends:
        copy.wait_recv()
    seq_at = y * 2 + core
    gain_out[...] = (gain_sum[3, seq_at] + gain_came[3, seq_at]) + (gain_came[4, seq_at] + gain_came[5, seq_at])
    for group in (down, up, qkv, plane):
        group.drain()
    for pair in range(3):
        for t in range(Z_SIZE):
            pair_copy(pair, t, "x").wait_send()
            if t:
                pair_copy(pair, t, "z_back").wait_send()
    for copy in gain_copies + [piece_copy] + [copy for _, copy in first_copies]:
        copy.wait_send()


def back(weight_inputs, attention_inputs, tokens, gains, second_gain, weights, mixed_grad):
    rows, width = tokens.shape
    dma, arrays = pltpu.SemaphoreType.DMA, []
    for shape in ((144, 1056 - PLANE_LANES), (288, 768), (288, 240)):
        arrays += [pltpu.VMEM((Z_SIZE,) + shape, BF16)] * 5 + [pltpu.VMEM((Z_SIZE - 1,) + shape, BF16)]
    arrays.append(pltpu.VMEM((Z_SIZE, 2, 2, 144, PLANE_LANES), BF16))
    arrays += [pltpu.VMEM((144, PLANE_LANES), BF16)] * 3
    return pl.pallas_call(
        back_kernel,
        out_shape=(
            jax.ShapeDtypeStruct((144, 1056), F32),
            jax.ShapeDtypeStruct((288, 768), F32),
            jax.ShapeDtypeStruct((288, 240), F32),
            jax.ShapeDtypeStruct((rows, width), F32),
            jax.ShapeDtypeStruct((8, 288), F32),
        ),
        in_specs=vmem_specs(17) + any_specs(2),
        out_specs=tuple(vmem_specs(5)),
        scratch_shapes=arrays
        + [
            pltpu.VMEM((8, 512, LANES), BF16),
            pltpu.VMEM((8, LANES, 512), BF16),
            pltpu.VMEM((8, 512, LANES), BF16),
            pltpu.VMEM((6 * rows, LANES), BF16),
            pltpu.VMEM((6 * rows, LANES), BF16),
            pltpu.VMEM((3, LANES, rows), F32),
            pltpu.VMEM((6, 1, rows), F32),
            pltpu.VMEM((3, 2, Z_SIZE, 256, 2 * LANES), BF16),
            pltpu.VMEM((3, Z_SIZE, 256, 2 * LANES), BF16),
            pltpu.VMEM((3, Z_SIZE - 1, 256, 2 * LANES), BF16),
            pltpu.VMEM((9, rows, LANES), BF16),
            pltpu.VMEM((rows, 1920), F32),
            pltpu.VMEM((8, 2 * rows, 240), BF16),
            pltpu.VMEM((4, 288, rows), BF16),
            pltpu.VMEM((2, 288, 2 * rows), BF16),
            pltpu.VMEM((2, 4, 288, 240), BF16),
            pltpu.VMEM((4, 4, 8, 288), F32),
            pltpu.VMEM((6, 4, 8, 288), F32),
        ]
        + [dma((19,))] * 6
        + [dma((15,))] * 2
        + [dma((21,))] * 2
        + [dma((3,))] * 2
        + [dma((6,))] * 2
        + [dma((3,)), dma((2,))],
        compiler_params=pltpu.CompilerParams(
            vmem_limit_bytes=VMEM_LIMIT, collective_id=3, has_side_effects=True
        ),
        cost_estimate=cost(4 * 18 * rows * 2048 * 128 * 10, 4e8, 18 * rows * 2048),
        name="back",
    )(*weight_inputs, *attention_inputs, tokens, gains, second_gain, weights, mixed_grad)


def finish_kernel(output, input_grad, gains, qkv, down, up, *outs):
    turned = qkv[...].T
    outs[0][...] = output[...]
    outs[1][...] = input_grad[...]
    outs[2][...] = gains[...]
    outs[3][...] = turned[:144]
    outs[4][...] = turned[144:192]
    outs[5][...] = turned[192:]
    outs[6][...] = down[:, 768:]
    outs[7][...] = down[:, :768]
    outs[8][...] = up[:, :384]
    outs[9][...] = up[:, 384:]


def finish(*parts):
    rows, width = parts[0].shape
    shapes = ((8, 288), (144, 288), (48, 288), (48, 288), (144, 288), (144, 768), (288, 384), (288, 384))
    return pl.pallas_call(
        finish_kernel,
        out_shape=(jax.ShapeDtypeStruct((rows, width), BF16), jax.ShapeDtypeStruct((rows, width), F32))
        + tuple(jax.ShapeDtypeStruct(shape, F32) for shape in shapes),
        in_specs=vmem_specs(6),
        out_specs=tuple(vmem_specs(10)),
        cost_estimate=cost(1e6, 8e6),
        name="finish",
    )(*parts)


def permuted_device(
    tokens, prefix, gain_one, w_query, w_key, value_weight, w_out, gain_two, w_gate, w_up, w_down, cotangent
):
    tokens, cotangent = tokens[0], cotangent[0]
    half = HEAD_SIZE // 2
    frequency = ROTARY_BASE ** (-jnp.arange(half, dtype=F32) * 2.0 / HEAD_SIZE)
    (
        qkv,
        pairs,
        *weight_inputs,
        query,
        attended,
        log_total,
        gains,
        output,
        mixed_grad,
        attended_grad,
        second_gain,
        cosine,
        sine,
        limit,
    ) = front(
        prefix,
        jnp.tile(frequency, 4)[None, :],
        (w_query.T, w_key.T, value_weight.T, w_out.T, w_gate, w_up, w_down.T),
        jnp.stack([gain_one, gain_two]).astype(F32),
        tokens,
        cotangent,
    )
    grad_down_out, grad_up, grad_qkv, input_grad, gain_grads = back(
        weight_inputs,
        (query, attended, attended_grad, log_total, limit, cosine, sine, pairs),
        tokens,
        gains,
        second_gain,
        qkv,
        mixed_grad,
    )
    output, input_grad, gain_grads, query_t, key_t, value_t, out_t, down_t, gate, up = finish(
        output, input_grad, gain_grads, grad_qkv, grad_down_out, grad_up
    )
    return (
        output[None],
        input_grad[None],
        gain_grads[0],
        query_t.T,
        key_t.T,
        value_t.T,
        out_t.T,
        gain_grads[1],
        gate,
        up,
        down_t.T,
    )


def permute_plan_fits(mesh, tokens):
    return dict(mesh.shape) == {"seq": 4, "ctx": 8} and tokens.shape == (4, 2048, 1152)


def solution(mesh):
    placed = (
        P("seq", "ctx", None),
        P("seq"),
        P("seq"),
        P("seq", "ctx"),
        P("seq", "ctx"),
        P("seq", "ctx"),
        P("seq", "ctx"),
        P("seq"),
        P("seq", "ctx"),
        P("seq", "ctx"),
        P("seq", "ctx"),
        P("seq", "ctx", None),
    )

    def mapped(device_function):
        return jax.shard_map(
            device_function,
            mesh=mesh,
            in_specs=placed,
            out_specs=(
                P("seq", "ctx", None),
                P("seq", "ctx", None),
                P("seq"),
                P("seq", "ctx"),
                P("seq", "ctx"),
                P("seq", "ctx"),
                P("seq", "ctx"),
                P("seq"),
                P("seq", "ctx"),
                P("seq", "ctx"),
                P("seq", "ctx"),
            ),
            check_vma=False,
        )

    def layer(tokens, *rest):
        return mapped(permuted_device if permute_plan_fits(mesh, tokens) else per_device)(tokens, *rest)

    return layer
```
